32 devices in a mesh: groups: 2 (over y), ctx: 4 (over z), fsdp: 2 (over x), head: 2 (over core).
Axes of the slice: x: 2, y: 2, z: 4, core: 2. Of those that a mesh axis runs over, the one named last changes fastest.
Arguments:
- tokens: bfloat16 [1024, 2304], P(('groups', 'ctx')), parts along dimension 0, may hold values from -6 to 6
- w_query: bfloat16 [2304, 4096], P('ctx', ('fsdp', 'head')), may hold values from -0.125 to 0.125
- w_key: bfloat16 [2304, 4096], P('ctx', ('fsdp', 'head')), may hold values from -0.125 to 0.125
- w_value: bfloat16 [2304, 4096], P('ctx', ('fsdp', 'head')), may hold values from -0.125 to 0.125
- beta_logit: float32 [32, 1024], P(('fsdp', 'head'), ('groups', 'ctx')), parts along dimension 1, may hold values from -6 to 6
- log_decay: float32 [1024, 4096], P(('groups', 'ctx'), ('fsdp', 'head')), parts along dimension 0, may hold values from -0.6 to 0, as said below
- grad_out: bfloat16 [1024, 4096], P(('groups', 'ctx'), ('fsdp', 'head')), parts along dimension 0, may hold values from -6 to 6
Outputs:
- attn_out: bfloat16 [1024, 4096], P(('groups', 'ctx'), ('fsdp', 'head')), parts along dimension 0
- grad_w_query: float32 [4608, 4096], P(('groups', 'ctx'), ('fsdp', 'head')), parts along dimension 0
- grad_w_key: float32 [4608, 4096], P(('groups', 'ctx'), ('fsdp', 'head')), parts along dimension 0
- grad_w_value: float32 [4608, 4096], P(('groups', 'ctx'), ('fsdp', 'head')), parts along dimension 0
- grad_beta: float32 [32, 1024], P(('fsdp', 'head'), ('groups', 'ctx')), parts along dimension 1
- grad_decay: float32 [1024, 4096], P(('groups', 'ctx'), ('fsdp', 'head')), parts along dimension 0
The draws below stay inside these ranges and needn't reach their ends.
There are 2 independent parts, one for each index of `groups`. The reference program is written for one: setup_inputs(seed, part) draws one part's arguments, and reference() takes and returns one part's arrays. A program takes and returns all parts, laid end to end along the dimension named above; an argument that names none is the same for every part. Nothing has to cross between parts.
Inputs may be any that keep to these rules, and one draw needn't show every extreme that they name: `log_decay`: every entry is at most zero.
All inputs are finite; a program needn't handle non-finite values.
Results may differ from the reference program's by a relative error of at most 0.014.
Values may be sent and summed in bfloat16 or wider, within the bound.
No kernel may reach another device: no remote copies, remote signals or barrier semaphores. Data moves between devices by JAX's collectives and lax.ppermute only.
A program may use at most 128 MiB of HBM per device.

```python
import math
import jax
import jax.numpy as jnp
from jax import lax

D = 2304
H = 32
DK = 128
DV = 128
SPAN = 64
TOK_DEV = 128
TOKENS = 512
N_CTX = 4


def draw_log_decay(key, part):
    subkeys = jax.random.split(key, 8)
    slow_share = 0.5
    slow_head = jax.random.bernoulli(subkeys[0], slow_share, (H,))
    spread = jnp.exp(jax.random.uniform(subkeys[1], (H, DK), jnp.float32, math.log(0.25), 0.0))
    slow_rate = 0.8 / TOKENS * spread
    fast_rate = 1.0 / 40.0 * jnp.exp(jax.random.uniform(subkeys[2], (H, DK), jnp.float32, math.log(0.75), math.log(1.33)))
    base_rate = jnp.where(slow_head[:, None], slow_rate, fast_rate)
    shards = TOKENS // TOK_DEV
    shard_factor = jnp.exp(jax.random.uniform(subkeys[3], (shards, H), jnp.float32, math.log(0.7), math.log(1.4)))
    shard_factor = jnp.repeat(shard_factor, TOK_DEV, axis=0)
    jitter = jax.random.uniform(subkeys[4], (TOKENS, H, DK), jnp.float32, 0.5, 1.5)
    forgetting_speeds = base_rate[None, :, :] * shard_factor[:, :, None] * jitter
    middle = TOKENS // 2
    preceding_indices = jax.random.randint(subkeys[5], (H,), 0, middle)
    following_indices = jax.random.randint(subkeys[6], (H,), middle, TOKENS)
    discarded_proportion = jax.random.uniform(subkeys[7], (2, H), jnp.float32, 0.2, 0.4)
    element_indices = jnp.arange(TOKENS)[:, None]
    sequence_segments = jnp.where(element_indices == preceding_indices[None, :], jnp.log(1.0 - discarded_proportion[0])[None, :], 0.0)
    sequence_segments = sequence_segments + jnp.where(element_indices == following_indices[None, :], jnp.log(1.0 - discarded_proportion[1])[None, :], 0.0)
    forgetting_exponent = -forgetting_speeds + sequence_segments[:, :, None]
    return forgetting_exponent.reshape(TOKENS, H * DK).astype(jnp.float32)


def raised(drawn, rng, source, target, blocks, factor):
    def block_of(position):
        return (jnp.arange(drawn.shape[position]) // (drawn.shape[position] // blocks)).reshape((-1,) + (1,) * (drawn.ndim - 1 - position))

    near = jax.random.permutation(rng, blocks)[block_of(target)]
    far = (block_of(target) + blocks // 2) % blocks
    return jnp.where((block_of(source) == near) | (block_of(source) == far), factor * drawn, drawn)


def shard_levels(stream_key, extent, pieces, low, high):
    gain = 1.0
    for axis_at, shards_of in pieces:
        draws = jax.random.uniform(jax.random.fold_in(jax.random.fold_in(stream_key, 6), axis_at), (shards_of,), jnp.float32, low / len(pieces), high / len(pieces))
        gain = gain * jnp.repeat(jnp.exp(draws), extent[axis_at] // shards_of).reshape((-1,) + (1,) * (len(extent) - 1 - axis_at))
    return gain


def centred(stream_key, dims, width, most, cuts=(), held_as=jnp.bfloat16):
    values = jax.random.normal(stream_key, dims, jnp.float32) * width
    if len(cuts) > 0:
        values = shard_levels(stream_key, dims, cuts, -0.22, 0.18) * values
    return jnp.clip(values, min=-most, max=most).astype(held_as)


def bell_draw_with(stream_key, extent, deviation, limit, cuts, heavy, kind=jnp.bfloat16):
    entries = deviation * jax.random.normal(stream_key, extent, jnp.float32)
    if cuts:
        entries = entries * shard_levels(stream_key, extent, cuts, -0.22, 0.18)
    return jnp.clip(raised(entries, jax.random.fold_in(stream_key, 3), *heavy), -limit, limit).astype(kind)


def setup_inputs(seed: int = 0, part: int = 0) -> dict:
    key_list = jax.random.split(jax.random.key(seed), 8)
    part_keys = jax.random.split(jax.random.fold_in(key_list[7], part), 8)
    return {
        "tokens": bell_draw_with(part_keys[0], (TOKENS, D), 1.0, 6.0, ((0, 4),), (0, 1, 4, 2.0)),
        "w_query": centred(key_list[1], (D, H * DK), D ** -0.5, 0.125, ((0, 4), (1, 4))),
        "w_key": centred(key_list[2], (D, H * DK), D ** -0.5, 0.125, ((0, 4), (1, 4))),
        "w_value": centred(key_list[3], (D, H * DV), D ** -0.5, 0.125, ((0, 4), (1, 4))),
        "beta_logit": centred(part_keys[4], (H, TOKENS), 1.5, 6.0, ((0, 4), (1, 4)), jnp.float32),
        "log_decay": draw_log_decay(jax.random.fold_in(jax.random.fold_in(key_list[7], part), 71), part),
        "grad_out": centred(part_keys[6], (TOKENS, H * DV), 1.0, 6.0, ((0, 4), (1, 4))),
    }


epsilon = 1e-06

def normalize(vectors):
    return vectors * lax.rsqrt(lax.optimization_barrier(jnp.sum(vectors * vectors, axis=-1, keepdims=True)) + epsilon)

def heads_first(matrix, heads):
    return matrix.reshape(matrix.shape[0], heads, -1).transpose(1, 0, 2)

def span_step(memory, queries, key_vecs, val_vecs, strength, forgetting_exponent):
    largest_value = lax.Precision.HIGHEST
    length = queries.shape[1]
    cumulate = jnp.cumsum(forgetting_exponent, axis=1)
    growth = jnp.exp(cumulate)
    shrink = jnp.exp(-cumulate)
    key_up = key_vecs * growth
    key_down = key_vecs * shrink
    query_up = queries * growth
    row_ids = lax.broadcasted_iota(jnp.int32, (length, length), 0)
    col_ids = lax.broadcasted_iota(jnp.int32, (length, length), 1)
    strict = (row_ids > col_ids).astype(jnp.float32)
    within = (row_ids >= col_ids).astype(jnp.float32)
    affinity = jnp.einsum('bcd,bsd->bcs', key_up, key_down, precision=largest_value) * strict
    system = jnp.eye(length, dtype=jnp.float32) + strength[:, :, None] * affinity
    target = strength[:, :, None] * (val_vecs - jnp.einsum('bcd,bdw->bcw', key_up, memory, precision=largest_value))
    update = lax.linalg.triangular_solve(system, target, left_side=True, lower=True)
    scores = jnp.einsum('bcd,bsd->bcs', query_up, key_down, precision=largest_value) * within
    emitted = jnp.einsum('bcd,bdw->bcw', query_up, memory, precision=largest_value)
    emitted = emitted + jnp.einsum('bcs,bsw->bcw', scores, update, precision=largest_value)
    at_end = growth[:, -1, :]
    renewed = at_end[:, :, None] * memory + jnp.einsum('bsd,bsw->bdw', key_down * at_end[:, None, :], update, precision=largest_value)
    return (emitted, renewed)

def scan_spans(memory, queries, key_vecs, val_vecs, strength, forgetting_exponent):
    count = queries.shape[1] // SPAN

    def to_blocks(array):
        shaped = array.reshape((array.shape[0], count, SPAN) + array.shape[2:])
        return jnp.swapaxes(shaped, 0, 1)

    def advance(carried, blocks):
        emitted, renewed = span_step(carried, *blocks)
        return (renewed, emitted)
    blocks = (to_blocks(queries), to_blocks(key_vecs), to_blocks(val_vecs), to_blocks(strength), to_blocks(forgetting_exponent))
    final, emitted = lax.scan(advance, memory, blocks)
    emitted = jnp.swapaxes(emitted, 0, 1)
    return (emitted.reshape(emitted.shape[0], count * SPAN, emitted.shape[-1]), final)

def run_layer(query_raw, key_raw, value_raw, beta_logit, log_decay):
    queries = normalize(heads_first(query_raw, H))
    key_vecs = normalize(heads_first(key_raw, H))
    val_vecs = heads_first(value_raw, H)
    initial = jnp.zeros((H, DK, DV), jnp.float32)
    emitted, final = scan_spans(initial, queries, key_vecs, val_vecs, jax.nn.sigmoid(beta_logit), heads_first(log_decay, H))
    return emitted.transpose(1, 0, 2).reshape(emitted.shape[1], H * DV)

def reference(tokens, w_query, w_key, w_value, beta_logit, log_decay, grad_out):
    query_raw = jnp.dot(tokens.astype(jnp.float32), w_query.astype(jnp.float32), preferred_element_type=jnp.float32)
    key_raw = jnp.dot(tokens.astype(jnp.float32), w_key.astype(jnp.float32), preferred_element_type=jnp.float32)
    value_raw = jnp.dot(tokens.astype(jnp.float32), w_value.astype(jnp.float32), preferred_element_type=jnp.float32)
    mixed_out, pullback = jax.vjp(run_layer, query_raw, key_raw, value_raw, beta_logit, log_decay)
    d_query, d_key, d_value, grad_beta, grad_decay = pullback(grad_out.astype(jnp.float32))
    grad_projected = jnp.concatenate([d_query, d_key, d_value], axis=1).astype(jnp.bfloat16)
    tok_blocks = tokens.reshape(N_CTX, TOK_DEV, D)
    grad_blocks = grad_projected.reshape(N_CTX, TOK_DEV, grad_projected.shape[1])

    def accumulate(running, pairs):
        tok_block, grad_block = pairs
        term = jnp.dot(tok_block.T.astype(jnp.float32), grad_block.astype(jnp.float32), preferred_element_type=jnp.float32).astype(jnp.bfloat16)
        term = lax.optimization_barrier(term).astype(jnp.float32)
        return (running + term, None)
    start_sum = jnp.zeros((D, grad_projected.shape[1]), jnp.float32)
    summed, unused = lax.scan(accumulate, start_sum, (tok_blocks, grad_blocks))
    width_qk = H * DK
    return (mixed_out.astype(jnp.bfloat16), summed[:, :width_qk], summed[:, width_qk:2 * width_qk], summed[:, 2 * width_qk:], grad_beta, grad_decay)
```

```python
import jax
import jax.numpy as jnp
from jax import lax
from jax.experimental import pallas as pl
from jax.experimental.pallas import tpu as pltpu
from jax.sharding import PartitionSpec as P

DK = 128
DV = 128
SPAN = 64
CHUNK = 128

epsilon = 1e-06
HIGHEST = lax.Precision.HIGHEST


def dot_nn(a, b, precision=HIGHEST):
    return lax.dot_general(
        a, b, (((1,), (0,)), ((), ())), precision=precision, preferred_element_type=jnp.float32
    )


def dot_nt(a, b, precision=HIGHEST):
    return lax.dot_general(
        a, b, (((1,), (1,)), ((), ())), precision=precision, preferred_element_type=jnp.float32
    )


def dot_tn(a, b, precision=HIGHEST):
    return lax.dot_general(
        a, b, (((0,), (0,)), ((), ())), precision=precision, preferred_element_type=jnp.float32
    )


def head_kernel(raw_ref, decay_ref, logit_ref, cot_ref, out_ref, grad_ref, dlogit_ref, ddecay_ref):
    count = raw_ref.shape[0] // CHUNK
    spans = range(count)
    rows = lax.broadcasted_iota(jnp.int32, (CHUNK, CHUNK), 0)
    cols = lax.broadcasted_iota(jnp.int32, (CHUNK, CHUNK), 1)
    within = rows >= cols
    strict = rows > cols
    diagonal = rows == cols
    running = within.astype(jnp.float32)

    q, k, v, rq, rk, up, down, end = [], [], [], [], [], [], [], []
    qu, ku, kd, kend, beta_row, cot = [], [], [], [], [], []
    for n in spans:
        here = slice(n * CHUNK, (n + 1) * CHUNK)
        q_raw = raw_ref[here, 0:DK]
        k_raw = raw_ref[here, DK : 2 * DK]
        v.append(raw_ref[here, 2 * DK : 3 * DK])
        rq.append(lax.rsqrt(jnp.sum(q_raw * q_raw, axis=1, keepdims=True) + epsilon))
        rk.append(lax.rsqrt(jnp.sum(k_raw * k_raw, axis=1, keepdims=True) + epsilon))
        q.append(q_raw * rq[n])
        k.append(k_raw * rk[n])
        summed = dot_nn(running, decay_ref[here, :])
        up.append(jnp.exp(summed))
        down.append(jnp.exp(-summed))
        end.append(up[n][CHUNK - 1 : CHUNK, :])
        qu.append(q[n] * up[n])
        ku.append(k[n] * up[n])
        kd.append(k[n] * down[n])
        kend.append(kd[n] * end[n])
        beta_row.append(jax.nn.sigmoid(logit_ref[n : n + 1, :]))
        cot.append(cot_ref[here, :].astype(jnp.float32))

    scores, system, inverse = [], [], []
    for n in spans:
        pairs = dot_nt(jnp.concatenate([qu[n], ku[n]], axis=0), kd[n])
        scores.append(jnp.where(within, pairs[:CHUNK], 0.0))
        beta_col = jnp.transpose(jnp.broadcast_to(beta_row[n], (CHUNK, CHUNK)))
        system.append(jnp.where(strict, pairs[CHUNK:] * beta_col, 0.0))
        pair_block = (rows // 2) == (cols // 2)
        inverse.append(diagonal.astype(jnp.float32) - jnp.where(pair_block, system[n], 0.0))
    size = 2
    while size < CHUNK:
        joined = ((rows // (2 * size)) == (cols // (2 * size))) & ((rows // size) != (cols // size))
        halves = [dot_nn(jnp.where(joined, system[n], 0.0), inverse[n]) for n in spans]
        inverse = [inverse[n] - dot_nn(inverse[n], halves[n]) for n in spans]
        size *= 2

    solve = [inverse[n] * beta_row[n] for n in spans]
    wu = [dot_nn(solve[n], jnp.concatenate([ku[n], v[n]], axis=1)) for n in spans]
    pwu = [dot_nn(scores[n], wu[n]) for n in spans]
    kwu = [dot_tn(kend[n], wu[n]) for n in spans]
    query_through = [qu[n] - pwu[n][:, :DK] for n in spans]
    transit = [
        jnp.where(diagonal, jnp.broadcast_to(end[n], (DK, DK)), 0.0) - kwu[n][:, :DK] for n in spans
    ]
    sent = [dot_tn(query_through[n], cot[n]) for n in spans]

    state = [None] * (count + 1)
    adjoint = [None] * (count + 1)
    for n in spans:
        m = count - 1 - n
        own = kwu[n][:, DK:]
        state[n + 1] = own if n == 0 else dot_nn(transit[n], state[n]) + own
        adjoint[m] = sent[m] if n == 0 else dot_tn(transit[m], adjoint[m + 1]) + sent[m]

    for n in spans:
        here = slice(n * CHUNK, (n + 1) * CHUNK)
        w = wu[n][:, :DK]
        update = wu[n][:, DK:]
        emitted = pwu[n][:, DK:]
        d_update = dot_tn(scores[n], cot[n])
        if n > 0:
            emitted = emitted + dot_nn(query_through[n], state[n])
            update = update - dot_nn(w, state[n])
        if n < count - 1:
            d_update = d_update + dot_nn(kend[n], adjoint[n + 1])
        out_ref[here, :] = emitted.astype(out_ref.dtype)
        d_value = dot_tn(solve[n], d_update)
        both = jnp.concatenate([cot[n], -d_value], axis=0)
        pairs = dot_nt(both, update)
        d_pairs = jnp.concatenate(
            [jnp.where(within, pairs[:CHUNK], 0.0), jnp.where(strict, pairs[CHUNK:], 0.0)], axis=0
        )
        d_up = dot_nn(d_pairs, kd[n])
        if n > 0:
            d_up = d_up + dot_nt(both, state[n])
        d_qu, d_ku = d_up[:CHUNK], d_up[CHUNK:]
        d_kd = dot_tn(d_pairs, jnp.concatenate([qu[n], ku[n]], axis=0))
        d_k = d_ku * up[n] + d_kd * down[n]
        d_sum = d_qu * qu[n] + d_ku * ku[n] - d_kd * kd[n]
        d_decay_end = jnp.zeros((1, DK), jnp.float32)
        if n < count - 1:
            d_kend = dot_nt(update, adjoint[n + 1])
            d_k = d_k + d_kend * (end[n] * down[n])
            ended = d_kend * kend[n]
            d_sum = d_sum - ended
            d_decay_end = jnp.sum(ended, axis=0, keepdims=True)
            if n > 0:
                kept = jnp.sum(jnp.transpose(adjoint[n + 1] * state[n]), axis=0, keepdims=True)
                d_decay_end = d_decay_end + end[n] * kept
        ddecay_ref[here, :] = dot_tn(running, d_sum) + d_decay_end
        d_q = d_qu * up[n]
        d_q = rq[n] * (d_q - q[n] * jnp.sum(q[n] * d_q, axis=1, keepdims=True))
        d_k = rk[n] * (d_k - k[n] * jnp.sum(k[n] * d_k, axis=1, keepdims=True))
        grad_ref[here, 0:DK] = d_q.astype(grad_ref.dtype)
        grad_ref[here, DK : 2 * DK] = d_k.astype(grad_ref.dtype)
        grad_ref[here, 2 * DK : 3 * DK] = d_value.astype(grad_ref.dtype)
        aligned = jnp.sum(jnp.transpose(d_value * update), axis=0, keepdims=True)
        dlogit_ref[n : n + 1, :] = aligned * jnp.exp(-logit_ref[n : n + 1, :])


def run_head(raw, decay, logit, cot):
    tokens = raw.shape[0]
    whole = pl.BlockSpec(memory_space=pltpu.VMEM)
    return pl.pallas_call(
        head_kernel,
        out_shape=(
            jax.ShapeDtypeStruct((tokens, DV), jnp.bfloat16),
            jax.ShapeDtypeStruct((tokens, 2 * DK + DV), jnp.bfloat16),
            jax.ShapeDtypeStruct((tokens // CHUNK, CHUNK), jnp.float32),
            jax.ShapeDtypeStruct((tokens, DK), jnp.float32),
        ),
        in_specs=[whole] * 4,
        out_specs=(whole,) * 4,
        name="head",
    )(raw, decay, logit, cot)


def swap_ctx(x):
    return lax.all_to_all(x, "ctx", 0, 0)


def spread(x, axis):
    count = lax.axis_size(axis)
    return lax.all_to_all(jnp.broadcast_to(x[None], (count,) + x.shape), axis, 0, 0)


def head_split(tokens, w_query, w_key, w_value, beta_logit, log_decay, grad_out):
    ctx = lax.axis_size("ctx")
    place = lax.axis_index("ctx")
    group = lax.axis_index("groups")
    length, depth = tokens.shape
    rows, columns = w_query.shape
    per = columns // DK // ctx
    share = depth // ctx

    blocks = tokens.reshape(length, ctx, share).transpose(1, 0, 2)
    mine = lax.dynamic_index_in_dim(blocks, lax.axis_index("fsdp") * lax.axis_size("head") + lax.axis_index("head"), 0, False)
    mine = spread(mine, "ctx").reshape(ctx * length, share)
    all_blocks = spread(mine, ("fsdp", "head"))

    def for_slot(x, slot):
        parted = x.reshape(x.shape[0], ctx, per, DK)
        return lax.dynamic_index_in_dim(parted, slot, 2, False)

    joined = jnp.concatenate(
        [for_slot(w, group) for w in (w_query, w_key, w_value)], axis=2
    ).transpose(1, 0, 2)
    w_first = swap_ctx(joined)
    w_second = lax.ppermute(w_first, "groups", [(0, 1), (1, 0)])

    def by_slot(x):
        parted = swap_ctx(x.reshape(length, ctx, per * DK).transpose(1, 0, 2))
        parted = parted.reshape(ctx * length, per, DK)
        return tuple(lax.dynamic_index_in_dim(parted, s, 1, False) for s in (group, 1 - group))

    decays = by_slot(log_decay)
    cots = by_slot(grad_out)
    logits = swap_ctx(beta_logit.reshape(ctx, per, length))
    logits = tuple(lax.dynamic_index_in_dim(logits, s, 1, False) for s in (group, 1 - group))

    done = []
    for weights, decay, logit, cot in zip((w_first, w_second), decays, logits, cots):
        raw = jnp.einsum(
            "btk,bkc->tc", all_blocks, weights, preferred_element_type=jnp.float32
        )
        done.append(run_head(raw, decay, logit, cot))

    def back(first, second):
        pair = jnp.stack([jnp.where(group == 0, first, second), jnp.where(group == 0, second, first)], axis=1)
        parted = swap_ctx(pair.reshape(ctx, length, per * DK))
        return parted.transpose(1, 0, 2).reshape(length, columns)

    attn_out = back(done[0][0], done[1][0])
    grad_decay = back(done[0][3], done[1][3])
    pair = jnp.stack(
        [jnp.where(group == 0, done[0][2], done[1][2]), jnp.where(group == 0, done[1][2], done[0][2])], axis=1
    )
    grad_beta = swap_ctx(pair).reshape(ctx * per, length)

    own_columns = lax.dynamic_index_in_dim(all_blocks, place, 0, False)
    grads = []
    for slot in range(2):
        gathered = spread(done[slot][1], "ctx")
        total = 0.0
        for n in range(ctx):
            here = slice(n * length, (n + 1) * length)
            product = jnp.einsum(
                "td,xtc->dxc", own_columns[here], gathered[:, here], preferred_element_type=jnp.float32
            )
            total = total + product.astype(jnp.bfloat16).astype(jnp.float32)
        grads.append(total)
    results = []
    for part in range(3):
        first, second = (g[:, :, part * DK : (part + 1) * DK] for g in grads)
        pair = jnp.stack([jnp.where(group == 0, first, second), jnp.where(group == 0, second, first)], axis=2)
        results.append(pair.reshape(rows, columns))
    return (attn_out, results[0], results[1], results[2], grad_beta, grad_decay)


def prefix_2(x, axis, join, neutral, backward):
    count = lax.axis_size(axis)
    place = lax.axis_index(axis)
    ahead = count - 1 - place if backward else place
    gathered = jax.tree.map(
        lambda a, kind: lax.all_gather(a.astype(kind), axis), x, (jnp.bfloat16, jnp.bfloat16)
    )
    state = jax.tree.map(lambda a, e: jnp.zeros_like(a) + jnp.asarray(e, a.dtype), x, neutral)

    def one(hop, state):
        source = count - 1 - hop if backward else hop
        return join(
            state,
            jax.tree.map(
                lambda a, own: lax.dynamic_index_in_dim(a, source, 0, False).astype(own.dtype),
                gathered,
                x,
            ),
        )

    return lax.fori_loop(0, ahead, one, state)


def normalize(vectors):
    return vectors * lax.rsqrt(jnp.sum(vectors * vectors, axis=-1, keepdims=True) + epsilon)


def heads_first(matrix, heads):
    return matrix.reshape(matrix.shape[0], heads, -1).transpose(1, 0, 2)


def span_step(memory, queries, key_vecs, val_vecs, strength, forgetting_exponent):
    largest_value = lax.Precision.HIGHEST
    length = queries.shape[1]
    cumulate = jnp.cumsum(forgetting_exponent, axis=1)
    growth = jnp.exp(cumulate)
    shrink = jnp.exp(-cumulate)
    key_up = key_vecs * growth
    key_down = key_vecs * shrink
    query_up = queries * growth
    row_ids = lax.broadcasted_iota(jnp.int32, (length, length), 0)
    col_ids = lax.broadcasted_iota(jnp.int32, (length, length), 1)
    strict = (row_ids > col_ids).astype(jnp.float32)
    within = (row_ids >= col_ids).astype(jnp.float32)
    affinity = jnp.einsum("bcd,bsd->bcs", key_up, key_down, precision=largest_value) * strict
    system = jnp.eye(length, dtype=jnp.float32) + strength[:, :, None] * affinity
    target = strength[:, :, None] * (
        val_vecs - jnp.einsum("bcd,bdw->bcw", key_up, memory, precision=largest_value)
    )
    update = lax.linalg.triangular_solve(system, target, left_side=True, lower=True)
    scores = jnp.einsum("bcd,bsd->bcs", query_up, key_down, precision=largest_value) * within
    emitted = jnp.einsum("bcd,bdw->bcw", query_up, memory, precision=largest_value)
    emitted = emitted + jnp.einsum("bcs,bsw->bcw", scores, update, precision=largest_value)
    at_end = growth[:, -1, :]
    renewed = at_end[:, :, None] * memory + jnp.einsum(
        "bsd,bsw->bdw", key_down * at_end[:, None, :], update, precision=largest_value
    )
    return (emitted, renewed)


def scan_spans(memory, queries, key_vecs, val_vecs, strength, forgetting_exponent):
    count = queries.shape[1] // SPAN

    def to_blocks(array):
        shaped = array.reshape((array.shape[0], count, SPAN) + array.shape[2:])
        return jnp.swapaxes(shaped, 0, 1)

    def advance(carried, blocks):
        emitted, renewed = span_step(carried, *blocks)
        return (renewed, emitted)

    blocks = (
        to_blocks(queries),
        to_blocks(key_vecs),
        to_blocks(val_vecs),
        to_blocks(strength),
        to_blocks(forgetting_exponent),
    )
    final, emitted = lax.scan(advance, memory, blocks)
    emitted = jnp.swapaxes(emitted, 0, 1)
    return (emitted.reshape(emitted.shape[0], count * SPAN, emitted.shape[-1]), final)


def compose(earlier, later):
    largest_value = lax.Precision.HIGHEST
    joined = jnp.einsum("hij,hjk->hik", later[0], earlier[0], precision=largest_value)
    shifted = jnp.einsum("hij,hjv->hiv", later[0], earlier[1], precision=largest_value) + later[1]
    return (joined, shifted)


def per_device(tokens, w_query, w_key, w_value, beta_logit, log_decay, grad_out):
    largest_value = lax.Precision.HIGHEST
    length = tokens.shape[0]
    columns = w_query.shape[1]
    heads = columns // DK
    shard_rows = (
        lax.all_gather(w_query, "ctx", axis=0, tiled=True),
        lax.all_gather(w_key, "ctx", axis=0, tiled=True),
        lax.all_gather(w_value, "ctx", axis=0, tiled=True),
    )
    window = tokens
    query_raw, key_raw, value_raw = tuple(
        (jnp.dot(window, weights, preferred_element_type=jnp.float32) for weights in shard_rows)
    )

    def shard_pass(query_in, key_in, value_in, logits, log_gates):
        queries = normalize(heads_first(query_in, heads))
        key_vecs = normalize(heads_first(key_in, heads))
        val_vecs = heads_first(value_in, heads)
        widened = jnp.concatenate([jnp.zeros((heads, length, DK), jnp.float32), val_vecs], axis=2)
        initial = jnp.concatenate(
            [
                jnp.broadcast_to(jnp.eye(DK, dtype=jnp.float32), (heads, DK, DK)),
                jnp.zeros((heads, DK, DV), jnp.float32),
            ],
            axis=2,
        )
        return scan_spans(
            initial,
            queries,
            key_vecs,
            widened,
            jax.nn.sigmoid(logits),
            heads_first(log_gates, heads),
        )

    (mixed, final), pullback = jax.vjp(
        shard_pass, query_raw, key_raw, value_raw, beta_logit, log_decay
    )
    transit = final[:, :, :DK]
    offset = final[:, :, DK:]
    query_carried_over = mixed[:, :, :DK]
    local_output = mixed[:, :, DK:]
    output_cotangent = grad_out.reshape(length, heads, DV).transpose(1, 0, 2).astype(jnp.float32)
    contribution = jnp.einsum(
        "mij,mif->mjf", query_carried_over, output_cotangent, precision=largest_value
    )
    identity = (
        jnp.broadcast_to(jnp.eye(DK, dtype=jnp.float32), (heads, DK, DK)),
        jnp.zeros((heads, DK, DV), jnp.float32),
    )
    prefix = prefix_2((transit, offset), "ctx", compose, identity, False)
    incoming_state = prefix[1]
    suffix = prefix_2((jnp.swapaxes(transit, 1, 2), contribution), "ctx", compose, identity, True)
    adjoint_state = suffix[1]
    complete_output = local_output + jnp.einsum(
        "npg,ngj->npj", query_carried_over, incoming_state, precision=largest_value
    )
    attn_out = complete_output.transpose(1, 0, 2).reshape(length, heads * DV).astype(jnp.bfloat16)
    d_mixed = jnp.concatenate(
        [
            jnp.einsum("efu,egu->efg", output_cotangent, incoming_state, precision=largest_value),
            output_cotangent,
        ],
        axis=2,
    )
    d_final = jnp.concatenate(
        [
            jnp.einsum("pgx,pcx->pgc", adjoint_state, incoming_state, precision=largest_value),
            adjoint_state,
        ],
        axis=2,
    )
    d_query, d_key, d_value, grad_beta, grad_decay = pullback((d_mixed, d_final))
    grad_projected = jnp.concatenate([d_query, d_key, d_value], axis=1).astype(jnp.bfloat16)
    window = tokens
    summed = lax.psum_scatter(
        jnp.einsum("td,tc->dc", window, grad_projected, preferred_element_type=jnp.float32).astype(
            jnp.bfloat16
        ),
        "ctx",
        scatter_dimension=0,
        tiled=True,
    ).astype(jnp.float32)
    return (
        attn_out,
        summed[:, :columns],
        summed[:, columns : 2 * columns],
        summed[:, 2 * columns :],
        grad_beta,
        grad_decay,
    )


def device_program(tokens, w_query, *rest):
    ctx, shared = lax.axis_size("ctx"), lax.axis_size("fsdp") * lax.axis_size("head")
    heads = w_query.shape[1] // DK
    split = heads == 2 * ctx and lax.axis_size("groups") == 2 and shared == ctx
    split = split and tokens.shape[0] == CHUNK and w_query.shape[0] * ctx == tokens.shape[1]
    return (head_split if split else per_device)(tokens, w_query, *rest)


def solution(mesh):
    return jax.shard_map(
        device_program,
        mesh=mesh,
        in_specs=(
            P(("groups", "ctx"), None),
            P("ctx", ("fsdp", "head")),
            P("ctx", ("fsdp", "head")),
            P("ctx", ("fsdp", "head")),
            P(("fsdp", "head"), ("groups", "ctx")),
            P(("groups", "ctx"), ("fsdp", "head")),
            P(("groups", "ctx"), ("fsdp", "head")),
        ),
        out_specs=(
            P(("groups", "ctx"), ("fsdp", "head")),
            P(("groups", "ctx"), ("fsdp", "head")),
            P(("groups", "ctx"), ("fsdp", "head")),
            P(("groups", "ctx"), ("fsdp", "head")),
            P(("fsdp", "head"), ("groups", "ctx")),
            P(("groups", "ctx"), ("fsdp", "head")),
        ),
        check_vma=False,
    )
```

```python
import functools

import jax
import jax.numpy as jnp
from jax import lax
from jax.experimental import pallas as pl
from jax.experimental.pallas import tpu as pltpu
from jax.sharding import PartitionSpec as P

DK = 128
DV = 128
SPAN = 64
CHUNK = 128
TAIL = 16
HEAD_COLUMNS = 2 * DK + DV

epsilon = 1e-06
HIGHEST = lax.Precision.HIGHEST
NN = (((1,), (0,)), ((), ()))
NT = (((1,), (1,)), ((), ()))
TN = (((0,), (0,)), ((), ()))


def narrow(x):
    return x.astype(jnp.bfloat16)


def dot(a, b, dims, passes):
    if passes == 6:
        return lax.dot_general(a, b, dims, precision=HIGHEST, preferred_element_type=jnp.float32)
    a_high, b_high = narrow(a), narrow(b)
    total = lax.dot_general(a_high, b_high, dims, preferred_element_type=jnp.float32)
    if passes >= 3:
        a_low = narrow(a - a_high.astype(jnp.float32))
        b_low = narrow(b - b_high.astype(jnp.float32))
        total = total + lax.dot_general(a_high, b_low, dims, preferred_element_type=jnp.float32)
        total = total + lax.dot_general(a_low, b_high, dims, preferred_element_type=jnp.float32)
    return total


PASSES = dict(
    decay=6, pairs=6, inverse=6, solve=6, read=6, carry=6, sent=6, scan=6, emit=6, update=6,
    d_update=6, d_value=6, d_pairs=6, d_up=6, d_up_state=6, d_kd=6, d_kend=6, d_decay=6,
)


def run(name, a, b, dims):
    return dot(a, b, dims, PASSES[name])


def recurrence(raw_ref, decay_ref, logit_ref, cot_ref, out_ref, grad_ref, dlogit_ref, ddecay_ref):
    count = raw_ref.shape[0] // CHUNK
    spans = range(count)
    rows = lax.broadcasted_iota(jnp.int32, (CHUNK, CHUNK), 0)
    cols = lax.broadcasted_iota(jnp.int32, (CHUNK, CHUNK), 1)
    within = rows >= cols
    strict = rows > cols
    diagonal = rows == cols
    running = within.astype(jnp.float32)

    q, k, v, rq, rk, up, down, end = [], [], [], [], [], [], [], []
    qu, ku, kd, kend, beta_row, cot = [], [], [], [], [], []
    for n in spans:
        here = slice(n * CHUNK, (n + 1) * CHUNK)
        q_raw = raw_ref[here, 0:DK]
        k_raw = raw_ref[here, DK : 2 * DK]
        v.append(raw_ref[here, 2 * DK : 3 * DK])
        rq.append(lax.rsqrt(jnp.sum(q_raw * q_raw, axis=1, keepdims=True) + epsilon))
        rk.append(lax.rsqrt(jnp.sum(k_raw * k_raw, axis=1, keepdims=True) + epsilon))
        q.append(q_raw * rq[n])
        k.append(k_raw * rk[n])
        summed = run("decay", running, decay_ref[here, :], NN)
        up.append(jnp.exp(summed))
        down.append(jnp.exp(-summed))
        end.append(up[n][CHUNK - 1 : CHUNK, :])
        qu.append(q[n] * up[n])
        ku.append(k[n] * up[n])
        kd.append(k[n] * down[n])
        kend.append(kd[n] * end[n])
        beta_row.append(jax.nn.sigmoid(logit_ref[n : n + 1, :]))
        cot.append(cot_ref[here, :])

    scores, system, inverse = [], [], []
    for n in spans:
        pairs = run("pairs", jnp.concatenate([qu[n], ku[n]], axis=0), kd[n], NT)
        scores.append(jnp.where(within, pairs[:CHUNK], 0.0))
        beta_col = jnp.transpose(jnp.broadcast_to(beta_row[n], (CHUNK, CHUNK)))
        system.append(jnp.where(strict, pairs[CHUNK:] * beta_col, 0.0))
        pair_block = (rows // 2) == (cols // 2)
        inverse.append(diagonal.astype(jnp.float32) - jnp.where(pair_block, system[n], 0.0))
    size = 2
    while size < CHUNK:
        joined = ((rows // (2 * size)) == (cols // (2 * size))) & ((rows // size) != (cols // size))
        halves = [run("inverse", jnp.where(joined, system[n], 0.0), inverse[n], NN) for n in spans]
        inverse = [inverse[n] - run("inverse", inverse[n], halves[n], NN) for n in spans]
        size *= 2

    solve = [inverse[n] * beta_row[n] for n in spans]
    wu = [run("solve", solve[n], jnp.concatenate([ku[n], v[n]], axis=1), NN) for n in spans]
    pwu = [run("read", scores[n], wu[n], NN) for n in spans]
    kwu = [run("carry", kend[n], wu[n], TN) for n in spans]
    query_through = [qu[n] - pwu[n][:, :DK] for n in spans]
    transit = [
        jnp.where(diagonal, jnp.broadcast_to(end[n], (DK, DK)), 0.0) - kwu[n][:, :DK] for n in spans
    ]
    sent = [run("sent", query_through[n], cot[n], TN) for n in spans]

    state = [None] * (count + 1)
    adjoint = [None] * (count + 1)
    for n in spans:
        m = count - 1 - n
        own = kwu[n][:, DK:]
        state[n + 1] = own if n == 0 else run("scan", transit[n], state[n], NN) + own
        adjoint[m] = sent[m] if n == 0 else run("scan", transit[m], adjoint[m + 1], TN) + sent[m]

    for n in spans:
        here = slice(n * CHUNK, (n + 1) * CHUNK)
        w = wu[n][:, :DK]
        update = wu[n][:, DK:]
        emitted = pwu[n][:, DK:]
        d_update = run("d_update", scores[n], cot[n], TN)
        if n > 0:
            emitted = emitted + run("emit", query_through[n], state[n], NN)
            update = update - run("update", w, state[n], NN)
        if n < count - 1:
            d_update = d_update + run("d_update", kend[n], adjoint[n + 1], NN)
        out_ref[n] = emitted.astype(out_ref.dtype)
        d_value = run("d_value", solve[n], d_update, TN)
        both = jnp.concatenate([cot[n], -d_value], axis=0)
        pairs = run("d_pairs", both, update, NT)
        d_pairs = jnp.concatenate(
            [jnp.where(within, pairs[:CHUNK], 0.0), jnp.where(strict, pairs[CHUNK:], 0.0)], axis=0
        )
        d_up = run("d_up", d_pairs, kd[n], NN)
        if n > 0:
            d_up = d_up + run("d_up_state", both, state[n], NT)
        d_qu, d_ku = d_up[:CHUNK], d_up[CHUNK:]
        d_kd = run("d_kd", d_pairs, jnp.concatenate([qu[n], ku[n]], axis=0), TN)
        d_k = d_ku * up[n] + d_kd * down[n]
        d_sum = d_qu * qu[n] + d_ku * ku[n] - d_kd * kd[n]
        d_decay_end = jnp.zeros((1, DK), jnp.float32)
        if n < count - 1:
            d_kend = run("d_kend", update, adjoint[n + 1], NT)
            d_k = d_k + d_kend * (end[n] * down[n])
            ended = d_kend * kend[n]
            d_sum = d_sum - ended
            d_decay_end = jnp.sum(ended, axis=0, keepdims=True)
            if n > 0:
                kept = jnp.sum(jnp.transpose(adjoint[n + 1] * state[n]), axis=0, keepdims=True)
                d_decay_end = d_decay_end + end[n] * kept
        ddecay_ref[n] = (run("d_decay", running, d_sum, TN) + d_decay_end).astype(ddecay_ref.dtype)
        d_q = d_qu * up[n]
        d_q = rq[n] * (d_q - q[n] * jnp.sum(q[n] * d_q, axis=1, keepdims=True))
        d_k = rk[n] * (d_k - k[n] * jnp.sum(k[n] * d_k, axis=1, keepdims=True))
        grad_ref[here, 0:DK] = d_q.astype(grad_ref.dtype)
        grad_ref[here, DK : 2 * DK] = d_k.astype(grad_ref.dtype)
        grad_ref[here, 2 * DK : 3 * DK] = d_value.astype(grad_ref.dtype)
        aligned = jnp.sum(jnp.transpose(d_value * update), axis=0, keepdims=True)
        dlogit_ref[n : n + 1, :] = aligned * jnp.exp(-logit_ref[n : n + 1, :])


def split_two(x):
    high = narrow(x)
    return high, narrow(x - high.astype(jnp.float32))


def tail_rows(x):
    high, low = split_two(x)
    index = lax.broadcasted_iota(jnp.int32, (TAIL, x.shape[1]), 0)
    high = jnp.broadcast_to(high.astype(jnp.float32), index.shape)
    low = jnp.broadcast_to(low.astype(jnp.float32), index.shape)
    return narrow(jnp.where(index == 0, high, jnp.where(index == 1, low, 0.0)))


def lanes(start):
    return pl.ds(pl.multiple_of(start, DK), DK)


def pack_small_kernel(where_ref, tokens_ref, decay_ref, cot_ref, logit_ref, tok_ref, *x_refs):
    ctx = len(x_refs)
    place, block = where_ref[0], where_ref[2]
    share = tok_ref.shape[1]
    for j in range(tokens_ref.shape[1] // share):

        @pl.when(block == j)
        def _(j=j):
            tok_ref[...] = tokens_ref[:, j * share : (j + 1) * share]

    for d in range(ctx):
        target = lax.rem(place + d, ctx)
        for s in range(2):
            lane = slice(s * DK, (s + 1) * DK)
            column = lanes((2 * target + s) * DK)
            x_refs[d][0:CHUNK, lane] = narrow(decay_ref[:, column])
            x_refs[d][CHUNK : 2 * CHUNK, lane] = cot_ref[:, column]
            x_refs[d][2 * CHUNK :, lane] = tail_rows(logit_ref[pl.ds(2 * target + s, 1), :])


def pack_weights_kernel(where_ref, wq_ref, wk_ref, wv_ref, *out_refs):
    ctx = len(out_refs) // 2
    place, group = where_ref[0], where_ref[1]
    half = wq_ref.shape[0] // 2
    upper = pl.ds(pl.multiple_of(group * half, 32), half)
    for s in range(2):
        for d in range(ctx):
            target = lax.rem(place + d, ctx)
            column = lanes((2 * target + s) * DK)
            for part, ref in enumerate((wq_ref, wk_ref, wv_ref)):
                rows = slice(None) if d == 0 else upper
                out_refs[s * ctx + d][:, part * DK : (part + 1) * DK] = ref[rows, column]


def head_kernel(ctx, slot, where_ref, *refs):
    tok_refs, refs = refs[:4], refs[4:]
    own_ref, refs = refs[0], refs[1:]
    direct, refs = refs[: ctx - 1], refs[ctx - 1 :]
    swapped, refs = refs[: ctx - 1], refs[ctx - 1 :]
    x_refs, refs = refs[:ctx], refs[ctx:]
    grad_ref, back_refs = refs[0], refs[1 : 1 + ctx]
    w, raw, decay, cot, logit, out, dlogit, ddecay = refs[1 + ctx :]
    place, group = where_ref[0], where_ref[1]
    share = own_ref.shape[0]
    half = share // 2
    w[pl.ds(pl.multiple_of(place * share, 32), share), :] = own_ref[...]
    lane = slice(slot * DK, (slot + 1) * DK)
    for d in range(ctx):
        source = lax.rem(place + ctx - d, ctx)
        if d > 0:
            for kind, ref in ((group, direct[d - 1]), (1 - group, swapped[d - 1])):
                w[pl.ds(pl.multiple_of(source * share + kind * half, 32), half), :] = ref[...]
        rows = pl.ds(pl.multiple_of(source * CHUNK, CHUNK), CHUNK)
        decay[rows, :] = x_refs[d][0:CHUNK, lane].astype(jnp.float32)
        cot[rows, :] = x_refs[d][CHUNK : 2 * CHUNK, lane].astype(jnp.float32)
        tail = x_refs[d][2 * CHUNK :, lane].astype(jnp.float32)
        logit[pl.ds(source, 1), :] = tail[0:1] + tail[1:2]
    projected = 0.0
    for j in range(4):
        block = where_ref[2 + j]
        projected = projected + lax.dot_general(
            tok_refs[j][...],
            w[pl.ds(pl.multiple_of(block * share, 32), share), :],
            NN,
            preferred_element_type=jnp.float32,
        )
    for d in range(ctx):
        source = lax.rem(place + ctx - d, ctx)
        raw[pl.ds(pl.multiple_of(source * CHUNK, CHUNK), CHUNK), :] = projected[d * CHUNK : (d + 1) * CHUNK]
    recurrence(raw, decay, logit, cot, out, grad_ref, dlogit, ddecay)
    for d in range(ctx):
        target = lax.rem(place + d, ctx)
        back_refs[d][0:CHUNK, :] = out[target]
        back_refs[d][CHUNK : 2 * CHUNK, :] = ddecay[target]
        back_refs[d][2 * CHUNK :, :] = tail_rows(dlogit[pl.ds(target, 1), :])


def weight_gradient_kernel(ctx, slot, where_ref, own_ref, *refs):
    grad_refs, refs = refs[:ctx], refs[ctx:]
    out_refs = refs[-3:]
    for d in range(ctx):

        @pl.when(pl.program_id(0) == d)
        def _(d=d):
            product = lax.dot_general(own_ref[...], grad_refs[d][...], TN, preferred_element_type=jnp.float32)
            for part in range(3):
                out_refs[part][...] = product[:, part * DK : (part + 1) * DK]


def unpack_kernel(ctx, where_ref, *refs):
    backs, (out_ref, dlogit_ref, ddecay_ref) = refs[: 2 * ctx], refs[2 * ctx :]
    place = where_ref[0]
    for s in range(2):
        for d in range(ctx):
            source = lax.rem(place + ctx - d, ctx)
            ref = backs[s * ctx + d]
            column = lanes((2 * source + s) * DK)
            out_ref[:, column] = ref[0:CHUNK, :]
            ddecay_ref[:, column] = ref[CHUNK : 2 * CHUNK, :].astype(jnp.float32)
            tail = ref[2 * CHUNK :, :].astype(jnp.float32)
            dlogit_ref[pl.ds(2 * source + s, 1), :] = tail[0:1] + tail[1:2]


def head_split(tokens, w_query, w_key, w_value, beta_logit, log_decay, grad_out):
    ctx = lax.axis_size("ctx")
    place = lax.axis_index("ctx")
    group = lax.axis_index("groups")
    across, core = lax.axis_index("fsdp"), lax.axis_index("head")
    length, depth = tokens.shape
    share, columns = w_query.shape
    total = ctx * length
    bf16, f32 = jnp.bfloat16, jnp.float32
    whole = pl.BlockSpec(memory_space=pltpu.VMEM)
    scalars = pl.BlockSpec(memory_space=pltpu.SMEM)
    own_block = 2 * across + core
    where = jnp.stack(
        [place, group, own_block, 2 * (1 - across) + core, 2 * across + 1 - core, 2 * (1 - across) + 1 - core]
    ).astype(jnp.int32)

    def shape(dims, kind):
        return jax.ShapeDtypeStruct(dims, kind)

    def along(x, axis, hop):
        count = lax.axis_size(axis)
        return lax.ppermute(x, axis, [(i, (i + hop) % count) for i in range(count)])

    tok, *small = pl.pallas_call(
        pack_small_kernel,
        out_shape=[shape((length, share), bf16)] + [shape((2 * CHUNK + TAIL, 2 * DK), bf16)] * ctx,
        in_specs=[scalars] + [whole] * 4,
        out_specs=[whole] * (1 + ctx),
        name="pack_small",
    )(where, tokens, log_decay, grad_out, beta_logit)
    packed = pl.pallas_call(
        pack_weights_kernel,
        out_shape=([shape((share, HEAD_COLUMNS), bf16)] + [shape((share // 2, HEAD_COLUMNS), bf16)] * (ctx - 1)) * 2,
        in_specs=[scalars] + [whole] * 3,
        out_specs=[whole] * (2 * ctx),
        name="pack_weights",
    )(where, w_query, w_key, w_value)

    tok = jnp.concatenate([tok] + [along(tok, "ctx", d) for d in range(1, ctx)], axis=0)
    tok_x = along(tok, "fsdp", 1)
    toks = (tok, tok_x, along(tok, "head", 1), along(tok_x, "head", 1))
    small = [small[0]] + [along(small[d], "ctx", d) for d in range(1, ctx)]

    done = []
    for slot in range(2):
        own, *away = packed[slot * ctx : (slot + 1) * ctx]
        direct = [along(x, "ctx", d + 1) for d, x in enumerate(away)]
        swapped = [along(x, "groups", 1) for x in direct]
        grad, *backs = pl.pallas_call(
            functools.partial(head_kernel, ctx, slot),
            out_shape=[shape((total, HEAD_COLUMNS), bf16)] + [shape((2 * CHUNK + TAIL, DK), bf16)] * ctx,
            in_specs=[scalars] + [whole] * (4 + 1 + 2 * (ctx - 1) + ctx),
            out_specs=[whole] * (1 + ctx),
            scratch_shapes=[
                pltpu.VMEM((depth, HEAD_COLUMNS), bf16),
                pltpu.VMEM((total, HEAD_COLUMNS), f32),
                pltpu.VMEM((total, DK), f32),
                pltpu.VMEM((total, DV), f32),
                pltpu.VMEM((ctx, CHUNK), f32),
                pltpu.VMEM((ctx, CHUNK, DV), bf16),
                pltpu.VMEM((ctx, CHUNK), f32),
                pltpu.VMEM((ctx, CHUNK, DK), bf16),
            ],
            name=f"head_{slot}",
        )(where, *toks, own, *direct, *swapped, *small)
        grads = [grad] + [along(grad, "ctx", d) for d in range(1, ctx)]
        backs = [backs[0]] + [along(backs[d], "ctx", d) for d in range(1, ctx)]
        done.append((grads, backs))

    picked = [jnp.where(where[2 + j] == place, toks[j], 0) for j in range(4)]
    own_columns = picked[0] + picked[1] + picked[2] + picked[3]
    pieces = [own_columns[d * length : (d + 1) * length] for d in range(ctx)]
    own_columns = jnp.zeros_like(own_columns)
    for d in range(ctx):
        own_columns = lax.dynamic_update_slice_in_dim(
            own_columns, pieces[d], lax.rem(place + ctx - d, ctx) * length, 0
        )

    results = None
    for slot in range(2):
        grads = done[slot][0]
        anywhere = [pl.BlockSpec(memory_space=pl.ANY)] * 3 if slot else []
        column = pl.BlockSpec(
            (share, DK), lambda d, where_ref, s=slot: (0, 2 * lax.rem(where_ref[0] + ctx - d, ctx) + s)
        )
        fixed = lambda dims: pl.BlockSpec(dims, lambda d, where_ref: (0, 0))
        results = pl.pallas_call(
            functools.partial(weight_gradient_kernel, ctx, slot),
            grid_spec=pltpu.PrefetchScalarGridSpec(
                num_scalar_prefetch=1,
                grid=(ctx,),
                in_specs=[fixed((total, share))] + [fixed((total, HEAD_COLUMNS))] * ctx + anywhere,
                out_specs=[column] * 3,
            ),
            out_shape=[shape((share, columns), f32)] * 3,
            input_output_aliases={2 + ctx + i: i for i in range(3)} if slot else {},
            name=f"weight_gradient_{slot}",
        )(where, own_columns, *grads, *(results or ()))

    attn_out, grad_beta, grad_decay = pl.pallas_call(
        functools.partial(unpack_kernel, ctx),
        out_shape=[shape((length, columns), bf16), shape((columns // DK, length), f32), shape((length, columns), f32)],
        in_specs=[scalars] + [whole] * (2 * ctx),
        out_specs=[whole] * 3,
        name="unpack",
    )(where, *done[0][1], *done[1][1])
    return (attn_out, *results, grad_beta, grad_decay)


def prefix_2(x, axis, join, neutral, backward):
    count = lax.axis_size(axis)
    place = lax.axis_index(axis)
    ahead = count - 1 - place if backward else place
    gathered = jax.tree.map(
        lambda a, kind: lax.all_gather(a.astype(kind), axis), x, (jnp.bfloat16, jnp.bfloat16)
    )
    state = jax.tree.map(lambda a, e: jnp.zeros_like(a) + jnp.asarray(e, a.dtype), x, neutral)

    def one(hop, state):
        source = count - 1 - hop if backward else hop
        return join(
            state,
            jax.tree.map(
                lambda a, own: lax.dynamic_index_in_dim(a, source, 0, False).astype(own.dtype),
                gathered,
                x,
            ),
        )

    return lax.fori_loop(0, ahead, one, state)


def normalize(vectors):
    return vectors * lax.rsqrt(jnp.sum(vectors * vectors, axis=-1, keepdims=True) + epsilon)


def heads_first(matrix, heads):
    return matrix.reshape(matrix.shape[0], heads, -1).transpose(1, 0, 2)


def span_step(memory, queries, key_vecs, val_vecs, strength, forgetting_exponent):
    largest_value = lax.Precision.HIGHEST
    length = queries.shape[1]
    cumulate = jnp.cumsum(forgetting_exponent, axis=1)
    growth = jnp.exp(cumulate)
    shrink = jnp.exp(-cumulate)
    key_up = key_vecs * growth
    key_down = key_vecs * shrink
    query_up = queries * growth
    row_ids = lax.broadcasted_iota(jnp.int32, (length, length), 0)
    col_ids = lax.broadcasted_iota(jnp.int32, (length, length), 1)
    strict = (row_ids > col_ids).astype(jnp.float32)
    within = (row_ids >= col_ids).astype(jnp.float32)
    affinity = jnp.einsum("bcd,bsd->bcs", key_up, key_down, precision=largest_value) * strict
    system = jnp.eye(length, dtype=jnp.float32) + strength[:, :, None] * affinity
    target = strength[:, :, None] * (
        val_vecs - jnp.einsum("bcd,bdw->bcw", key_up, memory, precision=largest_value)
    )
    update = lax.linalg.triangular_solve(system, target, left_side=True, lower=True)
    scores = jnp.einsum("bcd,bsd->bcs", query_up, key_down, precision=largest_value) * within
    emitted = jnp.einsum("bcd,bdw->bcw", query_up, memory, precision=largest_value)
    emitted = emitted + jnp.einsum("bcs,bsw->bcw", scores, update, precision=largest_value)
    at_end = growth[:, -1, :]
    renewed = at_end[:, :, None] * memory + jnp.einsum(
        "bsd,bsw->bdw", key_down * at_end[:, None, :], update, precision=largest_value
    )
    return (emitted, renewed)


def scan_spans(memory, queries, key_vecs, val_vecs, strength, forgetting_exponent):
    count = queries.shape[1] // SPAN

    def to_blocks(array):
        shaped = array.reshape((array.shape[0], count, SPAN) + array.shape[2:])
        return jnp.swapaxes(shaped, 0, 1)

    def advance(carried, blocks):
        emitted, renewed = span_step(carried, *blocks)
        return (renewed, emitted)

    blocks = (
        to_blocks(queries),
        to_blocks(key_vecs),
        to_blocks(val_vecs),
        to_blocks(strength),
        to_blocks(forgetting_exponent),
    )
    final, emitted = lax.scan(advance, memory, blocks)
    emitted = jnp.swapaxes(emitted, 0, 1)
    return (emitted.reshape(emitted.shape[0], count * SPAN, emitted.shape[-1]), final)


def compose(earlier, later):
    largest_value = lax.Precision.HIGHEST
    joined = jnp.einsum("hij,hjk->hik", later[0], earlier[0], precision=largest_value)
    shifted = jnp.einsum("hij,hjv->hiv", later[0], earlier[1], precision=largest_value) + later[1]
    return (joined, shifted)


def per_device(tokens, w_query, w_key, w_value, beta_logit, log_decay, grad_out):
    largest_value = lax.Precision.HIGHEST
    length = tokens.shape[0]
    columns = w_query.shape[1]
    heads = columns // DK
    shard_rows = (
        lax.all_gather(w_query, "ctx", axis=0, tiled=True),
        lax.all_gather(w_key, "ctx", axis=0, tiled=True),
        lax.all_gather(w_value, "ctx", axis=0, tiled=True),
    )
    window = tokens
    query_raw, key_raw, value_raw = tuple(
        (jnp.dot(window, weights, preferred_element_type=jnp.float32) for weights in shard_rows)
    )

    def shard_pass(query_in, key_in, value_in, logits, log_gates):
        queries = normalize(heads_first(query_in, heads))
        key_vecs = normalize(heads_first(key_in, heads))
        val_vecs = heads_first(value_in, heads)
        widened = jnp.concatenate([jnp.zeros((heads, length, DK), jnp.float32), val_vecs], axis=2)
        initial = jnp.concatenate(
            [
                jnp.broadcast_to(jnp.eye(DK, dtype=jnp.float32), (heads, DK, DK)),
                jnp.zeros((heads, DK, DV), jnp.float32),
            ],
            axis=2,
        )
        return scan_spans(
            initial,
            queries,
            key_vecs,
            widened,
            jax.nn.sigmoid(logits),
            heads_first(log_gates, heads),
        )

    (mixed, final), pullback = jax.vjp(
        shard_pass, query_raw, key_raw, value_raw, beta_logit, log_decay
    )
    transit = final[:, :, :DK]
    offset = final[:, :, DK:]
    query_carried_over = mixed[:, :, :DK]
    local_output = mixed[:, :, DK:]
    output_cotangent = grad_out.reshape(length, heads, DV).transpose(1, 0, 2).astype(jnp.float32)
    contribution = jnp.einsum(
        "mij,mif->mjf", query_carried_over, output_cotangent, precision=largest_value
    )
    identity = (
        jnp.broadcast_to(jnp.eye(DK, dtype=jnp.float32), (heads, DK, DK)),
        jnp.zeros((heads, DK, DV), jnp.float32),
    )
    prefix = prefix_2((transit, offset), "ctx", compose, identity, False)
    incoming_state = prefix[1]
    suffix = prefix_2((jnp.swapaxes(transit, 1, 2), contribution), "ctx", compose, identity, True)
    adjoint_state = suffix[1]
    complete_output = local_output + jnp.einsum(
        "npg,ngj->npj", query_carried_over, incoming_state, precision=largest_value
    )
    attn_out = complete_output.transpose(1, 0, 2).reshape(length, heads * DV).astype(jnp.bfloat16)
    d_mixed = jnp.concatenate(
        [
            jnp.einsum("efu,egu->efg", output_cotangent, incoming_state, precision=largest_value),
            output_cotangent,
        ],
        axis=2,
    )
    d_final = jnp.concatenate(
        [
            jnp.einsum("pgx,pcx->pgc", adjoint_state, incoming_state, precision=largest_value),
            adjoint_state,
        ],
        axis=2,
    )
    d_query, d_key, d_value, grad_beta, grad_decay = pullback((d_mixed, d_final))
    grad_projected = jnp.concatenate([d_query, d_key, d_value], axis=1).astype(jnp.bfloat16)
    window = tokens
    summed = lax.psum_scatter(
        jnp.einsum("td,tc->dc", window, grad_projected, preferred_element_type=jnp.float32).astype(
            jnp.bfloat16
        ),
        "ctx",
        scatter_dimension=0,
        tiled=True,
    ).astype(jnp.float32)
    return (
        attn_out,
        summed[:, :columns],
        summed[:, columns : 2 * columns],
        summed[:, 2 * columns :],
        grad_beta,
        grad_decay,
    )


def device_program(tokens, w_query, *rest):
    ctx = lax.axis_size("ctx")
    heads = w_query.shape[1] // DK
    split = heads == 2 * ctx and ctx == 4 and tokens.shape[0] == CHUNK and w_query.shape[0] * ctx == tokens.shape[1]
    split = split and lax.axis_size("groups") == lax.axis_size("fsdp") == lax.axis_size("head") == 2
    split = split and w_query.shape[0] % 64 == 0
    return (head_split if split else per_device)(tokens, w_query, *rest)


def solution(mesh):
    return jax.shard_map(
        device_program,
        mesh=mesh,
        in_specs=(
            P(("groups", "ctx"), None),
            P("ctx", ("fsdp", "head")),
            P("ctx", ("fsdp", "head")),
            P("ctx", ("fsdp", "head")),
            P(("fsdp", "head"), ("groups", "ctx")),
            P(("groups", "ctx"), ("fsdp", "head")),
            P(("groups", "ctx"), ("fsdp", "head")),
        ),
        out_specs=(
            P(("groups", "ctx"), ("fsdp", "head")),
            P(("groups", "ctx"), ("fsdp", "head")),
            P(("groups", "ctx"), ("fsdp", "head")),
            P(("groups", "ctx"), ("fsdp", "head")),
            P(("fsdp", "head"), ("groups", "ctx")),
            P(("groups", "ctx"), ("fsdp", "head")),
        ),
        check_vma=False,
    )
```

```python
import functools

import jax
import jax.numpy as jnp
from jax import lax
from jax.experimental import pallas as pl
from jax.experimental.pallas import tpu as pltpu
from jax.sharding import PartitionSpec as P

DK = 128
DV = 128
SPAN = 64
CHUNK = 128
TAIL = 16
EXTRA = 96
HEAD_COLUMNS = 2 * DK + DV

epsilon = 1e-06
HIGHEST = lax.Precision.HIGHEST
NN = (((1,), (0,)), ((), ()))
NT = (((1,), (1,)), ((), ()))
TN = (((0,), (0,)), ((), ()))


def narrow(x):
    return x.astype(jnp.bfloat16)


def dot(a, b, dims, passes):
    if passes == 6:
        return lax.dot_general(a, b, dims, precision=HIGHEST, preferred_element_type=jnp.float32)
    a_high, b_high = narrow(a), narrow(b)
    total = lax.dot_general(a_high, b_high, dims, preferred_element_type=jnp.float32)
    if passes >= 3:
        a_low = narrow(a - a_high.astype(jnp.float32))
        b_low = narrow(b - b_high.astype(jnp.float32))
        total = total + lax.dot_general(a_high, b_low, dims, preferred_element_type=jnp.float32)
        total = total + lax.dot_general(a_low, b_high, dims, preferred_element_type=jnp.float32)
    return total


PASSES = dict(
    decay=1, pairs=3, inverse=3, solve=3, read=1, carry=3, sent=1, scan=1, emit=1, update=1,
    d_update=3, d_value=3, d_pairs=1, d_up=1, d_up_state=1, d_kd=1, d_kend=1, d_decay=3,
)


def run(name, a, b, dims):
    return dot(a, b, dims, PASSES[name])


def recurrence(raw_ref, decay_ref, logit_ref, cot_ref, out_ref, grad_ref, dlogit_ref, ddecay_ref):
    count = raw_ref.shape[0] // CHUNK
    spans = range(count)
    rows = lax.broadcasted_iota(jnp.int32, (CHUNK, CHUNK), 0)
    cols = lax.broadcasted_iota(jnp.int32, (CHUNK, CHUNK), 1)
    within = rows >= cols
    strict = rows > cols
    diagonal = rows == cols
    running = within.astype(jnp.float32)

    q, k, v, rq, rk, up, down, end = [], [], [], [], [], [], [], []
    qu, ku, kd, kend, beta_row, cot = [], [], [], [], [], []
    for n in spans:
        here = slice(n * CHUNK, (n + 1) * CHUNK)
        q_raw = raw_ref[here, 0:DK]
        k_raw = raw_ref[here, DK : 2 * DK]
        v.append(raw_ref[here, 2 * DK : 3 * DK])
        rq.append(lax.rsqrt(jnp.sum(q_raw * q_raw, axis=1, keepdims=True) + epsilon))
        rk.append(lax.rsqrt(jnp.sum(k_raw * k_raw, axis=1, keepdims=True) + epsilon))
        q.append(q_raw * rq[n])
        k.append(k_raw * rk[n])
        summed = run("decay", running, decay_ref[here, :], NN)
        up.append(jnp.exp(summed))
        down.append(jnp.exp(-summed))
        end.append(up[n][CHUNK - 1 : CHUNK, :])
        qu.append(q[n] * up[n])
        ku.append(k[n] * up[n])
        kd.append(k[n] * down[n])
        kend.append(kd[n] * end[n])
        beta_row.append(jax.nn.sigmoid(logit_ref[n : n + 1, :]))
        cot.append(cot_ref[here, :])

    scores, system, inverse = [], [], []
    for n in spans:
        pairs = run("pairs", jnp.concatenate([qu[n], ku[n]], axis=0), kd[n], NT)
        scores.append(jnp.where(within, pairs[:CHUNK], 0.0))
        beta_col = jnp.transpose(jnp.broadcast_to(beta_row[n], (CHUNK, CHUNK)))
        system.append(jnp.where(strict, pairs[CHUNK:] * beta_col, 0.0))
        pair_block = (rows // 2) == (cols // 2)
        inverse.append(diagonal.astype(jnp.float32) - jnp.where(pair_block, system[n], 0.0))
    size = 2
    while size < CHUNK:
        joined = ((rows // (2 * size)) == (cols // (2 * size))) & ((rows // size) != (cols // size))
        halves = [run("inverse", jnp.where(joined, system[n], 0.0), inverse[n], NN) for n in spans]
        inverse = [inverse[n] - run("inverse", inverse[n], halves[n], NN) for n in spans]
        size *= 2

    solve = [inverse[n] * beta_row[n] for n in spans]
    wu = [run("solve", solve[n], jnp.concatenate([ku[n], v[n]], axis=1), NN) for n in spans]
    pwu = [run("read", scores[n], wu[n], NN) for n in spans]
    kwu = [run("carry", kend[n], wu[n], TN) for n in spans]
    query_through = [qu[n] - pwu[n][:, :DK] for n in spans]
    transit = [
        jnp.where(diagonal, jnp.broadcast_to(end[n], (DK, DK)), 0.0) - kwu[n][:, :DK] for n in spans
    ]
    sent = [run("sent", query_through[n], cot[n], TN) for n in spans]

    state = [None] * (count + 1)
    adjoint = [None] * (count + 1)
    for n in spans:
        m = count - 1 - n
        own = kwu[n][:, DK:]
        state[n + 1] = own if n == 0 else run("scan", transit[n], state[n], NN) + own
        adjoint[m] = sent[m] if n == 0 else run("scan", transit[m], adjoint[m + 1], TN) + sent[m]

    for n in spans:
        here = slice(n * CHUNK, (n + 1) * CHUNK)
        w = wu[n][:, :DK]
        update = wu[n][:, DK:]
        emitted = pwu[n][:, DK:]
        d_update = run("d_update", scores[n], cot[n], TN)
        if n > 0:
            emitted = emitted + run("emit", query_through[n], state[n], NN)
            update = update - run("update", w, state[n], NN)
        if n < count - 1:
            d_update = d_update + run("d_update", kend[n], adjoint[n + 1], NN)
        out_ref[n] = emitted.astype(out_ref.dtype)
        d_value = run("d_value", solve[n], d_update, TN)
        both = jnp.concatenate([cot[n], -d_value], axis=0)
        pairs = run("d_pairs", both, update, NT)
        d_pairs = jnp.concatenate(
            [jnp.where(within, pairs[:CHUNK], 0.0), jnp.where(strict, pairs[CHUNK:], 0.0)], axis=0
        )
        d_up = run("d_up", d_pairs, kd[n], NN)
        if n > 0:
            d_up = d_up + run("d_up_state", both, state[n], NT)
        d_qu, d_ku = d_up[:CHUNK], d_up[CHUNK:]
        d_kd = run("d_kd", d_pairs, jnp.concatenate([qu[n], ku[n]], axis=0), TN)
        d_k = d_ku * up[n] + d_kd * down[n]
        d_sum = d_qu * qu[n] + d_ku * ku[n] - d_kd * kd[n]
        d_decay_end = jnp.zeros((1, DK), jnp.float32)
        if n < count - 1:
            d_kend = run("d_kend", update, adjoint[n + 1], NT)
            d_k = d_k + d_kend * (end[n] * down[n])
            ended = d_kend * kend[n]
            d_sum = d_sum - ended
            d_decay_end = jnp.sum(ended, axis=0, keepdims=True)
            if n > 0:
                kept = jnp.sum(jnp.transpose(adjoint[n + 1] * state[n]), axis=0, keepdims=True)
                d_decay_end = d_decay_end + end[n] * kept
        ddecay_ref[n] = (run("d_decay", running, d_sum, TN) + d_decay_end).astype(ddecay_ref.dtype)
        d_q = d_qu * up[n]
        d_q = rq[n] * (d_q - q[n] * jnp.sum(q[n] * d_q, axis=1, keepdims=True))
        d_k = rk[n] * (d_k - k[n] * jnp.sum(k[n] * d_k, axis=1, keepdims=True))
        grad_ref[here, 0:DK] = d_q.astype(grad_ref.dtype)
        grad_ref[here, DK : 2 * DK] = d_k.astype(grad_ref.dtype)
        grad_ref[here, 2 * DK : 3 * DK] = d_value.astype(grad_ref.dtype)
        aligned = jnp.sum(jnp.transpose(d_value * update), axis=0, keepdims=True)
        dlogit_ref[n : n + 1, :] = aligned * jnp.exp(-logit_ref[n : n + 1, :])


def split_two(x):
    high = narrow(x)
    return high, narrow(x - high.astype(jnp.float32))


def tail_rows(x):
    high, low = split_two(x)
    index = lax.broadcasted_iota(jnp.int32, (TAIL, x.shape[1]), 0)
    high = jnp.broadcast_to(high.astype(jnp.float32), index.shape)
    low = jnp.broadcast_to(low.astype(jnp.float32), index.shape)
    return narrow(jnp.where(index == 0, high, jnp.where(index == 1, low, 0.0)))


def lanes(start):
    return pl.ds(pl.multiple_of(start, DK), DK)


def tile_rows(start, size):
    return pl.ds(pl.multiple_of(start, 32), size)


def pack_tokens_kernel(where_ref, tokens_ref, tok_ref):
    share = tok_ref.shape[0]
    for j in range(tokens_ref.shape[1] // share):

        @pl.when(where_ref[2] == j)
        def _(j=j):
            block = tokens_ref[:, j * share : (j + 1) * share]
            full = share // DK
            for g in range(full):
                tok_ref[g * CHUNK : (g + 1) * CHUNK, :] = block[:, g * DK : (g + 1) * DK]
            rest = block[:, full * DK :]
            tok_ref[full * CHUNK :, :] = jnp.concatenate([rest[: CHUNK // 2], rest[CHUNK // 2 :]], axis=1)


def unpack_tokens_kernel(ctx, where_ref, *refs):
    tok_refs, all_ref, own_ref = refs[:4], refs[4], refs[5]
    place = where_ref[0]
    share = own_ref.shape[0]
    full = share // DK
    for j in range(4):
        block = where_ref[2 + j]
        for d in range(ctx):
            source = lax.rem(place + ctx - d, ctx)
            start = source * CHUNK
            base = d * share
            for g in range(full):
                piece = tok_refs[j][base + g * CHUNK : base + (g + 1) * CHUNK, :]
                all_ref[block, tile_rows(start, CHUNK), g * DK : (g + 1) * DK] = piece
            rest = tok_refs[j][base + full * CHUNK : base + share, :]
            all_ref[block, tile_rows(start, CHUNK // 2), full * DK :] = rest[:, : DK // 2]
            all_ref[block, tile_rows(start + CHUNK // 2, CHUNK // 2), full * DK :] = rest[:, DK // 2 :]
    for n in range(ctx):
        piece = all_ref[place, n * CHUNK : (n + 1) * CHUNK, :].astype(jnp.float32)
        own_ref[:, n * CHUNK : (n + 1) * CHUNK] = narrow(jnp.transpose(piece))


def pack_kernel(ctx, where_ref, wq_ref, wk_ref, wv_ref, decay_ref, cot_ref, logit_ref, *out_refs):
    place, group = where_ref[0], where_ref[1]
    half = wq_ref.shape[0] // 2
    for s in range(2):
        for d in range(ctx):
            head = 2 * lax.rem(place + d, ctx) + s
            column = lanes(head * DK)
            out = out_refs[s * ctx + d]
            size = out.shape[0] - EXTRA
            rows = slice(None) if d == 0 else tile_rows(group * half, half)
            for part, ref in enumerate((wq_ref, wk_ref, wv_ref)):
                out[0:size, part * DK : (part + 1) * DK] = ref[rows, column]
            decay = narrow(decay_ref[:, column])
            cot = cot_ref[:, column]
            out[size : size + 96, 0:DK] = decay[0:96]
            out[size : size + 32, DK : 2 * DK] = decay[96:128]
            out[size + 32 : size + 96, DK : 2 * DK] = cot[0:64]
            out[size : size + 64, 2 * DK : 3 * DK] = cot[64:128]
            out[size + 64 : size + 80, 2 * DK : 3 * DK] = tail_rows(logit_ref[pl.ds(head, 1), :])
            out[size + 80 : size + 96, 2 * DK : 3 * DK] = jnp.zeros((16, DK), out.dtype)


def head_kernel(ctx, slot, where_ref, *refs):
    all_ref, refs = refs[0], refs[1:]
    direct, refs = refs[:ctx], refs[ctx:]
    swapped, refs = refs[: ctx - 1], refs[ctx - 1 :]
    if slot:
        earlier_ref, refs = refs[0], refs[1:]
    grad_ref, back_ref, w, raw, decay, cot, logit, out, dlogit, ddecay = refs
    place, group = where_ref[0], where_ref[1]
    share = direct[0].shape[0] - EXTRA
    half = share // 2
    for d in range(ctx):
        source = lax.rem(place + ctx - d, ctx)
        ref = direct[d]
        if d == 0:
            w[tile_rows(source * share, share), :] = ref[0:share, :]
            size = share
        else:
            w[tile_rows(source * share + group * half, half), :] = ref[0:half, :]
            w[tile_rows(source * share + (1 - group) * half, half), :] = swapped[d - 1][0:half, :]
            size = half
        start = source * CHUNK
        decay[tile_rows(start, 96), :] = ref[size : size + 96, 0:DK].astype(jnp.float32)
        decay[tile_rows(start + 96, 32), :] = ref[size : size + 32, DK : 2 * DK].astype(jnp.float32)
        cot[tile_rows(start, 64), :] = ref[size + 32 : size + 96, DK : 2 * DK].astype(jnp.float32)
        cot[tile_rows(start + 64, 64), :] = ref[size : size + 64, 2 * DK : 3 * DK].astype(jnp.float32)
        tail = ref[size + 64 : size + 80, 2 * DK : 3 * DK].astype(jnp.float32)
        logit[pl.ds(source, 1), :] = tail[0:1] + tail[1:2]
    projected = 0.0
    for j in range(ctx):
        projected = projected + lax.dot_general(
            all_ref[j], w[j * share : (j + 1) * share, :], NN, preferred_element_type=jnp.float32
        )
    raw[...] = projected
    recurrence(raw, decay, logit, cot, out, grad_ref, dlogit, ddecay)
    lane = slice(slot * DK, (slot + 1) * DK)
    if slot:
        back_ref[:, :, 0:DK] = earlier_ref[...]
    for n in range(ctx):
        back_ref[n, 0:CHUNK, lane] = out[n]
        back_ref[n, CHUNK : 2 * CHUNK, lane] = ddecay[n]
        back_ref[n, 2 * CHUNK :, lane] = tail_rows(dlogit[n : n + 1, :])


def weight_gradient_kernel(steps, where_ref, own_ref, *refs):
    out_refs = refs[-3:]

    def block(gradient):
        product = lax.dot_general(own_ref[...], gradient, NN, preferred_element_type=jnp.float32)
        for part in range(3):
            out_refs[part][...] = product[:, part * DK : (part + 1) * DK]

    for at, step in enumerate(steps):

        @pl.when(pl.program_id(0) == at)
        def _(at=at, step=step):
            if step < 3:
                block(refs[at][...])
            else:
                block(jnp.where(where_ref[10] == 1, refs[at + 1][...], refs[at][...]))


def unpack_kernel(back_ref, out_ref, dlogit_ref, ddecay_ref):
    for source in range(back_ref.shape[0]):
        column = slice(2 * source * DK, 2 * (source + 1) * DK)
        out_ref[:, column] = back_ref[source, 0:CHUNK, :]
        ddecay_ref[:, column] = back_ref[source, CHUNK : 2 * CHUNK, :].astype(jnp.float32)
        tail = back_ref[source, 2 * CHUNK :, :].astype(jnp.float32)
        row = tail[0:1] + tail[1:2]
        for s in range(2):
            dlogit_ref[2 * source + s : 2 * source + s + 1, :] = row[:, s * DK : (s + 1) * DK]


def head_split(tokens, w_query, w_key, w_value, beta_logit, log_decay, grad_out):
    ctx = lax.axis_size("ctx")
    place = lax.axis_index("ctx")
    group = lax.axis_index("groups")
    across, core = lax.axis_index("fsdp"), lax.axis_index("head")
    length, depth = tokens.shape
    share, columns = w_query.shape
    total = ctx * length
    bf16, f32 = jnp.bfloat16, jnp.float32
    whole = pl.BlockSpec(memory_space=pltpu.VMEM)
    scalars = pl.BlockSpec(memory_space=pltpu.SMEM)
    sources = [place, place + 1 - 2 * (place % 2), (place + 2) % ctx, ctx - 1 - place]
    where = jnp.stack(
        [place, group]
        + [2 * a + c for c in (core, 1 - core) for a in (across, 1 - across)]
        + sources
        + [((place == 0) | (place == ctx - 1)).astype(jnp.int32)]
    ).astype(jnp.int32)

    def shape(dims, kind):
        return jax.ShapeDtypeStruct(dims, kind)

    def along(x, axis, hop):
        count = lax.axis_size(axis)
        return lax.ppermute(x, axis, [(i, (i + hop) % count) for i in range(count)])

    tok = pl.pallas_call(
        pack_tokens_kernel,
        out_shape=shape((share, length), bf16),
        in_specs=[scalars, whole],
        out_specs=whole,
        name="pack_tokens",
    )(where, tokens)
    sizes = [share + EXTRA] + [share // 2 + EXTRA] * (ctx - 1)
    packed = pl.pallas_call(
        functools.partial(pack_kernel, ctx),
        out_shape=[shape((size, HEAD_COLUMNS), bf16) for size in sizes * 2],
        in_specs=[scalars] + [whole] * 6,
        out_specs=[whole] * (2 * ctx),
        name="pack",
    )(where, w_query, w_key, w_value, log_decay, grad_out, beta_logit)

    near = [along(tok, "ctx", d) for d in range(1, ctx)]
    first, near[0] = lax.optimization_barrier((packed[1:ctx], near[0]))
    tok = jnp.concatenate([tok] + near, axis=0)
    tok_x = along(tok, "fsdp", 1)
    toks = (tok, tok_x, along(tok, "head", 1), along(tok_x, "head", 1))
    all_tokens, own = pl.pallas_call(
        functools.partial(unpack_tokens_kernel, ctx),
        out_shape=[shape((ctx, total, share), bf16), shape((share, total), bf16)],
        in_specs=[scalars] + [whole] * 4,
        out_specs=[whole] * 2,
        name="unpack_tokens",
    )(where, *toks)
    first = [along(x, "ctx", d + 1) for d, x in enumerate(first)]
    second, first[0] = lax.optimization_barrier((packed[ctx + 1 :], first[0]))
    second = [along(x, "ctx", d + 1) for d, x in enumerate(second)]

    grads = []
    back = None
    for slot, direct in enumerate((first, second)):
        swapped = [along(x, "groups", 1) for x in direct]
        earlier = [] if back is None else [back]
        grad, back = pl.pallas_call(
            functools.partial(head_kernel, ctx, slot),
            out_shape=[
                shape((total, HEAD_COLUMNS), bf16),
                shape((ctx, 2 * CHUNK + TAIL, (slot + 1) * DK), bf16),
            ],
            in_specs=[scalars] + [whole] * (1 + ctx + ctx - 1 + slot),
            out_specs=[whole] * 2,
            scratch_shapes=[
                pltpu.VMEM((depth, HEAD_COLUMNS), bf16),
                pltpu.VMEM((total, HEAD_COLUMNS), f32),
                pltpu.VMEM((total, DK), f32),
                pltpu.VMEM((total, DV), f32),
                pltpu.VMEM((ctx, CHUNK), f32),
                pltpu.VMEM((ctx, CHUNK, DV), bf16),
                pltpu.VMEM((ctx, CHUNK), f32),
                pltpu.VMEM((ctx, CHUNK, DK), bf16),
            ],
            cost_estimate=pl.CostEstimate(flops=12_000_000_000, transcendentals=0, bytes_accessed=8_000_000),
            name=f"head_{slot}",
        )(where, all_tokens, packed[slot * ctx], *direct, *swapped, *earlier)
        two = lax.ppermute(grad, "ctx", [(0, 2), (1, 3), (2, 0), (3, 1)])
        pair = lax.ppermute(grad, "ctx", [(0, 1), (1, 0), (2, 3), (3, 2)])
        middle = lax.ppermute(grad, "ctx", [(1, 2), (2, 1)])
        far = lax.ppermute(two, "ctx", [(2, 3), (1, 0)])
        grads.append((grad, pair, two, middle, far))
    back = lax.all_to_all(back, "ctx", 0, 0)

    results = ()
    for slot, steps in ((0, (0, 1, 2, 3)), (1, (0, 1, 2)), (1, (3,))):
        parts = [grads[slot][step] for step in steps] + ([grads[slot][4]] if 3 in steps else [])
        column = pl.BlockSpec((share, DK), lambda i, ref, s=slot, b=steps[0]: (0, 2 * ref[6 + b + i] + s))
        fixed = lambda dims: pl.BlockSpec(dims, lambda i, ref: (0, 0))
        results = pl.pallas_call(
            functools.partial(weight_gradient_kernel, steps),
            grid_spec=pltpu.PrefetchScalarGridSpec(
                num_scalar_prefetch=1,
                grid=(len(steps),),
                in_specs=[fixed((share, total))]
                + [fixed((total, HEAD_COLUMNS))] * len(parts)
                + [pl.BlockSpec(memory_space=pl.ANY)] * len(results),
                out_specs=[column] * 3,
            ),
            out_shape=[shape((share, columns), f32)] * 3,
            input_output_aliases={2 + len(parts) + i: i for i in range(len(results))},
            name=f"weight_gradient_{slot}_{steps[0]}",
        )(where, own, *parts, *results)

    attn_out, grad_beta, grad_decay = pl.pallas_call(
        unpack_kernel,
        out_shape=[shape((length, columns), bf16), shape((columns // DK, length), f32), shape((length, columns), f32)],
        in_specs=[whole],
        out_specs=[whole] * 3,
        name="unpack",
    )(back)
    return (attn_out, *results, grad_beta, grad_decay)


def prefix_2(x, axis, join, neutral, backward):
    count = lax.axis_size(axis)
    place = lax.axis_index(axis)
    ahead = count - 1 - place if backward else place
    gathered = jax.tree.map(
        lambda a, kind: lax.all_gather(a.astype(kind), axis), x, (jnp.bfloat16, jnp.bfloat16)
    )
    state = jax.tree.map(lambda a, e: jnp.zeros_like(a) + jnp.asarray(e, a.dtype), x, neutral)

    def one(hop, state):
        source = count - 1 - hop if backward else hop
        return join(
            state,
            jax.tree.map(
                lambda a, own: lax.dynamic_index_in_dim(a, source, 0, False).astype(own.dtype),
                gathered,
                x,
            ),
        )

    return lax.fori_loop(0, ahead, one, state)


def normalize(vectors):
    return vectors * lax.rsqrt(jnp.sum(vectors * vectors, axis=-1, keepdims=True) + epsilon)


def heads_first(matrix, heads):
    return matrix.reshape(matrix.shape[0], heads, -1).transpose(1, 0, 2)


def span_step(memory, queries, key_vecs, val_vecs, strength, forgetting_exponent):
    largest_value = lax.Precision.HIGHEST
    length = queries.shape[1]
    cumulate = jnp.cumsum(forgetting_exponent, axis=1)
    growth = jnp.exp(cumulate)
    shrink = jnp.exp(-cumulate)
    key_up = key_vecs * growth
    key_down = key_vecs * shrink
    query_up = queries * growth
    row_ids = lax.broadcasted_iota(jnp.int32, (length, length), 0)
    col_ids = lax.broadcasted_iota(jnp.int32, (length, length), 1)
    strict = (row_ids > col_ids).astype(jnp.float32)
    within = (row_ids >= col_ids).astype(jnp.float32)
    affinity = jnp.einsum("bcd,bsd->bcs", key_up, key_down, precision=largest_value) * strict
    system = jnp.eye(length, dtype=jnp.float32) + strength[:, :, None] * affinity
    target = strength[:, :, None] * (
        val_vecs - jnp.einsum("bcd,bdw->bcw", key_up, memory, precision=largest_value)
    )
    update = lax.linalg.triangular_solve(system, target, left_side=True, lower=True)
    scores = jnp.einsum("bcd,bsd->bcs", query_up, key_down, precision=largest_value) * within
    emitted = jnp.einsum("bcd,bdw->bcw", query_up, memory, precision=largest_value)
    emitted = emitted + jnp.einsum("bcs,bsw->bcw", scores, update, precision=largest_value)
    at_end = growth[:, -1, :]
    renewed = at_end[:, :, None] * memory + jnp.einsum(
        "bsd,bsw->bdw", key_down * at_end[:, None, :], update, precision=largest_value
    )
    return (emitted, renewed)


def scan_spans(memory, queries, key_vecs, val_vecs, strength, forgetting_exponent):
    count = queries.shape[1] // SPAN

    def to_blocks(array):
        shaped = array.reshape((array.shape[0], count, SPAN) + array.shape[2:])
        return jnp.swapaxes(shaped, 0, 1)

    def advance(carried, blocks):
        emitted, renewed = span_step(carried, *blocks)
        return (renewed, emitted)

    blocks = (
        to_blocks(queries),
        to_blocks(key_vecs),
        to_blocks(val_vecs),
        to_blocks(strength),
        to_blocks(forgetting_exponent),
    )
    final, emitted = lax.scan(advance, memory, blocks)
    emitted = jnp.swapaxes(emitted, 0, 1)
    return (emitted.reshape(emitted.shape[0], count * SPAN, emitted.shape[-1]), final)


def compose(earlier, later):
    largest_value = lax.Precision.HIGHEST
    joined = jnp.einsum("hij,hjk->hik", later[0], earlier[0], precision=largest_value)
    shifted = jnp.einsum("hij,hjv->hiv", later[0], earlier[1], precision=largest_value) + later[1]
    return (joined, shifted)


def per_device(tokens, w_query, w_key, w_value, beta_logit, log_decay, grad_out):
    largest_value = lax.Precision.HIGHEST
    length = tokens.shape[0]
    columns = w_query.shape[1]
    heads = columns // DK
    shard_rows = (
        lax.all_gather(w_query, "ctx", axis=0, tiled=True),
        lax.all_gather(w_key, "ctx", axis=0, tiled=True),
        lax.all_gather(w_value, "ctx", axis=0, tiled=True),
    )
    window = tokens
    query_raw, key_raw, value_raw = tuple(
        (jnp.dot(window, weights, preferred_element_type=jnp.float32) for weights in shard_rows)
    )

    def shard_pass(query_in, key_in, value_in, logits, log_gates):
        queries = normalize(heads_first(query_in, heads))
        key_vecs = normalize(heads_first(key_in, heads))
        val_vecs = heads_first(value_in, heads)
        widened = jnp.concatenate([jnp.zeros((heads, length, DK), jnp.float32), val_vecs], axis=2)
        initial = jnp.concatenate(
            [
                jnp.broadcast_to(jnp.eye(DK, dtype=jnp.float32), (heads, DK, DK)),
                jnp.zeros((heads, DK, DV), jnp.float32),
            ],
            axis=2,
        )
        return scan_spans(
            initial,
            queries,
            key_vecs,
            widened,
            jax.nn.sigmoid(logits),
            heads_first(log_gates, heads),
        )

    (mixed, final), pullback = jax.vjp(
        shard_pass, query_raw, key_raw, value_raw, beta_logit, log_decay
    )
    transit = final[:, :, :DK]
    offset = final[:, :, DK:]
    query_carried_over = mixed[:, :, :DK]
    local_output = mixed[:, :, DK:]
    output_cotangent = grad_out.reshape(length, heads, DV).transpose(1, 0, 2).astype(jnp.float32)
    contribution = jnp.einsum(
        "mij,mif->mjf", query_carried_over, output_cotangent, precision=largest_value
    )
    identity = (
        jnp.broadcast_to(jnp.eye(DK, dtype=jnp.float32), (heads, DK, DK)),
        jnp.zeros((heads, DK, DV), jnp.float32),
    )
    prefix = prefix_2((transit, offset), "ctx", compose, identity, False)
    incoming_state = prefix[1]
    suffix = prefix_2((jnp.swapaxes(transit, 1, 2), contribution), "ctx", compose, identity, True)
    adjoint_state = suffix[1]
    complete_output = local_output + jnp.einsum(
        "npg,ngj->npj", query_carried_over, incoming_state, precision=largest_value
    )
    attn_out = complete_output.transpose(1, 0, 2).reshape(length, heads * DV).astype(jnp.bfloat16)
    d_mixed = jnp.concatenate(
        [
            jnp.einsum("efu,egu->efg", output_cotangent, incoming_state, precision=largest_value),
            output_cotangent,
        ],
        axis=2,
    )
    d_final = jnp.concatenate(
        [
            jnp.einsum("pgx,pcx->pgc", adjoint_state, incoming_state, precision=largest_value),
            adjoint_state,
        ],
        axis=2,
    )
    d_query, d_key, d_value, grad_beta, grad_decay = pullback((d_mixed, d_final))
    grad_projected = jnp.concatenate([d_query, d_key, d_value], axis=1).astype(jnp.bfloat16)
    window = tokens
    summed = lax.psum_scatter(
        jnp.einsum("td,tc->dc", window, grad_projected, preferred_element_type=jnp.float32).astype(
            jnp.bfloat16
        ),
        "ctx",
        scatter_dimension=0,
        tiled=True,
    ).astype(jnp.float32)
    return (
        attn_out,
        summed[:, :columns],
        summed[:, columns : 2 * columns],
        summed[:, 2 * columns :],
        grad_beta,
        grad_decay,
    )


def device_program(tokens, w_query, *rest):
    ctx = lax.axis_size("ctx")
    heads = w_query.shape[1] // DK
    split = heads == 2 * ctx and ctx == 4 and tokens.shape[0] == CHUNK and w_query.shape[0] * ctx == tokens.shape[1]
    split = split and lax.axis_size("groups") == lax.axis_size("fsdp") == lax.axis_size("head") == 2
    split = split and w_query.shape[0] % 64 == 0
    return (head_split if split else per_device)(tokens, w_query, *rest)


def solution(mesh):
    return jax.shard_map(
        device_program,
        mesh=mesh,
        in_specs=(
            P(("groups", "ctx"), None),
            P("ctx", ("fsdp", "head")),
            P("ctx", ("fsdp", "head")),
            P("ctx", ("fsdp", "head")),
            P(("fsdp", "head"), ("groups", "ctx")),
            P(("groups", "ctx"), ("fsdp", "head")),
            P(("groups", "ctx"), ("fsdp", "head")),
        ),
        out_specs=(
            P(("groups", "ctx"), ("fsdp", "head")),
            P(("groups", "ctx"), ("fsdp", "head")),
            P(("groups", "ctx"), ("fsdp", "head")),
            P(("groups", "ctx"), ("fsdp", "head")),
            P(("fsdp", "head"), ("groups", "ctx")),
            P(("groups", "ctx"), ("fsdp", "head")),
        ),
        check_vma=False,
    )
```

```python
import functools

import jax
import jax.numpy as jnp
from jax import lax
from jax.experimental import pallas as pl
from jax.experimental.pallas import tpu as pltpu
from jax.sharding import PartitionSpec as P

DK = 128
DV = 128
SPAN = 64
CHUNK = 128
TAIL = 16
EXTRA = 96
HEAD_COLUMNS = 2 * DK + DV

epsilon = 1e-06
HIGHEST = lax.Precision.HIGHEST
NN = (((1,), (0,)), ((), ()))
NT = (((1,), (1,)), ((), ()))
TN = (((0,), (0,)), ((), ()))


def narrow(x):
    return x.astype(jnp.bfloat16)


def dot(a, b, dims, passes):
    if passes == 6:
        return lax.dot_general(a, b, dims, precision=HIGHEST, preferred_element_type=jnp.float32)
    a_high, b_high = narrow(a), narrow(b)
    total = lax.dot_general(a_high, b_high, dims, preferred_element_type=jnp.float32)
    if passes >= 3:
        a_low = narrow(a - a_high.astype(jnp.float32))
        b_low = narrow(b - b_high.astype(jnp.float32))
        total = total + lax.dot_general(a_high, b_low, dims, preferred_element_type=jnp.float32)
        total = total + lax.dot_general(a_low, b_high, dims, preferred_element_type=jnp.float32)
    return total


PASSES = dict(
    decay=1, pairs=3, inverse=3, solve=3, read=1, carry=3, sent=1, scan=1, emit=1, update=1,
    d_update=3, d_value=3, d_pairs=1, d_up=1, d_up_state=1, d_kd=1, d_kend=1, d_decay=3,
)


def run(name, a, b, dims):
    return dot(a, b, dims, PASSES[name])


def recurrence(raw_ref, decay_ref, logit_ref, cot_ref, out_ref, grad_ref, dlogit_ref, ddecay_ref):
    count = raw_ref.shape[0] // CHUNK
    spans = range(count)
    rows = lax.broadcasted_iota(jnp.int32, (CHUNK, CHUNK), 0)
    cols = lax.broadcasted_iota(jnp.int32, (CHUNK, CHUNK), 1)
    within = rows >= cols
    strict = rows > cols
    diagonal = rows == cols
    running = within.astype(jnp.float32)

    q, k, v, rq, rk, up, down, end = [], [], [], [], [], [], [], []
    qu, ku, kd, kend, beta_row, cot = [], [], [], [], [], []
    for n in spans:
        here = slice(n * CHUNK, (n + 1) * CHUNK)
        q_raw = raw_ref[here, 0:DK]
        k_raw = raw_ref[here, DK : 2 * DK]
        v.append(raw_ref[here, 2 * DK : 3 * DK])
        rq.append(lax.rsqrt(jnp.sum(q_raw * q_raw, axis=1, keepdims=True) + epsilon))
        rk.append(lax.rsqrt(jnp.sum(k_raw * k_raw, axis=1, keepdims=True) + epsilon))
        q.append(q_raw * rq[n])
        k.append(k_raw * rk[n])
        summed = run("decay", running, decay_ref[here, :], NN)
        up.append(jnp.exp(summed))
        down.append(jnp.exp(-summed))
        end.append(up[n][CHUNK - 1 : CHUNK, :])
        qu.append(q[n] * up[n])
        ku.append(k[n] * up[n])
        kd.append(k[n] * down[n])
        kend.append(kd[n] * end[n])
        beta_row.append(jax.nn.sigmoid(logit_ref[n : n + 1, :]))
        cot.append(cot_ref[here, :])

    scores, system, inverse = [], [], []
    for n in spans:
        pairs = run("pairs", jnp.concatenate([qu[n], ku[n]], axis=0), kd[n], NT)
        scores.append(jnp.where(within, pairs[:CHUNK], 0.0))
        beta_col = jnp.transpose(jnp.broadcast_to(beta_row[n], (CHUNK, CHUNK)))
        system.append(jnp.where(strict, pairs[CHUNK:] * beta_col, 0.0))
        pair_block = (rows // 2) == (cols // 2)
        inverse.append(diagonal.astype(jnp.float32) - jnp.where(pair_block, system[n], 0.0))
    size = 2
    while size < CHUNK:
        joined = ((rows // (2 * size)) == (cols // (2 * size))) & ((rows // size) != (cols // size))
        halves = [run("inverse", jnp.where(joined, system[n], 0.0), inverse[n], NN) for n in spans]
        inverse = [inverse[n] - run("inverse", inverse[n], halves[n], NN) for n in spans]
        size *= 2

    solve = [inverse[n] * beta_row[n] for n in spans]
    wu = [run("solve", solve[n], jnp.concatenate([ku[n], v[n]], axis=1), NN) for n in spans]
    pwu = [run("read", scores[n], wu[n], NN) for n in spans]
    kwu = [run("carry", kend[n], wu[n], TN) for n in spans]
    query_through = [qu[n] - pwu[n][:, :DK] for n in spans]
    transit = [
        jnp.where(diagonal, jnp.broadcast_to(end[n], (DK, DK)), 0.0) - kwu[n][:, :DK] for n in spans
    ]
    sent = [run("sent", query_through[n], cot[n], TN) for n in spans]

    state = [None] * (count + 1)
    adjoint = [None] * (count + 1)
    for n in spans:
        m = count - 1 - n
        own = kwu[n][:, DK:]
        state[n + 1] = own if n == 0 else run("scan", transit[n], state[n], NN) + own
        adjoint[m] = sent[m] if n == 0 else run("scan", transit[m], adjoint[m + 1], TN) + sent[m]

    for n in spans:
        here = slice(n * CHUNK, (n + 1) * CHUNK)
        w = wu[n][:, :DK]
        update = wu[n][:, DK:]
        emitted = pwu[n][:, DK:]
        d_update = run("d_update", scores[n], cot[n], TN)
        if n > 0:
            emitted = emitted + run("emit", query_through[n], state[n], NN)
            update = update - run("update", w, state[n], NN)
        if n < count - 1:
            d_update = d_update + run("d_update", kend[n], adjoint[n + 1], NN)
        out_ref[n] = emitted.astype(out_ref.dtype)
        d_value = run("d_value", solve[n], d_update, TN)
        both = jnp.concatenate([cot[n], -d_value], axis=0)
        pairs = run("d_pairs", both, update, NT)
        d_pairs = jnp.concatenate(
            [jnp.where(within, pairs[:CHUNK], 0.0), jnp.where(strict, pairs[CHUNK:], 0.0)], axis=0
        )
        d_up = run("d_up", d_pairs, kd[n], NN)
        if n > 0:
            d_up = d_up + run("d_up_state", both, state[n], NT)
        d_qu, d_ku = d_up[:CHUNK], d_up[CHUNK:]
        d_kd = run("d_kd", d_pairs, jnp.concatenate([qu[n], ku[n]], axis=0), TN)
        d_k = d_ku * up[n] + d_kd * down[n]
        d_sum = d_qu * qu[n] + d_ku * ku[n] - d_kd * kd[n]
        d_decay_end = jnp.zeros((1, DK), jnp.float32)
        if n < count - 1:
            d_kend = run("d_kend", update, adjoint[n + 1], NT)
            d_k = d_k + d_kend * (end[n] * down[n])
            ended = d_kend * kend[n]
            d_sum = d_sum - ended
            d_decay_end = jnp.sum(ended, axis=0, keepdims=True)
            if n > 0:
                kept = jnp.sum(jnp.transpose(adjoint[n + 1] * state[n]), axis=0, keepdims=True)
                d_decay_end = d_decay_end + end[n] * kept
        ddecay_ref[n] = (run("d_decay", running, d_sum, TN) + d_decay_end).astype(ddecay_ref.dtype)
        d_q = d_qu * up[n]
        d_q = rq[n] * (d_q - q[n] * jnp.sum(q[n] * d_q, axis=1, keepdims=True))
        d_k = rk[n] * (d_k - k[n] * jnp.sum(k[n] * d_k, axis=1, keepdims=True))
        grad_ref[here, 0:DK] = d_q.astype(grad_ref.dtype)
        grad_ref[here, DK : 2 * DK] = d_k.astype(grad_ref.dtype)
        grad_ref[here, 2 * DK : 3 * DK] = d_value.astype(grad_ref.dtype)
        aligned = jnp.sum(jnp.transpose(d_value * update), axis=0, keepdims=True)
        dlogit_ref[n : n + 1, :] = aligned * jnp.exp(-logit_ref[n : n + 1, :])


def split_two(x):
    high = narrow(x)
    return high, narrow(x - high.astype(jnp.float32))


def tail_rows(x):
    high, low = split_two(x)
    index = lax.broadcasted_iota(jnp.int32, (TAIL, x.shape[1]), 0)
    high = jnp.broadcast_to(high.astype(jnp.float32), index.shape)
    low = jnp.broadcast_to(low.astype(jnp.float32), index.shape)
    return narrow(jnp.where(index == 0, high, jnp.where(index == 1, low, 0.0)))


def lanes(start):
    return pl.ds(pl.multiple_of(start, DK), DK)


def tile_rows(start, size):
    return pl.ds(pl.multiple_of(start, 32), size)


def pack_tokens_kernel(where_ref, tokens_ref, tok_ref):
    share = tok_ref.shape[0]
    for j in range(tokens_ref.shape[1] // share):

        @pl.when(where_ref[2] == j)
        def _(j=j):
            block = tokens_ref[:, j * share : (j + 1) * share]
            full = share // DK
            for g in range(full):
                tok_ref[g * CHUNK : (g + 1) * CHUNK, :] = block[:, g * DK : (g + 1) * DK]
            rest = block[:, full * DK :]
            tok_ref[full * CHUNK :, :] = jnp.concatenate([rest[: CHUNK // 2], rest[CHUNK // 2 :]], axis=1)


def unpack_tokens_kernel(ctx, where_ref, *refs):
    tok_refs, all_ref, own_ref = refs[:4], refs[4], refs[5]
    place = where_ref[0]
    share = own_ref.shape[0]
    full = share // DK
    for j in range(4):
        block = where_ref[2 + j]
        for d in range(ctx):
            source = lax.rem(place + ctx - d, ctx)
            start = source * CHUNK
            base = d * share
            for g in range(full):
                piece = tok_refs[j][base + g * CHUNK : base + (g + 1) * CHUNK, :]
                all_ref[block, tile_rows(start, CHUNK), g * DK : (g + 1) * DK] = piece
            rest = tok_refs[j][base + full * CHUNK : base + share, :]
            all_ref[block, tile_rows(start, CHUNK // 2), full * DK :] = rest[:, : DK // 2]
            all_ref[block, tile_rows(start + CHUNK // 2, CHUNK // 2), full * DK :] = rest[:, DK // 2 :]
    for n in range(ctx):
        piece = all_ref[place, n * CHUNK : (n + 1) * CHUNK, :].astype(jnp.float32)
        own_ref[:, n * CHUNK : (n + 1) * CHUNK] = narrow(jnp.transpose(piece))


def pack_kernel(ctx, where_ref, wq_ref, wk_ref, wv_ref, decay_ref, cot_ref, logit_ref, *out_refs):
    place, group = where_ref[0], where_ref[1]
    half = wq_ref.shape[0] // 2
    for s in range(2):
        for d in range(ctx):
            head = 2 * lax.rem(place + d, ctx) + s
            column = lanes(head * DK)
            out = out_refs[s * ctx + d]
            size = out.shape[0] - EXTRA
            rows = slice(None) if d == 0 else tile_rows(group * half, half)
            for part, ref in enumerate((wq_ref, wk_ref, wv_ref)):
                out[0:size, part * DK : (part + 1) * DK] = ref[rows, column]
            decay = narrow(decay_ref[:, column])
            cot = cot_ref[:, column]
            out[size : size + 96, 0:DK] = decay[0:96]
            out[size : size + 32, DK : 2 * DK] = decay[96:128]
            out[size + 32 : size + 96, DK : 2 * DK] = cot[0:64]
            out[size : size + 64, 2 * DK : 3 * DK] = cot[64:128]
            out[size + 64 : size + 80, 2 * DK : 3 * DK] = tail_rows(logit_ref[pl.ds(head, 1), :])
            out[size + 80 : size + 96, 2 * DK : 3 * DK] = jnp.zeros((16, DK), out.dtype)


def head_kernel(ctx, slot, where_ref, *refs):
    all_ref, refs = refs[0], refs[1:]
    direct, refs = refs[:ctx], refs[ctx:]
    swapped, refs = refs[: ctx - 1], refs[ctx - 1 :]
    if slot:
        earlier_ref, refs = refs[0], refs[1:]
    grad_ref, back_ref, w, raw, decay, cot, logit, out, dlogit, ddecay = refs
    place, group = where_ref[0], where_ref[1]
    share = direct[0].shape[0] - EXTRA
    half = share // 2
    for d in range(ctx):
        source = lax.rem(place + ctx - d, ctx)
        ref = direct[d]
        if d == 0:
            w[tile_rows(source * share, share), :] = ref[0:share, :]
            size = share
        else:
            w[tile_rows(source * share + group * half, half), :] = ref[0:half, :]
            w[tile_rows(source * share + (1 - group) * half, half), :] = swapped[d - 1][0:half, :]
            size = half
        start = source * CHUNK
        decay[tile_rows(start, 96), :] = ref[size : size + 96, 0:DK].astype(jnp.float32)
        decay[tile_rows(start + 96, 32), :] = ref[size : size + 32, DK : 2 * DK].astype(jnp.float32)
        cot[tile_rows(start, 64), :] = ref[size + 32 : size + 96, DK : 2 * DK].astype(jnp.float32)
        cot[tile_rows(start + 64, 64), :] = ref[size : size + 64, 2 * DK : 3 * DK].astype(jnp.float32)
        tail = ref[size + 64 : size + 80, 2 * DK : 3 * DK].astype(jnp.float32)
        logit[pl.ds(source, 1), :] = tail[0:1] + tail[1:2]
    projected = 0.0
    for j in range(ctx):
        projected = projected + lax.dot_general(
            all_ref[j], w[j * share : (j + 1) * share, :], NN, preferred_element_type=jnp.float32
        )
    raw[...] = projected
    recurrence(raw, decay, logit, cot, out, grad_ref, dlogit, ddecay)
    lane = slice(slot * DK, (slot + 1) * DK)
    if slot:
        back_ref[:, :, 0:DK] = earlier_ref[...]
    for n in range(ctx):
        back_ref[n, 0:CHUNK, lane] = out[n]
        back_ref[n, CHUNK : 2 * CHUNK, lane] = ddecay[n]
        back_ref[n, 2 * CHUNK :, lane] = tail_rows(dlogit[n : n + 1, :])


def weight_gradient_kernel(steps, where_ref, own_ref, *refs):
    out_refs = refs[-3:]

    def block(gradient):
        product = lax.dot_general(own_ref[...], gradient, NN, preferred_element_type=jnp.float32)
        for part in range(3):
            out_refs[part][...] = product[:, part * DK : (part + 1) * DK]

    for at, step in enumerate(steps):

        @pl.when(pl.program_id(0) == at)
        def _(at=at, step=step):
            if step < 3:
                block(refs[at][...])
            else:
                block(jnp.where(where_ref[10] == 1, refs[at + 1][...], refs[at][...]))


def unpack_kernel(back_ref, out_ref, dlogit_ref, ddecay_ref):
    for source in range(back_ref.shape[0]):
        column = slice(2 * source * DK, 2 * (source + 1) * DK)
        out_ref[:, column] = back_ref[source, 0:CHUNK, :]
        ddecay_ref[:, column] = back_ref[source, CHUNK : 2 * CHUNK, :].astype(jnp.float32)
        tail = back_ref[source, 2 * CHUNK :, :].astype(jnp.float32)
        row = tail[0:1] + tail[1:2]
        for s in range(2):
            dlogit_ref[2 * source + s : 2 * source + s + 1, :] = row[:, s * DK : (s + 1) * DK]


def head_split(tokens, w_query, w_key, w_value, beta_logit, log_decay, grad_out):
    ctx = lax.axis_size("ctx")
    place = lax.axis_index("ctx")
    group = lax.axis_index("groups")
    across, core = lax.axis_index("fsdp"), lax.axis_index("head")
    length, depth = tokens.shape
    share, columns = w_query.shape
    total = ctx * length
    bf16, f32 = jnp.bfloat16, jnp.float32
    whole = pl.BlockSpec(memory_space=pltpu.VMEM)
    scalars = pl.BlockSpec(memory_space=pltpu.SMEM)
    sources = [place, place + 1 - 2 * (place % 2), (place + 2) % ctx, ctx - 1 - place]
    where = jnp.stack(
        [place, group]
        + [2 * a + c for c in (core, 1 - core) for a in (across, 1 - across)]
        + sources
        + [((place == 0) | (place == ctx - 1)).astype(jnp.int32)]
    ).astype(jnp.int32)

    def shape(dims, kind):
        return jax.ShapeDtypeStruct(dims, kind)

    def after(x, earlier):
        return lax.optimization_barrier((x, earlier))

    def along(x, axis, hop):
        count = lax.axis_size(axis)
        return lax.ppermute(x, axis, [(i, (i + hop) % count) for i in range(count)])

    tok = pl.pallas_call(
        pack_tokens_kernel,
        out_shape=shape((share, length), bf16),
        in_specs=[scalars, whole],
        out_specs=whole,
        name="pack_tokens",
    )(where, tokens)
    sizes = [share + EXTRA] + [share // 2 + EXTRA] * (ctx - 1)
    packed = pl.pallas_call(
        functools.partial(pack_kernel, ctx),
        out_shape=[shape((size, HEAD_COLUMNS), bf16) for size in sizes * 2],
        in_specs=[scalars] + [whole] * 6,
        out_specs=[whole] * (2 * ctx),
        name="pack",
    )(where, w_query, w_key, w_value, log_decay, grad_out, beta_logit)

    near = [along(tok, "ctx", d) for d in range(1, ctx)]
    first, near[0] = after(packed[1:ctx], near[0])
    first = [along(x, "ctx", d + 1) for d, x in enumerate(first)]
    tok = jnp.concatenate([tok] + near, axis=0)
    tok_x = along(tok, "fsdp", 1)
    (tok_c, tok_xc), first = after((tok, tok_x), first)
    toks = (tok, tok_x, along(tok_c, "head", 1), along(tok_xc, "head", 1))
    all_tokens, own = pl.pallas_call(
        functools.partial(unpack_tokens_kernel, ctx),
        out_shape=[shape((ctx, total, share), bf16), shape((share, total), bf16)],
        in_specs=[scalars] + [whole] * 4,
        out_specs=[whole] * 2,
        name="unpack_tokens",
    )(where, *toks)
    first_swapped = [along(x, "groups", 1) for x in first]
    second, (first[2], first_swapped[0], first_swapped[1]) = after(
        packed[ctx + 1 :], (first[2], first_swapped[0], first_swapped[1])
    )
    second = [along(x, "ctx", d + 1) for d, x in enumerate(second)]

    grads = []
    back = None
    for slot, direct in enumerate((first, second)):
        if slot:
            direct, back = after(direct, back)
        swapped = [along(x, "groups", 1) for x in direct] if slot else first_swapped
        earlier = [] if back is None else [back]
        grad, back = pl.pallas_call(
            functools.partial(head_kernel, ctx, slot),
            out_shape=[
                shape((total, HEAD_COLUMNS), bf16),
                shape((ctx, 2 * CHUNK + TAIL, (slot + 1) * DK), bf16),
            ],
            in_specs=[scalars] + [whole] * (1 + ctx + ctx - 1 + slot),
            out_specs=[whole] * 2,
            scratch_shapes=[
                pltpu.VMEM((depth, HEAD_COLUMNS), bf16),
                pltpu.VMEM((total, HEAD_COLUMNS), f32),
                pltpu.VMEM((total, DK), f32),
                pltpu.VMEM((total, DV), f32),
                pltpu.VMEM((ctx, CHUNK), f32),
                pltpu.VMEM((ctx, CHUNK, DV), bf16),
                pltpu.VMEM((ctx, CHUNK), f32),
                pltpu.VMEM((ctx, CHUNK, DK), bf16),
            ],
            cost_estimate=pl.CostEstimate(flops=12_000_000_000, transcendentals=0, bytes_accessed=8_000_000),
            name=f"head_{slot}",
        )(where, all_tokens, packed[slot * ctx], *direct, *swapped, *earlier)
        if slot:
            grad, grads[0][1:3] = after(grad, grads[0][1:3])
        two = lax.ppermute(grad, "ctx", [(0, 2), (1, 3), (2, 0), (3, 1)])
        pair = lax.ppermute(grad, "ctx", [(0, 1), (1, 0), (2, 3), (3, 2)])
        (grad, two), pair = after((grad, two), pair)
        if slot:
            (grad, two, back), grads[0][3:5] = after((grad, two, back), grads[0][3:5])
        middle = lax.ppermute(grad, "ctx", [(1, 2), (2, 1)])
        far = lax.ppermute(two, "ctx", [(2, 3), (1, 0)])
        grads.append([grad, pair, two, middle, far])
    back = lax.all_to_all(back, "ctx", 0, 0)

    results = ()
    for slot, steps in ((0, (0, 1, 2, 3)), (1, (0, 1, 2)), (1, (3,))):
        parts = [grads[slot][step] for step in steps] + ([grads[slot][4]] if 3 in steps else [])
        column = pl.BlockSpec((share, DK), lambda i, ref, s=slot, b=steps[0]: (0, 2 * ref[6 + b + i] + s))
        results = pl.pallas_call(
            functools.partial(weight_gradient_kernel, steps),
            grid_spec=pltpu.PrefetchScalarGridSpec(
                num_scalar_prefetch=1,
                grid=(len(steps),),
                in_specs=[whole] * (1 + len(parts))
                + [pl.BlockSpec(memory_space=pl.ANY)] * len(results),
                out_specs=[column] * 3,
            ),
            out_shape=[shape((share, columns), f32)] * 3,
            input_output_aliases={2 + len(parts) + i: i for i in range(len(results))},
            name=f"weight_gradient_{slot}_{steps[0]}",
        )(where, own, *parts, *results)

    attn_out, grad_beta, grad_decay = pl.pallas_call(
        unpack_kernel,
        out_shape=[shape((length, columns), bf16), shape((columns // DK, length), f32), shape((length, columns), f32)],
        in_specs=[whole],
        out_specs=[whole] * 3,
        name="unpack",
    )(back)
    return (attn_out, *results, grad_beta, grad_decay)


def prefix_2(x, axis, join, neutral, backward):
    count = lax.axis_size(axis)
    place = lax.axis_index(axis)
    ahead = count - 1 - place if backward else place
    gathered = jax.tree.map(
        lambda a, kind: lax.all_gather(a.astype(kind), axis), x, (jnp.bfloat16, jnp.bfloat16)
    )
    state = jax.tree.map(lambda a, e: jnp.zeros_like(a) + jnp.asarray(e, a.dtype), x, neutral)

    def one(hop, state):
        source = count - 1 - hop if backward else hop
        return join(
            state,
            jax.tree.map(
                lambda a, own: lax.dynamic_index_in_dim(a, source, 0, False).astype(own.dtype),
                gathered,
                x,
            ),
        )

    return lax.fori_loop(0, ahead, one, state)


def normalize(vectors):
    return vectors * lax.rsqrt(jnp.sum(vectors * vectors, axis=-1, keepdims=True) + epsilon)


def heads_first(matrix, heads):
    return matrix.reshape(matrix.shape[0], heads, -1).transpose(1, 0, 2)


def span_step(memory, queries, key_vecs, val_vecs, strength, forgetting_exponent):
    largest_value = lax.Precision.HIGHEST
    length = queries.shape[1]
    cumulate = jnp.cumsum(forgetting_exponent, axis=1)
    growth = jnp.exp(cumulate)
    shrink = jnp.exp(-cumulate)
    key_up = key_vecs * growth
    key_down = key_vecs * shrink
    query_up = queries * growth
    row_ids = lax.broadcasted_iota(jnp.int32, (length, length), 0)
    col_ids = lax.broadcasted_iota(jnp.int32, (length, length), 1)
    strict = (row_ids > col_ids).astype(jnp.float32)
    within = (row_ids >= col_ids).astype(jnp.float32)
    affinity = jnp.einsum("bcd,bsd->bcs", key_up, key_down, precision=largest_value) * strict
    system = jnp.eye(length, dtype=jnp.float32) + strength[:, :, None] * affinity
    target = strength[:, :, None] * (
        val_vecs - jnp.einsum("bcd,bdw->bcw", key_up, memory, precision=largest_value)
    )
    update = lax.linalg.triangular_solve(system, target, left_side=True, lower=True)
    scores = jnp.einsum("bcd,bsd->bcs", query_up, key_down, precision=largest_value) * within
    emitted = jnp.einsum("bcd,bdw->bcw", query_up, memory, precision=largest_value)
    emitted = emitted + jnp.einsum("bcs,bsw->bcw", scores, update, precision=largest_value)
    at_end = growth[:, -1, :]
    renewed = at_end[:, :, None] * memory + jnp.einsum(
        "bsd,bsw->bdw", key_down * at_end[:, None, :], update, precision=largest_value
    )
    return (emitted, renewed)


def scan_spans(memory, queries, key_vecs, val_vecs, strength, forgetting_exponent):
    count = queries.shape[1] // SPAN

    def to_blocks(array):
        shaped = array.reshape((array.shape[0], count, SPAN) + array.shape[2:])
        return jnp.swapaxes(shaped, 0, 1)

    def advance(carried, blocks):
        emitted, renewed = span_step(carried, *blocks)
        return (renewed, emitted)

    blocks = (
        to_blocks(queries),
        to_blocks(key_vecs),
        to_blocks(val_vecs),
        to_blocks(strength),
        to_blocks(forgetting_exponent),
    )
    final, emitted = lax.scan(advance, memory, blocks)
    emitted = jnp.swapaxes(emitted, 0, 1)
    return (emitted.reshape(emitted.shape[0], count * SPAN, emitted.shape[-1]), final)


def compose(earlier, later):
    largest_value = lax.Precision.HIGHEST
    joined = jnp.einsum("hij,hjk->hik", later[0], earlier[0], precision=largest_value)
    shifted = jnp.einsum("hij,hjv->hiv", later[0], earlier[1], precision=largest_value) + later[1]
    return (joined, shifted)


def per_device(tokens, w_query, w_key, w_value, beta_logit, log_decay, grad_out):
    largest_value = lax.Precision.HIGHEST
    length = tokens.shape[0]
    columns = w_query.shape[1]
    heads = columns // DK
    shard_rows = (
        lax.all_gather(w_query, "ctx", axis=0, tiled=True),
        lax.all_gather(w_key, "ctx", axis=0, tiled=True),
        lax.all_gather(w_value, "ctx", axis=0, tiled=True),
    )
    window = tokens
    query_raw, key_raw, value_raw = tuple(
        (jnp.dot(window, weights, preferred_element_type=jnp.float32) for weights in shard_rows)
    )

    def shard_pass(query_in, key_in, value_in, logits, log_gates):
        queries = normalize(heads_first(query_in, heads))
        key_vecs = normalize(heads_first(key_in, heads))
        val_vecs = heads_first(value_in, heads)
        widened = jnp.concatenate([jnp.zeros((heads, length, DK), jnp.float32), val_vecs], axis=2)
        initial = jnp.concatenate(
            [
                jnp.broadcast_to(jnp.eye(DK, dtype=jnp.float32), (heads, DK, DK)),
                jnp.zeros((heads, DK, DV), jnp.float32),
            ],
            axis=2,
        )
        return scan_spans(
            initial,
            queries,
            key_vecs,
            widened,
            jax.nn.sigmoid(logits),
            heads_first(log_gates, heads),
        )

    (mixed, final), pullback = jax.vjp(
        shard_pass, query_raw, key_raw, value_raw, beta_logit, log_decay
    )
    transit = final[:, :, :DK]
    offset = final[:, :, DK:]
    query_carried_over = mixed[:, :, :DK]
    local_output = mixed[:, :, DK:]
    output_cotangent = grad_out.reshape(length, heads, DV).transpose(1, 0, 2).astype(jnp.float32)
    contribution = jnp.einsum(
        "mij,mif->mjf", query_carried_over, output_cotangent, precision=largest_value
    )
    identity = (
        jnp.broadcast_to(jnp.eye(DK, dtype=jnp.float32), (heads, DK, DK)),
        jnp.zeros((heads, DK, DV), jnp.float32),
    )
    prefix = prefix_2((transit, offset), "ctx", compose, identity, False)
    incoming_state = prefix[1]
    suffix = prefix_2((jnp.swapaxes(transit, 1, 2), contribution), "ctx", compose, identity, True)
    adjoint_state = suffix[1]
    complete_output = local_output + jnp.einsum(
        "npg,ngj->npj", query_carried_over, incoming_state, precision=largest_value
    )
    attn_out = complete_output.transpose(1, 0, 2).reshape(length, heads * DV).astype(jnp.bfloat16)
    d_mixed = jnp.concatenate(
        [
            jnp.einsum("efu,egu->efg", output_cotangent, incoming_state, precision=largest_value),
            output_cotangent,
        ],
        axis=2,
    )
    d_final = jnp.concatenate(
        [
            jnp.einsum("pgx,pcx->pgc", adjoint_state, incoming_state, precision=largest_value),
            adjoint_state,
        ],
        axis=2,
    )
    d_query, d_key, d_value, grad_beta, grad_decay = pullback((d_mixed, d_final))
    grad_projected = jnp.concatenate([d_query, d_key, d_value], axis=1).astype(jnp.bfloat16)
    window = tokens
    summed = lax.psum_scatter(
        jnp.einsum("td,tc->dc", window, grad_projected, preferred_element_type=jnp.float32).astype(
            jnp.bfloat16
        ),
        "ctx",
        scatter_dimension=0,
        tiled=True,
    ).astype(jnp.float32)
    return (
        attn_out,
        summed[:, :columns],
        summed[:, columns : 2 * columns],
        summed[:, 2 * columns :],
        grad_beta,
        grad_decay,
    )


def device_program(tokens, w_query, *rest):
    ctx = lax.axis_size("ctx")
    heads = w_query.shape[1] // DK
    split = heads == 2 * ctx and ctx == 4 and tokens.shape[0] == CHUNK and w_query.shape[0] * ctx == tokens.shape[1]
    split = split and lax.axis_size("groups") == lax.axis_size("fsdp") == lax.axis_size("head") == 2
    split = split and w_query.shape[0] % 64 == 0
    return (head_split if split else per_device)(tokens, w_query, *rest)


def solution(mesh):
    return jax.shard_map(
        device_program,
        mesh=mesh,
        in_specs=(
            P(("groups", "ctx"), None),
            P("ctx", ("fsdp", "head")),
            P("ctx", ("fsdp", "head")),
            P("ctx", ("fsdp", "head")),
            P(("fsdp", "head"), ("groups", "ctx")),
            P(("groups", "ctx"), ("fsdp", "head")),
            P(("groups", "ctx"), ("fsdp", "head")),
        ),
        out_specs=(
            P(("groups", "ctx"), ("fsdp", "head")),
            P(("groups", "ctx"), ("fsdp", "head")),
            P(("groups", "ctx"), ("fsdp", "head")),
            P(("groups", "ctx"), ("fsdp", "head")),
            P(("fsdp", "head"), ("groups", "ctx")),
            P(("groups", "ctx"), ("fsdp", "head")),
        ),
        check_vma=False,
    )
```

```python
import functools

import jax
import jax.numpy as jnp
from jax import lax
from jax.experimental import pallas as pl
from jax.experimental.pallas import tpu as pltpu
from jax.sharding import PartitionSpec as P

DK = 128
DV = 128
SPAN = 64
CHUNK = 128
TAIL = 16
EXTRA = 96
HEAD_COLUMNS = 2 * DK + DV

epsilon = 1e-06
HIGHEST = lax.Precision.HIGHEST
NN = (((1,), (0,)), ((), ()))
NT = (((1,), (1,)), ((), ()))
TN = (((0,), (0,)), ((), ()))


def narrow(x):
    return x.astype(jnp.bfloat16)


def dot(a, b, dims, passes):
    if passes == 6:
        return lax.dot_general(a, b, dims, precision=HIGHEST, preferred_element_type=jnp.float32)
    a_high, b_high = narrow(a), narrow(b)
    total = lax.dot_general(a_high, b_high, dims, preferred_element_type=jnp.float32)
    if passes >= 3:
        a_low = narrow(a - a_high.astype(jnp.float32))
        b_low = narrow(b - b_high.astype(jnp.float32))
        total = total + lax.dot_general(a_high, b_low, dims, preferred_element_type=jnp.float32)
        total = total + lax.dot_general(a_low, b_high, dims, preferred_element_type=jnp.float32)
    return total


PASSES = dict(
    decay=1, pairs=3, inverse=3, solve=3, read=1, carry=3, sent=1, scan=1, emit=1, update=1,
    d_update=3, d_value=3, d_pairs=1, d_up=1, d_up_state=1, d_kd=1, d_kend=1, d_decay=3,
)


def run(name, a, b, dims):
    return dot(a, b, dims, PASSES[name])


def recurrence(raw_ref, decay_ref, logit_ref, cot_ref, out_ref, grad_ref, dlogit_ref, ddecay_ref):
    count = raw_ref.shape[0] // CHUNK
    spans = range(count)
    rows = lax.broadcasted_iota(jnp.int32, (CHUNK, CHUNK), 0)
    cols = lax.broadcasted_iota(jnp.int32, (CHUNK, CHUNK), 1)
    within = rows >= cols
    strict = rows > cols
    diagonal = rows == cols
    running = within.astype(jnp.float32)

    q, k, v, rq, rk, up, down, end = [], [], [], [], [], [], [], []
    qu, ku, kd, kend, beta_row, cot = [], [], [], [], [], []
    for n in spans:
        here = slice(n * CHUNK, (n + 1) * CHUNK)
        q_raw = raw_ref[here, 0:DK]
        k_raw = raw_ref[here, DK : 2 * DK]
        v.append(raw_ref[here, 2 * DK : 3 * DK])
        rq.append(lax.rsqrt(jnp.sum(q_raw * q_raw, axis=1, keepdims=True) + epsilon))
        rk.append(lax.rsqrt(jnp.sum(k_raw * k_raw, axis=1, keepdims=True) + epsilon))
        q.append(q_raw * rq[n])
        k.append(k_raw * rk[n])
        summed = run("decay", running, decay_ref[here, :], NN)
        up.append(jnp.exp(summed))
        down.append(jnp.exp(-summed))
        end.append(up[n][CHUNK - 1 : CHUNK, :])
        qu.append(q[n] * up[n])
        ku.append(k[n] * up[n])
        kd.append(k[n] * down[n])
        kend.append(kd[n] * end[n])
        beta_row.append(jax.nn.sigmoid(logit_ref[n : n + 1, :]))
        cot.append(cot_ref[here, :])

    scores, system, inverse = [], [], []
    for n in spans:
        pairs = run("pairs", jnp.concatenate([qu[n], ku[n]], axis=0), kd[n], NT)
        scores.append(jnp.where(within, pairs[:CHUNK], 0.0))
        beta_col = jnp.transpose(jnp.broadcast_to(beta_row[n], (CHUNK, CHUNK)))
        system.append(jnp.where(strict, pairs[CHUNK:] * beta_col, 0.0))
        pair_block = (rows // 2) == (cols // 2)
        inverse.append(diagonal.astype(jnp.float32) - jnp.where(pair_block, system[n], 0.0))
    size = 2
    while size < CHUNK:
        joined = ((rows // (2 * size)) == (cols // (2 * size))) & ((rows // size) != (cols // size))
        halves = [run("inverse", jnp.where(joined, system[n], 0.0), inverse[n], NN) for n in spans]
        inverse = [inverse[n] - run("inverse", inverse[n], halves[n], NN) for n in spans]
        size *= 2

    solve = [inverse[n] * beta_row[n] for n in spans]
    wu = [run("solve", solve[n], jnp.concatenate([ku[n], v[n]], axis=1), NN) for n in spans]
    pwu = [run("read", scores[n], wu[n], NN) for n in spans]
    kwu = [run("carry", kend[n], wu[n], TN) for n in spans]
    query_through = [qu[n] - pwu[n][:, :DK] for n in spans]
    transit = [
        jnp.where(diagonal, jnp.broadcast_to(end[n], (DK, DK)), 0.0) - kwu[n][:, :DK] for n in spans
    ]
    sent = [run("sent", query_through[n], cot[n], TN) for n in spans]

    state = [None] * (count + 1)
    adjoint = [None] * (count + 1)
    for n in spans:
        m = count - 1 - n
        own = kwu[n][:, DK:]
        state[n + 1] = own if n == 0 else run("scan", transit[n], state[n], NN) + own
        adjoint[m] = sent[m] if n == 0 else run("scan", transit[m], adjoint[m + 1], TN) + sent[m]

    for n in spans:
        here = slice(n * CHUNK, (n + 1) * CHUNK)
        w = wu[n][:, :DK]
        update = wu[n][:, DK:]
        emitted = pwu[n][:, DK:]
        d_update = run("d_update", scores[n], cot[n], TN)
        if n > 0:
            emitted = emitted + run("emit", query_through[n], state[n], NN)
            update = update - run("update", w, state[n], NN)
        if n < count - 1:
            d_update = d_update + run("d_update", kend[n], adjoint[n + 1], NN)
        out_ref[n] = emitted.astype(out_ref.dtype)
        d_value = run("d_value", solve[n], d_update, TN)
        both = jnp.concatenate([cot[n], -d_value], axis=0)
        pairs = run("d_pairs", both, update, NT)
        d_pairs = jnp.concatenate(
            [jnp.where(within, pairs[:CHUNK], 0.0), jnp.where(strict, pairs[CHUNK:], 0.0)], axis=0
        )
        d_up = run("d_up", d_pairs, kd[n], NN)
        if n > 0:
            d_up = d_up + run("d_up_state", both, state[n], NT)
        d_qu, d_ku = d_up[:CHUNK], d_up[CHUNK:]
        d_kd = run("d_kd", d_pairs, jnp.concatenate([qu[n], ku[n]], axis=0), TN)
        d_k = d_ku * up[n] + d_kd * down[n]
        d_sum = d_qu * qu[n] + d_ku * ku[n] - d_kd * kd[n]
        d_decay_end = jnp.zeros((1, DK), jnp.float32)
        if n < count - 1:
            d_kend = run("d_kend", update, adjoint[n + 1], NT)
            d_k = d_k + d_kend * (end[n] * down[n])
            ended = d_kend * kend[n]
            d_sum = d_sum - ended
            d_decay_end = jnp.sum(ended, axis=0, keepdims=True)
            if n > 0:
                kept = jnp.sum(jnp.transpose(adjoint[n + 1] * state[n]), axis=0, keepdims=True)
                d_decay_end = d_decay_end + end[n] * kept
        ddecay_ref[n] = (run("d_decay", running, d_sum, TN) + d_decay_end).astype(ddecay_ref.dtype)
        d_q = d_qu * up[n]
        d_q = rq[n] * (d_q - q[n] * jnp.sum(q[n] * d_q, axis=1, keepdims=True))
        d_k = rk[n] * (d_k - k[n] * jnp.sum(k[n] * d_k, axis=1, keepdims=True))
        grad_ref[here, 0:DK] = d_q.astype(grad_ref.dtype)
        grad_ref[here, DK : 2 * DK] = d_k.astype(grad_ref.dtype)
        grad_ref[here, 2 * DK : 3 * DK] = d_value.astype(grad_ref.dtype)
        aligned = jnp.sum(jnp.transpose(d_value * update), axis=0, keepdims=True)
        dlogit_ref[n : n + 1, :] = aligned * jnp.exp(-logit_ref[n : n + 1, :])


def split_two(x):
    high = narrow(x)
    return high, narrow(x - high.astype(jnp.float32))


def tail_rows(x):
    high, low = split_two(x)
    index = lax.broadcasted_iota(jnp.int32, (TAIL, x.shape[1]), 0)
    high = jnp.broadcast_to(high.astype(jnp.float32), index.shape)
    low = jnp.broadcast_to(low.astype(jnp.float32), index.shape)
    return narrow(jnp.where(index == 0, high, jnp.where(index == 1, low, 0.0)))


def lanes(start):
    return pl.ds(pl.multiple_of(start, DK), DK)


def tile_rows(start, size):
    return pl.ds(pl.multiple_of(start, 32), size)


def pack_tokens_kernel(where_ref, tokens_ref, tok_ref):
    share = tok_ref.shape[0]
    for j in range(tokens_ref.shape[1] // share):

        @pl.when(where_ref[2] == j)
        def _(j=j):
            block = tokens_ref[:, j * share : (j + 1) * share]
            full = share // DK
            for g in range(full):
                tok_ref[g * CHUNK : (g + 1) * CHUNK, :] = block[:, g * DK : (g + 1) * DK]
            rest = block[:, full * DK :]
            tok_ref[full * CHUNK :, :] = jnp.concatenate([rest[: CHUNK // 2], rest[CHUNK // 2 :]], axis=1)


def unpack_tokens_kernel(ctx, where_ref, *refs):
    tok_refs, all_ref, own_ref = refs[:4], refs[4], refs[5]
    place = where_ref[0]
    share = own_ref.shape[0]
    full = share // DK
    for j in range(4):
        block = where_ref[2 + j]
        for d in range(ctx):
            source = lax.rem(place + ctx - d, ctx)
            start = source * CHUNK
            base = d * share
            for g in range(full):
                piece = tok_refs[j][base + g * CHUNK : base + (g + 1) * CHUNK, :]
                all_ref[block, tile_rows(start, CHUNK), g * DK : (g + 1) * DK] = piece
            rest = tok_refs[j][base + full * CHUNK : base + share, :]
            all_ref[block, tile_rows(start, CHUNK // 2), full * DK :] = rest[:, : DK // 2]
            all_ref[block, tile_rows(start + CHUNK // 2, CHUNK // 2), full * DK :] = rest[:, DK // 2 :]
    for n in range(ctx):
        piece = all_ref[place, n * CHUNK : (n + 1) * CHUNK, :].astype(jnp.float32)
        own_ref[:, n * CHUNK : (n + 1) * CHUNK] = narrow(jnp.transpose(piece))


def pack_kernel(ctx, where_ref, wq_ref, wk_ref, wv_ref, decay_ref, cot_ref, logit_ref, *out_refs):
    place, group = where_ref[0], where_ref[1]
    half = wq_ref.shape[0] // 2
    for s in range(2):
        for d in range(ctx):
            head = 2 * lax.rem(place + d, ctx) + s
            column = lanes(head * DK)
            out = out_refs[s * ctx + d]
            size = out.shape[0] - EXTRA
            rows = slice(None) if d == 0 else tile_rows(group * half, half)
            for part, ref in enumerate((wq_ref, wk_ref, wv_ref)):
                out[0:size, part * DK : (part + 1) * DK] = ref[rows, column]
            decay = narrow(decay_ref[:, column])
            cot = cot_ref[:, column]
            out[size : size + 96, 0:DK] = decay[0:96]
            out[size : size + 32, DK : 2 * DK] = decay[96:128]
            out[size + 32 : size + 96, DK : 2 * DK] = cot[0:64]
            out[size : size + 64, 2 * DK : 3 * DK] = cot[64:128]
            out[size + 64 : size + 80, 2 * DK : 3 * DK] = tail_rows(logit_ref[pl.ds(head, 1), :])
            out[size + 80 : size + 96, 2 * DK : 3 * DK] = jnp.zeros((16, DK), out.dtype)


def head_kernel(ctx, slot, where_ref, *refs):
    all_ref, refs = refs[0], refs[1:]
    direct, refs = refs[:ctx], refs[ctx:]
    swapped, refs = refs[: ctx - 1], refs[ctx - 1 :]
    if slot:
        earlier_ref, refs = refs[0], refs[1:]
    grad_ref, back_ref, w, raw, decay, cot, logit, out, dlogit, ddecay = refs
    place, group = where_ref[0], where_ref[1]
    share = direct[0].shape[0] - EXTRA
    half = share // 2
    for d in range(ctx):
        source = lax.rem(place + ctx - d, ctx)
        ref = direct[d]
        if d == 0:
            w[tile_rows(source * share, share), :] = ref[0:share, :]
            size = share
        else:
            w[tile_rows(source * share + group * half, half), :] = ref[0:half, :]
            w[tile_rows(source * share + (1 - group) * half, half), :] = swapped[d - 1][0:half, :]
            size = half
        start = source * CHUNK
        decay[tile_rows(start, 96), :] = ref[size : size + 96, 0:DK].astype(jnp.float32)
        decay[tile_rows(start + 96, 32), :] = ref[size : size + 32, DK : 2 * DK].astype(jnp.float32)
        cot[tile_rows(start, 64), :] = ref[size + 32 : size + 96, DK : 2 * DK].astype(jnp.float32)
        cot[tile_rows(start + 64, 64), :] = ref[size : size + 64, 2 * DK : 3 * DK].astype(jnp.float32)
        tail = ref[size + 64 : size + 80, 2 * DK : 3 * DK].astype(jnp.float32)
        logit[pl.ds(source, 1), :] = tail[0:1] + tail[1:2]
    projected = 0.0
    for j in range(ctx):
        projected = projected + lax.dot_general(
            all_ref[j], w[j * share : (j + 1) * share, :], NN, preferred_element_type=jnp.float32
        )
    raw[...] = projected
    recurrence(raw, decay, logit, cot, out, grad_ref, dlogit, ddecay)
    lane = slice(slot * DK, (slot + 1) * DK)
    if slot:
        back_ref[:, :, 0:DK] = earlier_ref[...]
    for n in range(ctx):
        back_ref[n, 0:CHUNK, lane] = out[n]
        back_ref[n, CHUNK : 2 * CHUNK, lane] = ddecay[n]
        back_ref[n, 2 * CHUNK :, lane] = tail_rows(dlogit[n : n + 1, :])


def weight_gradient_kernel(steps, forwarded, where_ref, own_ref, *refs):
    out_refs = refs[-3:]

    def block(gradient):
        product = lax.dot_general(own_ref[...], gradient, NN, preferred_element_type=jnp.float32)
        for part in range(3):
            out_refs[part][...] = product[:, part * DK : (part + 1) * DK]

    for at, step in enumerate(steps):

        @pl.when(pl.program_id(0) == at)
        def _(at=at, step=step):
            if step < 3 or not forwarded:
                block(refs[at][...])
            else:
                block(jnp.where(where_ref[14] == 1, refs[at + 1][...], refs[at][...]))


def unpack_kernel(back_ref, out_ref, dlogit_ref, ddecay_ref):
    for source in range(back_ref.shape[0]):
        column = slice(2 * source * DK, 2 * (source + 1) * DK)
        out_ref[:, column] = back_ref[source, 0:CHUNK, :]
        ddecay_ref[:, column] = back_ref[source, CHUNK : 2 * CHUNK, :].astype(jnp.float32)
        tail = back_ref[source, 2 * CHUNK :, :].astype(jnp.float32)
        row = tail[0:1] + tail[1:2]
        for s in range(2):
            dlogit_ref[2 * source + s : 2 * source + s + 1, :] = row[:, s * DK : (s + 1) * DK]


def head_split(tokens, w_query, w_key, w_value, beta_logit, log_decay, grad_out):
    ctx = lax.axis_size("ctx")
    place = lax.axis_index("ctx")
    group = lax.axis_index("groups")
    across, core = lax.axis_index("fsdp"), lax.axis_index("head")
    length, depth = tokens.shape
    share, columns = w_query.shape
    total = ctx * length
    bf16, f32 = jnp.bfloat16, jnp.float32
    whole = pl.BlockSpec(memory_space=pltpu.VMEM)
    scalars = pl.BlockSpec(memory_space=pltpu.SMEM)
    sources = [place, place + 1 - 2 * (place % 2), (place + 2) % ctx, ctx - 1 - place]
    where = jnp.stack(
        [place, group]
        + [2 * a + c for c in (core, 1 - core) for a in (across, 1 - across)]
        + [(place + ctx - d) % ctx for d in range(ctx)]
        + sources
        + [((place == 0) | (place == ctx - 1)).astype(jnp.int32)]
    ).astype(jnp.int32)

    def shape(dims, kind):
        return jax.ShapeDtypeStruct(dims, kind)

    def after(x, earlier):
        return lax.optimization_barrier((x, earlier))

    def along(x, axis, hop):
        count = lax.axis_size(axis)
        return lax.ppermute(x, axis, [(i, (i + hop) % count) for i in range(count)])

    tok = pl.pallas_call(
        pack_tokens_kernel,
        out_shape=shape((share, length), bf16),
        in_specs=[scalars, whole],
        out_specs=whole,
        name="pack_tokens",
    )(where, tokens)
    sizes = [share + EXTRA] + [share // 2 + EXTRA] * (ctx - 1)
    packed = pl.pallas_call(
        functools.partial(pack_kernel, ctx),
        out_shape=[shape((size, HEAD_COLUMNS), bf16) for size in sizes * 2],
        in_specs=[scalars] + [whole] * 6,
        out_specs=[whole] * (2 * ctx),
        name="pack",
    )(where, w_query, w_key, w_value, log_decay, grad_out, beta_logit)

    near = [along(tok, "ctx", d) for d in range(1, ctx)]
    first, near[0] = after(packed[1:ctx], near[0])
    first = [along(x, "ctx", d + 1) for d, x in enumerate(first)]
    tok = jnp.concatenate([tok] + near, axis=0)
    tok_x = along(tok, "fsdp", 1)
    half = share // 2
    swapped = [along(first[0][:half], "groups", 1)]
    (tok_c, tok_xc, first[1], first[2]), swapped[0] = after((tok, tok_x, first[1], first[2]), swapped[0])
    toks = (tok, tok_x, along(tok_c, "head", 1), along(tok_xc, "head", 1))
    swapped += [along(x[:half], "groups", 1) for x in first[1:]]
    all_tokens, own = pl.pallas_call(
        functools.partial(unpack_tokens_kernel, ctx),
        out_shape=[shape((ctx, total, share), bf16), shape((share, total), bf16)],
        in_specs=[scalars] + [whole] * 4,
        out_specs=[whole] * 2,
        name="unpack_tokens",
    )(where, *toks)
    second, (first[1], first[2], own) = after(packed[ctx + 1 :], (first[1], first[2], own))
    second = [along(x, "ctx", d + 1) for d, x in enumerate(second)]

    grads = []
    back = None
    for slot, direct in enumerate((first, second)):
        if slot:
            direct, back = after(direct, back)
            swapped = [along(x[:half], "groups", 1) for x in direct]
        earlier = [] if back is None else [back]
        grad, back = pl.pallas_call(
            functools.partial(head_kernel, ctx, slot),
            out_shape=[
                shape((total, HEAD_COLUMNS), bf16),
                shape((ctx, 2 * CHUNK + TAIL, (slot + 1) * DK), bf16),
            ],
            in_specs=[scalars] + [whole] * (1 + ctx + ctx - 1 + slot),
            out_specs=[whole] * 2,
            scratch_shapes=[
                pltpu.VMEM((depth, HEAD_COLUMNS), bf16),
                pltpu.VMEM((total, HEAD_COLUMNS), f32),
                pltpu.VMEM((total, DK), f32),
                pltpu.VMEM((total, DV), f32),
                pltpu.VMEM((ctx, CHUNK), f32),
                pltpu.VMEM((ctx, CHUNK, DV), bf16),
                pltpu.VMEM((ctx, CHUNK), f32),
                pltpu.VMEM((ctx, CHUNK, DK), bf16),
            ],
            cost_estimate=pl.CostEstimate(flops=12_000_000_000, transcendentals=0, bytes_accessed=8_000_000),
            name=f"head_{slot}",
        )(where, all_tokens, packed[slot * ctx], *direct, *swapped, *earlier)
        if slot == 0:
            hops = [along(grad, "ctx", d) for d in range(1, ctx)]
            grads.append([grad] + hops)
            continue
        (grad, back), grads[0] = after((grad, back), grads[0])
        two = lax.ppermute(grad, "ctx", [(0, 2), (1, 3), (2, 0), (3, 1)])
        pair = lax.ppermute(grad, "ctx", [(0, 1), (1, 0), (2, 3), (3, 2)])
        (grad, two), pair = after((grad, two), pair)
        middle = lax.ppermute(grad, "ctx", [(1, 2), (2, 1)])
        far = lax.ppermute(two, "ctx", [(2, 3), (1, 0)])
        grads.append([grad, pair, two, middle, far])
    back = lax.all_to_all(back, "ctx", 0, 0)

    results = ()
    for slot, steps in ((0, (0, 1, 2, 3)), (1, (0, 1, 2)), (1, (3,))):
        parts = [grads[slot][step] for step in steps] + ([grads[slot][4]] if slot and 3 in steps else [])
        column = pl.BlockSpec((share, DK), lambda i, ref, s=slot, b=steps[0]: (0, 2 * ref[6 + 4 * s + b + i] + s))
        results = pl.pallas_call(
            functools.partial(weight_gradient_kernel, steps, slot == 1),
            grid_spec=pltpu.PrefetchScalarGridSpec(
                num_scalar_prefetch=1,
                grid=(len(steps),),
                in_specs=[whole] * (1 + len(parts))
                + [pl.BlockSpec(memory_space=pl.ANY)] * len(results),
                out_specs=[column] * 3,
            ),
            out_shape=[shape((share, columns), f32)] * 3,
            input_output_aliases={2 + len(parts) + i: i for i in range(len(results))},
            name=f"weight_gradient_{slot}_{steps[0]}",
        )(where, own, *parts, *results)

    attn_out, grad_beta, grad_decay = pl.pallas_call(
        unpack_kernel,
        out_shape=[shape((length, columns), bf16), shape((columns // DK, length), f32), shape((length, columns), f32)],
        in_specs=[whole],
        out_specs=[whole] * 3,
        name="unpack",
    )(back)
    return (attn_out, *results, grad_beta, grad_decay)


def prefix_2(x, axis, join, neutral, backward):
    count = lax.axis_size(axis)
    place = lax.axis_index(axis)
    ahead = count - 1 - place if backward else place
    gathered = jax.tree.map(
        lambda a, kind: lax.all_gather(a.astype(kind), axis), x, (jnp.bfloat16, jnp.bfloat16)
    )
    state = jax.tree.map(lambda a, e: jnp.zeros_like(a) + jnp.asarray(e, a.dtype), x, neutral)

    def one(hop, state):
        source = count - 1 - hop if backward else hop
        return join(
            state,
            jax.tree.map(
                lambda a, own: lax.dynamic_index_in_dim(a, source, 0, False).astype(own.dtype),
                gathered,
                x,
            ),
        )

    return lax.fori_loop(0, ahead, one, state)


def normalize(vectors):
    return vectors * lax.rsqrt(jnp.sum(vectors * vectors, axis=-1, keepdims=True) + epsilon)


def heads_first(matrix, heads):
    return matrix.reshape(matrix.shape[0], heads, -1).transpose(1, 0, 2)


def span_step(memory, queries, key_vecs, val_vecs, strength, forgetting_exponent):
    largest_value = lax.Precision.HIGHEST
    length = queries.shape[1]
    cumulate = jnp.cumsum(forgetting_exponent, axis=1)
    growth = jnp.exp(cumulate)
    shrink = jnp.exp(-cumulate)
    key_up = key_vecs * growth
    key_down = key_vecs * shrink
    query_up = queries * growth
    row_ids = lax.broadcasted_iota(jnp.int32, (length, length), 0)
    col_ids = lax.broadcasted_iota(jnp.int32, (length, length), 1)
    strict = (row_ids > col_ids).astype(jnp.float32)
    within = (row_ids >= col_ids).astype(jnp.float32)
    affinity = jnp.einsum("bcd,bsd->bcs", key_up, key_down, precision=largest_value) * strict
    system = jnp.eye(length, dtype=jnp.float32) + strength[:, :, None] * affinity
    target = strength[:, :, None] * (
        val_vecs - jnp.einsum("bcd,bdw->bcw", key_up, memory, precision=largest_value)
    )
    update = lax.linalg.triangular_solve(system, target, left_side=True, lower=True)
    scores = jnp.einsum("bcd,bsd->bcs", query_up, key_down, precision=largest_value) * within
    emitted = jnp.einsum("bcd,bdw->bcw", query_up, memory, precision=largest_value)
    emitted = emitted + jnp.einsum("bcs,bsw->bcw", scores, update, precision=largest_value)
    at_end = growth[:, -1, :]
    renewed = at_end[:, :, None] * memory + jnp.einsum(
        "bsd,bsw->bdw", key_down * at_end[:, None, :], update, precision=largest_value
    )
    return (emitted, renewed)


def scan_spans(memory, queries, key_vecs, val_vecs, strength, forgetting_exponent):
    count = queries.shape[1] // SPAN

    def to_blocks(array):
        shaped = array.reshape((array.shape[0], count, SPAN) + array.shape[2:])
        return jnp.swapaxes(shaped, 0, 1)

    def advance(carried, blocks):
        emitted, renewed = span_step(carried, *blocks)
        return (renewed, emitted)

    blocks = (
        to_blocks(queries),
        to_blocks(key_vecs),
        to_blocks(val_vecs),
        to_blocks(strength),
        to_blocks(forgetting_exponent),
    )
    final, emitted = lax.scan(advance, memory, blocks)
    emitted = jnp.swapaxes(emitted, 0, 1)
    return (emitted.reshape(emitted.shape[0], count * SPAN, emitted.shape[-1]), final)


def compose(earlier, later):
    largest_value = lax.Precision.HIGHEST
    joined = jnp.einsum("hij,hjk->hik", later[0], earlier[0], precision=largest_value)
    shifted = jnp.einsum("hij,hjv->hiv", later[0], earlier[1], precision=largest_value) + later[1]
    return (joined, shifted)


def per_device(tokens, w_query, w_key, w_value, beta_logit, log_decay, grad_out):
    largest_value = lax.Precision.HIGHEST
    length = tokens.shape[0]
    columns = w_query.shape[1]
    heads = columns // DK
    shard_rows = (
        lax.all_gather(w_query, "ctx", axis=0, tiled=True),
        lax.all_gather(w_key, "ctx", axis=0, tiled=True),
        lax.all_gather(w_value, "ctx", axis=0, tiled=True),
    )
    window = tokens
    query_raw, key_raw, value_raw = tuple(
        (jnp.dot(window, weights, preferred_element_type=jnp.float32) for weights in shard_rows)
    )

    def shard_pass(query_in, key_in, value_in, logits, log_gates):
        queries = normalize(heads_first(query_in, heads))
        key_vecs = normalize(heads_first(key_in, heads))
        val_vecs = heads_first(value_in, heads)
        widened = jnp.concatenate([jnp.zeros((heads, length, DK), jnp.float32), val_vecs], axis=2)
        initial = jnp.concatenate(
            [
                jnp.broadcast_to(jnp.eye(DK, dtype=jnp.float32), (heads, DK, DK)),
                jnp.zeros((heads, DK, DV), jnp.float32),
            ],
            axis=2,
        )
        return scan_spans(
            initial,
            queries,
            key_vecs,
            widened,
            jax.nn.sigmoid(logits),
            heads_first(log_gates, heads),
        )

    (mixed, final), pullback = jax.vjp(
        shard_pass, query_raw, key_raw, value_raw, beta_logit, log_decay
    )
    transit = final[:, :, :DK]
    offset = final[:, :, DK:]
    query_carried_over = mixed[:, :, :DK]
    local_output = mixed[:, :, DK:]
    output_cotangent = grad_out.reshape(length, heads, DV).transpose(1, 0, 2).astype(jnp.float32)
    contribution = jnp.einsum(
        "mij,mif->mjf", query_carried_over, output_cotangent, precision=largest_value
    )
    identity = (
        jnp.broadcast_to(jnp.eye(DK, dtype=jnp.float32), (heads, DK, DK)),
        jnp.zeros((heads, DK, DV), jnp.float32),
    )
    prefix = prefix_2((transit, offset), "ctx", compose, identity, False)
    incoming_state = prefix[1]
    suffix = prefix_2((jnp.swapaxes(transit, 1, 2), contribution), "ctx", compose, identity, True)
    adjoint_state = suffix[1]
    complete_output = local_output + jnp.einsum(
        "npg,ngj->npj", query_carried_over, incoming_state, precision=largest_value
    )
    attn_out = complete_output.transpose(1, 0, 2).reshape(length, heads * DV).astype(jnp.bfloat16)
    d_mixed = jnp.concatenate(
        [
            jnp.einsum("efu,egu->efg", output_cotangent, incoming_state, precision=largest_value),
            output_cotangent,
        ],
        axis=2,
    )
    d_final = jnp.concatenate(
        [
            jnp.einsum("pgx,pcx->pgc", adjoint_state, incoming_state, precision=largest_value),
            adjoint_state,
        ],
        axis=2,
    )
    d_query, d_key, d_value, grad_beta, grad_decay = pullback((d_mixed, d_final))
    grad_projected = jnp.concatenate([d_query, d_key, d_value], axis=1).astype(jnp.bfloat16)
    window = tokens
    summed = lax.psum_scatter(
        jnp.einsum("td,tc->dc", window, grad_projected, preferred_element_type=jnp.float32).astype(
            jnp.bfloat16
        ),
        "ctx",
        scatter_dimension=0,
        tiled=True,
    ).astype(jnp.float32)
    return (
        attn_out,
        summed[:, :columns],
        summed[:, columns : 2 * columns],
        summed[:, 2 * columns :],
        grad_beta,
        grad_decay,
    )


def device_program(tokens, w_query, *rest):
    ctx = lax.axis_size("ctx")
    heads = w_query.shape[1] // DK
    split = heads == 2 * ctx and ctx == 4 and tokens.shape[0] == CHUNK and w_query.shape[0] * ctx == tokens.shape[1]
    split = split and lax.axis_size("groups") == lax.axis_size("fsdp") == lax.axis_size("head") == 2
    split = split and w_query.shape[0] % 64 == 0
    return (head_split if split else per_device)(tokens, w_query, *rest)


def solution(mesh):
    return jax.shard_map(
        device_program,
        mesh=mesh,
        in_specs=(
            P(("groups", "ctx"), None),
            P("ctx", ("fsdp", "head")),
            P("ctx", ("fsdp", "head")),
            P("ctx", ("fsdp", "head")),
            P(("fsdp", "head"), ("groups", "ctx")),
            P(("groups", "ctx"), ("fsdp", "head")),
            P(("groups", "ctx"), ("fsdp", "head")),
        ),
        out_specs=(
            P(("groups", "ctx"), ("fsdp", "head")),
            P(("groups", "ctx"), ("fsdp", "head")),
            P(("groups", "ctx"), ("fsdp", "head")),
            P(("groups", "ctx"), ("fsdp", "head")),
            P(("fsdp", "head"), ("groups", "ctx")),
            P(("groups", "ctx"), ("fsdp", "head")),
        ),
        check_vma=False,
    )
```

```python
import functools

import jax
import jax.numpy as jnp
from jax import lax
from jax.experimental import pallas as pl
from jax.experimental.pallas import tpu as pltpu
from jax.sharding import PartitionSpec as P

DK = 128
DV = 128
SPAN = 64
CHUNK = 128
TAIL = 16
EXTRA = 96
HEAD_COLUMNS = 2 * DK + DV

epsilon = 1e-06
HIGHEST = lax.Precision.HIGHEST
NN = (((1,), (0,)), ((), ()))
NT = (((1,), (1,)), ((), ()))
TN = (((0,), (0,)), ((), ()))


def narrow(x):
    return x.astype(jnp.bfloat16)


def dot(a, b, dims, passes):
    if passes == 6:
        return lax.dot_general(a, b, dims, precision=HIGHEST, preferred_element_type=jnp.float32)
    a_high, b_high = narrow(a), narrow(b)
    total = lax.dot_general(a_high, b_high, dims, preferred_element_type=jnp.float32)
    if passes >= 3:
        a_low = narrow(a - a_high.astype(jnp.float32))
        b_low = narrow(b - b_high.astype(jnp.float32))
        total = total + lax.dot_general(a_high, b_low, dims, preferred_element_type=jnp.float32)
        total = total + lax.dot_general(a_low, b_high, dims, preferred_element_type=jnp.float32)
    return total


PASSES = dict(
    decay=1, pairs=3, inverse=3, solve=3, read=1, carry=3, sent=1, scan=1, emit=1, update=1,
    d_update=3, d_value=3, d_pairs=1, d_up=1, d_up_state=1, d_kd=1, d_kend=1, d_decay=3,
)


def run(name, a, b, dims):
    return dot(a, b, dims, PASSES[name])


def recurrence(raw_ref, decay_ref, logit_ref, cot_ref, out_ref, grad_ref, dlogit_ref, ddecay_ref):
    count = raw_ref.shape[0] // CHUNK
    spans = range(count)
    rows = lax.broadcasted_iota(jnp.int32, (CHUNK, CHUNK), 0)
    cols = lax.broadcasted_iota(jnp.int32, (CHUNK, CHUNK), 1)
    within = rows >= cols
    strict = rows > cols
    diagonal = rows == cols
    running = within.astype(jnp.float32)

    q, k, v, rq, rk, up, down, end = [], [], [], [], [], [], [], []
    qu, ku, kd, kend, beta_row, cot = [], [], [], [], [], []
    for n in spans:
        here = slice(n * CHUNK, (n + 1) * CHUNK)
        q_raw = raw_ref[here, 0:DK]
        k_raw = raw_ref[here, DK : 2 * DK]
        v.append(raw_ref[here, 2 * DK : 3 * DK])
        rq.append(lax.rsqrt(jnp.sum(q_raw * q_raw, axis=1, keepdims=True) + epsilon))
        rk.append(lax.rsqrt(jnp.sum(k_raw * k_raw, axis=1, keepdims=True) + epsilon))
        q.append(q_raw * rq[n])
        k.append(k_raw * rk[n])
        summed = run("decay", running, decay_ref[here, :], NN)
        up.append(jnp.exp(summed))
        down.append(jnp.exp(-summed))
        end.append(up[n][CHUNK - 1 : CHUNK, :])
        qu.append(q[n] * up[n])
        ku.append(k[n] * up[n])
        kd.append(k[n] * down[n])
        kend.append(kd[n] * end[n])
        beta_row.append(jax.nn.sigmoid(logit_ref[n : n + 1, :]))
        cot.append(cot_ref[here, :])

    scores, system, inverse = [], [], []
    for n in spans:
        pairs = run("pairs", jnp.concatenate([qu[n], ku[n]], axis=0), kd[n], NT)
        scores.append(jnp.where(within, pairs[:CHUNK], 0.0))
        beta_col = jnp.transpose(jnp.broadcast_to(beta_row[n], (CHUNK, CHUNK)))
        system.append(jnp.where(strict, pairs[CHUNK:] * beta_col, 0.0))
        pair_block = (rows // 2) == (cols // 2)
        inverse.append(diagonal.astype(jnp.float32) - jnp.where(pair_block, system[n], 0.0))
    size = 2
    while size < CHUNK:
        joined = ((rows // (2 * size)) == (cols // (2 * size))) & ((rows // size) != (cols // size))
        halves = [run("inverse", jnp.where(joined, system[n], 0.0), inverse[n], NN) for n in spans]
        inverse = [inverse[n] - run("inverse", inverse[n], halves[n], NN) for n in spans]
        size *= 2

    solve = [inverse[n] * beta_row[n] for n in spans]
    wu = [run("solve", solve[n], jnp.concatenate([ku[n], v[n]], axis=1), NN) for n in spans]
    pwu = [run("read", scores[n], wu[n], NN) for n in spans]
    kwu = [run("carry", kend[n], wu[n], TN) for n in spans]
    query_through = [qu[n] - pwu[n][:, :DK] for n in spans]
    transit = [
        jnp.where(diagonal, jnp.broadcast_to(end[n], (DK, DK)), 0.0) - kwu[n][:, :DK] for n in spans
    ]
    sent = [run("sent", query_through[n], cot[n], TN) for n in spans]

    state = [None] * (count + 1)
    adjoint = [None] * (count + 1)
    for n in spans:
        m = count - 1 - n
        own = kwu[n][:, DK:]
        state[n + 1] = own if n == 0 else run("scan", transit[n], state[n], NN) + own
        adjoint[m] = sent[m] if n == 0 else run("scan", transit[m], adjoint[m + 1], TN) + sent[m]

    for n in spans:
        here = slice(n * CHUNK, (n + 1) * CHUNK)
        w = wu[n][:, :DK]
        update = wu[n][:, DK:]
        emitted = pwu[n][:, DK:]
        d_update = run("d_update", scores[n], cot[n], TN)
        if n > 0:
            emitted = emitted + run("emit", query_through[n], state[n], NN)
            update = update - run("update", w, state[n], NN)
        if n < count - 1:
            d_update = d_update + run("d_update", kend[n], adjoint[n + 1], NN)
        out_ref[n] = emitted.astype(out_ref.dtype)
        d_value = run("d_value", solve[n], d_update, TN)
        both = jnp.concatenate([cot[n], -d_value], axis=0)
        pairs = run("d_pairs", both, update, NT)
        d_pairs = jnp.concatenate(
            [jnp.where(within, pairs[:CHUNK], 0.0), jnp.where(strict, pairs[CHUNK:], 0.0)], axis=0
        )
        d_up = run("d_up", d_pairs, kd[n], NN)
        if n > 0:
            d_up = d_up + run("d_up_state", both, state[n], NT)
        d_qu, d_ku = d_up[:CHUNK], d_up[CHUNK:]
        d_kd = run("d_kd", d_pairs, jnp.concatenate([qu[n], ku[n]], axis=0), TN)
        d_k = d_ku * up[n] + d_kd * down[n]
        d_sum = d_qu * qu[n] + d_ku * ku[n] - d_kd * kd[n]
        d_decay_end = jnp.zeros((1, DK), jnp.float32)
        if n < count - 1:
            d_kend = run("d_kend", update, adjoint[n + 1], NT)
            d_k = d_k + d_kend * (end[n] * down[n])
            ended = d_kend * kend[n]
            d_sum = d_sum - ended
            d_decay_end = jnp.sum(ended, axis=0, keepdims=True)
            if n > 0:
                kept = jnp.sum(jnp.transpose(adjoint[n + 1] * state[n]), axis=0, keepdims=True)
                d_decay_end = d_decay_end + end[n] * kept
        ddecay_ref[n] = (run("d_decay", running, d_sum, TN) + d_decay_end).astype(ddecay_ref.dtype)
        d_q = d_qu * up[n]
        d_q = rq[n] * (d_q - q[n] * jnp.sum(q[n] * d_q, axis=1, keepdims=True))
        d_k = rk[n] * (d_k - k[n] * jnp.sum(k[n] * d_k, axis=1, keepdims=True))
        grad_ref[here, 0:DK] = d_q.astype(grad_ref.dtype)
        grad_ref[here, DK : 2 * DK] = d_k.astype(grad_ref.dtype)
        grad_ref[here, 2 * DK : 3 * DK] = d_value.astype(grad_ref.dtype)
        aligned = jnp.sum(jnp.transpose(d_value * update), axis=0, keepdims=True)
        dlogit_ref[n : n + 1, :] = aligned * jnp.exp(-logit_ref[n : n + 1, :])


def split_two(x):
    high = narrow(x)
    return high, narrow(x - high.astype(jnp.float32))


def tail_rows(x):
    high, low = split_two(x)
    index = lax.broadcasted_iota(jnp.int32, (TAIL, x.shape[1]), 0)
    high = jnp.broadcast_to(high.astype(jnp.float32), index.shape)
    low = jnp.broadcast_to(low.astype(jnp.float32), index.shape)
    return narrow(jnp.where(index == 0, high, jnp.where(index == 1, low, 0.0)))


def lanes(start):
    return pl.ds(pl.multiple_of(start, DK), DK)


def tile_rows(start, size):
    return pl.ds(pl.multiple_of(start, 32), size)


def pack_tokens_kernel(where_ref, tokens_ref, tok_ref):
    share = tok_ref.shape[0]
    for j in range(tokens_ref.shape[1] // share):

        @pl.when(where_ref[2] == j)
        def _(j=j):
            block = tokens_ref[:, j * share : (j + 1) * share]
            full = share // DK
            for g in range(full):
                tok_ref[g * CHUNK : (g + 1) * CHUNK, :] = block[:, g * DK : (g + 1) * DK]
            rest = block[:, full * DK :]
            tok_ref[full * CHUNK :, :] = jnp.concatenate([rest[: CHUNK // 2], rest[CHUNK // 2 :]], axis=1)


def unpack_tokens_kernel(ctx, where_ref, *refs):
    tok_refs, all_ref, own_ref = refs[:4], refs[4], refs[5]
    place = where_ref[0]
    share = own_ref.shape[0]
    full = share // DK
    for j in range(4):
        block = where_ref[2 + j]
        for d in range(ctx):
            source = lax.rem(place + ctx - d, ctx)
            start = source * CHUNK
            base = d * share
            for g in range(full):
                piece = tok_refs[j][base + g * CHUNK : base + (g + 1) * CHUNK, :]
                all_ref[block, tile_rows(start, CHUNK), g * DK : (g + 1) * DK] = piece
            rest = tok_refs[j][base + full * CHUNK : base + share, :]
            all_ref[block, tile_rows(start, CHUNK // 2), full * DK :] = rest[:, : DK // 2]
            all_ref[block, tile_rows(start + CHUNK // 2, CHUNK // 2), full * DK :] = rest[:, DK // 2 :]
    for n in range(ctx):
        piece = all_ref[place, n * CHUNK : (n + 1) * CHUNK, :].astype(jnp.float32)
        own_ref[:, n * CHUNK : (n + 1) * CHUNK] = narrow(jnp.transpose(piece))


def pack_kernel(ctx, where_ref, wq_ref, wk_ref, wv_ref, decay_ref, cot_ref, logit_ref, *out_refs):
    place, group = where_ref[0], where_ref[1]
    half = wq_ref.shape[0] // 2
    for s in range(2):
        for d in range(ctx):
            head = 2 * lax.rem(place + d, ctx) + s
            column = lanes(head * DK)
            out = out_refs[s * ctx + d]
            size = out.shape[0] - EXTRA
            rows = slice(None) if d == 0 else tile_rows(group * half, half)
            for part, ref in enumerate((wq_ref, wk_ref, wv_ref)):
                out[0:size, part * DK : (part + 1) * DK] = ref[rows, column]
            decay = narrow(decay_ref[:, column])
            cot = cot_ref[:, column]
            out[size : size + 96, 0:DK] = decay[0:96]
            out[size : size + 32, DK : 2 * DK] = decay[96:128]
            out[size + 32 : size + 96, DK : 2 * DK] = cot[0:64]
            out[size : size + 64, 2 * DK : 3 * DK] = cot[64:128]
            out[size + 64 : size + 80, 2 * DK : 3 * DK] = tail_rows(logit_ref[pl.ds(head, 1), :])
            out[size + 80 : size + 96, 2 * DK : 3 * DK] = jnp.zeros((16, DK), out.dtype)


def head_kernel(ctx, slot, where_ref, *refs):
    all_ref, refs = refs[0], refs[1:]
    direct, refs = refs[:ctx], refs[ctx:]
    swapped, refs = refs[: ctx - 1], refs[ctx - 1 :]
    if slot:
        earlier_ref, refs = refs[0], refs[1:]
    grad_ref, back_ref, w, raw, decay, cot, logit, out, dlogit, ddecay = refs
    place, group = where_ref[0], where_ref[1]
    share = direct[0].shape[0] - EXTRA
    half = share // 2
    for d in range(ctx):
        source = lax.rem(place + ctx - d, ctx)
        ref = direct[d]
        if d == 0:
            w[tile_rows(source * share, share), :] = ref[0:share, :]
            size = share
        else:
            w[tile_rows(source * share + group * half, half), :] = ref[0:half, :]
            w[tile_rows(source * share + (1 - group) * half, half), :] = swapped[d - 1][0:half, :]
            size = half
        start = source * CHUNK
        decay[tile_rows(start, 96), :] = ref[size : size + 96, 0:DK].astype(jnp.float32)
        decay[tile_rows(start + 96, 32), :] = ref[size : size + 32, DK : 2 * DK].astype(jnp.float32)
        cot[tile_rows(start, 64), :] = ref[size + 32 : size + 96, DK : 2 * DK].astype(jnp.float32)
        cot[tile_rows(start + 64, 64), :] = ref[size : size + 64, 2 * DK : 3 * DK].astype(jnp.float32)
        tail = ref[size + 64 : size + 80, 2 * DK : 3 * DK].astype(jnp.float32)
        logit[pl.ds(source, 1), :] = tail[0:1] + tail[1:2]
    projected = 0.0
    for j in range(ctx):
        projected = projected + lax.dot_general(
            all_ref[j], w[j * share : (j + 1) * share, :], NN, preferred_element_type=jnp.float32
        )
    raw[...] = projected
    recurrence(raw, decay, logit, cot, out, grad_ref, dlogit, ddecay)
    lane = slice(slot * DK, (slot + 1) * DK)
    if slot:
        back_ref[:, :, 0:DK] = earlier_ref[...]
    for n in range(ctx):
        back_ref[n, 0:CHUNK, lane] = out[n]
        back_ref[n, CHUNK : 2 * CHUNK, lane] = ddecay[n]
        back_ref[n, 2 * CHUNK :, lane] = tail_rows(dlogit[n : n + 1, :])


def weight_gradient_kernel(steps, forwarded, where_ref, own_ref, *refs):
    out_refs = refs[-3:]

    def block(gradient):
        product = lax.dot_general(own_ref[...], gradient, NN, preferred_element_type=jnp.float32)
        for part in range(3):
            out_refs[part][...] = product[:, part * DK : (part + 1) * DK]

    for at, step in enumerate(steps):

        @pl.when(pl.program_id(0) == at)
        def _(at=at, step=step):
            if step < 3 or not forwarded:
                block(refs[at][...])
            else:
                block(jnp.where(where_ref[14] == 1, refs[at + 1][...], refs[at][...]))


def unpack_kernel(back_ref, out_ref, dlogit_ref, ddecay_ref):
    for source in range(back_ref.shape[0]):
        column = slice(2 * source * DK, 2 * (source + 1) * DK)
        out_ref[:, column] = back_ref[source, 0:CHUNK, :]
        ddecay_ref[:, column] = back_ref[source, CHUNK : 2 * CHUNK, :].astype(jnp.float32)
        tail = back_ref[source, 2 * CHUNK :, :].astype(jnp.float32)
        row = tail[0:1] + tail[1:2]
        for s in range(2):
            dlogit_ref[2 * source + s : 2 * source + s + 1, :] = row[:, s * DK : (s + 1) * DK]


def head_split(tokens, w_query, w_key, w_value, beta_logit, log_decay, grad_out):
    ctx = lax.axis_size("ctx")
    place = lax.axis_index("ctx")
    group = lax.axis_index("groups")
    across, core = lax.axis_index("fsdp"), lax.axis_index("head")
    length, depth = tokens.shape
    share, columns = w_query.shape
    total = ctx * length
    bf16, f32 = jnp.bfloat16, jnp.float32
    whole = pl.BlockSpec(memory_space=pltpu.VMEM)
    scalars = pl.BlockSpec(memory_space=pltpu.SMEM)
    sources = [place, place + 1 - 2 * (place % 2), (place + 2) % ctx, ctx - 1 - place]
    where = jnp.stack(
        [place, group]
        + [2 * a + c for c in (core, 1 - core) for a in (across, 1 - across)]
        + [(place + ctx - d) % ctx for d in range(ctx)]
        + sources
        + [((place == 0) | (place == ctx - 1)).astype(jnp.int32)]
    ).astype(jnp.int32)

    def shape(dims, kind):
        return jax.ShapeDtypeStruct(dims, kind)

    def after(x, earlier):
        return lax.optimization_barrier((x, earlier))

    def along(x, axis, hop):
        count = lax.axis_size(axis)
        return lax.ppermute(x, axis, [(i, (i + hop) % count) for i in range(count)])

    tok = pl.pallas_call(
        pack_tokens_kernel,
        out_shape=shape((share, length), bf16),
        in_specs=[scalars, whole],
        out_specs=whole,
        name="pack_tokens",
    )(where, tokens)
    sizes = [share + EXTRA] + [share // 2 + EXTRA] * (ctx - 1)
    packed = pl.pallas_call(
        functools.partial(pack_kernel, ctx),
        out_shape=[shape((size, HEAD_COLUMNS), bf16) for size in sizes * 2],
        in_specs=[scalars] + [whole] * 6,
        out_specs=[whole] * (2 * ctx),
        name="pack",
    )(where, w_query, w_key, w_value, log_decay, grad_out, beta_logit)

    near = [along(tok, "ctx", d) for d in range(1, ctx)]
    first, near[0] = after(packed[1:ctx], near[0])
    first = [along(x, "ctx", d + 1) for d, x in enumerate(first)]
    tok = jnp.concatenate([tok] + near, axis=0)
    tok_x = along(tok, "fsdp", 1)
    half = share // 2
    swapped = [along(first[0][:half], "groups", 1)]
    (tok_c, tok_xc, first[1], first[2]), swapped[0] = after((tok, tok_x, first[1], first[2]), swapped[0])
    toks = (tok, tok_x, along(tok_c, "head", 1), along(tok_xc, "head", 1))
    all_tokens, own = pl.pallas_call(
        functools.partial(unpack_tokens_kernel, ctx),
        out_shape=[shape((ctx, total, share), bf16), shape((share, total), bf16)],
        in_specs=[scalars] + [whole] * 4,
        out_specs=[whole] * 2,
        name="unpack_tokens",
    )(where, *toks)
    swapped += [along(x[:half], "groups", 1) for x in first[1:]]
    second, first[1:] = after(packed[ctx + 1 :], first[1:])
    second = [along(x, "ctx", d + 1) for d, x in enumerate(second)]

    def products(slot, steps, parts, results):
        column = pl.BlockSpec((share, DK), lambda i, ref: (0, 2 * ref[6 + 4 * slot + steps[0] + i] + slot))
        return pl.pallas_call(
            functools.partial(weight_gradient_kernel, steps, slot == 1),
            grid_spec=pltpu.PrefetchScalarGridSpec(
                num_scalar_prefetch=1,
                grid=(len(steps),),
                in_specs=[whole] * (1 + len(parts)) + [pl.BlockSpec(memory_space=pl.ANY)] * len(results),
                out_specs=[column] * 3,
            ),
            out_shape=[shape((share, columns), f32)] * 3,
            input_output_aliases={2 + len(parts) + i: i for i in range(len(results))},
            name=f"weight_gradient_{slot}_{steps[0]}",
        )(where, own, *parts, *results)

    grads = []
    back = None
    for slot, direct in enumerate((first, second)):
        if slot:
            direct, back = after(direct, back)
            swapped = [along(x[:half], "groups", 1) for x in direct]
        earlier = [] if back is None else [back]
        grad, back = pl.pallas_call(
            functools.partial(head_kernel, ctx, slot),
            out_shape=[
                shape((total, HEAD_COLUMNS), bf16),
                shape((ctx, 2 * CHUNK + TAIL, (slot + 1) * DK), bf16),
            ],
            in_specs=[scalars] + [whole] * (1 + ctx + ctx - 1 + slot),
            out_specs=[whole] * 2,
            scratch_shapes=[
                pltpu.VMEM((depth, HEAD_COLUMNS), bf16),
                pltpu.VMEM((total, HEAD_COLUMNS), f32),
                pltpu.VMEM((total, DK), f32),
                pltpu.VMEM((total, DV), f32),
                pltpu.VMEM((ctx, CHUNK), f32),
                pltpu.VMEM((ctx, CHUNK, DV), bf16),
                pltpu.VMEM((ctx, CHUNK), f32),
                pltpu.VMEM((ctx, CHUNK, DK), bf16),
            ],
            cost_estimate=pl.CostEstimate(flops=12_000_000_000, transcendentals=0, bytes_accessed=8_000_000),
            name=f"head_{slot}",
        )(where, all_tokens, packed[slot * ctx], *direct, *swapped, *earlier)
        if slot == 0:
            hops = [along(grad, "ctx", d) for d in range(1, ctx)]
            grads.append([grad] + hops)
            continue
        grad, grads[0] = after(grad, grads[0])
        two = lax.ppermute(grad, "ctx", [(0, 2), (1, 3), (2, 0), (3, 1)])
        pair = lax.ppermute(grad, "ctx", [(0, 1), (1, 0), (2, 3), (3, 2)])
        results = products(0, (0, 1, 2, 3), grads[0], ())
        (grad, two), (pair, results) = after((grad, two), (pair, results))
        middle = lax.ppermute(grad, "ctx", [(1, 2), (2, 1)])
        far = lax.ppermute(two, "ctx", [(2, 3), (1, 0)])
        results = products(1, (0, 1, 2), [grad, pair, two], results)
        results = products(1, (3,), [middle, far], results)
    back = lax.all_to_all(back, "ctx", 0, 0)

    attn_out, grad_beta, grad_decay = pl.pallas_call(
        unpack_kernel,
        out_shape=[shape((length, columns), bf16), shape((columns // DK, length), f32), shape((length, columns), f32)],
        in_specs=[whole],
        out_specs=[whole] * 3,
        name="unpack",
    )(back)
    return (attn_out, *results, grad_beta, grad_decay)


def prefix_2(x, axis, join, neutral, backward):
    count = lax.axis_size(axis)
    place = lax.axis_index(axis)
    ahead = count - 1 - place if backward else place
    gathered = jax.tree.map(
        lambda a, kind: lax.all_gather(a.astype(kind), axis), x, (jnp.bfloat16, jnp.bfloat16)
    )
    state = jax.tree.map(lambda a, e: jnp.zeros_like(a) + jnp.asarray(e, a.dtype), x, neutral)

    def one(hop, state):
        source = count - 1 - hop if backward else hop
        return join(
            state,
            jax.tree.map(
                lambda a, own: lax.dynamic_index_in_dim(a, source, 0, False).astype(own.dtype),
                gathered,
                x,
            ),
        )

    return lax.fori_loop(0, ahead, one, state)


def normalize(vectors):
    return vectors * lax.rsqrt(jnp.sum(vectors * vectors, axis=-1, keepdims=True) + epsilon)


def heads_first(matrix, heads):
    return matrix.reshape(matrix.shape[0], heads, -1).transpose(1, 0, 2)


def span_step(memory, queries, key_vecs, val_vecs, strength, forgetting_exponent):
    largest_value = lax.Precision.HIGHEST
    length = queries.shape[1]
    cumulate = jnp.cumsum(forgetting_exponent, axis=1)
    growth = jnp.exp(cumulate)
    shrink = jnp.exp(-cumulate)
    key_up = key_vecs * growth
    key_down = key_vecs * shrink
    query_up = queries * growth
    row_ids = lax.broadcasted_iota(jnp.int32, (length, length), 0)
    col_ids = lax.broadcasted_iota(jnp.int32, (length, length), 1)
    strict = (row_ids > col_ids).astype(jnp.float32)
    within = (row_ids >= col_ids).astype(jnp.float32)
    affinity = jnp.einsum("bcd,bsd->bcs", key_up, key_down, precision=largest_value) * strict
    system = jnp.eye(length, dtype=jnp.float32) + strength[:, :, None] * affinity
    target = strength[:, :, None] * (
        val_vecs - jnp.einsum("bcd,bdw->bcw", key_up, memory, precision=largest_value)
    )
    update = lax.linalg.triangular_solve(system, target, left_side=True, lower=True)
    scores = jnp.einsum("bcd,bsd->bcs", query_up, key_down, precision=largest_value) * within
    emitted = jnp.einsum("bcd,bdw->bcw", query_up, memory, precision=largest_value)
    emitted = emitted + jnp.einsum("bcs,bsw->bcw", scores, update, precision=largest_value)
    at_end = growth[:, -1, :]
    renewed = at_end[:, :, None] * memory + jnp.einsum(
        "bsd,bsw->bdw", key_down * at_end[:, None, :], update, precision=largest_value
    )
    return (emitted, renewed)


def scan_spans(memory, queries, key_vecs, val_vecs, strength, forgetting_exponent):
    count = queries.shape[1] // SPAN

    def to_blocks(array):
        shaped = array.reshape((array.shape[0], count, SPAN) + array.shape[2:])
        return jnp.swapaxes(shaped, 0, 1)

    def advance(carried, blocks):
        emitted, renewed = span_step(carried, *blocks)
        return (renewed, emitted)

    blocks = (
        to_blocks(queries),
        to_blocks(key_vecs),
        to_blocks(val_vecs),
        to_blocks(strength),
        to_blocks(forgetting_exponent),
    )
    final, emitted = lax.scan(advance, memory, blocks)
    emitted = jnp.swapaxes(emitted, 0, 1)
    return (emitted.reshape(emitted.shape[0], count * SPAN, emitted.shape[-1]), final)


def compose(earlier, later):
    largest_value = lax.Precision.HIGHEST
    joined = jnp.einsum("hij,hjk->hik", later[0], earlier[0], precision=largest_value)
    shifted = jnp.einsum("hij,hjv->hiv", later[0], earlier[1], precision=largest_value) + later[1]
    return (joined, shifted)


def per_device(tokens, w_query, w_key, w_value, beta_logit, log_decay, grad_out):
    largest_value = lax.Precision.HIGHEST
    length = tokens.shape[0]
    columns = w_query.shape[1]
    heads = columns // DK
    shard_rows = (
        lax.all_gather(w_query, "ctx", axis=0, tiled=True),
        lax.all_gather(w_key, "ctx", axis=0, tiled=True),
        lax.all_gather(w_value, "ctx", axis=0, tiled=True),
    )
    window = tokens
    query_raw, key_raw, value_raw = tuple(
        (jnp.dot(window, weights, preferred_element_type=jnp.float32) for weights in shard_rows)
    )

    def shard_pass(query_in, key_in, value_in, logits, log_gates):
        queries = normalize(heads_first(query_in, heads))
        key_vecs = normalize(heads_first(key_in, heads))
        val_vecs = heads_first(value_in, heads)
        widened = jnp.concatenate([jnp.zeros((heads, length, DK), jnp.float32), val_vecs], axis=2)
        initial = jnp.concatenate(
            [
                jnp.broadcast_to(jnp.eye(DK, dtype=jnp.float32), (heads, DK, DK)),
                jnp.zeros((heads, DK, DV), jnp.float32),
            ],
            axis=2,
        )
        return scan_spans(
            initial,
            queries,
            key_vecs,
            widened,
            jax.nn.sigmoid(logits),
            heads_first(log_gates, heads),
        )

    (mixed, final), pullback = jax.vjp(
        shard_pass, query_raw, key_raw, value_raw, beta_logit, log_decay
    )
    transit = final[:, :, :DK]
    offset = final[:, :, DK:]
    query_carried_over = mixed[:, :, :DK]
    local_output = mixed[:, :, DK:]
    output_cotangent = grad_out.reshape(length, heads, DV).transpose(1, 0, 2).astype(jnp.float32)
    contribution = jnp.einsum(
        "mij,mif->mjf", query_carried_over, output_cotangent, precision=largest_value
    )
    identity = (
        jnp.broadcast_to(jnp.eye(DK, dtype=jnp.float32), (heads, DK, DK)),
        jnp.zeros((heads, DK, DV), jnp.float32),
    )
    prefix = prefix_2((transit, offset), "ctx", compose, identity, False)
    incoming_state = prefix[1]
    suffix = prefix_2((jnp.swapaxes(transit, 1, 2), contribution), "ctx", compose, identity, True)
    adjoint_state = suffix[1]
    complete_output = local_output + jnp.einsum(
        "npg,ngj->npj", query_carried_over, incoming_state, precision=largest_value
    )
    attn_out = complete_output.transpose(1, 0, 2).reshape(length, heads * DV).astype(jnp.bfloat16)
    d_mixed = jnp.concatenate(
        [
            jnp.einsum("efu,egu->efg", output_cotangent, incoming_state, precision=largest_value),
            output_cotangent,
        ],
        axis=2,
    )
    d_final = jnp.concatenate(
        [
            jnp.einsum("pgx,pcx->pgc", adjoint_state, incoming_state, precision=largest_value),
            adjoint_state,
        ],
        axis=2,
    )
    d_query, d_key, d_value, grad_beta, grad_decay = pullback((d_mixed, d_final))
    grad_projected = jnp.concatenate([d_query, d_key, d_value], axis=1).astype(jnp.bfloat16)
    window = tokens
    summed = lax.psum_scatter(
        jnp.einsum("td,tc->dc", window, grad_projected, preferred_element_type=jnp.float32).astype(
            jnp.bfloat16
        ),
        "ctx",
        scatter_dimension=0,
        tiled=True,
    ).astype(jnp.float32)
    return (
        attn_out,
        summed[:, :columns],
        summed[:, columns : 2 * columns],
        summed[:, 2 * columns :],
        grad_beta,
        grad_decay,
    )


def device_program(tokens, w_query, *rest):
    ctx = lax.axis_size("ctx")
    heads = w_query.shape[1] // DK
    split = heads == 2 * ctx and ctx == 4 and tokens.shape[0] == CHUNK and w_query.shape[0] * ctx == tokens.shape[1]
    split = split and lax.axis_size("groups") == lax.axis_size("fsdp") == lax.axis_size("head") == 2
    split = split and w_query.shape[0] % 64 == 0
    return (head_split if split else per_device)(tokens, w_query, *rest)


def solution(mesh):
    return jax.shard_map(
        device_program,
        mesh=mesh,
        in_specs=(
            P(("groups", "ctx"), None),
            P("ctx", ("fsdp", "head")),
            P("ctx", ("fsdp", "head")),
            P("ctx", ("fsdp", "head")),
            P(("fsdp", "head"), ("groups", "ctx")),
            P(("groups", "ctx"), ("fsdp", "head")),
            P(("groups", "ctx"), ("fsdp", "head")),
        ),
        out_specs=(
            P(("groups", "ctx"), ("fsdp", "head")),
            P(("groups", "ctx"), ("fsdp", "head")),
            P(("groups", "ctx"), ("fsdp", "head")),
            P(("groups", "ctx"), ("fsdp", "head")),
            P(("fsdp", "head"), ("groups", "ctx")),
            P(("groups", "ctx"), ("fsdp", "head")),
        ),
        check_vma=False,
    )
```

```python
import functools

import jax
import jax.numpy as jnp
from jax import lax
from jax.experimental import pallas as pl
from jax.experimental.pallas import tpu as pltpu
from jax.sharding import PartitionSpec as P

DK = 128
DV = 128
SPAN = 64
CHUNK = 128
TAIL = 16
EXTRA = 96
FLOPS = (12_000_000_000, 1_000)
HEAD_COLUMNS = 2 * DK + DV

epsilon = 1e-06
HIGHEST = lax.Precision.HIGHEST
NN = (((1,), (0,)), ((), ()))
NT = (((1,), (1,)), ((), ()))
TN = (((0,), (0,)), ((), ()))


def narrow(x):
    return x.astype(jnp.bfloat16)


def dot(a, b, dims, passes):
    if passes == 6:
        return lax.dot_general(a, b, dims, precision=HIGHEST, preferred_element_type=jnp.float32)
    a_high, b_high = narrow(a), narrow(b)
    total = lax.dot_general(a_high, b_high, dims, preferred_element_type=jnp.float32)
    if passes >= 3:
        a_low = narrow(a - a_high.astype(jnp.float32))
        b_low = narrow(b - b_high.astype(jnp.float32))
        total = total + lax.dot_general(a_high, b_low, dims, preferred_element_type=jnp.float32)
        total = total + lax.dot_general(a_low, b_high, dims, preferred_element_type=jnp.float32)
    return total


PASSES = dict(
    decay=1, pairs=3, inverse=3, solve=3, read=1, carry=3, sent=1, scan=1, emit=1, update=1,
    d_update=3, d_value=3, d_pairs=1, d_up=1, d_up_state=1, d_kd=1, d_kend=1, d_decay=3,
)


def run(name, a, b, dims):
    return dot(a, b, dims, PASSES[name])


def recurrence(raw_ref, decay_ref, logit_ref, cot_ref, out_ref, grad_ref, dlogit_ref, ddecay_ref):
    count = raw_ref.shape[0] // CHUNK
    spans = range(count)
    rows = lax.broadcasted_iota(jnp.int32, (CHUNK, CHUNK), 0)
    cols = lax.broadcasted_iota(jnp.int32, (CHUNK, CHUNK), 1)
    within = rows >= cols
    strict = rows > cols
    diagonal = rows == cols
    running = within.astype(jnp.float32)

    q, k, v, rq, rk, up, down, end = [], [], [], [], [], [], [], []
    qu, ku, kd, kend, beta_row, cot = [], [], [], [], [], []
    for n in spans:
        here = slice(n * CHUNK, (n + 1) * CHUNK)
        q_raw = raw_ref[here, 0:DK]
        k_raw = raw_ref[here, DK : 2 * DK]
        v.append(raw_ref[here, 2 * DK : 3 * DK])
        rq.append(lax.rsqrt(jnp.sum(q_raw * q_raw, axis=1, keepdims=True) + epsilon))
        rk.append(lax.rsqrt(jnp.sum(k_raw * k_raw, axis=1, keepdims=True) + epsilon))
        q.append(q_raw * rq[n])
        k.append(k_raw * rk[n])
        summed = run("decay", running, decay_ref[here, :], NN)
        up.append(jnp.exp(summed))
        down.append(jnp.exp(-summed))
        end.append(up[n][CHUNK - 1 : CHUNK, :])
        qu.append(q[n] * up[n])
        ku.append(k[n] * up[n])
        kd.append(k[n] * down[n])
        kend.append(kd[n] * end[n])
        beta_row.append(jax.nn.sigmoid(logit_ref[n : n + 1, :]))
        cot.append(cot_ref[here, :])

    scores, system, inverse = [], [], []
    for n in spans:
        pairs = run("pairs", jnp.concatenate([qu[n], ku[n]], axis=0), kd[n], NT)
        scores.append(jnp.where(within, pairs[:CHUNK], 0.0))
        beta_col = jnp.transpose(jnp.broadcast_to(beta_row[n], (CHUNK, CHUNK)))
        system.append(jnp.where(strict, pairs[CHUNK:] * beta_col, 0.0))
        pair_block = (rows // 2) == (cols // 2)
        inverse.append(diagonal.astype(jnp.float32) - jnp.where(pair_block, system[n], 0.0))
    size = 2
    while size < CHUNK:
        joined = ((rows // (2 * size)) == (cols // (2 * size))) & ((rows // size) != (cols // size))
        halves = [run("inverse", jnp.where(joined, system[n], 0.0), inverse[n], NN) for n in spans]
        inverse = [inverse[n] - run("inverse", inverse[n], halves[n], NN) for n in spans]
        size *= 2

    solve = [inverse[n] * beta_row[n] for n in spans]
    wu = [run("solve", solve[n], jnp.concatenate([ku[n], v[n]], axis=1), NN) for n in spans]
    pwu = [run("read", scores[n], wu[n], NN) for n in spans]
    kwu = [run("carry", kend[n], wu[n], TN) for n in spans]
    query_through = [qu[n] - pwu[n][:, :DK] for n in spans]
    transit = [
        jnp.where(diagonal, jnp.broadcast_to(end[n], (DK, DK)), 0.0) - kwu[n][:, :DK] for n in spans
    ]
    sent = [run("sent", query_through[n], cot[n], TN) for n in spans]

    state = [None] * (count + 1)
    adjoint = [None] * (count + 1)
    for n in spans:
        m = count - 1 - n
        own = kwu[n][:, DK:]
        state[n + 1] = own if n == 0 else run("scan", transit[n], state[n], NN) + own
        adjoint[m] = sent[m] if n == 0 else run("scan", transit[m], adjoint[m + 1], TN) + sent[m]

    for n in spans:
        here = slice(n * CHUNK, (n + 1) * CHUNK)
        w = wu[n][:, :DK]
        update = wu[n][:, DK:]
        emitted = pwu[n][:, DK:]
        d_update = run("d_update", scores[n], cot[n], TN)
        if n > 0:
            emitted = emitted + run("emit", query_through[n], state[n], NN)
            update = update - run("update", w, state[n], NN)
        if n < count - 1:
            d_update = d_update + run("d_update", kend[n], adjoint[n + 1], NN)
        out_ref[n] = emitted.astype(out_ref.dtype)
        d_value = run("d_value", solve[n], d_update, TN)
        both = jnp.concatenate([cot[n], -d_value], axis=0)
        pairs = run("d_pairs", both, update, NT)
        d_pairs = jnp.concatenate(
            [jnp.where(within, pairs[:CHUNK], 0.0), jnp.where(strict, pairs[CHUNK:], 0.0)], axis=0
        )
        d_up = run("d_up", d_pairs, kd[n], NN)
        if n > 0:
            d_up = d_up + run("d_up_state", both, state[n], NT)
        d_qu, d_ku = d_up[:CHUNK], d_up[CHUNK:]
        d_kd = run("d_kd", d_pairs, jnp.concatenate([qu[n], ku[n]], axis=0), TN)
        d_k = d_ku * up[n] + d_kd * down[n]
        d_sum = d_qu * qu[n] + d_ku * ku[n] - d_kd * kd[n]
        d_decay_end = jnp.zeros((1, DK), jnp.float32)
        if n < count - 1:
            d_kend = run("d_kend", update, adjoint[n + 1], NT)
            d_k = d_k + d_kend * (end[n] * down[n])
            ended = d_kend * kend[n]
            d_sum = d_sum - ended
            d_decay_end = jnp.sum(ended, axis=0, keepdims=True)
            if n > 0:
                kept = jnp.sum(jnp.transpose(adjoint[n + 1] * state[n]), axis=0, keepdims=True)
                d_decay_end = d_decay_end + end[n] * kept
        ddecay_ref[n] = (run("d_decay", running, d_sum, TN) + d_decay_end).astype(ddecay_ref.dtype)
        d_q = d_qu * up[n]
        d_q = rq[n] * (d_q - q[n] * jnp.sum(q[n] * d_q, axis=1, keepdims=True))
        d_k = rk[n] * (d_k - k[n] * jnp.sum(k[n] * d_k, axis=1, keepdims=True))
        grad_ref[here, 0:DK] = d_q.astype(grad_ref.dtype)
        grad_ref[here, DK : 2 * DK] = d_k.astype(grad_ref.dtype)
        grad_ref[here, 2 * DK : 3 * DK] = d_value.astype(grad_ref.dtype)
        aligned = jnp.sum(jnp.transpose(d_value * update), axis=0, keepdims=True)
        dlogit_ref[n : n + 1, :] = aligned * jnp.exp(-logit_ref[n : n + 1, :])


def split_two(x):
    high = narrow(x)
    return high, narrow(x - high.astype(jnp.float32))


def tail_rows(x):
    high, low = split_two(x)
    index = lax.broadcasted_iota(jnp.int32, (TAIL, x.shape[1]), 0)
    high = jnp.broadcast_to(high.astype(jnp.float32), index.shape)
    low = jnp.broadcast_to(low.astype(jnp.float32), index.shape)
    return narrow(jnp.where(index == 0, high, jnp.where(index == 1, low, 0.0)))


def lanes(start):
    return pl.ds(pl.multiple_of(start, DK), DK)


def tile_rows(start, size):
    return pl.ds(pl.multiple_of(start, 32), size)


def pack_tokens_kernel(where_ref, tokens_ref, tok_ref):
    share = tok_ref.shape[0]
    for j in range(tokens_ref.shape[1] // share):

        @pl.when(where_ref[2] == j)
        def _(j=j):
            block = tokens_ref[:, j * share : (j + 1) * share]
            full = share // DK
            for g in range(full):
                tok_ref[g * CHUNK : (g + 1) * CHUNK, :] = block[:, g * DK : (g + 1) * DK]
            rest = block[:, full * DK :]
            tok_ref[full * CHUNK :, :] = jnp.concatenate([rest[: CHUNK // 2], rest[CHUNK // 2 :]], axis=1)


def unpack_tokens_kernel(ctx, where_ref, *refs):
    tok_refs, all_ref, own_ref = refs[:4], refs[4], refs[5]
    place = where_ref[0]
    share = own_ref.shape[0]
    full = share // DK
    for j in range(4):
        block = where_ref[2 + j]
        for d in range(ctx):
            source = lax.rem(place + ctx - d, ctx)
            start = source * CHUNK
            base = d * share
            for g in range(full):
                piece = tok_refs[j][base + g * CHUNK : base + (g + 1) * CHUNK, :]
                all_ref[block, tile_rows(start, CHUNK), g * DK : (g + 1) * DK] = piece
            rest = tok_refs[j][base + full * CHUNK : base + share, :]
            all_ref[block, tile_rows(start, CHUNK // 2), full * DK :] = rest[:, : DK // 2]
            all_ref[block, tile_rows(start + CHUNK // 2, CHUNK // 2), full * DK :] = rest[:, DK // 2 :]
    for n in range(ctx):
        piece = all_ref[place, n * CHUNK : (n + 1) * CHUNK, :].astype(jnp.float32)
        own_ref[:, n * CHUNK : (n + 1) * CHUNK] = narrow(jnp.transpose(piece))


def pack_kernel(ctx, where_ref, wq_ref, wk_ref, wv_ref, decay_ref, cot_ref, logit_ref, *out_refs):
    place, group = where_ref[0], where_ref[1]
    half = wq_ref.shape[0] // 2
    for s in range(2):
        for d in range(ctx):
            head = 2 * lax.rem(place + d, ctx) + s
            column = lanes(head * DK)
            out = out_refs[s * ctx + d]
            size = out.shape[0] - EXTRA
            rows = slice(None) if d == 0 else tile_rows(group * half, half)
            for part, ref in enumerate((wq_ref, wk_ref, wv_ref)):
                out[0:size, part * DK : (part + 1) * DK] = ref[rows, column]
            decay = narrow(decay_ref[:, column])
            cot = cot_ref[:, column]
            out[size : size + 96, 0:DK] = decay[0:96]
            out[size : size + 32, DK : 2 * DK] = decay[96:128]
            out[size + 32 : size + 96, DK : 2 * DK] = cot[0:64]
            out[size : size + 64, 2 * DK : 3 * DK] = cot[64:128]
            out[size + 64 : size + 80, 2 * DK : 3 * DK] = tail_rows(logit_ref[pl.ds(head, 1), :])
            out[size + 80 : size + 96, 2 * DK : 3 * DK] = jnp.zeros((16, DK), out.dtype)


def head_kernel(ctx, slot, where_ref, *refs):
    all_ref, refs = refs[0], refs[1:]
    direct, refs = refs[:ctx], refs[ctx:]
    swapped, refs = refs[: ctx - 1], refs[ctx - 1 :]
    if slot:
        earlier_ref, refs = refs[0], refs[1:]
    grad_ref, back_ref, w, raw, decay, cot, logit, out, dlogit, ddecay = refs
    place, group = where_ref[0], where_ref[1]
    share = direct[0].shape[0] - EXTRA
    half = share // 2
    for d in range(ctx):
        source = lax.rem(place + ctx - d, ctx)
        ref = direct[d]
        if d == 0:
            w[tile_rows(source * share, share), :] = ref[0:share, :]
            size = share
        else:
            w[tile_rows(source * share + group * half, half), :] = ref[0:half, :]
            w[tile_rows(source * share + (1 - group) * half, half), :] = swapped[d - 1][0:half, :]
            size = half
        start = source * CHUNK
        decay[tile_rows(start, 96), :] = ref[size : size + 96, 0:DK].astype(jnp.float32)
        decay[tile_rows(start + 96, 32), :] = ref[size : size + 32, DK : 2 * DK].astype(jnp.float32)
        cot[tile_rows(start, 64), :] = ref[size + 32 : size + 96, DK : 2 * DK].astype(jnp.float32)
        cot[tile_rows(start + 64, 64), :] = ref[size : size + 64, 2 * DK : 3 * DK].astype(jnp.float32)
        tail = ref[size + 64 : size + 80, 2 * DK : 3 * DK].astype(jnp.float32)
        logit[pl.ds(source, 1), :] = tail[0:1] + tail[1:2]
    projected = 0.0
    for j in range(ctx):
        projected = projected + lax.dot_general(
            all_ref[j], w[j * share : (j + 1) * share, :], NN, preferred_element_type=jnp.float32
        )
    raw[...] = projected
    recurrence(raw, decay, logit, cot, out, grad_ref, dlogit, ddecay)
    lane = slice(slot * DK, (slot + 1) * DK)
    if slot:
        back_ref[:, :, 0:DK] = earlier_ref[...]
    for n in range(ctx):
        back_ref[n, 0:CHUNK, lane] = out[n]
        back_ref[n, CHUNK : 2 * CHUNK, lane] = ddecay[n]
        back_ref[n, 2 * CHUNK :, lane] = tail_rows(dlogit[n : n + 1, :])


def weight_gradient_kernel(steps, forwarded, where_ref, own_ref, *refs):
    out_refs = refs[-3:]

    def block(gradient):
        product = lax.dot_general(own_ref[...], gradient, NN, preferred_element_type=jnp.float32)
        for part in range(3):
            out_refs[part][...] = product[:, part * DK : (part + 1) * DK]

    for at, step in enumerate(steps):

        @pl.when(pl.program_id(0) == at)
        def _(at=at, step=step):
            if step < 3 or not forwarded:
                block(refs[at][...])
            else:
                block(jnp.where(where_ref[14] == 1, refs[at + 1][...], refs[at][...]))


def unpack_kernel(back_ref, out_ref, dlogit_ref, ddecay_ref):
    for source in range(back_ref.shape[0]):
        column = slice(2 * source * DK, 2 * (source + 1) * DK)
        out_ref[:, column] = back_ref[source, 0:CHUNK, :]
        ddecay_ref[:, column] = back_ref[source, CHUNK : 2 * CHUNK, :].astype(jnp.float32)
        tail = back_ref[source, 2 * CHUNK :, :].astype(jnp.float32)
        row = tail[0:1] + tail[1:2]
        for s in range(2):
            dlogit_ref[2 * source + s : 2 * source + s + 1, :] = row[:, s * DK : (s + 1) * DK]


def head_split(tokens, w_query, w_key, w_value, beta_logit, log_decay, grad_out):
    ctx = lax.axis_size("ctx")
    place = lax.axis_index("ctx")
    group = lax.axis_index("groups")
    across, core = lax.axis_index("fsdp"), lax.axis_index("head")
    length, depth = tokens.shape
    share, columns = w_query.shape
    total = ctx * length
    bf16, f32 = jnp.bfloat16, jnp.float32
    whole = pl.BlockSpec(memory_space=pltpu.VMEM)
    scalars = pl.BlockSpec(memory_space=pltpu.SMEM)
    sources = [place, place + 1 - 2 * (place % 2), (place + 2) % ctx, ctx - 1 - place]
    where = jnp.stack(
        [place, group]
        + [2 * a + c for c in (core, 1 - core) for a in (across, 1 - across)]
        + [(place + ctx - d) % ctx for d in range(ctx)]
        + sources
        + [((place == 0) | (place == ctx - 1)).astype(jnp.int32)]
    ).astype(jnp.int32)

    def shape(dims, kind):
        return jax.ShapeDtypeStruct(dims, kind)

    def after(x, earlier):
        return lax.optimization_barrier((x, earlier))

    def along(x, axis, hop):
        count = lax.axis_size(axis)
        return lax.ppermute(x, axis, [(i, (i + hop) % count) for i in range(count)])

    tok = pl.pallas_call(
        pack_tokens_kernel,
        out_shape=shape((share, length), bf16),
        in_specs=[scalars, whole],
        out_specs=whole,
        name="pack_tokens",
    )(where, tokens)
    sizes = [share + EXTRA] + [share // 2 + EXTRA] * (ctx - 1)
    packed = pl.pallas_call(
        functools.partial(pack_kernel, ctx),
        out_shape=[shape((size, HEAD_COLUMNS), bf16) for size in sizes * 2],
        in_specs=[scalars] + [whole] * 6,
        out_specs=[whole] * (2 * ctx),
        name="pack",
    )(where, w_query, w_key, w_value, log_decay, grad_out, beta_logit)

    near = [along(tok, "ctx", d) for d in range(1, ctx)]
    first, near[0] = after(packed[1:ctx], near[0])
    first = [along(x, "ctx", d + 1) for d, x in enumerate(first)]
    tok = jnp.concatenate([tok] + near, axis=0)
    tok_x = along(tok, "fsdp", 1)
    half = share // 2
    swapped = [along(first[0][:half], "groups", 1)]
    (tok_c, tok_xc, first[1], first[2]), swapped[0] = after((tok, tok_x, first[1], first[2]), swapped[0])
    toks = (tok, tok_x, along(tok_c, "head", 1), along(tok_xc, "head", 1))
    all_tokens, own = pl.pallas_call(
        functools.partial(unpack_tokens_kernel, ctx),
        out_shape=[shape((ctx, total, share), bf16), shape((share, total), bf16)],
        in_specs=[scalars] + [whole] * 4,
        out_specs=[whole] * 2,
        name="unpack_tokens",
    )(where, *toks)
    swapped += [along(x[:half], "groups", 1) for x in first[1:]]
    second, first[1:] = after(packed[ctx + 1 :], first[1:])
    second = [along(x, "ctx", d + 1) for d, x in enumerate(second)]

    def products(slot, steps, parts, results):
        column = pl.BlockSpec((share, DK), lambda i, ref: (0, 2 * ref[6 + 4 * slot + steps[0] + i] + slot))
        return pl.pallas_call(
            functools.partial(weight_gradient_kernel, steps, slot == 1),
            grid_spec=pltpu.PrefetchScalarGridSpec(
                num_scalar_prefetch=1,
                grid=(len(steps),),
                in_specs=[whole] * (1 + len(parts)) + [pl.BlockSpec(memory_space=pl.ANY)] * len(results),
                out_specs=[column] * 3,
            ),
            out_shape=[shape((share, columns), f32)] * 3,
            input_output_aliases={2 + len(parts) + i: i for i in range(len(results))},
            name=f"weight_gradient_{slot}_{steps[0]}",
        )(where, own, *parts, *results)

    grads = []
    back = None
    for slot, direct in enumerate((first, second)):
        if slot:
            for d in range(ctx - 1):
                direct[d], back = after(direct[d], back)
            swapped = [along(x[:half], "groups", 1) for x in direct]
        earlier = [] if back is None else [back]
        grad, back = pl.pallas_call(
            functools.partial(head_kernel, ctx, slot),
            out_shape=[
                shape((total, HEAD_COLUMNS), bf16),
                shape((ctx, 2 * CHUNK + TAIL, (slot + 1) * DK), bf16),
            ],
            in_specs=[scalars] + [whole] * (1 + ctx + ctx - 1 + slot),
            out_specs=[whole] * 2,
            scratch_shapes=[
                pltpu.VMEM((depth, HEAD_COLUMNS), bf16),
                pltpu.VMEM((total, HEAD_COLUMNS), f32),
                pltpu.VMEM((total, DK), f32),
                pltpu.VMEM((total, DV), f32),
                pltpu.VMEM((ctx, CHUNK), f32),
                pltpu.VMEM((ctx, CHUNK, DV), bf16),
                pltpu.VMEM((ctx, CHUNK), f32),
                pltpu.VMEM((ctx, CHUNK, DK), bf16),
            ],
            cost_estimate=pl.CostEstimate(flops=FLOPS[slot], transcendentals=0, bytes_accessed=FLOPS[slot] // 1000),
            name=f"head_{slot}",
        )(where, all_tokens, packed[slot * ctx], *direct, *swapped, *earlier)
        if slot == 0:
            hops = [along(grad, "ctx", d) for d in range(1, ctx)]
            grads.append([grad] + hops)
            continue
        grad, grads[0] = after(grad, grads[0])
        two = lax.ppermute(grad, "ctx", [(0, 2), (1, 3), (2, 0), (3, 1)])
        pair = lax.ppermute(grad, "ctx", [(0, 1), (1, 0), (2, 3), (3, 2)])
        results = products(0, (0, 1, 2, 3), grads[0], ())
        (grad, two), (pair, results) = after((grad, two), (pair, results))
        middle = lax.ppermute(grad, "ctx", [(1, 2), (2, 1)])
        far = lax.ppermute(two, "ctx", [(2, 3), (1, 0)])
        results = products(1, (0, 1, 2), [grad, pair, two], results)
        results = products(1, (3,), [middle, far], results)
    back = lax.all_to_all(back, "ctx", 0, 0)

    attn_out, grad_beta, grad_decay = pl.pallas_call(
        unpack_kernel,
        out_shape=[shape((length, columns), bf16), shape((columns // DK, length), f32), shape((length, columns), f32)],
        in_specs=[whole],
        out_specs=[whole] * 3,
        name="unpack",
    )(back)
    return (attn_out, *results, grad_beta, grad_decay)


def prefix_2(x, axis, join, neutral, backward):
    count = lax.axis_size(axis)
    place = lax.axis_index(axis)
    ahead = count - 1 - place if backward else place
    gathered = jax.tree.map(
        lambda a, kind: lax.all_gather(a.astype(kind), axis), x, (jnp.bfloat16, jnp.bfloat16)
    )
    state = jax.tree.map(lambda a, e: jnp.zeros_like(a) + jnp.asarray(e, a.dtype), x, neutral)

    def one(hop, state):
        source = count - 1 - hop if backward else hop
        return join(
            state,
            jax.tree.map(
                lambda a, own: lax.dynamic_index_in_dim(a, source, 0, False).astype(own.dtype),
                gathered,
                x,
            ),
        )

    return lax.fori_loop(0, ahead, one, state)


def normalize(vectors):
    return vectors * lax.rsqrt(jnp.sum(vectors * vectors, axis=-1, keepdims=True) + epsilon)


def heads_first(matrix, heads):
    return matrix.reshape(matrix.shape[0], heads, -1).transpose(1, 0, 2)


def span_step(memory, queries, key_vecs, val_vecs, strength, forgetting_exponent):
    largest_value = lax.Precision.HIGHEST
    length = queries.shape[1]
    cumulate = jnp.cumsum(forgetting_exponent, axis=1)
    growth = jnp.exp(cumulate)
    shrink = jnp.exp(-cumulate)
    key_up = key_vecs * growth
    key_down = key_vecs * shrink
    query_up = queries * growth
    row_ids = lax.broadcasted_iota(jnp.int32, (length, length), 0)
    col_ids = lax.broadcasted_iota(jnp.int32, (length, length), 1)
    strict = (row_ids > col_ids).astype(jnp.float32)
    within = (row_ids >= col_ids).astype(jnp.float32)
    affinity = jnp.einsum("bcd,bsd->bcs", key_up, key_down, precision=largest_value) * strict
    system = jnp.eye(length, dtype=jnp.float32) + strength[:, :, None] * affinity
    target = strength[:, :, None] * (
        val_vecs - jnp.einsum("bcd,bdw->bcw", key_up, memory, precision=largest_value)
    )
    update = lax.linalg.triangular_solve(system, target, left_side=True, lower=True)
    scores = jnp.einsum("bcd,bsd->bcs", query_up, key_down, precision=largest_value) * within
    emitted = jnp.einsum("bcd,bdw->bcw", query_up, memory, precision=largest_value)
    emitted = emitted + jnp.einsum("bcs,bsw->bcw", scores, update, precision=largest_value)
    at_end = growth[:, -1, :]
    renewed = at_end[:, :, None] * memory + jnp.einsum(
        "bsd,bsw->bdw", key_down * at_end[:, None, :], update, precision=largest_value
    )
    return (emitted, renewed)


def scan_spans(memory, queries, key_vecs, val_vecs, strength, forgetting_exponent):
    count = queries.shape[1] // SPAN

    def to_blocks(array):
        shaped = array.reshape((array.shape[0], count, SPAN) + array.shape[2:])
        return jnp.swapaxes(shaped, 0, 1)

    def advance(carried, blocks):
        emitted, renewed = span_step(carried, *blocks)
        return (renewed, emitted)

    blocks = (
        to_blocks(queries),
        to_blocks(key_vecs),
        to_blocks(val_vecs),
        to_blocks(strength),
        to_blocks(forgetting_exponent),
    )
    final, emitted = lax.scan(advance, memory, blocks)
    emitted = jnp.swapaxes(emitted, 0, 1)
    return (emitted.reshape(emitted.shape[0], count * SPAN, emitted.shape[-1]), final)


def compose(earlier, later):
    largest_value = lax.Precision.HIGHEST
    joined = jnp.einsum("hij,hjk->hik", later[0], earlier[0], precision=largest_value)
    shifted = jnp.einsum("hij,hjv->hiv", later[0], earlier[1], precision=largest_value) + later[1]
    return (joined, shifted)


def per_device(tokens, w_query, w_key, w_value, beta_logit, log_decay, grad_out):
    largest_value = lax.Precision.HIGHEST
    length = tokens.shape[0]
    columns = w_query.shape[1]
    heads = columns // DK
    shard_rows = (
        lax.all_gather(w_query, "ctx", axis=0, tiled=True),
        lax.all_gather(w_key, "ctx", axis=0, tiled=True),
        lax.all_gather(w_value, "ctx", axis=0, tiled=True),
    )
    window = tokens
    query_raw, key_raw, value_raw = tuple(
        (jnp.dot(window, weights, preferred_element_type=jnp.float32) for weights in shard_rows)
    )

    def shard_pass(query_in, key_in, value_in, logits, log_gates):
        queries = normalize(heads_first(query_in, heads))
        key_vecs = normalize(heads_first(key_in, heads))
        val_vecs = heads_first(value_in, heads)
        widened = jnp.concatenate([jnp.zeros((heads, length, DK), jnp.float32), val_vecs], axis=2)
        initial = jnp.concatenate(
            [
                jnp.broadcast_to(jnp.eye(DK, dtype=jnp.float32), (heads, DK, DK)),
                jnp.zeros((heads, DK, DV), jnp.float32),
            ],
            axis=2,
        )
        return scan_spans(
            initial,
            queries,
            key_vecs,
            widened,
            jax.nn.sigmoid(logits),
            heads_first(log_gates, heads),
        )

    (mixed, final), pullback = jax.vjp(
        shard_pass, query_raw, key_raw, value_raw, beta_logit, log_decay
    )
    transit = final[:, :, :DK]
    offset = final[:, :, DK:]
    query_carried_over = mixed[:, :, :DK]
    local_output = mixed[:, :, DK:]
    output_cotangent = grad_out.reshape(length, heads, DV).transpose(1, 0, 2).astype(jnp.float32)
    contribution = jnp.einsum(
        "mij,mif->mjf", query_carried_over, output_cotangent, precision=largest_value
    )
    identity = (
        jnp.broadcast_to(jnp.eye(DK, dtype=jnp.float32), (heads, DK, DK)),
        jnp.zeros((heads, DK, DV), jnp.float32),
    )
    prefix = prefix_2((transit, offset), "ctx", compose, identity, False)
    incoming_state = prefix[1]
    suffix = prefix_2((jnp.swapaxes(transit, 1, 2), contribution), "ctx", compose, identity, True)
    adjoint_state = suffix[1]
    complete_output = local_output + jnp.einsum(
        "npg,ngj->npj", query_carried_over, incoming_state, precision=largest_value
    )
    attn_out = complete_output.transpose(1, 0, 2).reshape(length, heads * DV).astype(jnp.bfloat16)
    d_mixed = jnp.concatenate(
        [
            jnp.einsum("efu,egu->efg", output_cotangent, incoming_state, precision=largest_value),
            output_cotangent,
        ],
        axis=2,
    )
    d_final = jnp.concatenate(
        [
            jnp.einsum("pgx,pcx->pgc", adjoint_state, incoming_state, precision=largest_value),
            adjoint_state,
        ],
        axis=2,
    )
    d_query, d_key, d_value, grad_beta, grad_decay = pullback((d_mixed, d_final))
    grad_projected = jnp.concatenate([d_query, d_key, d_value], axis=1).astype(jnp.bfloat16)
    window = tokens
    summed = lax.psum_scatter(
        jnp.einsum("td,tc->dc", window, grad_projected, preferred_element_type=jnp.float32).astype(
            jnp.bfloat16
        ),
        "ctx",
        scatter_dimension=0,
        tiled=True,
    ).astype(jnp.float32)
    return (
        attn_out,
        summed[:, :columns],
        summed[:, columns : 2 * columns],
        summed[:, 2 * columns :],
        grad_beta,
        grad_decay,
    )


def device_program(tokens, w_query, *rest):
    ctx = lax.axis_size("ctx")
    heads = w_query.shape[1] // DK
    split = heads == 2 * ctx and ctx == 4 and tokens.shape[0] == CHUNK and w_query.shape[0] * ctx == tokens.shape[1]
    split = split and lax.axis_size("groups") == lax.axis_size("fsdp") == lax.axis_size("head") == 2
    split = split and w_query.shape[0] % 64 == 0
    return (head_split if split else per_device)(tokens, w_query, *rest)


def solution(mesh):
    return jax.shard_map(
        device_program,
        mesh=mesh,
        in_specs=(
            P(("groups", "ctx"), None),
            P("ctx", ("fsdp", "head")),
            P("ctx", ("fsdp", "head")),
            P("ctx", ("fsdp", "head")),
            P(("fsdp", "head"), ("groups", "ctx")),
            P(("groups", "ctx"), ("fsdp", "head")),
            P(("groups", "ctx"), ("fsdp", "head")),
        ),
        out_specs=(
            P(("groups", "ctx"), ("fsdp", "head")),
            P(("groups", "ctx"), ("fsdp", "head")),
            P(("groups", "ctx"), ("fsdp", "head")),
            P(("groups", "ctx"), ("fsdp", "head")),
            P(("fsdp", "head"), ("groups", "ctx")),
            P(("groups", "ctx"), ("fsdp", "head")),
        ),
        check_vma=False,
    )
```

```python
import functools

import jax
import jax.numpy as jnp
from jax import lax
from jax.experimental import pallas as pl
from jax.experimental.pallas import tpu as pltpu
from jax.sharding import PartitionSpec as P

DK = 128
DV = 128
SPAN = 64
CHUNK = 128
TAIL = 16
EXTRA = 96
VMEM_LIMIT = 20 * 2**20
FLOPS = (12_000_000_000, 1_000)
HEAD_COLUMNS = 2 * DK + DV

epsilon = 1e-06
HIGHEST = lax.Precision.HIGHEST
NN = (((1,), (0,)), ((), ()))
NT = (((1,), (1,)), ((), ()))
TN = (((0,), (0,)), ((), ()))


def narrow(x):
    return x.astype(jnp.bfloat16)


def dot(a, b, dims, passes):
    if passes == 6:
        return lax.dot_general(a, b, dims, precision=HIGHEST, preferred_element_type=jnp.float32)
    a_high, b_high = narrow(a), narrow(b)
    total = lax.dot_general(a_high, b_high, dims, preferred_element_type=jnp.float32)
    if passes >= 3:
        a_low = narrow(a - a_high.astype(jnp.float32))
        b_low = narrow(b - b_high.astype(jnp.float32))
        total = total + lax.dot_general(a_high, b_low, dims, preferred_element_type=jnp.float32)
        total = total + lax.dot_general(a_low, b_high, dims, preferred_element_type=jnp.float32)
    return total


PASSES = dict(
    decay=1, pairs=3, inverse=3, solve=3, read=1, carry=3, sent=1, scan=1, emit=1, update=1,
    d_update=3, d_value=3, d_pairs=1, d_up=1, d_up_state=1, d_kd=1, d_kend=1, d_decay=3,
)


def run(name, a, b, dims):
    return dot(a, b, dims, PASSES[name])


def recurrence(raw_ref, decay_ref, logit_ref, cot_ref, out_ref, grad_ref, dlogit_ref, ddecay_ref):
    count = raw_ref.shape[0] // CHUNK
    spans = range(count)
    rows = lax.broadcasted_iota(jnp.int32, (CHUNK, CHUNK), 0)
    cols = lax.broadcasted_iota(jnp.int32, (CHUNK, CHUNK), 1)
    within = rows >= cols
    strict = rows > cols
    diagonal = rows == cols
    running = within.astype(jnp.float32)

    q, k, v, rq, rk, up, down, end = [], [], [], [], [], [], [], []
    qu, ku, kd, kend, beta_row, cot = [], [], [], [], [], []
    for n in spans:
        here = slice(n * CHUNK, (n + 1) * CHUNK)
        q_raw = raw_ref[here, 0:DK]
        k_raw = raw_ref[here, DK : 2 * DK]
        v.append(raw_ref[here, 2 * DK : 3 * DK])
        rq.append(lax.rsqrt(jnp.sum(q_raw * q_raw, axis=1, keepdims=True) + epsilon))
        rk.append(lax.rsqrt(jnp.sum(k_raw * k_raw, axis=1, keepdims=True) + epsilon))
        q.append(q_raw * rq[n])
        k.append(k_raw * rk[n])
        summed = run("decay", running, decay_ref[here, :], NN)
        up.append(jnp.exp(summed))
        down.append(jnp.exp(-summed))
        end.append(up[n][CHUNK - 1 : CHUNK, :])
        qu.append(q[n] * up[n])
        ku.append(k[n] * up[n])
        kd.append(k[n] * down[n])
        kend.append(kd[n] * end[n])
        beta_row.append(jax.nn.sigmoid(logit_ref[n : n + 1, :]))
        cot.append(cot_ref[here, :])

    scores, system, inverse = [], [], []
    for n in spans:
        pairs = run("pairs", jnp.concatenate([qu[n], ku[n]], axis=0), kd[n], NT)
        scores.append(jnp.where(within, pairs[:CHUNK], 0.0))
        beta_col = jnp.transpose(jnp.broadcast_to(beta_row[n], (CHUNK, CHUNK)))
        system.append(jnp.where(strict, pairs[CHUNK:] * beta_col, 0.0))
        pair_block = (rows // 2) == (cols // 2)
        inverse.append(diagonal.astype(jnp.float32) - jnp.where(pair_block, system[n], 0.0))
    size = 2
    while size < CHUNK:
        joined = ((rows // (2 * size)) == (cols // (2 * size))) & ((rows // size) != (cols // size))
        halves = [run("inverse", jnp.where(joined, system[n], 0.0), inverse[n], NN) for n in spans]
        inverse = [inverse[n] - run("inverse", inverse[n], halves[n], NN) for n in spans]
        size *= 2

    solve = [inverse[n] * beta_row[n] for n in spans]
    wu = [run("solve", solve[n], jnp.concatenate([ku[n], v[n]], axis=1), NN) for n in spans]
    pwu = [run("read", scores[n], wu[n], NN) for n in spans]
    kwu = [run("carry", kend[n], wu[n], TN) for n in spans]
    query_through = [qu[n] - pwu[n][:, :DK] for n in spans]
    transit = [
        jnp.where(diagonal, jnp.broadcast_to(end[n], (DK, DK)), 0.0) - kwu[n][:, :DK] for n in spans
    ]
    sent = [run("sent", query_through[n], cot[n], TN) for n in spans]

    state = [None] * (count + 1)
    adjoint = [None] * (count + 1)
    for n in spans:
        m = count - 1 - n
        own = kwu[n][:, DK:]
        state[n + 1] = own if n == 0 else run("scan", transit[n], state[n], NN) + own
        adjoint[m] = sent[m] if n == 0 else run("scan", transit[m], adjoint[m + 1], TN) + sent[m]

    for n in spans:
        here = slice(n * CHUNK, (n + 1) * CHUNK)
        w = wu[n][:, :DK]
        update = wu[n][:, DK:]
        emitted = pwu[n][:, DK:]
        d_update = run("d_update", scores[n], cot[n], TN)
        if n > 0:
            emitted = emitted + run("emit", query_through[n], state[n], NN)
            update = update - run("update", w, state[n], NN)
        if n < count - 1:
            d_update = d_update + run("d_update", kend[n], adjoint[n + 1], NN)
        out_ref[n] = emitted.astype(out_ref.dtype)
        d_value = run("d_value", solve[n], d_update, TN)
        both = jnp.concatenate([cot[n], -d_value], axis=0)
        pairs = run("d_pairs", both, update, NT)
        d_pairs = jnp.concatenate(
            [jnp.where(within, pairs[:CHUNK], 0.0), jnp.where(strict, pairs[CHUNK:], 0.0)], axis=0
        )
        d_up = run("d_up", d_pairs, kd[n], NN)
        if n > 0:
            d_up = d_up + run("d_up_state", both, state[n], NT)
        d_qu, d_ku = d_up[:CHUNK], d_up[CHUNK:]
        d_kd = run("d_kd", d_pairs, jnp.concatenate([qu[n], ku[n]], axis=0), TN)
        d_k = d_ku * up[n] + d_kd * down[n]
        d_sum = d_qu * qu[n] + d_ku * ku[n] - d_kd * kd[n]
        d_decay_end = jnp.zeros((1, DK), jnp.float32)
        if n < count - 1:
            d_kend = run("d_kend", update, adjoint[n + 1], NT)
            d_k = d_k + d_kend * (end[n] * down[n])
            ended = d_kend * kend[n]
            d_sum = d_sum - ended
            d_decay_end = jnp.sum(ended, axis=0, keepdims=True)
            if n > 0:
                kept = jnp.sum(jnp.transpose(adjoint[n + 1] * state[n]), axis=0, keepdims=True)
                d_decay_end = d_decay_end + end[n] * kept
        ddecay_ref[n] = (run("d_decay", running, d_sum, TN) + d_decay_end).astype(ddecay_ref.dtype)
        d_q = d_qu * up[n]
        d_q = rq[n] * (d_q - q[n] * jnp.sum(q[n] * d_q, axis=1, keepdims=True))
        d_k = rk[n] * (d_k - k[n] * jnp.sum(k[n] * d_k, axis=1, keepdims=True))
        grad_ref[here, 0:DK] = d_q.astype(grad_ref.dtype)
        grad_ref[here, DK : 2 * DK] = d_k.astype(grad_ref.dtype)
        grad_ref[here, 2 * DK : 3 * DK] = d_value.astype(grad_ref.dtype)
        aligned = jnp.sum(jnp.transpose(d_value * update), axis=0, keepdims=True)
        dlogit_ref[n : n + 1, :] = aligned * jnp.exp(-logit_ref[n : n + 1, :])


def split_two(x):
    high = narrow(x)
    return high, narrow(x - high.astype(jnp.float32))


def tail_rows(x):
    high, low = split_two(x)
    index = lax.broadcasted_iota(jnp.int32, (TAIL, x.shape[1]), 0)
    high = jnp.broadcast_to(high.astype(jnp.float32), index.shape)
    low = jnp.broadcast_to(low.astype(jnp.float32), index.shape)
    return narrow(jnp.where(index == 0, high, jnp.where(index == 1, low, 0.0)))


def lanes(start):
    return pl.ds(pl.multiple_of(start, DK), DK)


def tile_rows(start, size):
    return pl.ds(pl.multiple_of(start, 32), size)


def pack_tokens_kernel(where_ref, tokens_ref, tok_ref):
    share = tok_ref.shape[0]
    for j in range(tokens_ref.shape[1] // share):

        @pl.when(where_ref[2] == j)
        def _(j=j):
            block = tokens_ref[:, j * share : (j + 1) * share]
            full = share // DK
            for g in range(full):
                tok_ref[g * CHUNK : (g + 1) * CHUNK, :] = block[:, g * DK : (g + 1) * DK]
            rest = block[:, full * DK :]
            tok_ref[full * CHUNK :, :] = jnp.concatenate([rest[: CHUNK // 2], rest[CHUNK // 2 :]], axis=1)


def unpack_tokens_kernel(ctx, where_ref, *refs):
    tok_refs, all_ref, own_ref = refs[:4], refs[4], refs[5]
    place = where_ref[0]
    share = own_ref.shape[0]
    full = share // DK
    for j in range(4):
        block = where_ref[2 + j]
        for d in range(ctx):
            source = lax.rem(place + ctx - d, ctx)
            start = source * CHUNK
            base = d * share
            for g in range(full):
                piece = tok_refs[j][base + g * CHUNK : base + (g + 1) * CHUNK, :]
                all_ref[block, tile_rows(start, CHUNK), g * DK : (g + 1) * DK] = piece
            rest = tok_refs[j][base + full * CHUNK : base + share, :]
            all_ref[block, tile_rows(start, CHUNK // 2), full * DK :] = rest[:, : DK // 2]
            all_ref[block, tile_rows(start + CHUNK // 2, CHUNK // 2), full * DK :] = rest[:, DK // 2 :]
    for n in range(ctx):
        piece = all_ref[place, n * CHUNK : (n + 1) * CHUNK, :].astype(jnp.float32)
        own_ref[:, n * CHUNK : (n + 1) * CHUNK] = narrow(jnp.transpose(piece))


def pack_kernel(ctx, where_ref, wq_ref, wk_ref, wv_ref, decay_ref, cot_ref, logit_ref, *out_refs):
    place, group = where_ref[0], where_ref[1]
    half = wq_ref.shape[0] // 2
    for s in range(2):
        for d in range(ctx):
            head = 2 * lax.rem(place + d, ctx) + s
            column = lanes(head * DK)
            out = out_refs[s * ctx + d]
            size = out.shape[0] - EXTRA
            rows = slice(None) if d == 0 else tile_rows(group * half, half)
            for part, ref in enumerate((wq_ref, wk_ref, wv_ref)):
                out[0:size, part * DK : (part + 1) * DK] = ref[rows, column]
            decay = narrow(decay_ref[:, column])
            cot = cot_ref[:, column]
            out[size : size + 96, 0:DK] = decay[0:96]
            out[size : size + 32, DK : 2 * DK] = decay[96:128]
            out[size + 32 : size + 96, DK : 2 * DK] = cot[0:64]
            out[size : size + 64, 2 * DK : 3 * DK] = cot[64:128]
            out[size + 64 : size + 80, 2 * DK : 3 * DK] = tail_rows(logit_ref[pl.ds(head, 1), :])
            out[size + 80 : size + 96, 2 * DK : 3 * DK] = jnp.zeros((16, DK), out.dtype)


def head_kernel(ctx, slot, where_ref, *refs):
    all_ref, refs = refs[0], refs[1:]
    direct, refs = refs[:ctx], refs[ctx:]
    swapped, refs = refs[: ctx - 1], refs[ctx - 1 :]
    if slot:
        earlier_ref, refs = refs[0], refs[1:]
    grad_ref, back_ref, w, raw, decay, cot, logit, out, dlogit, ddecay = refs
    place, group = where_ref[0], where_ref[1]
    share = direct[0].shape[0] - EXTRA
    half = share // 2
    for d in range(ctx):
        source = lax.rem(place + ctx - d, ctx)
        ref = direct[d]
        if d == 0:
            w[tile_rows(source * share, share), :] = ref[0:share, :]
            size = share
        else:
            w[tile_rows(source * share + group * half, half), :] = ref[0:half, :]
            w[tile_rows(source * share + (1 - group) * half, half), :] = swapped[d - 1][0:half, :]
            size = half
        start = source * CHUNK
        decay[tile_rows(start, 96), :] = ref[size : size + 96, 0:DK].astype(jnp.float32)
        decay[tile_rows(start + 96, 32), :] = ref[size : size + 32, DK : 2 * DK].astype(jnp.float32)
        cot[tile_rows(start, 64), :] = ref[size + 32 : size + 96, DK : 2 * DK].astype(jnp.float32)
        cot[tile_rows(start + 64, 64), :] = ref[size : size + 64, 2 * DK : 3 * DK].astype(jnp.float32)
        tail = ref[size + 64 : size + 80, 2 * DK : 3 * DK].astype(jnp.float32)
        logit[pl.ds(source, 1), :] = tail[0:1] + tail[1:2]
    projected = 0.0
    for j in range(ctx):
        projected = projected + lax.dot_general(
            all_ref[j], w[j * share : (j + 1) * share, :], NN, preferred_element_type=jnp.float32
        )
    raw[...] = projected
    recurrence(raw, decay, logit, cot, out, grad_ref, dlogit, ddecay)
    lane = slice(slot * DK, (slot + 1) * DK)
    if slot:
        back_ref[:, :, 0:DK] = earlier_ref[...]
    for n in range(ctx):
        back_ref[n, 0:CHUNK, lane] = out[n]
        back_ref[n, CHUNK : 2 * CHUNK, lane] = ddecay[n]
        back_ref[n, 2 * CHUNK :, lane] = tail_rows(dlogit[n : n + 1, :])


def weight_gradient_kernel(steps, forwarded, where_ref, own_ref, *refs):
    out_refs = refs[-3:]

    def block(gradient):
        product = lax.dot_general(own_ref[...], gradient, NN, preferred_element_type=jnp.float32)
        for part in range(3):
            out_refs[part][...] = product[:, part * DK : (part + 1) * DK]

    for at, step in enumerate(steps):

        @pl.when(pl.program_id(0) == at)
        def _(at=at, step=step):
            if step < 3 or not forwarded:
                block(refs[at][...])
            else:
                block(jnp.where(where_ref[14] == 1, refs[at + 1][...], refs[at][...]))


def unpack_kernel(back_ref, out_ref, dlogit_ref, ddecay_ref):
    for source in range(back_ref.shape[0]):
        column = slice(2 * source * DK, 2 * (source + 1) * DK)
        out_ref[:, column] = back_ref[source, 0:CHUNK, :]
        ddecay_ref[:, column] = back_ref[source, CHUNK : 2 * CHUNK, :].astype(jnp.float32)
        tail = back_ref[source, 2 * CHUNK :, :].astype(jnp.float32)
        row = tail[0:1] + tail[1:2]
        for s in range(2):
            dlogit_ref[2 * source + s : 2 * source + s + 1, :] = row[:, s * DK : (s + 1) * DK]


def head_split(tokens, w_query, w_key, w_value, beta_logit, log_decay, grad_out):
    ctx = lax.axis_size("ctx")
    place = lax.axis_index("ctx")
    group = lax.axis_index("groups")
    across, core = lax.axis_index("fsdp"), lax.axis_index("head")
    length, depth = tokens.shape
    share, columns = w_query.shape
    total = ctx * length
    bf16, f32 = jnp.bfloat16, jnp.float32
    whole = pl.BlockSpec(memory_space=pltpu.VMEM)
    scalars = pl.BlockSpec(memory_space=pltpu.SMEM)
    sources = [place, place + 1 - 2 * (place % 2), (place + 2) % ctx, ctx - 1 - place]
    where = jnp.stack(
        [place, group]
        + [2 * a + c for c in (core, 1 - core) for a in (across, 1 - across)]
        + [(place + ctx - d) % ctx for d in range(ctx)]
        + sources
        + [((place == 0) | (place == ctx - 1)).astype(jnp.int32)]
    ).astype(jnp.int32)

    def shape(dims, kind):
        return jax.ShapeDtypeStruct(dims, kind)

    def after(x, earlier):
        return lax.optimization_barrier((x, earlier))

    def along(x, axis, hop):
        count = lax.axis_size(axis)
        return lax.ppermute(x, axis, [(i, (i + hop) % count) for i in range(count)])

    tok = pl.pallas_call(
        pack_tokens_kernel,
        out_shape=shape((share, length), bf16),
        in_specs=[scalars, whole],
        out_specs=whole,
        compiler_params=pltpu.CompilerParams(vmem_limit_bytes=VMEM_LIMIT),
        name="pack_tokens",
    )(where, tokens)
    sizes = [share + EXTRA] + [share // 2 + EXTRA] * (ctx - 1)
    packed = pl.pallas_call(
        functools.partial(pack_kernel, ctx),
        out_shape=[shape((size, HEAD_COLUMNS), bf16) for size in sizes * 2],
        in_specs=[scalars] + [whole] * 6,
        out_specs=[whole] * (2 * ctx),
        compiler_params=pltpu.CompilerParams(vmem_limit_bytes=VMEM_LIMIT),
        name="pack",
    )(where, w_query, w_key, w_value, log_decay, grad_out, beta_logit)

    near = [along(tok, "ctx", d) for d in range(1, ctx)]
    first, near[0] = after(packed[1:ctx], near[0])
    first = [along(x, "ctx", d + 1) for d, x in enumerate(first)]
    tok = jnp.concatenate([tok] + near, axis=0)
    tok_x = along(tok, "fsdp", 1)
    half = share // 2
    swapped = [along(first[0][:half], "groups", 1)]
    (tok_c, tok_xc, first[1], first[2]), swapped[0] = after((tok, tok_x, first[1], first[2]), swapped[0])
    toks = (tok, tok_x, along(tok_c, "head", 1), along(tok_xc, "head", 1))
    all_tokens, own = pl.pallas_call(
        functools.partial(unpack_tokens_kernel, ctx),
        out_shape=[shape((ctx, total, share), bf16), shape((share, total), bf16)],
        in_specs=[scalars] + [whole] * 4,
        out_specs=[whole] * 2,
        compiler_params=pltpu.CompilerParams(vmem_limit_bytes=VMEM_LIMIT),
        name="unpack_tokens",
    )(where, *toks)
    swapped += [along(x[:half], "groups", 1) for x in first[1:]]
    second, first[1:] = after(packed[ctx + 1 :], first[1:])
    second = [along(x, "ctx", d + 1) for d, x in enumerate(second)]

    def products(slot, steps, parts, results):
        column = pl.BlockSpec((share, DK), lambda i, ref: (0, 2 * ref[6 + 4 * slot + steps[0] + i] + slot))
        return pl.pallas_call(
            functools.partial(weight_gradient_kernel, steps, slot == 1),
            grid_spec=pltpu.PrefetchScalarGridSpec(
                num_scalar_prefetch=1,
                grid=(len(steps),),
                in_specs=[whole] * (1 + len(parts)) + [pl.BlockSpec(memory_space=pl.ANY)] * len(results),
                out_specs=[column] * 3,
            ),
            out_shape=[shape((share, columns), f32)] * 3,
            input_output_aliases={2 + len(parts) + i: i for i in range(len(results))},
            compiler_params=pltpu.CompilerParams(vmem_limit_bytes=VMEM_LIMIT),
            name=f"weight_gradient_{slot}_{steps[0]}",
        )(where, own, *parts, *results)

    grads = []
    back = None
    for slot, direct in enumerate((first, second)):
        if slot:
            for d in range(ctx - 1):
                direct[d], back = after(direct[d], back)
            swapped = [along(x[:half], "groups", 1) for x in direct]
        earlier = [] if back is None else [back]
        grad, back = pl.pallas_call(
            functools.partial(head_kernel, ctx, slot),
            out_shape=[
                shape((total, HEAD_COLUMNS), bf16),
                shape((ctx, 2 * CHUNK + TAIL, (slot + 1) * DK), bf16),
            ],
            in_specs=[scalars] + [whole] * (1 + ctx + ctx - 1 + slot),
            out_specs=[whole] * 2,
            scratch_shapes=[
                pltpu.VMEM((depth, HEAD_COLUMNS), bf16),
                pltpu.VMEM((total, HEAD_COLUMNS), f32),
                pltpu.VMEM((total, DK), f32),
                pltpu.VMEM((total, DV), f32),
                pltpu.VMEM((ctx, CHUNK), f32),
                pltpu.VMEM((ctx, CHUNK, DV), bf16),
                pltpu.VMEM((ctx, CHUNK), f32),
                pltpu.VMEM((ctx, CHUNK, DK), bf16),
            ],
            cost_estimate=pl.CostEstimate(flops=FLOPS[slot], transcendentals=0, bytes_accessed=FLOPS[slot] // 1000),
            compiler_params=pltpu.CompilerParams(vmem_limit_bytes=VMEM_LIMIT),
            name=f"head_{slot}",
        )(where, all_tokens, packed[slot * ctx], *direct, *swapped, *earlier)
        if slot == 0:
            hops = [along(grad, "ctx", d) for d in range(1, ctx)]
            grads.append([grad] + hops)
            continue
        grad, grads[0][1:3] = after(grad, grads[0][1:3])
        two = lax.ppermute(grad, "ctx", [(0, 2), (1, 3), (2, 0), (3, 1)])
        pair = lax.ppermute(grad, "ctx", [(0, 1), (1, 0), (2, 3), (3, 2)])
        results = products(0, (0, 1, 2, 3), grads[0], ())
        (grad, two), (pair, results) = after((grad, two), (pair, results))
        middle = lax.ppermute(grad, "ctx", [(1, 2), (2, 1)])
        far = lax.ppermute(two, "ctx", [(2, 3), (1, 0)])
        results = products(1, (0, 1, 2), [grad, pair, two], results)
        results = products(1, (3,), [middle, far], results)
    back = lax.all_to_all(back, "ctx", 0, 0)

    attn_out, grad_beta, grad_decay = pl.pallas_call(
        unpack_kernel,
        out_shape=[shape((length, columns), bf16), shape((columns // DK, length), f32), shape((length, columns), f32)],
        in_specs=[whole],
        out_specs=[whole] * 3,
        compiler_params=pltpu.CompilerParams(vmem_limit_bytes=VMEM_LIMIT),
        name="unpack",
    )(back)
    return (attn_out, *results, grad_beta, grad_decay)


def prefix_2(x, axis, join, neutral, backward):
    count = lax.axis_size(axis)
    place = lax.axis_index(axis)
    ahead = count - 1 - place if backward else place
    gathered = jax.tree.map(
        lambda a, kind: lax.all_gather(a.astype(kind), axis), x, (jnp.bfloat16, jnp.bfloat16)
    )
    state = jax.tree.map(lambda a, e: jnp.zeros_like(a) + jnp.asarray(e, a.dtype), x, neutral)

    def one(hop, state):
        source = count - 1 - hop if backward else hop
        return join(
            state,
            jax.tree.map(
                lambda a, own: lax.dynamic_index_in_dim(a, source, 0, False).astype(own.dtype),
                gathered,
                x,
            ),
        )

    return lax.fori_loop(0, ahead, one, state)


def normalize(vectors):
    return vectors * lax.rsqrt(jnp.sum(vectors * vectors, axis=-1, keepdims=True) + epsilon)


def heads_first(matrix, heads):
    return matrix.reshape(matrix.shape[0], heads, -1).transpose(1, 0, 2)


def span_step(memory, queries, key_vecs, val_vecs, strength, forgetting_exponent):
    largest_value = lax.Precision.HIGHEST
    length = queries.shape[1]
    cumulate = jnp.cumsum(forgetting_exponent, axis=1)
    growth = jnp.exp(cumulate)
    shrink = jnp.exp(-cumulate)
    key_up = key_vecs * growth
    key_down = key_vecs * shrink
    query_up = queries * growth
    row_ids = lax.broadcasted_iota(jnp.int32, (length, length), 0)
    col_ids = lax.broadcasted_iota(jnp.int32, (length, length), 1)
    strict = (row_ids > col_ids).astype(jnp.float32)
    within = (row_ids >= col_ids).astype(jnp.float32)
    affinity = jnp.einsum("bcd,bsd->bcs", key_up, key_down, precision=largest_value) * strict
    system = jnp.eye(length, dtype=jnp.float32) + strength[:, :, None] * affinity
    target = strength[:, :, None] * (
        val_vecs - jnp.einsum("bcd,bdw->bcw", key_up, memory, precision=largest_value)
    )
    update = lax.linalg.triangular_solve(system, target, left_side=True, lower=True)
    scores = jnp.einsum("bcd,bsd->bcs", query_up, key_down, precision=largest_value) * within
    emitted = jnp.einsum("bcd,bdw->bcw", query_up, memory, precision=largest_value)
    emitted = emitted + jnp.einsum("bcs,bsw->bcw", scores, update, precision=largest_value)
    at_end = growth[:, -1, :]
    renewed = at_end[:, :, None] * memory + jnp.einsum(
        "bsd,bsw->bdw", key_down * at_end[:, None, :], update, precision=largest_value
    )
    return (emitted, renewed)


def scan_spans(memory, queries, key_vecs, val_vecs, strength, forgetting_exponent):
    count = queries.shape[1] // SPAN

    def to_blocks(array):
        shaped = array.reshape((array.shape[0], count, SPAN) + array.shape[2:])
        return jnp.swapaxes(shaped, 0, 1)

    def advance(carried, blocks):
        emitted, renewed = span_step(carried, *blocks)
        return (renewed, emitted)

    blocks = (
        to_blocks(queries),
        to_blocks(key_vecs),
        to_blocks(val_vecs),
        to_blocks(strength),
        to_blocks(forgetting_exponent),
    )
    final, emitted = lax.scan(advance, memory, blocks)
    emitted = jnp.swapaxes(emitted, 0, 1)
    return (emitted.reshape(emitted.shape[0], count * SPAN, emitted.shape[-1]), final)


def compose(earlier, later):
    largest_value = lax.Precision.HIGHEST
    joined = jnp.einsum("hij,hjk->hik", later[0], earlier[0], precision=largest_value)
    shifted = jnp.einsum("hij,hjv->hiv", later[0], earlier[1], precision=largest_value) + later[1]
    return (joined, shifted)


def per_device(tokens, w_query, w_key, w_value, beta_logit, log_decay, grad_out):
    largest_value = lax.Precision.HIGHEST
    length = tokens.shape[0]
    columns = w_query.shape[1]
    heads = columns // DK
    shard_rows = (
        lax.all_gather(w_query, "ctx", axis=0, tiled=True),
        lax.all_gather(w_key, "ctx", axis=0, tiled=True),
        lax.all_gather(w_value, "ctx", axis=0, tiled=True),
    )
    window = tokens
    query_raw, key_raw, value_raw = tuple(
        (jnp.dot(window, weights, preferred_element_type=jnp.float32) for weights in shard_rows)
    )

    def shard_pass(query_in, key_in, value_in, logits, log_gates):
        queries = normalize(heads_first(query_in, heads))
        key_vecs = normalize(heads_first(key_in, heads))
        val_vecs = heads_first(value_in, heads)
        widened = jnp.concatenate([jnp.zeros((heads, length, DK), jnp.float32), val_vecs], axis=2)
        initial = jnp.concatenate(
            [
                jnp.broadcast_to(jnp.eye(DK, dtype=jnp.float32), (heads, DK, DK)),
                jnp.zeros((heads, DK, DV), jnp.float32),
            ],
            axis=2,
        )
        return scan_spans(
            initial,
            queries,
            key_vecs,
            widened,
            jax.nn.sigmoid(logits),
            heads_first(log_gates, heads),
        )

    (mixed, final), pullback = jax.vjp(
        shard_pass, query_raw, key_raw, value_raw, beta_logit, log_decay
    )
    transit = final[:, :, :DK]
    offset = final[:, :, DK:]
    query_carried_over = mixed[:, :, :DK]
    local_output = mixed[:, :, DK:]
    output_cotangent = grad_out.reshape(length, heads, DV).transpose(1, 0, 2).astype(jnp.float32)
    contribution = jnp.einsum(
        "mij,mif->mjf", query_carried_over, output_cotangent, precision=largest_value
    )
    identity = (
        jnp.broadcast_to(jnp.eye(DK, dtype=jnp.float32), (heads, DK, DK)),
        jnp.zeros((heads, DK, DV), jnp.float32),
    )
    prefix = prefix_2((transit, offset), "ctx", compose, identity, False)
    incoming_state = prefix[1]
    suffix = prefix_2((jnp.swapaxes(transit, 1, 2), contribution), "ctx", compose, identity, True)
    adjoint_state = suffix[1]
    complete_output = local_output + jnp.einsum(
        "npg,ngj->npj", query_carried_over, incoming_state, precision=largest_value
    )
    attn_out = complete_output.transpose(1, 0, 2).reshape(length, heads * DV).astype(jnp.bfloat16)
    d_mixed = jnp.concatenate(
        [
            jnp.einsum("efu,egu->efg", output_cotangent, incoming_state, precision=largest_value),
            output_cotangent,
        ],
        axis=2,
    )
    d_final = jnp.concatenate(
        [
            jnp.einsum("pgx,pcx->pgc", adjoint_state, incoming_state, precision=largest_value),
            adjoint_state,
        ],
        axis=2,
    )
    d_query, d_key, d_value, grad_beta, grad_decay = pullback((d_mixed, d_final))
    grad_projected = jnp.concatenate([d_query, d_key, d_value], axis=1).astype(jnp.bfloat16)
    window = tokens
    summed = lax.psum_scatter(
        jnp.einsum("td,tc->dc", window, grad_projected, preferred_element_type=jnp.float32).astype(
            jnp.bfloat16
        ),
        "ctx",
        scatter_dimension=0,
        tiled=True,
    ).astype(jnp.float32)
    return (
        attn_out,
        summed[:, :columns],
        summed[:, columns : 2 * columns],
        summed[:, 2 * columns :],
        grad_beta,
        grad_decay,
    )


def device_program(tokens, w_query, *rest):
    ctx = lax.axis_size("ctx")
    heads = w_query.shape[1] // DK
    split = heads == 2 * ctx and ctx == 4 and tokens.shape[0] == CHUNK and w_query.shape[0] * ctx == tokens.shape[1]
    split = split and lax.axis_size("groups") == lax.axis_size("fsdp") == lax.axis_size("head") == 2
    split = split and w_query.shape[0] % 64 == 0
    return (head_split if split else per_device)(tokens, w_query, *rest)


def solution(mesh):
    return jax.shard_map(
        device_program,
        mesh=mesh,
        in_specs=(
            P(("groups", "ctx"), None),
            P("ctx", ("fsdp", "head")),
            P("ctx", ("fsdp", "head")),
            P("ctx", ("fsdp", "head")),
            P(("fsdp", "head"), ("groups", "ctx")),
            P(("groups", "ctx"), ("fsdp", "head")),
            P(("groups", "ctx"), ("fsdp", "head")),
        ),
        out_specs=(
            P(("groups", "ctx"), ("fsdp", "head")),
            P(("groups", "ctx"), ("fsdp", "head")),
            P(("groups", "ctx"), ("fsdp", "head")),
            P(("groups", "ctx"), ("fsdp", "head")),
            P(("fsdp", "head"), ("groups", "ctx")),
            P(("groups", "ctx"), ("fsdp", "head")),
        ),
        check_vma=False,
    )
```

```python
import functools

import jax
import jax.numpy as jnp
from jax import lax
from jax.experimental import pallas as pl
from jax.experimental.pallas import tpu as pltpu
from jax.sharding import PartitionSpec as P

DK = 128
DV = 128
SPAN = 64
CHUNK = 128
TAIL = 16
EXTRA = 96
VMEM_LIMIT = 20 * 2**20
FLOPS = (12_000_000_000, 12_000_000_000)
HEAD_COLUMNS = 2 * DK + DV

epsilon = 1e-06
HIGHEST = lax.Precision.HIGHEST
NN = (((1,), (0,)), ((), ()))
NT = (((1,), (1,)), ((), ()))
TN = (((0,), (0,)), ((), ()))


def narrow(x):
    return x.astype(jnp.bfloat16)


def dot(a, b, dims, passes):
    if passes == 6:
        return lax.dot_general(a, b, dims, precision=HIGHEST, preferred_element_type=jnp.float32)
    a_high, b_high = narrow(a), narrow(b)
    total = lax.dot_general(a_high, b_high, dims, preferred_element_type=jnp.float32)
    if passes >= 3:
        a_low = narrow(a - a_high.astype(jnp.float32))
        b_low = narrow(b - b_high.astype(jnp.float32))
        total = total + lax.dot_general(a_high, b_low, dims, preferred_element_type=jnp.float32)
        total = total + lax.dot_general(a_low, b_high, dims, preferred_element_type=jnp.float32)
    return total


PASSES = dict(
    decay=1, pairs=3, inverse=3, solve=3, read=1, carry=3, sent=1, scan=1, emit=1, update=1,
    d_update=3, d_value=3, d_pairs=1, d_up=1, d_up_state=1, d_kd=1, d_kend=1, d_decay=3,
)


def run(name, a, b, dims):
    return dot(a, b, dims, PASSES[name])


def recurrence(raw_ref, decay_ref, logit_ref, cot_ref, out_ref, grad_ref, dlogit_ref, ddecay_ref):
    count = raw_ref.shape[0] // CHUNK
    spans = range(count)
    rows = lax.broadcasted_iota(jnp.int32, (CHUNK, CHUNK), 0)
    cols = lax.broadcasted_iota(jnp.int32, (CHUNK, CHUNK), 1)
    within = rows >= cols
    strict = rows > cols
    diagonal = rows == cols
    running = within.astype(jnp.float32)

    q, k, v, rq, rk, up, down, end = [], [], [], [], [], [], [], []
    qu, ku, kd, kend, beta_row, cot = [], [], [], [], [], []
    for n in spans:
        here = slice(n * CHUNK, (n + 1) * CHUNK)
        q_raw = raw_ref[here, 0:DK]
        k_raw = raw_ref[here, DK : 2 * DK]
        v.append(raw_ref[here, 2 * DK : 3 * DK])
        rq.append(lax.rsqrt(jnp.sum(q_raw * q_raw, axis=1, keepdims=True) + epsilon))
        rk.append(lax.rsqrt(jnp.sum(k_raw * k_raw, axis=1, keepdims=True) + epsilon))
        q.append(q_raw * rq[n])
        k.append(k_raw * rk[n])
        summed = run("decay", running, decay_ref[here, :], NN)
        up.append(jnp.exp(summed))
        down.append(jnp.exp(-summed))
        end.append(up[n][CHUNK - 1 : CHUNK, :])
        qu.append(q[n] * up[n])
        ku.append(k[n] * up[n])
        kd.append(k[n] * down[n])
        kend.append(kd[n] * end[n])
        beta_row.append(jax.nn.sigmoid(logit_ref[n : n + 1, :]))
        cot.append(cot_ref[here, :])

    scores, system, inverse = [], [], []
    for n in spans:
        pairs = run("pairs", jnp.concatenate([qu[n], ku[n]], axis=0), kd[n], NT)
        scores.append(jnp.where(within, pairs[:CHUNK], 0.0))
        beta_col = jnp.transpose(jnp.broadcast_to(beta_row[n], (CHUNK, CHUNK)))
        system.append(jnp.where(strict, pairs[CHUNK:] * beta_col, 0.0))
        pair_block = (rows // 2) == (cols // 2)
        inverse.append(diagonal.astype(jnp.float32) - jnp.where(pair_block, system[n], 0.0))
    size = 2
    while size < CHUNK:
        joined = ((rows // (2 * size)) == (cols // (2 * size))) & ((rows // size) != (cols // size))
        halves = [run("inverse", jnp.where(joined, system[n], 0.0), inverse[n], NN) for n in spans]
        inverse = [inverse[n] - run("inverse", inverse[n], halves[n], NN) for n in spans]
        size *= 2

    solve = [inverse[n] * beta_row[n] for n in spans]
    wu = [run("solve", solve[n], jnp.concatenate([ku[n], v[n]], axis=1), NN) for n in spans]
    pwu = [run("read", scores[n], wu[n], NN) for n in spans]
    kwu = [run("carry", kend[n], wu[n], TN) for n in spans]
    query_through = [qu[n] - pwu[n][:, :DK] for n in spans]
    transit = [
        jnp.where(diagonal, jnp.broadcast_to(end[n], (DK, DK)), 0.0) - kwu[n][:, :DK] for n in spans
    ]
    sent = [run("sent", query_through[n], cot[n], TN) for n in spans]

    state = [None] * (count + 1)
    adjoint = [None] * (count + 1)
    for n in spans:
        m = count - 1 - n
        own = kwu[n][:, DK:]
        state[n + 1] = own if n == 0 else run("scan", transit[n], state[n], NN) + own
        adjoint[m] = sent[m] if n == 0 else run("scan", transit[m], adjoint[m + 1], TN) + sent[m]

    for n in spans:
        here = slice(n * CHUNK, (n + 1) * CHUNK)
        w = wu[n][:, :DK]
        update = wu[n][:, DK:]
        emitted = pwu[n][:, DK:]
        d_update = run("d_update", scores[n], cot[n], TN)
        if n > 0:
            emitted = emitted + run("emit", query_through[n], state[n], NN)
            update = update - run("update", w, state[n], NN)
        if n < count - 1:
            d_update = d_update + run("d_update", kend[n], adjoint[n + 1], NN)
        out_ref[n] = emitted.astype(out_ref.dtype)
        d_value = run("d_value", solve[n], d_update, TN)
        both = jnp.concatenate([cot[n], -d_value], axis=0)
        pairs = run("d_pairs", both, update, NT)
        d_pairs = jnp.concatenate(
            [jnp.where(within, pairs[:CHUNK], 0.0), jnp.where(strict, pairs[CHUNK:], 0.0)], axis=0
        )
        d_up = run("d_up", d_pairs, kd[n], NN)
        if n > 0:
            d_up = d_up + run("d_up_state", both, state[n], NT)
        d_qu, d_ku = d_up[:CHUNK], d_up[CHUNK:]
        d_kd = run("d_kd", d_pairs, jnp.concatenate([qu[n], ku[n]], axis=0), TN)
        d_k = d_ku * up[n] + d_kd * down[n]
        d_sum = d_qu * qu[n] + d_ku * ku[n] - d_kd * kd[n]
        d_decay_end = jnp.zeros((1, DK), jnp.float32)
        if n < count - 1:
            d_kend = run("d_kend", update, adjoint[n + 1], NT)
            d_k = d_k + d_kend * (end[n] * down[n])
            ended = d_kend * kend[n]
            d_sum = d_sum - ended
            d_decay_end = jnp.sum(ended, axis=0, keepdims=True)
            if n > 0:
                kept = jnp.sum(jnp.transpose(adjoint[n + 1] * state[n]), axis=0, keepdims=True)
                d_decay_end = d_decay_end + end[n] * kept
        ddecay_ref[n] = (run("d_decay", running, d_sum, TN) + d_decay_end).astype(ddecay_ref.dtype)
        d_q = d_qu * up[n]
        d_q = rq[n] * (d_q - q[n] * jnp.sum(q[n] * d_q, axis=1, keepdims=True))
        d_k = rk[n] * (d_k - k[n] * jnp.sum(k[n] * d_k, axis=1, keepdims=True))
        grad_ref[here, 0:DK] = d_q.astype(grad_ref.dtype)
        grad_ref[here, DK : 2 * DK] = d_k.astype(grad_ref.dtype)
        grad_ref[here, 2 * DK : 3 * DK] = d_value.astype(grad_ref.dtype)
        aligned = jnp.sum(jnp.transpose(d_value * update), axis=0, keepdims=True)
        dlogit_ref[n : n + 1, :] = aligned * jnp.exp(-logit_ref[n : n + 1, :])


def split_two(x):
    high = narrow(x)
    return high, narrow(x - high.astype(jnp.float32))


def tail_rows(x):
    high, low = split_two(x)
    index = lax.broadcasted_iota(jnp.int32, (TAIL, x.shape[1]), 0)
    high = jnp.broadcast_to(high.astype(jnp.float32), index.shape)
    low = jnp.broadcast_to(low.astype(jnp.float32), index.shape)
    return narrow(jnp.where(index == 0, high, jnp.where(index == 1, low, 0.0)))


def lanes(start):
    return pl.ds(pl.multiple_of(start, DK), DK)


def tile_rows(start, size):
    return pl.ds(pl.multiple_of(start, 32), size)


def pack_tokens_kernel(where_ref, tokens_ref, tok_ref):
    share = tok_ref.shape[0]
    for j in range(tokens_ref.shape[1] // share):

        @pl.when(where_ref[2] == j)
        def _(j=j):
            block = tokens_ref[:, j * share : (j + 1) * share]
            full = share // DK
            for g in range(full):
                tok_ref[g * CHUNK : (g + 1) * CHUNK, :] = block[:, g * DK : (g + 1) * DK]
            rest = block[:, full * DK :]
            tok_ref[full * CHUNK :, :] = jnp.concatenate([rest[: CHUNK // 2], rest[CHUNK // 2 :]], axis=1)


def unpack_tokens_kernel(ctx, where_ref, *refs):
    tok_refs, all_ref, own_ref = refs[:4], refs[4], refs[5]
    place = where_ref[0]
    share = own_ref.shape[0]
    full = share // DK
    for j in range(4):
        block = where_ref[2 + j]
        for d in range(ctx):
            source = lax.rem(place + ctx - d, ctx)
            start = source * CHUNK
            base = d * share
            for g in range(full):
                piece = tok_refs[j][base + g * CHUNK : base + (g + 1) * CHUNK, :]
                all_ref[block, tile_rows(start, CHUNK), g * DK : (g + 1) * DK] = piece
            rest = tok_refs[j][base + full * CHUNK : base + share, :]
            all_ref[block, tile_rows(start, CHUNK // 2), full * DK :] = rest[:, : DK // 2]
            all_ref[block, tile_rows(start + CHUNK // 2, CHUNK // 2), full * DK :] = rest[:, DK // 2 :]
    for n in range(ctx):
        piece = all_ref[place, n * CHUNK : (n + 1) * CHUNK, :].astype(jnp.float32)
        own_ref[:, n * CHUNK : (n + 1) * CHUNK] = narrow(jnp.transpose(piece))


def pack_kernel(ctx, where_ref, wq_ref, wk_ref, wv_ref, decay_ref, cot_ref, logit_ref, *out_refs):
    place, group = where_ref[0], where_ref[1]
    half = wq_ref.shape[0] // 2
    for s in range(2):
        for d in range(ctx):
            head = 2 * lax.rem(place + d, ctx) + s
            column = lanes(head * DK)
            out = out_refs[s * ctx + d]
            size = out.shape[0] - EXTRA
            rows = slice(None) if d == 0 else tile_rows(group * half, half)
            for part, ref in enumerate((wq_ref, wk_ref, wv_ref)):
                out[0:size, part * DK : (part + 1) * DK] = ref[rows, column]
            decay = narrow(decay_ref[:, column])
            cot = cot_ref[:, column]
            out[size : size + 96, 0:DK] = decay[0:96]
            out[size : size + 32, DK : 2 * DK] = decay[96:128]
            out[size + 32 : size + 96, DK : 2 * DK] = cot[0:64]
            out[size : size + 64, 2 * DK : 3 * DK] = cot[64:128]
            out[size + 64 : size + 80, 2 * DK : 3 * DK] = tail_rows(logit_ref[pl.ds(head, 1), :])
            out[size + 80 : size + 96, 2 * DK : 3 * DK] = jnp.zeros((16, DK), out.dtype)


def head_kernel(ctx, slot, where_ref, *refs):
    all_ref, refs = refs[0], refs[1:]
    direct, refs = refs[:ctx], refs[ctx:]
    swapped, refs = refs[: ctx - 1], refs[ctx - 1 :]
    if slot:
        earlier_ref, refs = refs[0], refs[1:]
    grad_ref, back_ref, w, raw, decay, cot, logit, out, dlogit, ddecay = refs
    place, group = where_ref[0], where_ref[1]
    share = direct[0].shape[0] - EXTRA
    half = share // 2
    for d in range(ctx):
        source = lax.rem(place + ctx - d, ctx)
        ref = direct[d]
        if d == 0:
            w[tile_rows(source * share, share), :] = ref[0:share, :]
            size = share
        else:
            w[tile_rows(source * share + group * half, half), :] = ref[0:half, :]
            w[tile_rows(source * share + (1 - group) * half, half), :] = swapped[d - 1][0:half, :]
            size = half
        start = source * CHUNK
        decay[tile_rows(start, 96), :] = ref[size : size + 96, 0:DK].astype(jnp.float32)
        decay[tile_rows(start + 96, 32), :] = ref[size : size + 32, DK : 2 * DK].astype(jnp.float32)
        cot[tile_rows(start, 64), :] = ref[size + 32 : size + 96, DK : 2 * DK].astype(jnp.float32)
        cot[tile_rows(start + 64, 64), :] = ref[size : size + 64, 2 * DK : 3 * DK].astype(jnp.float32)
        tail = ref[size + 64 : size + 80, 2 * DK : 3 * DK].astype(jnp.float32)
        logit[pl.ds(source, 1), :] = tail[0:1] + tail[1:2]
    projected = 0.0
    for j in range(ctx):
        projected = projected + lax.dot_general(
            all_ref[j], w[j * share : (j + 1) * share, :], NN, preferred_element_type=jnp.float32
        )
    raw[...] = projected
    recurrence(raw, decay, logit, cot, out, grad_ref, dlogit, ddecay)
    lane = slice(slot * DK, (slot + 1) * DK)
    if slot:
        back_ref[:, :, 0:DK] = earlier_ref[...]
    for n in range(ctx):
        back_ref[n, 0:CHUNK, lane] = out[n]
        back_ref[n, CHUNK : 2 * CHUNK, lane] = ddecay[n]
        back_ref[n, 2 * CHUNK :, lane] = tail_rows(dlogit[n : n + 1, :])


def weight_gradient_kernel(steps, forwarded, where_ref, own_ref, *refs):
    out_refs = refs[-3:]

    def block(gradient):
        product = lax.dot_general(own_ref[...], gradient, NN, preferred_element_type=jnp.float32)
        for part in range(3):
            out_refs[part][...] = product[:, part * DK : (part + 1) * DK]

    for at, step in enumerate(steps):

        @pl.when(pl.program_id(0) == at)
        def _(at=at, step=step):
            if step < 3 or not forwarded:
                block(refs[at][...])
            else:
                block(jnp.where(where_ref[14] == 1, refs[at + 1][...], refs[at][...]))


def unpack_kernel(back_ref, out_ref, dlogit_ref, ddecay_ref):
    for source in range(back_ref.shape[0]):
        column = slice(2 * source * DK, 2 * (source + 1) * DK)
        out_ref[:, column] = back_ref[source, 0:CHUNK, :]
        ddecay_ref[:, column] = back_ref[source, CHUNK : 2 * CHUNK, :].astype(jnp.float32)
        tail = back_ref[source, 2 * CHUNK :, :].astype(jnp.float32)
        row = tail[0:1] + tail[1:2]
        for s in range(2):
            dlogit_ref[2 * source + s : 2 * source + s + 1, :] = row[:, s * DK : (s + 1) * DK]


def head_split(tokens, w_query, w_key, w_value, beta_logit, log_decay, grad_out):
    ctx = lax.axis_size("ctx")
    place = lax.axis_index("ctx")
    group = lax.axis_index("groups")
    across, core = lax.axis_index("fsdp"), lax.axis_index("head")
    length, depth = tokens.shape
    share, columns = w_query.shape
    total = ctx * length
    bf16, f32 = jnp.bfloat16, jnp.float32
    whole = pl.BlockSpec(memory_space=pltpu.VMEM)
    scalars = pl.BlockSpec(memory_space=pltpu.SMEM)
    sources = [place, place + 1 - 2 * (place % 2), (place + 2) % ctx, ctx - 1 - place]
    where = jnp.stack(
        [place, group]
        + [2 * a + c for c in (core, 1 - core) for a in (across, 1 - across)]
        + [(place + ctx - d) % ctx for d in range(ctx)]
        + sources
        + [((place == 0) | (place == ctx - 1)).astype(jnp.int32)]
    ).astype(jnp.int32)

    def shape(dims, kind):
        return jax.ShapeDtypeStruct(dims, kind)

    def after(x, earlier):
        return lax.optimization_barrier((x, earlier))

    def along(x, axis, hop):
        count = lax.axis_size(axis)
        return lax.ppermute(x, axis, [(i, (i + hop) % count) for i in range(count)])

    tok = pl.pallas_call(
        pack_tokens_kernel,
        out_shape=shape((share, length), bf16),
        in_specs=[scalars, whole],
        out_specs=whole,
        compiler_params=pltpu.CompilerParams(vmem_limit_bytes=VMEM_LIMIT),
        name="pack_tokens",
    )(where, tokens)
    sizes = [share + EXTRA] + [share // 2 + EXTRA] * (ctx - 1)
    packed = pl.pallas_call(
        functools.partial(pack_kernel, ctx),
        out_shape=[shape((size, HEAD_COLUMNS), bf16) for size in sizes * 2],
        in_specs=[scalars] + [whole] * 6,
        out_specs=[whole] * (2 * ctx),
        compiler_params=pltpu.CompilerParams(vmem_limit_bytes=VMEM_LIMIT),
        name="pack",
    )(where, w_query, w_key, w_value, log_decay, grad_out, beta_logit)

    near = [along(tok, "ctx", d) for d in range(1, ctx)]
    first, near[0] = after(packed[1:ctx], near[0])
    first = [along(x, "ctx", d + 1) for d, x in enumerate(first)]
    tok = jnp.concatenate([tok] + near, axis=0)
    tok_x = along(tok, "fsdp", 1)
    half = share // 2
    swapped = [along(first[0][:half], "groups", 1)]
    (tok_c, tok_xc, first[1], first[2]), swapped[0] = after((tok, tok_x, first[1], first[2]), swapped[0])
    toks = (tok, tok_x, along(tok_c, "head", 1), along(tok_xc, "head", 1))
    all_tokens, own = pl.pallas_call(
        functools.partial(unpack_tokens_kernel, ctx),
        out_shape=[shape((ctx, total, share), bf16), shape((share, total), bf16)],
        in_specs=[scalars] + [whole] * 4,
        out_specs=[whole] * 2,
        compiler_params=pltpu.CompilerParams(vmem_limit_bytes=VMEM_LIMIT),
        name="unpack_tokens",
    )(where, *toks)
    swapped += [along(x[:half], "groups", 1) for x in first[1:]]
    second, first[1:] = after(packed[ctx + 1 :], first[1:])
    second = [along(x, "ctx", d + 1) for d, x in enumerate(second)]

    def products(slot, steps, parts, results):
        column = pl.BlockSpec((share, DK), lambda i, ref: (0, 2 * ref[6 + 4 * slot + steps[0] + i] + slot))
        return pl.pallas_call(
            functools.partial(weight_gradient_kernel, steps, slot == 1),
            grid_spec=pltpu.PrefetchScalarGridSpec(
                num_scalar_prefetch=1,
                grid=(len(steps),),
                in_specs=[whole] * (1 + len(parts)) + [pl.BlockSpec(memory_space=pl.ANY)] * len(results),
                out_specs=[column] * 3,
            ),
            out_shape=[shape((share, columns), f32)] * 3,
            input_output_aliases={2 + len(parts) + i: i for i in range(len(results))},
            compiler_params=pltpu.CompilerParams(vmem_limit_bytes=VMEM_LIMIT),
            name=f"weight_gradient_{slot}_{steps[0]}",
        )(where, own, *parts, *results)

    grads = []
    back = None
    for slot, direct in enumerate((first, second)):
        if slot:
            for d in range(ctx - 1):
                direct[d], back = after(direct[d], back)
            swapped = [along(x[:half], "groups", 1) for x in direct]
        earlier = [] if back is None else [back]
        grad, back = pl.pallas_call(
            functools.partial(head_kernel, ctx, slot),
            out_shape=[
                shape((total, HEAD_COLUMNS), bf16),
                shape((ctx, 2 * CHUNK + TAIL, (slot + 1) * DK), bf16),
            ],
            in_specs=[scalars] + [whole] * (1 + ctx + ctx - 1 + slot),
            out_specs=[whole] * 2,
            scratch_shapes=[
                pltpu.VMEM((depth, HEAD_COLUMNS), bf16),
                pltpu.VMEM((total, HEAD_COLUMNS), f32),
                pltpu.VMEM((total, DK), f32),
                pltpu.VMEM((total, DV), f32),
                pltpu.VMEM((ctx, CHUNK), f32),
                pltpu.VMEM((ctx, CHUNK, DV), bf16),
                pltpu.VMEM((ctx, CHUNK), f32),
                pltpu.VMEM((ctx, CHUNK, DK), bf16),
            ],
            cost_estimate=pl.CostEstimate(flops=FLOPS[slot], transcendentals=0, bytes_accessed=FLOPS[slot] // 1000),
            compiler_params=pltpu.CompilerParams(vmem_limit_bytes=VMEM_LIMIT),
            name=f"head_{slot}",
        )(where, all_tokens, packed[slot * ctx], *direct, *swapped, *earlier)
        if slot == 0:
            hops = [along(grad, "ctx", d) for d in range(1, ctx)]
            grads.append([grad] + hops)
            continue
        grad, grads[0] = after(grad, grads[0])
        two = lax.ppermute(grad, "ctx", [(0, 2), (1, 3), (2, 0), (3, 1)])
        pair = lax.ppermute(grad, "ctx", [(0, 1), (1, 0), (2, 3), (3, 2)])
        results = products(0, (0, 1, 2, 3), grads[0], ())
        (grad, two), (pair, results) = after((grad, two), (pair, results))
        middle = lax.ppermute(grad, "ctx", [(1, 2), (2, 1)])
        far = lax.ppermute(two, "ctx", [(2, 3), (1, 0)])
        results = products(1, (0, 1, 2), [grad, pair, two], results)
        results = products(1, (3,), [middle, far], results)
    back = lax.all_to_all(back, "ctx", 0, 0)

    attn_out, grad_beta, grad_decay = pl.pallas_call(
        unpack_kernel,
        out_shape=[shape((length, columns), bf16), shape((columns // DK, length), f32), shape((length, columns), f32)],
        in_specs=[whole],
        out_specs=[whole] * 3,
        compiler_params=pltpu.CompilerParams(vmem_limit_bytes=VMEM_LIMIT),
        name="unpack",
    )(back)
    return (attn_out, *results, grad_beta, grad_decay)


def prefix_2(x, axis, join, neutral, backward):
    count = lax.axis_size(axis)
    place = lax.axis_index(axis)
    ahead = count - 1 - place if backward else place
    gathered = jax.tree.map(
        lambda a, kind: lax.all_gather(a.astype(kind), axis), x, (jnp.bfloat16, jnp.bfloat16)
    )
    state = jax.tree.map(lambda a, e: jnp.zeros_like(a) + jnp.asarray(e, a.dtype), x, neutral)

    def one(hop, state):
        source = count - 1 - hop if backward else hop
        return join(
            state,
            jax.tree.map(
                lambda a, own: lax.dynamic_index_in_dim(a, source, 0, False).astype(own.dtype),
                gathered,
                x,
            ),
        )

    return lax.fori_loop(0, ahead, one, state)


def normalize(vectors):
    return vectors * lax.rsqrt(jnp.sum(vectors * vectors, axis=-1, keepdims=True) + epsilon)


def heads_first(matrix, heads):
    return matrix.reshape(matrix.shape[0], heads, -1).transpose(1, 0, 2)


def span_step(memory, queries, key_vecs, val_vecs, strength, forgetting_exponent):
    largest_value = lax.Precision.HIGHEST
    length = queries.shape[1]
    cumulate = jnp.cumsum(forgetting_exponent, axis=1)
    growth = jnp.exp(cumulate)
    shrink = jnp.exp(-cumulate)
    key_up = key_vecs * growth
    key_down = key_vecs * shrink
    query_up = queries * growth
    row_ids = lax.broadcasted_iota(jnp.int32, (length, length), 0)
    col_ids = lax.broadcasted_iota(jnp.int32, (length, length), 1)
    strict = (row_ids > col_ids).astype(jnp.float32)
    within = (row_ids >= col_ids).astype(jnp.float32)
    affinity = jnp.einsum("bcd,bsd->bcs", key_up, key_down, precision=largest_value) * strict
    system = jnp.eye(length, dtype=jnp.float32) + strength[:, :, None] * affinity
    target = strength[:, :, None] * (
        val_vecs - jnp.einsum("bcd,bdw->bcw", key_up, memory, precision=largest_value)
    )
    update = lax.linalg.triangular_solve(system, target, left_side=True, lower=True)
    scores = jnp.einsum("bcd,bsd->bcs", query_up, key_down, precision=largest_value) * within
    emitted = jnp.einsum("bcd,bdw->bcw", query_up, memory, precision=largest_value)
    emitted = emitted + jnp.einsum("bcs,bsw->bcw", scores, update, precision=largest_value)
    at_end = growth[:, -1, :]
    renewed = at_end[:, :, None] * memory + jnp.einsum(
        "bsd,bsw->bdw", key_down * at_end[:, None, :], update, precision=largest_value
    )
    return (emitted, renewed)


def scan_spans(memory, queries, key_vecs, val_vecs, strength, forgetting_exponent):
    count = queries.shape[1] // SPAN

    def to_blocks(array):
        shaped = array.reshape((array.shape[0], count, SPAN) + array.shape[2:])
        return jnp.swapaxes(shaped, 0, 1)

    def advance(carried, blocks):
        emitted, renewed = span_step(carried, *blocks)
        return (renewed, emitted)

    blocks = (
        to_blocks(queries),
        to_blocks(key_vecs),
        to_blocks(val_vecs),
        to_blocks(strength),
        to_blocks(forgetting_exponent),
    )
    final, emitted = lax.scan(advance, memory, blocks)
    emitted = jnp.swapaxes(emitted, 0, 1)
    return (emitted.reshape(emitted.shape[0], count * SPAN, emitted.shape[-1]), final)


def compose(earlier, later):
    largest_value = lax.Precision.HIGHEST
    joined = jnp.einsum("hij,hjk->hik", later[0], earlier[0], precision=largest_value)
    shifted = jnp.einsum("hij,hjv->hiv", later[0], earlier[1], precision=largest_value) + later[1]
    return (joined, shifted)


def per_device(tokens, w_query, w_key, w_value, beta_logit, log_decay, grad_out):
    largest_value = lax.Precision.HIGHEST
    length = tokens.shape[0]
    columns = w_query.shape[1]
    heads = columns // DK
    shard_rows = (
        lax.all_gather(w_query, "ctx", axis=0, tiled=True),
        lax.all_gather(w_key, "ctx", axis=0, tiled=True),
        lax.all_gather(w_value, "ctx", axis=0, tiled=True),
    )
    window = tokens
    query_raw, key_raw, value_raw = tuple(
        (jnp.dot(window, weights, preferred_element_type=jnp.float32) for weights in shard_rows)
    )

    def shard_pass(query_in, key_in, value_in, logits, log_gates):
        queries = normalize(heads_first(query_in, heads))
        key_vecs = normalize(heads_first(key_in, heads))
        val_vecs = heads_first(value_in, heads)
        widened = jnp.concatenate([jnp.zeros((heads, length, DK), jnp.float32), val_vecs], axis=2)
        initial = jnp.concatenate(
            [
                jnp.broadcast_to(jnp.eye(DK, dtype=jnp.float32), (heads, DK, DK)),
                jnp.zeros((heads, DK, DV), jnp.float32),
            ],
            axis=2,
        )
        return scan_spans(
            initial,
            queries,
            key_vecs,
            widened,
            jax.nn.sigmoid(logits),
            heads_first(log_gates, heads),
        )

    (mixed, final), pullback = jax.vjp(
        shard_pass, query_raw, key_raw, value_raw, beta_logit, log_decay
    )
    transit = final[:, :, :DK]
    offset = final[:, :, DK:]
    query_carried_over = mixed[:, :, :DK]
    local_output = mixed[:, :, DK:]
    output_cotangent = grad_out.reshape(length, heads, DV).transpose(1, 0, 2).astype(jnp.float32)
    contribution = jnp.einsum(
        "mij,mif->mjf", query_carried_over, output_cotangent, precision=largest_value
    )
    identity = (
        jnp.broadcast_to(jnp.eye(DK, dtype=jnp.float32), (heads, DK, DK)),
        jnp.zeros((heads, DK, DV), jnp.float32),
    )
    prefix = prefix_2((transit, offset), "ctx", compose, identity, False)
    incoming_state = prefix[1]
    suffix = prefix_2((jnp.swapaxes(transit, 1, 2), contribution), "ctx", compose, identity, True)
    adjoint_state = suffix[1]
    complete_output = local_output + jnp.einsum(
        "npg,ngj->npj", query_carried_over, incoming_state, precision=largest_value
    )
    attn_out = complete_output.transpose(1, 0, 2).reshape(length, heads * DV).astype(jnp.bfloat16)
    d_mixed = jnp.concatenate(
        [
            jnp.einsum("efu,egu->efg", output_cotangent, incoming_state, precision=largest_value),
            output_cotangent,
        ],
        axis=2,
    )
    d_final = jnp.concatenate(
        [
            jnp.einsum("pgx,pcx->pgc", adjoint_state, incoming_state, precision=largest_value),
            adjoint_state,
        ],
        axis=2,
    )
    d_query, d_key, d_value, grad_beta, grad_decay = pullback((d_mixed, d_final))
    grad_projected = jnp.concatenate([d_query, d_key, d_value], axis=1).astype(jnp.bfloat16)
    window = tokens
    summed = lax.psum_scatter(
        jnp.einsum("td,tc->dc", window, grad_projected, preferred_element_type=jnp.float32).astype(
            jnp.bfloat16
        ),
        "ctx",
        scatter_dimension=0,
        tiled=True,
    ).astype(jnp.float32)
    return (
        attn_out,
        summed[:, :columns],
        summed[:, columns : 2 * columns],
        summed[:, 2 * columns :],
        grad_beta,
        grad_decay,
    )


def device_program(tokens, w_query, *rest):
    ctx = lax.axis_size("ctx")
    heads = w_query.shape[1] // DK
    split = heads == 2 * ctx and ctx == 4 and tokens.shape[0] == CHUNK and w_query.shape[0] * ctx == tokens.shape[1]
    split = split and lax.axis_size("groups") == lax.axis_size("fsdp") == lax.axis_size("head") == 2
    split = split and w_query.shape[0] % 64 == 0
    return (head_split if split else per_device)(tokens, w_query, *rest)


def solution(mesh):
    return jax.shard_map(
        device_program,
        mesh=mesh,
        in_specs=(
            P(("groups", "ctx"), None),
            P("ctx", ("fsdp", "head")),
            P("ctx", ("fsdp", "head")),
            P("ctx", ("fsdp", "head")),
            P(("fsdp", "head"), ("groups", "ctx")),
            P(("groups", "ctx"), ("fsdp", "head")),
            P(("groups", "ctx"), ("fsdp", "head")),
        ),
        out_specs=(
            P(("groups", "ctx"), ("fsdp", "head")),
            P(("groups", "ctx"), ("fsdp", "head")),
            P(("groups", "ctx"), ("fsdp", "head")),
            P(("groups", "ctx"), ("fsdp", "head")),
            P(("fsdp", "head"), ("groups", "ctx")),
            P(("groups", "ctx"), ("fsdp", "head")),
        ),
        check_vma=False,
    )
```

```python
import functools

import jax
import jax.numpy as jnp
from jax import lax
from jax.experimental import pallas as pl
from jax.experimental.pallas import tpu as pltpu
from jax.sharding import PartitionSpec as P

DK = 128
DV = 128
SPAN = 64
CHUNK = 128
TAIL = 16
EXTRA = 96
VMEM_LIMIT = 20 * 2**20
FLOPS = (12_000_000_000, 12_000_000_000)
HEAD_COLUMNS = 2 * DK + DV

epsilon = 1e-06
HIGHEST = lax.Precision.HIGHEST
NN = (((1,), (0,)), ((), ()))
NT = (((1,), (1,)), ((), ()))
TN = (((0,), (0,)), ((), ()))


def narrow(x):
    return x.astype(jnp.bfloat16)


def dot(a, b, dims, passes):
    if passes == 6:
        return lax.dot_general(a, b, dims, precision=HIGHEST, preferred_element_type=jnp.float32)
    a_high, b_high = narrow(a), narrow(b)
    total = lax.dot_general(a_high, b_high, dims, preferred_element_type=jnp.float32)
    if passes >= 3:
        a_low = narrow(a - a_high.astype(jnp.float32))
        b_low = narrow(b - b_high.astype(jnp.float32))
        total = total + lax.dot_general(a_high, b_low, dims, preferred_element_type=jnp.float32)
        total = total + lax.dot_general(a_low, b_high, dims, preferred_element_type=jnp.float32)
    return total


PASSES = dict(
    decay=1, pairs=3, inverse=3, solve=3, read=1, carry=3, sent=1, scan=1, emit=1, update=1,
    d_update=3, d_value=3, d_pairs=1, d_up=1, d_up_state=1, d_kd=1, d_kend=1, d_decay=3,
)


def run(name, a, b, dims):
    return dot(a, b, dims, PASSES[name])


def recurrence(raw_ref, decay_ref, logit_ref, cot_ref, out_ref, grad_ref, dlogit_ref, ddecay_ref):
    count = raw_ref.shape[0] // CHUNK
    spans = range(count)
    rows = lax.broadcasted_iota(jnp.int32, (CHUNK, CHUNK), 0)
    cols = lax.broadcasted_iota(jnp.int32, (CHUNK, CHUNK), 1)
    within = rows >= cols
    strict = rows > cols
    diagonal = rows == cols
    running = within.astype(jnp.float32)

    q, k, v, rq, rk, up, down, end = [], [], [], [], [], [], [], []
    qu, ku, kd, kend, beta_row, cot = [], [], [], [], [], []
    for n in spans:
        here = slice(n * CHUNK, (n + 1) * CHUNK)
        q_raw = raw_ref[here, 0:DK]
        k_raw = raw_ref[here, DK : 2 * DK]
        v.append(raw_ref[here, 2 * DK : 3 * DK])
        rq.append(lax.rsqrt(jnp.sum(q_raw * q_raw, axis=1, keepdims=True) + epsilon))
        rk.append(lax.rsqrt(jnp.sum(k_raw * k_raw, axis=1, keepdims=True) + epsilon))
        q.append(q_raw * rq[n])
        k.append(k_raw * rk[n])
        summed = run("decay", running, decay_ref[here, :], NN)
        up.append(jnp.exp(summed))
        down.append(jnp.exp(-summed))
        end.append(up[n][CHUNK - 1 : CHUNK, :])
        qu.append(q[n] * up[n])
        ku.append(k[n] * up[n])
        kd.append(k[n] * down[n])
        kend.append(kd[n] * end[n])
        beta_row.append(jax.nn.sigmoid(logit_ref[n : n + 1, :]))
        cot.append(cot_ref[here, :])

    scores, system, inverse = [], [], []
    for n in spans:
        pairs = run("pairs", jnp.concatenate([qu[n], ku[n]], axis=0), kd[n], NT)
        scores.append(jnp.where(within, pairs[:CHUNK], 0.0))
        beta_col = jnp.transpose(jnp.broadcast_to(beta_row[n], (CHUNK, CHUNK)))
        system.append(jnp.where(strict, pairs[CHUNK:] * beta_col, 0.0))
        pair_block = (rows // 2) == (cols // 2)
        inverse.append(diagonal.astype(jnp.float32) - jnp.where(pair_block, system[n], 0.0))
    size = 2
    while size < CHUNK:
        joined = ((rows // (2 * size)) == (cols // (2 * size))) & ((rows // size) != (cols // size))
        halves = [run("inverse", jnp.where(joined, system[n], 0.0), inverse[n], NN) for n in spans]
        inverse = [inverse[n] - run("inverse", inverse[n], halves[n], NN) for n in spans]
        size *= 2

    solve = [inverse[n] * beta_row[n] for n in spans]
    wu = [run("solve", solve[n], jnp.concatenate([ku[n], v[n]], axis=1), NN) for n in spans]
    pwu = [run("read", scores[n], wu[n], NN) for n in spans]
    kwu = [run("carry", kend[n], wu[n], TN) for n in spans]
    query_through = [qu[n] - pwu[n][:, :DK] for n in spans]
    transit = [
        jnp.where(diagonal, jnp.broadcast_to(end[n], (DK, DK)), 0.0) - kwu[n][:, :DK] for n in spans
    ]
    sent = [run("sent", query_through[n], cot[n], TN) for n in spans]

    state = [None] * (count + 1)
    adjoint = [None] * (count + 1)
    for n in spans:
        m = count - 1 - n
        own = kwu[n][:, DK:]
        state[n + 1] = own if n == 0 else run("scan", transit[n], state[n], NN) + own
        adjoint[m] = sent[m] if n == 0 else run("scan", transit[m], adjoint[m + 1], TN) + sent[m]

    for n in spans:
        here = slice(n * CHUNK, (n + 1) * CHUNK)
        w = wu[n][:, :DK]
        update = wu[n][:, DK:]
        emitted = pwu[n][:, DK:]
        d_update = run("d_update", scores[n], cot[n], TN)
        if n > 0:
            emitted = emitted + run("emit", query_through[n], state[n], NN)
            update = update - run("update", w, state[n], NN)
        if n < count - 1:
            d_update = d_update + run("d_update", kend[n], adjoint[n + 1], NN)
        out_ref[n] = emitted.astype(out_ref.dtype)
        d_value = run("d_value", solve[n], d_update, TN)
        both = jnp.concatenate([cot[n], -d_value], axis=0)
        pairs = run("d_pairs", both, update, NT)
        d_pairs = jnp.concatenate(
            [jnp.where(within, pairs[:CHUNK], 0.0), jnp.where(strict, pairs[CHUNK:], 0.0)], axis=0
        )
        d_up = run("d_up", d_pairs, kd[n], NN)
        if n > 0:
            d_up = d_up + run("d_up_state", both, state[n], NT)
        d_qu, d_ku = d_up[:CHUNK], d_up[CHUNK:]
        d_kd = run("d_kd", d_pairs, jnp.concatenate([qu[n], ku[n]], axis=0), TN)
        d_k = d_ku * up[n] + d_kd * down[n]
        d_sum = d_qu * qu[n] + d_ku * ku[n] - d_kd * kd[n]
        d_decay_end = jnp.zeros((1, DK), jnp.float32)
        if n < count - 1:
            d_kend = run("d_kend", update, adjoint[n + 1], NT)
            d_k = d_k + d_kend * (end[n] * down[n])
            ended = d_kend * kend[n]
            d_sum = d_sum - ended
            d_decay_end = jnp.sum(ended, axis=0, keepdims=True)
            if n > 0:
                kept = jnp.sum(jnp.transpose(adjoint[n + 1] * state[n]), axis=0, keepdims=True)
                d_decay_end = d_decay_end + end[n] * kept
        ddecay_ref[n] = (run("d_decay", running, d_sum, TN) + d_decay_end).astype(ddecay_ref.dtype)
        d_q = d_qu * up[n]
        d_q = rq[n] * (d_q - q[n] * jnp.sum(q[n] * d_q, axis=1, keepdims=True))
        d_k = rk[n] * (d_k - k[n] * jnp.sum(k[n] * d_k, axis=1, keepdims=True))
        grad_ref[here, 0:DK] = d_q.astype(grad_ref.dtype)
        grad_ref[here, DK : 2 * DK] = d_k.astype(grad_ref.dtype)
        grad_ref[here, 2 * DK : 3 * DK] = d_value.astype(grad_ref.dtype)
        aligned = jnp.sum(jnp.transpose(d_value * update), axis=0, keepdims=True)
        dlogit_ref[n : n + 1, :] = aligned * jnp.exp(-logit_ref[n : n + 1, :])


def split_two(x):
    high = narrow(x)
    return high, narrow(x - high.astype(jnp.float32))


def tail_rows(x):
    high, low = split_two(x)
    index = lax.broadcasted_iota(jnp.int32, (TAIL, x.shape[1]), 0)
    high = jnp.broadcast_to(high.astype(jnp.float32), index.shape)
    low = jnp.broadcast_to(low.astype(jnp.float32), index.shape)
    return narrow(jnp.where(index == 0, high, jnp.where(index == 1, low, 0.0)))


def lanes(start):
    return pl.ds(pl.multiple_of(start, DK), DK)


def tile_rows(start, size):
    return pl.ds(pl.multiple_of(start, 32), size)


def pack_tokens_kernel(where_ref, tokens_ref, tok_ref):
    share = tok_ref.shape[0]
    for j in range(tokens_ref.shape[1] // share):

        @pl.when(where_ref[2] == j)
        def _(j=j):
            block = tokens_ref[:, j * share : (j + 1) * share]
            full = share // DK
            for g in range(full):
                tok_ref[g * CHUNK : (g + 1) * CHUNK, :] = block[:, g * DK : (g + 1) * DK]
            rest = block[:, full * DK :]
            tok_ref[full * CHUNK :, :] = jnp.concatenate([rest[: CHUNK // 2], rest[CHUNK // 2 :]], axis=1)


def unpack_tokens_kernel(ctx, where_ref, *refs):
    tok_refs, all_ref, own_ref = refs[:4], refs[4], refs[5]
    place = where_ref[0]
    share = own_ref.shape[0]
    full = share // DK
    for j in range(4):
        block = where_ref[2 + j]
        for d in range(ctx):
            source = lax.rem(place + ctx - d, ctx)
            start = source * CHUNK
            base = d * share
            for g in range(full):
                piece = tok_refs[j][base + g * CHUNK : base + (g + 1) * CHUNK, :]
                all_ref[block, tile_rows(start, CHUNK), g * DK : (g + 1) * DK] = piece
            rest = tok_refs[j][base + full * CHUNK : base + share, :]
            all_ref[block, tile_rows(start, CHUNK // 2), full * DK :] = rest[:, : DK // 2]
            all_ref[block, tile_rows(start + CHUNK // 2, CHUNK // 2), full * DK :] = rest[:, DK // 2 :]
    for n in range(ctx):
        piece = all_ref[place, n * CHUNK : (n + 1) * CHUNK, :].astype(jnp.float32)
        own_ref[:, n * CHUNK : (n + 1) * CHUNK] = narrow(jnp.transpose(piece))


def pack_kernel(ctx, where_ref, wq_ref, wk_ref, wv_ref, decay_ref, cot_ref, logit_ref, *out_refs):
    place, group = where_ref[0], where_ref[1]
    half = wq_ref.shape[0] // 2
    for s in range(2):
        for d in range(ctx):
            head = 2 * lax.rem(place + d, ctx) + s
            column = lanes(head * DK)
            out = out_refs[s * ctx + d]
            size = out.shape[0] - EXTRA
            rows = slice(None) if d == 0 else tile_rows(group * half, half)
            for part, ref in enumerate((wq_ref, wk_ref, wv_ref)):
                out[0:size, part * DK : (part + 1) * DK] = ref[rows, column]
            decay = narrow(decay_ref[:, column])
            cot = cot_ref[:, column]
            out[size : size + 96, 0:DK] = decay[0:96]
            out[size : size + 32, DK : 2 * DK] = decay[96:128]
            out[size + 32 : size + 96, DK : 2 * DK] = cot[0:64]
            out[size : size + 64, 2 * DK : 3 * DK] = cot[64:128]
            out[size + 64 : size + 80, 2 * DK : 3 * DK] = tail_rows(logit_ref[pl.ds(head, 1), :])
            out[size + 80 : size + 96, 2 * DK : 3 * DK] = jnp.zeros((16, DK), out.dtype)


def head_kernel(ctx, slot, where_ref, *refs):
    all_ref, refs = refs[0], refs[1:]
    direct, refs = refs[:ctx], refs[ctx:]
    swapped, refs = refs[: ctx - 1], refs[ctx - 1 :]
    if slot:
        earlier_ref, refs = refs[0], refs[1:]
    grad_ref, back_ref, w, raw, decay, cot, logit, out, dlogit, ddecay = refs
    place, group = where_ref[0], where_ref[1]
    share = direct[0].shape[0] - EXTRA
    half = share // 2
    for d in range(ctx):
        source = lax.rem(place + ctx - d, ctx)
        ref = direct[d]
        if d == 0:
            w[tile_rows(source * share, share), :] = ref[0:share, :]
            size = share
        else:
            w[tile_rows(source * share + group * half, half), :] = ref[0:half, :]
            w[tile_rows(source * share + (1 - group) * half, half), :] = swapped[d - 1][0:half, :]
            size = half
        start = source * CHUNK
        decay[tile_rows(start, 96), :] = ref[size : size + 96, 0:DK].astype(jnp.float32)
        decay[tile_rows(start + 96, 32), :] = ref[size : size + 32, DK : 2 * DK].astype(jnp.float32)
        cot[tile_rows(start, 64), :] = ref[size + 32 : size + 96, DK : 2 * DK].astype(jnp.float32)
        cot[tile_rows(start + 64, 64), :] = ref[size : size + 64, 2 * DK : 3 * DK].astype(jnp.float32)
        tail = ref[size + 64 : size + 80, 2 * DK : 3 * DK].astype(jnp.float32)
        logit[pl.ds(source, 1), :] = tail[0:1] + tail[1:2]
    projected = 0.0
    for j in range(ctx):
        projected = projected + lax.dot_general(
            all_ref[j], w[j * share : (j + 1) * share, :], NN, preferred_element_type=jnp.float32
        )
    raw[...] = projected
    recurrence(raw, decay, logit, cot, out, grad_ref, dlogit, ddecay)
    lane = slice(slot * DK, (slot + 1) * DK)
    if slot:
        back_ref[:, :, 0:DK] = earlier_ref[...]
    for n in range(ctx):
        back_ref[n, 0:CHUNK, lane] = out[n]
        back_ref[n, CHUNK : 2 * CHUNK, lane] = ddecay[n]
        back_ref[n, 2 * CHUNK :, lane] = tail_rows(dlogit[n : n + 1, :])


def weight_gradient_kernel(steps, where_ref, own_ref, *refs):
    out_refs = refs[-3:]

    def block(gradient):
        product = lax.dot_general(own_ref[...], gradient, NN, preferred_element_type=jnp.float32)
        for part in range(3):
            out_refs[part][...] = product[:, part * DK : (part + 1) * DK]

    for at, step in enumerate(steps):

        @pl.when(pl.program_id(0) == at)
        def _(at=at, step=step):
            if step < 3:
                block(refs[at][...])
            else:
                block(jnp.where(where_ref[10] == 1, refs[at + 1][...], refs[at][...]))


def unpack_kernel(back_ref, out_ref, dlogit_ref, ddecay_ref):
    for source in range(back_ref.shape[0]):
        column = slice(2 * source * DK, 2 * (source + 1) * DK)
        out_ref[:, column] = back_ref[source, 0:CHUNK, :]
        ddecay_ref[:, column] = back_ref[source, CHUNK : 2 * CHUNK, :].astype(jnp.float32)
        tail = back_ref[source, 2 * CHUNK :, :].astype(jnp.float32)
        row = tail[0:1] + tail[1:2]
        for s in range(2):
            dlogit_ref[2 * source + s : 2 * source + s + 1, :] = row[:, s * DK : (s + 1) * DK]


def head_split(tokens, w_query, w_key, w_value, beta_logit, log_decay, grad_out):
    ctx = lax.axis_size("ctx")
    place = lax.axis_index("ctx")
    group = lax.axis_index("groups")
    across, core = lax.axis_index("fsdp"), lax.axis_index("head")
    length, depth = tokens.shape
    share, columns = w_query.shape
    total = ctx * length
    bf16, f32 = jnp.bfloat16, jnp.float32
    whole = pl.BlockSpec(memory_space=pltpu.VMEM)
    scalars = pl.BlockSpec(memory_space=pltpu.SMEM)
    sources = [place, place + 1 - 2 * (place % 2), (place + 2) % ctx, ctx - 1 - place]
    where = jnp.stack(
        [place, group]
        + [2 * a + c for c in (core, 1 - core) for a in (across, 1 - across)]
        + sources
        + [((place == 0) | (place == ctx - 1)).astype(jnp.int32)]
    ).astype(jnp.int32)

    def shape(dims, kind):
        return jax.ShapeDtypeStruct(dims, kind)

    def after(x, earlier):
        return lax.optimization_barrier((x, earlier))

    def along(x, axis, hop):
        count = lax.axis_size(axis)
        return lax.ppermute(x, axis, [(i, (i + hop) % count) for i in range(count)])

    tok = pl.pallas_call(
        pack_tokens_kernel,
        out_shape=shape((share, length), bf16),
        in_specs=[scalars, whole],
        out_specs=whole,
        compiler_params=pltpu.CompilerParams(vmem_limit_bytes=VMEM_LIMIT),
        name="pack_tokens",
    )(where, tokens)
    sizes = [share + EXTRA] + [share // 2 + EXTRA] * (ctx - 1)
    packed = pl.pallas_call(
        functools.partial(pack_kernel, ctx),
        out_shape=[shape((size, HEAD_COLUMNS), bf16) for size in sizes * 2],
        in_specs=[scalars] + [whole] * 6,
        out_specs=[whole] * (2 * ctx),
        compiler_params=pltpu.CompilerParams(vmem_limit_bytes=VMEM_LIMIT),
        name="pack",
    )(where, w_query, w_key, w_value, log_decay, grad_out, beta_logit)

    near = [along(tok, "ctx", d) for d in range(1, ctx)]
    first, near[0] = after(packed[1:ctx], near[0])
    first = [along(x, "ctx", d + 1) for d, x in enumerate(first)]
    tok = jnp.concatenate([tok] + near, axis=0)
    tok_x = along(tok, "fsdp", 1)
    half = share // 2
    swapped = [along(first[0][:half], "groups", 1)]
    (tok_c, tok_xc, first[1], first[2]), swapped[0] = after((tok, tok_x, first[1], first[2]), swapped[0])
    toks = (tok, tok_x, along(tok_c, "head", 1), along(tok_xc, "head", 1))
    all_tokens, own = pl.pallas_call(
        functools.partial(unpack_tokens_kernel, ctx),
        out_shape=[shape((ctx, total, share), bf16), shape((share, total), bf16)],
        in_specs=[scalars] + [whole] * 4,
        out_specs=[whole] * 2,
        compiler_params=pltpu.CompilerParams(vmem_limit_bytes=VMEM_LIMIT),
        name="unpack_tokens",
    )(where, *toks)
    swapped += [along(x[:half], "groups", 1) for x in first[1:]]
    second, first[1:] = after(packed[ctx + 1 :], first[1:])
    second = [along(x, "ctx", d + 1) for d, x in enumerate(second)]

    def products(slot, steps, parts, results):
        column = pl.BlockSpec((share, DK), lambda i, ref: (0, 2 * ref[6 + steps[0] + i] + slot))
        return pl.pallas_call(
            functools.partial(weight_gradient_kernel, steps),
            grid_spec=pltpu.PrefetchScalarGridSpec(
                num_scalar_prefetch=1,
                grid=(len(steps),),
                in_specs=[whole] * (1 + len(parts)) + [pl.BlockSpec(memory_space=pl.ANY)] * len(results),
                out_specs=[column] * 3,
            ),
            out_shape=[shape((share, columns), f32)] * 3,
            input_output_aliases={2 + len(parts) + i: i for i in range(len(results))},
            compiler_params=pltpu.CompilerParams(vmem_limit_bytes=VMEM_LIMIT),
            name=f"weight_gradient_{slot}_{steps[0]}",
        )(where, own, *parts, *results)

    grads = []
    back = None
    for slot, direct in enumerate((first, second)):
        if slot:
            for d in range(ctx - 1):
                direct[d], back = after(direct[d], back)
            swapped = [along(x[:half], "groups", 1) for x in direct]
        earlier = [] if back is None else [back]
        grad, back = pl.pallas_call(
            functools.partial(head_kernel, ctx, slot),
            out_shape=[
                shape((total, HEAD_COLUMNS), bf16),
                shape((ctx, 2 * CHUNK + TAIL, (slot + 1) * DK), bf16),
            ],
            in_specs=[scalars] + [whole] * (1 + ctx + ctx - 1 + slot),
            out_specs=[whole] * 2,
            scratch_shapes=[
                pltpu.VMEM((depth, HEAD_COLUMNS), bf16),
                pltpu.VMEM((total, HEAD_COLUMNS), f32),
                pltpu.VMEM((total, DK), f32),
                pltpu.VMEM((total, DV), f32),
                pltpu.VMEM((ctx, CHUNK), f32),
                pltpu.VMEM((ctx, CHUNK, DV), bf16),
                pltpu.VMEM((ctx, CHUNK), f32),
                pltpu.VMEM((ctx, CHUNK, DK), bf16),
            ],
            cost_estimate=pl.CostEstimate(flops=FLOPS[slot], transcendentals=0, bytes_accessed=FLOPS[slot] // 1000),
            compiler_params=pltpu.CompilerParams(vmem_limit_bytes=VMEM_LIMIT),
            name=f"head_{slot}",
        )(where, all_tokens, packed[slot * ctx], *direct, *swapped, *earlier)
        if slot:
            grad, grads[0][1:3] = after(grad, grads[0][1:3])
        two = lax.ppermute(grad, "ctx", [(0, 2), (1, 3), (2, 0), (3, 1)])
        pair = lax.ppermute(grad, "ctx", [(0, 1), (1, 0), (2, 3), (3, 2)])
        results = ()
        if slot:
            results = products(0, (0, 1, 2, 3), grads[0], ())
        (grad, two), (pair, results) = after((grad, two), (pair, results))
        middle = lax.ppermute(grad, "ctx", [(1, 2), (2, 1)])
        far = lax.ppermute(two, "ctx", [(2, 3), (1, 0)])
        grads.append([grad, pair, two, middle, far])
    results = products(1, (0, 1, 2), grads[1][:3], results)
    results = products(1, (3,), grads[1][3:], results)
    back = lax.all_to_all(back, "ctx", 0, 0)

    attn_out, grad_beta, grad_decay = pl.pallas_call(
        unpack_kernel,
        out_shape=[shape((length, columns), bf16), shape((columns // DK, length), f32), shape((length, columns), f32)],
        in_specs=[whole],
        out_specs=[whole] * 3,
        compiler_params=pltpu.CompilerParams(vmem_limit_bytes=VMEM_LIMIT),
        name="unpack",
    )(back)
    return (attn_out, *results, grad_beta, grad_decay)


def prefix_2(x, axis, join, neutral, backward):
    count = lax.axis_size(axis)
    place = lax.axis_index(axis)
    ahead = count - 1 - place if backward else place
    gathered = jax.tree.map(
        lambda a, kind: lax.all_gather(a.astype(kind), axis), x, (jnp.bfloat16, jnp.bfloat16)
    )
    state = jax.tree.map(lambda a, e: jnp.zeros_like(a) + jnp.asarray(e, a.dtype), x, neutral)

    def one(hop, state):
        source = count - 1 - hop if backward else hop
        return join(
            state,
            jax.tree.map(
                lambda a, own: lax.dynamic_index_in_dim(a, source, 0, False).astype(own.dtype),
                gathered,
                x,
            ),
        )

    return lax.fori_loop(0, ahead, one, state)


def normalize(vectors):
    return vectors * lax.rsqrt(jnp.sum(vectors * vectors, axis=-1, keepdims=True) + epsilon)


def heads_first(matrix, heads):
    return matrix.reshape(matrix.shape[0], heads, -1).transpose(1, 0, 2)


def span_step(memory, queries, key_vecs, val_vecs, strength, forgetting_exponent):
    largest_value = lax.Precision.HIGHEST
    length = queries.shape[1]
    cumulate = jnp.cumsum(forgetting_exponent, axis=1)
    growth = jnp.exp(cumulate)
    shrink = jnp.exp(-cumulate)
    key_up = key_vecs * growth
    key_down = key_vecs * shrink
    query_up = queries * growth
    row_ids = lax.broadcasted_iota(jnp.int32, (length, length), 0)
    col_ids = lax.broadcasted_iota(jnp.int32, (length, length), 1)
    strict = (row_ids > col_ids).astype(jnp.float32)
    within = (row_ids >= col_ids).astype(jnp.float32)
    affinity = jnp.einsum("bcd,bsd->bcs", key_up, key_down, precision=largest_value) * strict
    system = jnp.eye(length, dtype=jnp.float32) + strength[:, :, None] * affinity
    target = strength[:, :, None] * (
        val_vecs - jnp.einsum("bcd,bdw->bcw", key_up, memory, precision=largest_value)
    )
    update = lax.linalg.triangular_solve(system, target, left_side=True, lower=True)
    scores = jnp.einsum("bcd,bsd->bcs", query_up, key_down, precision=largest_value) * within
    emitted = jnp.einsum("bcd,bdw->bcw", query_up, memory, precision=largest_value)
    emitted = emitted + jnp.einsum("bcs,bsw->bcw", scores, update, precision=largest_value)
    at_end = growth[:, -1, :]
    renewed = at_end[:, :, None] * memory + jnp.einsum(
        "bsd,bsw->bdw", key_down * at_end[:, None, :], update, precision=largest_value
    )
    return (emitted, renewed)


def scan_spans(memory, queries, key_vecs, val_vecs, strength, forgetting_exponent):
    count = queries.shape[1] // SPAN

    def to_blocks(array):
        shaped = array.reshape((array.shape[0], count, SPAN) + array.shape[2:])
        return jnp.swapaxes(shaped, 0, 1)

    def advance(carried, blocks):
        emitted, renewed = span_step(carried, *blocks)
        return (renewed, emitted)

    blocks = (
        to_blocks(queries),
        to_blocks(key_vecs),
        to_blocks(val_vecs),
        to_blocks(strength),
        to_blocks(forgetting_exponent),
    )
    final, emitted = lax.scan(advance, memory, blocks)
    emitted = jnp.swapaxes(emitted, 0, 1)
    return (emitted.reshape(emitted.shape[0], count * SPAN, emitted.shape[-1]), final)


def compose(earlier, later):
    largest_value = lax.Precision.HIGHEST
    joined = jnp.einsum("hij,hjk->hik", later[0], earlier[0], precision=largest_value)
    shifted = jnp.einsum("hij,hjv->hiv", later[0], earlier[1], precision=largest_value) + later[1]
    return (joined, shifted)


def per_device(tokens, w_query, w_key, w_value, beta_logit, log_decay, grad_out):
    largest_value = lax.Precision.HIGHEST
    length = tokens.shape[0]
    columns = w_query.shape[1]
    heads = columns // DK
    shard_rows = (
        lax.all_gather(w_query, "ctx", axis=0, tiled=True),
        lax.all_gather(w_key, "ctx", axis=0, tiled=True),
        lax.all_gather(w_value, "ctx", axis=0, tiled=True),
    )
    window = tokens
    query_raw, key_raw, value_raw = tuple(
        (jnp.dot(window, weights, preferred_element_type=jnp.float32) for weights in shard_rows)
    )

    def shard_pass(query_in, key_in, value_in, logits, log_gates):
        queries = normalize(heads_first(query_in, heads))
        key_vecs = normalize(heads_first(key_in, heads))
        val_vecs = heads_first(value_in, heads)
        widened = jnp.concatenate([jnp.zeros((heads, length, DK), jnp.float32), val_vecs], axis=2)
        initial = jnp.concatenate(
            [
                jnp.broadcast_to(jnp.eye(DK, dtype=jnp.float32), (heads, DK, DK)),
                jnp.zeros((heads, DK, DV), jnp.float32),
            ],
            axis=2,
        )
        return scan_spans(
            initial,
            queries,
            key_vecs,
            widened,
            jax.nn.sigmoid(logits),
            heads_first(log_gates, heads),
        )

    (mixed, final), pullback = jax.vjp(
        shard_pass, query_raw, key_raw, value_raw, beta_logit, log_decay
    )
    transit = final[:, :, :DK]
    offset = final[:, :, DK:]
    query_carried_over = mixed[:, :, :DK]
    local_output = mixed[:, :, DK:]
    output_cotangent = grad_out.reshape(length, heads, DV).transpose(1, 0, 2).astype(jnp.float32)
    contribution = jnp.einsum(
        "mij,mif->mjf", query_carried_over, output_cotangent, precision=largest_value
    )
    identity = (
        jnp.broadcast_to(jnp.eye(DK, dtype=jnp.float32), (heads, DK, DK)),
        jnp.zeros((heads, DK, DV), jnp.float32),
    )
    prefix = prefix_2((transit, offset), "ctx", compose, identity, False)
    incoming_state = prefix[1]
    suffix = prefix_2((jnp.swapaxes(transit, 1, 2), contribution), "ctx", compose, identity, True)
    adjoint_state = suffix[1]
    complete_output = local_output + jnp.einsum(
        "npg,ngj->npj", query_carried_over, incoming_state, precision=largest_value
    )
    attn_out = complete_output.transpose(1, 0, 2).reshape(length, heads * DV).astype(jnp.bfloat16)
    d_mixed = jnp.concatenate(
        [
            jnp.einsum("efu,egu->efg", output_cotangent, incoming_state, precision=largest_value),
            output_cotangent,
        ],
        axis=2,
    )
    d_final = jnp.concatenate(
        [
            jnp.einsum("pgx,pcx->pgc", adjoint_state, incoming_state, precision=largest_value),
            adjoint_state,
        ],
        axis=2,
    )
    d_query, d_key, d_value, grad_beta, grad_decay = pullback((d_mixed, d_final))
    grad_projected = jnp.concatenate([d_query, d_key, d_value], axis=1).astype(jnp.bfloat16)
    window = tokens
    summed = lax.psum_scatter(
        jnp.einsum("td,tc->dc", window, grad_projected, preferred_element_type=jnp.float32).astype(
            jnp.bfloat16
        ),
        "ctx",
        scatter_dimension=0,
        tiled=True,
    ).astype(jnp.float32)
    return (
        attn_out,
        summed[:, :columns],
        summed[:, columns : 2 * columns],
        summed[:, 2 * columns :],
        grad_beta,
        grad_decay,
    )


def device_program(tokens, w_query, *rest):
    ctx = lax.axis_size("ctx")
    heads = w_query.shape[1] // DK
    split = heads == 2 * ctx and ctx == 4 and tokens.shape[0] == CHUNK and w_query.shape[0] * ctx == tokens.shape[1]
    split = split and lax.axis_size("groups") == lax.axis_size("fsdp") == lax.axis_size("head") == 2
    split = split and w_query.shape[0] % 64 == 0
    return (head_split if split else per_device)(tokens, w_query, *rest)


def solution(mesh):
    return jax.shard_map(
        device_program,
        mesh=mesh,
        in_specs=(
            P(("groups", "ctx"), None),
            P("ctx", ("fsdp", "head")),
            P("ctx", ("fsdp", "head")),
            P("ctx", ("fsdp", "head")),
            P(("fsdp", "head"), ("groups", "ctx")),
            P(("groups", "ctx"), ("fsdp", "head")),
            P(("groups", "ctx"), ("fsdp", "head")),
        ),
        out_specs=(
            P(("groups", "ctx"), ("fsdp", "head")),
            P(("groups", "ctx"), ("fsdp", "head")),
            P(("groups", "ctx"), ("fsdp", "head")),
            P(("groups", "ctx"), ("fsdp", "head")),
            P(("fsdp", "head"), ("groups", "ctx")),
            P(("groups", "ctx"), ("fsdp", "head")),
        ),
        check_vma=False,
    )
```

```python
import functools

import jax
import jax.numpy as jnp
from jax import lax
from jax.experimental import pallas as pl
from jax.experimental.pallas import tpu as pltpu
from jax.sharding import PartitionSpec as P

DK = 128
DV = 128
SPAN = 64
CHUNK = 128
TAIL = 16
EXTRA = 96
VMEM_LIMIT = 20 * 2**20
FLOPS = (12_000_000_000, 12_000_000_000)
HEAD_COLUMNS = 2 * DK + DV

epsilon = 1e-06
HIGHEST = lax.Precision.HIGHEST
NN = (((1,), (0,)), ((), ()))
NT = (((1,), (1,)), ((), ()))
TN = (((0,), (0,)), ((), ()))


def narrow(x):
    return x.astype(jnp.bfloat16)


def dot(a, b, dims, passes):
    if passes == 6:
        return lax.dot_general(a, b, dims, precision=HIGHEST, preferred_element_type=jnp.float32)
    a_high, b_high = narrow(a), narrow(b)
    total = lax.dot_general(a_high, b_high, dims, preferred_element_type=jnp.float32)
    if passes >= 3:
        a_low = narrow(a - a_high.astype(jnp.float32))
        b_low = narrow(b - b_high.astype(jnp.float32))
        total = total + lax.dot_general(a_high, b_low, dims, preferred_element_type=jnp.float32)
        total = total + lax.dot_general(a_low, b_high, dims, preferred_element_type=jnp.float32)
    return total


PASSES = dict(
    decay=1, pairs=3, inverse=3, solve=3, read=1, carry=3, sent=1, scan=1, emit=1, update=1,
    d_update=3, d_value=3, d_pairs=1, d_up=1, d_up_state=1, d_kd=1, d_kend=1, d_decay=3,
)


def run(name, a, b, dims):
    return dot(a, b, dims, PASSES[name])


def recurrence(raw_ref, decay_ref, logit_ref, cot_ref, out_ref, grad_ref, dlogit_ref, ddecay_ref):
    count = raw_ref.shape[0] // CHUNK
    spans = range(count)
    rows = lax.broadcasted_iota(jnp.int32, (CHUNK, CHUNK), 0)
    cols = lax.broadcasted_iota(jnp.int32, (CHUNK, CHUNK), 1)
    within = rows >= cols
    strict = rows > cols
    diagonal = rows == cols
    running = within.astype(jnp.float32)

    q, k, v, rq, rk, up, down, end = [], [], [], [], [], [], [], []
    qu, ku, kd, kend, beta_row, cot = [], [], [], [], [], []
    for n in spans:
        here = slice(n * CHUNK, (n + 1) * CHUNK)
        q_raw = raw_ref[here, 0:DK]
        k_raw = raw_ref[here, DK : 2 * DK]
        v.append(raw_ref[here, 2 * DK : 3 * DK])
        rq.append(lax.rsqrt(jnp.sum(q_raw * q_raw, axis=1, keepdims=True) + epsilon))
        rk.append(lax.rsqrt(jnp.sum(k_raw * k_raw, axis=1, keepdims=True) + epsilon))
        q.append(q_raw * rq[n])
        k.append(k_raw * rk[n])
        summed = run("decay", running, decay_ref[here, :], NN)
        up.append(jnp.exp(summed))
        down.append(jnp.exp(-summed))
        end.append(up[n][CHUNK - 1 : CHUNK, :])
        qu.append(q[n] * up[n])
        ku.append(k[n] * up[n])
        kd.append(k[n] * down[n])
        kend.append(kd[n] * end[n])
        beta_row.append(jax.nn.sigmoid(logit_ref[n : n + 1, :]))
        cot.append(cot_ref[here, :])

    scores, system, inverse = [], [], []
    for n in spans:
        pairs = run("pairs", jnp.concatenate([qu[n], ku[n]], axis=0), kd[n], NT)
        scores.append(jnp.where(within, pairs[:CHUNK], 0.0))
        beta_col = jnp.transpose(jnp.broadcast_to(beta_row[n], (CHUNK, CHUNK)))
        system.append(jnp.where(strict, pairs[CHUNK:] * beta_col, 0.0))
        pair_block = (rows // 2) == (cols // 2)
        inverse.append(diagonal.astype(jnp.float32) - jnp.where(pair_block, system[n], 0.0))
    size = 2
    while size < CHUNK:
        joined = ((rows // (2 * size)) == (cols // (2 * size))) & ((rows // size) != (cols // size))
        halves = [run("inverse", jnp.where(joined, system[n], 0.0), inverse[n], NN) for n in spans]
        inverse = [inverse[n] - run("inverse", inverse[n], halves[n], NN) for n in spans]
        size *= 2

    solve = [inverse[n] * beta_row[n] for n in spans]
    wu = [run("solve", solve[n], jnp.concatenate([ku[n], v[n]], axis=1), NN) for n in spans]
    pwu = [run("read", scores[n], wu[n], NN) for n in spans]
    kwu = [run("carry", kend[n], wu[n], TN) for n in spans]
    query_through = [qu[n] - pwu[n][:, :DK] for n in spans]
    transit = [
        jnp.where(diagonal, jnp.broadcast_to(end[n], (DK, DK)), 0.0) - kwu[n][:, :DK] for n in spans
    ]
    sent = [run("sent", query_through[n], cot[n], TN) for n in spans]

    state = [None] * (count + 1)
    adjoint = [None] * (count + 1)
    for n in spans:
        m = count - 1 - n
        own = kwu[n][:, DK:]
        state[n + 1] = own if n == 0 else run("scan", transit[n], state[n], NN) + own
        adjoint[m] = sent[m] if n == 0 else run("scan", transit[m], adjoint[m + 1], TN) + sent[m]

    for n in spans:
        here = slice(n * CHUNK, (n + 1) * CHUNK)
        w = wu[n][:, :DK]
        update = wu[n][:, DK:]
        emitted = pwu[n][:, DK:]
        d_update = run("d_update", scores[n], cot[n], TN)
        if n > 0:
            emitted = emitted + run("emit", query_through[n], state[n], NN)
            update = update - run("update", w, state[n], NN)
        if n < count - 1:
            d_update = d_update + run("d_update", kend[n], adjoint[n + 1], NN)
        out_ref[n] = emitted.astype(out_ref.dtype)
        d_value = run("d_value", solve[n], d_update, TN)
        both = jnp.concatenate([cot[n], -d_value], axis=0)
        pairs = run("d_pairs", both, update, NT)
        d_pairs = jnp.concatenate(
            [jnp.where(within, pairs[:CHUNK], 0.0), jnp.where(strict, pairs[CHUNK:], 0.0)], axis=0
        )
        d_up = run("d_up", d_pairs, kd[n], NN)
        if n > 0:
            d_up = d_up + run("d_up_state", both, state[n], NT)
        d_qu, d_ku = d_up[:CHUNK], d_up[CHUNK:]
        d_kd = run("d_kd", d_pairs, jnp.concatenate([qu[n], ku[n]], axis=0), TN)
        d_k = d_ku * up[n] + d_kd * down[n]
        d_sum = d_qu * qu[n] + d_ku * ku[n] - d_kd * kd[n]
        d_decay_end = jnp.zeros((1, DK), jnp.float32)
        if n < count - 1:
            d_kend = run("d_kend", update, adjoint[n + 1], NT)
            d_k = d_k + d_kend * (end[n] * down[n])
            ended = d_kend * kend[n]
            d_sum = d_sum - ended
            d_decay_end = jnp.sum(ended, axis=0, keepdims=True)
            if n > 0:
                kept = jnp.sum(jnp.transpose(adjoint[n + 1] * state[n]), axis=0, keepdims=True)
                d_decay_end = d_decay_end + end[n] * kept
        ddecay_ref[n] = (run("d_decay", running, d_sum, TN) + d_decay_end).astype(ddecay_ref.dtype)
        d_q = d_qu * up[n]
        d_q = rq[n] * (d_q - q[n] * jnp.sum(q[n] * d_q, axis=1, keepdims=True))
        d_k = rk[n] * (d_k - k[n] * jnp.sum(k[n] * d_k, axis=1, keepdims=True))
        grad_ref[here, 0:DK] = d_q.astype(grad_ref.dtype)
        grad_ref[here, DK : 2 * DK] = d_k.astype(grad_ref.dtype)
        grad_ref[here, 2 * DK : 3 * DK] = d_value.astype(grad_ref.dtype)
        aligned = jnp.sum(jnp.transpose(d_value * update), axis=0, keepdims=True)
        dlogit_ref[n : n + 1, :] = aligned * jnp.exp(-logit_ref[n : n + 1, :])


def split_two(x):
    high = narrow(x)
    return high, narrow(x - high.astype(jnp.float32))


def tail_rows(x):
    high, low = split_two(x)
    index = lax.broadcasted_iota(jnp.int32, (TAIL, x.shape[1]), 0)
    high = jnp.broadcast_to(high.astype(jnp.float32), index.shape)
    low = jnp.broadcast_to(low.astype(jnp.float32), index.shape)
    return narrow(jnp.where(index == 0, high, jnp.where(index == 1, low, 0.0)))


def lanes(start):
    return pl.ds(pl.multiple_of(start, DK), DK)


def tile_rows(start, size):
    return pl.ds(pl.multiple_of(start, 32), size)


def pack_tokens_kernel(where_ref, tokens_ref, tok_ref):
    share = tok_ref.shape[0]
    for j in range(tokens_ref.shape[1] // share):

        @pl.when(where_ref[2] == j)
        def _(j=j):
            block = tokens_ref[:, j * share : (j + 1) * share]
            full = share // DK
            for g in range(full):
                tok_ref[g * CHUNK : (g + 1) * CHUNK, :] = block[:, g * DK : (g + 1) * DK]
            rest = block[:, full * DK :]
            tok_ref[full * CHUNK :, :] = jnp.concatenate([rest[: CHUNK // 2], rest[CHUNK // 2 :]], axis=1)


def unpack_tokens_kernel(ctx, where_ref, *refs):
    tok_refs, all_ref, own_ref = refs[:4], refs[4], refs[5]
    place = where_ref[0]
    share = own_ref.shape[0]
    full = share // DK
    for j in range(4):
        block = where_ref[2 + j]
        for d in range(ctx):
            source = lax.rem(place + ctx - d, ctx)
            start = source * CHUNK
            base = d * share
            for g in range(full):
                piece = tok_refs[j][base + g * CHUNK : base + (g + 1) * CHUNK, :]
                all_ref[block, tile_rows(start, CHUNK), g * DK : (g + 1) * DK] = piece
            rest = tok_refs[j][base + full * CHUNK : base + share, :]
            all_ref[block, tile_rows(start, CHUNK // 2), full * DK :] = rest[:, : DK // 2]
            all_ref[block, tile_rows(start + CHUNK // 2, CHUNK // 2), full * DK :] = rest[:, DK // 2 :]
    for n in range(ctx):
        piece = all_ref[place, n * CHUNK : (n + 1) * CHUNK, :].astype(jnp.float32)
        own_ref[:, n * CHUNK : (n + 1) * CHUNK] = narrow(jnp.transpose(piece))


def pack_kernel(ctx, where_ref, wq_ref, wk_ref, wv_ref, decay_ref, cot_ref, logit_ref, *out_refs):
    place, group = where_ref[0], where_ref[1]
    half = wq_ref.shape[0] // 2
    for s in range(2):
        for d in range(ctx):
            head = 2 * lax.rem(place + d, ctx) + s
            column = lanes(head * DK)
            out = out_refs[s * ctx + d]
            size = out.shape[0] - EXTRA
            rows = slice(None) if d == 0 else tile_rows(group * half, half)
            for part, ref in enumerate((wq_ref, wk_ref, wv_ref)):
                out[0:size, part * DK : (part + 1) * DK] = ref[rows, column]
            decay = narrow(decay_ref[:, column])
            cot = cot_ref[:, column]
            out[size : size + 96, 0:DK] = decay[0:96]
            out[size : size + 32, DK : 2 * DK] = decay[96:128]
            out[size + 32 : size + 96, DK : 2 * DK] = cot[0:64]
            out[size : size + 64, 2 * DK : 3 * DK] = cot[64:128]
            out[size + 64 : size + 80, 2 * DK : 3 * DK] = tail_rows(logit_ref[pl.ds(head, 1), :])
            out[size + 80 : size + 96, 2 * DK : 3 * DK] = jnp.zeros((16, DK), out.dtype)


def head_kernel(ctx, where_ref, *refs):
    all_ref, refs = refs[0], refs[1:]
    direct, refs = refs[:ctx], refs[ctx:]
    swapped, refs = refs[: ctx - 1], refs[ctx - 1 :]
    grad_ref, back_ref, w, raw, decay, cot, logit, out, dlogit, ddecay = refs
    place, group = where_ref[0], where_ref[1]
    share = direct[0].shape[0] - EXTRA
    half = share // 2
    for d in range(ctx):
        source = lax.rem(place + ctx - d, ctx)
        ref = direct[d]
        if d == 0:
            w[tile_rows(source * share, share), :] = ref[0:share, :]
            size = share
        else:
            w[tile_rows(source * share + group * half, half), :] = ref[0:half, :]
            w[tile_rows(source * share + (1 - group) * half, half), :] = swapped[d - 1][0:half, :]
            size = half
        start = source * CHUNK
        decay[tile_rows(start, 96), :] = ref[size : size + 96, 0:DK].astype(jnp.float32)
        decay[tile_rows(start + 96, 32), :] = ref[size : size + 32, DK : 2 * DK].astype(jnp.float32)
        cot[tile_rows(start, 64), :] = ref[size + 32 : size + 96, DK : 2 * DK].astype(jnp.float32)
        cot[tile_rows(start + 64, 64), :] = ref[size : size + 64, 2 * DK : 3 * DK].astype(jnp.float32)
        tail = ref[size + 64 : size + 80, 2 * DK : 3 * DK].astype(jnp.float32)
        logit[pl.ds(source, 1), :] = tail[0:1] + tail[1:2]
    projected = 0.0
    for j in range(ctx):
        projected = projected + lax.dot_general(
            all_ref[j], w[j * share : (j + 1) * share, :], NN, preferred_element_type=jnp.float32
        )
    raw[...] = projected
    recurrence(raw, decay, logit, cot, out, grad_ref, dlogit, ddecay)
    for n in range(ctx):
        back_ref[n, 0:CHUNK, :] = out[n]
        back_ref[n, CHUNK : 2 * CHUNK, :] = ddecay[n]
        back_ref[n, 2 * CHUNK :, :] = tail_rows(dlogit[n : n + 1, :])


def weight_gradient_kernel(steps, where_ref, own_ref, *refs):
    out_refs = refs[-3:]

    def block(gradient):
        product = lax.dot_general(own_ref[...], gradient, NN, preferred_element_type=jnp.float32)
        for part in range(3):
            out_refs[part][...] = product[:, part * DK : (part + 1) * DK]

    for at, step in enumerate(steps):

        @pl.when(pl.program_id(0) == at)
        def _(at=at, step=step):
            if step < 3:
                block(refs[at][...])
            else:
                block(jnp.where(where_ref[10] == 1, refs[at + 1][...], refs[at][...]))


def unpack_kernel(first_ref, second_ref, out_ref, dlogit_ref, ddecay_ref):
    for source in range(first_ref.shape[0]):
        for s, ref in enumerate((first_ref, second_ref)):
            head = 2 * source + s
            column = slice(head * DK, (head + 1) * DK)
            out_ref[:, column] = ref[source, 0:CHUNK, :]
            ddecay_ref[:, column] = ref[source, CHUNK : 2 * CHUNK, :].astype(jnp.float32)
            tail = ref[source, 2 * CHUNK :, :].astype(jnp.float32)
            dlogit_ref[head : head + 1, :] = tail[0:1] + tail[1:2]


def head_split(tokens, w_query, w_key, w_value, beta_logit, log_decay, grad_out):
    ctx = lax.axis_size("ctx")
    place = lax.axis_index("ctx")
    group = lax.axis_index("groups")
    across, core = lax.axis_index("fsdp"), lax.axis_index("head")
    length, depth = tokens.shape
    share, columns = w_query.shape
    total = ctx * length
    bf16, f32 = jnp.bfloat16, jnp.float32
    whole = pl.BlockSpec(memory_space=pltpu.VMEM)
    scalars = pl.BlockSpec(memory_space=pltpu.SMEM)
    sources = [place, place + 1 - 2 * (place % 2), (place + 2) % ctx, ctx - 1 - place]
    where = jnp.stack(
        [place, group]
        + [2 * a + c for c in (core, 1 - core) for a in (across, 1 - across)]
        + sources
        + [((place == 0) | (place == ctx - 1)).astype(jnp.int32)]
    ).astype(jnp.int32)

    def shape(dims, kind):
        return jax.ShapeDtypeStruct(dims, kind)

    def after(x, earlier):
        return lax.optimization_barrier((x, earlier))

    def along(x, axis, hop):
        count = lax.axis_size(axis)
        return lax.ppermute(x, axis, [(i, (i + hop) % count) for i in range(count)])

    tok = pl.pallas_call(
        pack_tokens_kernel,
        out_shape=shape((share, length), bf16),
        in_specs=[scalars, whole],
        out_specs=whole,
        compiler_params=pltpu.CompilerParams(vmem_limit_bytes=VMEM_LIMIT),
        name="pack_tokens",
    )(where, tokens)
    sizes = [share + EXTRA] + [share // 2 + EXTRA] * (ctx - 1)
    packed = pl.pallas_call(
        functools.partial(pack_kernel, ctx),
        out_shape=[shape((size, HEAD_COLUMNS), bf16) for size in sizes * 2],
        in_specs=[scalars] + [whole] * 6,
        out_specs=[whole] * (2 * ctx),
        compiler_params=pltpu.CompilerParams(vmem_limit_bytes=VMEM_LIMIT),
        name="pack",
    )(where, w_query, w_key, w_value, log_decay, grad_out, beta_logit)

    near = [along(tok, "ctx", d) for d in range(1, ctx)]
    first, near[0] = after(packed[1:ctx], near[0])
    first = [along(x, "ctx", d + 1) for d, x in enumerate(first)]
    tok = jnp.concatenate([tok] + near, axis=0)
    tok_x = along(tok, "fsdp", 1)
    half = share // 2
    swapped = [along(first[0][:half], "groups", 1)]
    (tok_c, tok_xc, first[1], first[2]), swapped[0] = after((tok, tok_x, first[1], first[2]), swapped[0])
    toks = (tok, tok_x, along(tok_c, "head", 1), along(tok_xc, "head", 1))
    all_tokens, own = pl.pallas_call(
        functools.partial(unpack_tokens_kernel, ctx),
        out_shape=[shape((ctx, total, share), bf16), shape((share, total), bf16)],
        in_specs=[scalars] + [whole] * 4,
        out_specs=[whole] * 2,
        compiler_params=pltpu.CompilerParams(vmem_limit_bytes=VMEM_LIMIT),
        name="unpack_tokens",
    )(where, *toks)
    swapped += [along(x[:half], "groups", 1) for x in first[1:]]
    second, first[1:] = after(packed[ctx + 1 :], first[1:])
    second = [along(x, "ctx", d + 1) for d, x in enumerate(second)]

    def products(slot, steps, parts, results):
        column = pl.BlockSpec((share, DK), lambda i, ref: (0, 2 * ref[6 + steps[0] + i] + slot))
        return pl.pallas_call(
            functools.partial(weight_gradient_kernel, steps),
            grid_spec=pltpu.PrefetchScalarGridSpec(
                num_scalar_prefetch=1,
                grid=(len(steps),),
                in_specs=[whole] * (1 + len(parts)) + [pl.BlockSpec(memory_space=pl.ANY)] * len(results),
                out_specs=[column] * 3,
            ),
            out_shape=[shape((share, columns), f32)] * 3,
            input_output_aliases={2 + len(parts) + i: i for i in range(len(results))},
            compiler_params=pltpu.CompilerParams(vmem_limit_bytes=VMEM_LIMIT),
            name=f"weight_gradient_{slot}_{steps[0]}",
        )(where, own, *parts, *results)

    grads, backs = [], []
    for slot, direct in enumerate((first, second)):
        if slot:
            swapped = [along(x[:half], "groups", 1) for x in direct]
        grad, back = pl.pallas_call(
            functools.partial(head_kernel, ctx),
            out_shape=[
                shape((total, HEAD_COLUMNS), bf16),
                shape((ctx, 2 * CHUNK + TAIL, DK), bf16),
            ],
            in_specs=[scalars] + [whole] * (1 + ctx + ctx - 1),
            out_specs=[whole] * 2,
            scratch_shapes=[
                pltpu.VMEM((depth, HEAD_COLUMNS), bf16),
                pltpu.VMEM((total, HEAD_COLUMNS), f32),
                pltpu.VMEM((total, DK), f32),
                pltpu.VMEM((total, DV), f32),
                pltpu.VMEM((ctx, CHUNK), f32),
                pltpu.VMEM((ctx, CHUNK, DV), bf16),
                pltpu.VMEM((ctx, CHUNK), f32),
                pltpu.VMEM((ctx, CHUNK, DK), bf16),
            ],
            cost_estimate=pl.CostEstimate(flops=FLOPS[slot], transcendentals=0, bytes_accessed=FLOPS[slot] // 1000),
            compiler_params=pltpu.CompilerParams(vmem_limit_bytes=VMEM_LIMIT),
            name=f"head_{slot}",
        )(where, all_tokens, packed[slot * ctx], *direct, *swapped)
        if not slot:
            second[:], (grad, back) = after(second, (grad, back))
        backs.append(lax.all_to_all(back, "ctx", 0, 0))
        if slot:
            grad, (grads[0][1:3], backs[0]) = after(grad, (grads[0][1:3], backs[0]))
        two = lax.ppermute(grad, "ctx", [(0, 2), (1, 3), (2, 0), (3, 1)])
        pair = lax.ppermute(grad, "ctx", [(0, 1), (1, 0), (2, 3), (3, 2)])
        results = ()
        if slot:
            results = products(0, (0, 1, 2, 3), grads[0], ())
        (grad, two), (pair, results) = after((grad, two), (pair, results))
        middle = lax.ppermute(grad, "ctx", [(1, 2), (2, 1)])
        far = lax.ppermute(two, "ctx", [(2, 3), (1, 0)])
        grads.append([grad, pair, two, middle, far])
    results = products(1, (0, 1, 2), grads[1][:3], results)
    results = products(1, (3,), grads[1][3:], results)

    attn_out, grad_beta, grad_decay = pl.pallas_call(
        unpack_kernel,
        out_shape=[shape((length, columns), bf16), shape((columns // DK, length), f32), shape((length, columns), f32)],
        in_specs=[whole] * 2,
        out_specs=[whole] * 3,
        compiler_params=pltpu.CompilerParams(vmem_limit_bytes=VMEM_LIMIT),
        name="unpack",
    )(*backs)
    return (attn_out, *results, grad_beta, grad_decay)


def prefix_2(x, axis, join, neutral, backward):
    count = lax.axis_size(axis)
    place = lax.axis_index(axis)
    ahead = count - 1 - place if backward else place
    gathered = jax.tree.map(
        lambda a, kind: lax.all_gather(a.astype(kind), axis), x, (jnp.bfloat16, jnp.bfloat16)
    )
    state = jax.tree.map(lambda a, e: jnp.zeros_like(a) + jnp.asarray(e, a.dtype), x, neutral)

    def one(hop, state):
        source = count - 1 - hop if backward else hop
        return join(
            state,
            jax.tree.map(
                lambda a, own: lax.dynamic_index_in_dim(a, source, 0, False).astype(own.dtype),
                gathered,
                x,
            ),
        )

    return lax.fori_loop(0, ahead, one, state)


def normalize(vectors):
    return vectors * lax.rsqrt(jnp.sum(vectors * vectors, axis=-1, keepdims=True) + epsilon)


def heads_first(matrix, heads):
    return matrix.reshape(matrix.shape[0], heads, -1).transpose(1, 0, 2)


def span_step(memory, queries, key_vecs, val_vecs, strength, forgetting_exponent):
    largest_value = lax.Precision.HIGHEST
    length = queries.shape[1]
    cumulate = jnp.cumsum(forgetting_exponent, axis=1)
    growth = jnp.exp(cumulate)
    shrink = jnp.exp(-cumulate)
    key_up = key_vecs * growth
    key_down = key_vecs * shrink
    query_up = queries * growth
    row_ids = lax.broadcasted_iota(jnp.int32, (length, length), 0)
    col_ids = lax.broadcasted_iota(jnp.int32, (length, length), 1)
    strict = (row_ids > col_ids).astype(jnp.float32)
    within = (row_ids >= col_ids).astype(jnp.float32)
    affinity = jnp.einsum("bcd,bsd->bcs", key_up, key_down, precision=largest_value) * strict
    system = jnp.eye(length, dtype=jnp.float32) + strength[:, :, None] * affinity
    target = strength[:, :, None] * (
        val_vecs - jnp.einsum("bcd,bdw->bcw", key_up, memory, precision=largest_value)
    )
    update = lax.linalg.triangular_solve(system, target, left_side=True, lower=True)
    scores = jnp.einsum("bcd,bsd->bcs", query_up, key_down, precision=largest_value) * within
    emitted = jnp.einsum("bcd,bdw->bcw", query_up, memory, precision=largest_value)
    emitted = emitted + jnp.einsum("bcs,bsw->bcw", scores, update, precision=largest_value)
    at_end = growth[:, -1, :]
    renewed = at_end[:, :, None] * memory + jnp.einsum(
        "bsd,bsw->bdw", key_down * at_end[:, None, :], update, precision=largest_value
    )
    return (emitted, renewed)


def scan_spans(memory, queries, key_vecs, val_vecs, strength, forgetting_exponent):
    count = queries.shape[1] // SPAN

    def to_blocks(array):
        shaped = array.reshape((array.shape[0], count, SPAN) + array.shape[2:])
        return jnp.swapaxes(shaped, 0, 1)

    def advance(carried, blocks):
        emitted, renewed = span_step(carried, *blocks)
        return (renewed, emitted)

    blocks = (
        to_blocks(queries),
        to_blocks(key_vecs),
        to_blocks(val_vecs),
        to_blocks(strength),
        to_blocks(forgetting_exponent),
    )
    final, emitted = lax.scan(advance, memory, blocks)
    emitted = jnp.swapaxes(emitted, 0, 1)
    return (emitted.reshape(emitted.shape[0], count * SPAN, emitted.shape[-1]), final)


def compose(earlier, later):
    largest_value = lax.Precision.HIGHEST
    joined = jnp.einsum("hij,hjk->hik", later[0], earlier[0], precision=largest_value)
    shifted = jnp.einsum("hij,hjv->hiv", later[0], earlier[1], precision=largest_value) + later[1]
    return (joined, shifted)


def per_device(tokens, w_query, w_key, w_value, beta_logit, log_decay, grad_out):
    largest_value = lax.Precision.HIGHEST
    length = tokens.shape[0]
    columns = w_query.shape[1]
    heads = columns // DK
    shard_rows = (
        lax.all_gather(w_query, "ctx", axis=0, tiled=True),
        lax.all_gather(w_key, "ctx", axis=0, tiled=True),
        lax.all_gather(w_value, "ctx", axis=0, tiled=True),
    )
    window = tokens
    query_raw, key_raw, value_raw = tuple(
        (jnp.dot(window, weights, preferred_element_type=jnp.float32) for weights in shard_rows)
    )

    def shard_pass(query_in, key_in, value_in, logits, log_gates):
        queries = normalize(heads_first(query_in, heads))
        key_vecs = normalize(heads_first(key_in, heads))
        val_vecs = heads_first(value_in, heads)
        widened = jnp.concatenate([jnp.zeros((heads, length, DK), jnp.float32), val_vecs], axis=2)
        initial = jnp.concatenate(
            [
                jnp.broadcast_to(jnp.eye(DK, dtype=jnp.float32), (heads, DK, DK)),
                jnp.zeros((heads, DK, DV), jnp.float32),
            ],
            axis=2,
        )
        return scan_spans(
            initial,
            queries,
            key_vecs,
            widened,
            jax.nn.sigmoid(logits),
            heads_first(log_gates, heads),
        )

    (mixed, final), pullback = jax.vjp(
        shard_pass, query_raw, key_raw, value_raw, beta_logit, log_decay
    )
    transit = final[:, :, :DK]
    offset = final[:, :, DK:]
    query_carried_over = mixed[:, :, :DK]
    local_output = mixed[:, :, DK:]
    output_cotangent = grad_out.reshape(length, heads, DV).transpose(1, 0, 2).astype(jnp.float32)
    contribution = jnp.einsum(
        "mij,mif->mjf", query_carried_over, output_cotangent, precision=largest_value
    )
    identity = (
        jnp.broadcast_to(jnp.eye(DK, dtype=jnp.float32), (heads, DK, DK)),
        jnp.zeros((heads, DK, DV), jnp.float32),
    )
    prefix = prefix_2((transit, offset), "ctx", compose, identity, False)
    incoming_state = prefix[1]
    suffix = prefix_2((jnp.swapaxes(transit, 1, 2), contribution), "ctx", compose, identity, True)
    adjoint_state = suffix[1]
    complete_output = local_output + jnp.einsum(
        "npg,ngj->npj", query_carried_over, incoming_state, precision=largest_value
    )
    attn_out = complete_output.transpose(1, 0, 2).reshape(length, heads * DV).astype(jnp.bfloat16)
    d_mixed = jnp.concatenate(
        [
            jnp.einsum("efu,egu->efg", output_cotangent, incoming_state, precision=largest_value),
            output_cotangent,
        ],
        axis=2,
    )
    d_final = jnp.concatenate(
        [
            jnp.einsum("pgx,pcx->pgc", adjoint_state, incoming_state, precision=largest_value),
            adjoint_state,
        ],
        axis=2,
    )
    d_query, d_key, d_value, grad_beta, grad_decay = pullback((d_mixed, d_final))
    grad_projected = jnp.concatenate([d_query, d_key, d_value], axis=1).astype(jnp.bfloat16)
    window = tokens
    summed = lax.psum_scatter(
        jnp.einsum("td,tc->dc", window, grad_projected, preferred_element_type=jnp.float32).astype(
            jnp.bfloat16
        ),
        "ctx",
        scatter_dimension=0,
        tiled=True,
    ).astype(jnp.float32)
    return (
        attn_out,
        summed[:, :columns],
        summed[:, columns : 2 * columns],
        summed[:, 2 * columns :],
        grad_beta,
        grad_decay,
    )


def device_program(tokens, w_query, *rest):
    ctx = lax.axis_size("ctx")
    heads = w_query.shape[1] // DK
    split = heads == 2 * ctx and ctx == 4 and tokens.shape[0] == CHUNK and w_query.shape[0] * ctx == tokens.shape[1]
    split = split and lax.axis_size("groups") == lax.axis_size("fsdp") == lax.axis_size("head") == 2
    split = split and w_query.shape[0] % 64 == 0
    return (head_split if split else per_device)(tokens, w_query, *rest)


def solution(mesh):
    return jax.shard_map(
        device_program,
        mesh=mesh,
        in_specs=(
            P(("groups", "ctx"), None),
            P("ctx", ("fsdp", "head")),
            P("ctx", ("fsdp", "head")),
            P("ctx", ("fsdp", "head")),
            P(("fsdp", "head"), ("groups", "ctx")),
            P(("groups", "ctx"), ("fsdp", "head")),
            P(("groups", "ctx"), ("fsdp", "head")),
        ),
        out_specs=(
            P(("groups", "ctx"), ("fsdp", "head")),
            P(("groups", "ctx"), ("fsdp", "head")),
            P(("groups", "ctx"), ("fsdp", "head")),
            P(("groups", "ctx"), ("fsdp", "head")),
            P(("fsdp", "head"), ("groups", "ctx")),
            P(("groups", "ctx"), ("fsdp", "head")),
        ),
        check_vma=False,
    )
```

```python
import functools

import jax
import jax.numpy as jnp
from jax import lax
from jax.experimental import pallas as pl
from jax.experimental.pallas import tpu as pltpu
from jax.sharding import PartitionSpec as P

DK = 128
DV = 128
SPAN = 64
CHUNK = 128
TAIL = 16
EXTRA = 96
VMEM_LIMIT = 20 * 2**20
FLOPS = (12_000_000_000, 12_000_000_000)
HEAD_COLUMNS = 2 * DK + DV

epsilon = 1e-06
HIGHEST = lax.Precision.HIGHEST
NN = (((1,), (0,)), ((), ()))
NT = (((1,), (1,)), ((), ()))
TN = (((0,), (0,)), ((), ()))


def narrow(x):
    return x.astype(jnp.bfloat16)


def dot(a, b, dims, passes):
    if passes == 6:
        return lax.dot_general(a, b, dims, precision=HIGHEST, preferred_element_type=jnp.float32)
    a_high, b_high = narrow(a), narrow(b)
    total = lax.dot_general(a_high, b_high, dims, preferred_element_type=jnp.float32)
    if passes >= 3:
        a_low = narrow(a - a_high.astype(jnp.float32))
        b_low = narrow(b - b_high.astype(jnp.float32))
        total = total + lax.dot_general(a_high, b_low, dims, preferred_element_type=jnp.float32)
        total = total + lax.dot_general(a_low, b_high, dims, preferred_element_type=jnp.float32)
    return total


PASSES = dict(
    decay=1, pairs=3, inverse=3, solve=3, read=1, carry=3, sent=1, scan=1, emit=1, update=1,
    d_update=3, d_value=3, d_pairs=1, d_up=1, d_up_state=1, d_kd=1, d_kend=1, d_decay=3,
)


def run(name, a, b, dims):
    return dot(a, b, dims, PASSES[name])


def recurrence(raw_ref, decay_ref, logit_ref, cot_ref, out_ref, grad_ref, dlogit_ref, ddecay_ref):
    count = raw_ref.shape[0] // CHUNK
    spans = range(count)
    rows = lax.broadcasted_iota(jnp.int32, (CHUNK, CHUNK), 0)
    cols = lax.broadcasted_iota(jnp.int32, (CHUNK, CHUNK), 1)
    within = rows >= cols
    strict = rows > cols
    diagonal = rows == cols
    running = within.astype(jnp.float32)

    q, k, v, rq, rk, up, down, end = [], [], [], [], [], [], [], []
    qu, ku, kd, kend, beta_row, cot = [], [], [], [], [], []
    for n in spans:
        here = slice(n * CHUNK, (n + 1) * CHUNK)
        q_raw = raw_ref[here, 0:DK]
        k_raw = raw_ref[here, DK : 2 * DK]
        v.append(raw_ref[here, 2 * DK : 3 * DK])
        rq.append(lax.rsqrt(jnp.sum(q_raw * q_raw, axis=1, keepdims=True) + epsilon))
        rk.append(lax.rsqrt(jnp.sum(k_raw * k_raw, axis=1, keepdims=True) + epsilon))
        q.append(q_raw * rq[n])
        k.append(k_raw * rk[n])
        summed = run("decay", running, decay_ref[here, :], NN)
        up.append(jnp.exp(summed))
        down.append(jnp.exp(-summed))
        end.append(up[n][CHUNK - 1 : CHUNK, :])
        qu.append(q[n] * up[n])
        ku.append(k[n] * up[n])
        kd.append(k[n] * down[n])
        kend.append(kd[n] * end[n])
        beta_row.append(jax.nn.sigmoid(logit_ref[n : n + 1, :]))
        cot.append(cot_ref[here, :])

    scores, system, inverse = [], [], []
    for n in spans:
        pairs = run("pairs", jnp.concatenate([qu[n], ku[n]], axis=0), kd[n], NT)
        scores.append(jnp.where(within, pairs[:CHUNK], 0.0))
        beta_col = jnp.transpose(jnp.broadcast_to(beta_row[n], (CHUNK, CHUNK)))
        system.append(jnp.where(strict, pairs[CHUNK:] * beta_col, 0.0))
        pair_block = (rows // 2) == (cols // 2)
        inverse.append(diagonal.astype(jnp.float32) - jnp.where(pair_block, system[n], 0.0))
    size = 2
    while size < CHUNK:
        joined = ((rows // (2 * size)) == (cols // (2 * size))) & ((rows // size) != (cols // size))
        halves = [run("inverse", jnp.where(joined, system[n], 0.0), inverse[n], NN) for n in spans]
        inverse = [inverse[n] - run("inverse", inverse[n], halves[n], NN) for n in spans]
        size *= 2

    solve = [inverse[n] * beta_row[n] for n in spans]
    wu = [run("solve", solve[n], jnp.concatenate([ku[n], v[n]], axis=1), NN) for n in spans]
    pwu = [run("read", scores[n], wu[n], NN) for n in spans]
    kwu = [run("carry", kend[n], wu[n], TN) for n in spans]
    query_through = [qu[n] - pwu[n][:, :DK] for n in spans]
    transit = [
        jnp.where(diagonal, jnp.broadcast_to(end[n], (DK, DK)), 0.0) - kwu[n][:, :DK] for n in spans
    ]
    sent = [run("sent", query_through[n], cot[n], TN) for n in spans]

    state = [None] * (count + 1)
    adjoint = [None] * (count + 1)
    for n in spans:
        m = count - 1 - n
        own = kwu[n][:, DK:]
        state[n + 1] = own if n == 0 else run("scan", transit[n], state[n], NN) + own
        adjoint[m] = sent[m] if n == 0 else run("scan", transit[m], adjoint[m + 1], TN) + sent[m]

    for n in spans:
        here = slice(n * CHUNK, (n + 1) * CHUNK)
        w = wu[n][:, :DK]
        update = wu[n][:, DK:]
        emitted = pwu[n][:, DK:]
        d_update = run("d_update", scores[n], cot[n], TN)
        if n > 0:
            emitted = emitted + run("emit", query_through[n], state[n], NN)
            update = update - run("update", w, state[n], NN)
        if n < count - 1:
            d_update = d_update + run("d_update", kend[n], adjoint[n + 1], NN)
        out_ref[n] = emitted.astype(out_ref.dtype)
        d_value = run("d_value", solve[n], d_update, TN)
        both = jnp.concatenate([cot[n], -d_value], axis=0)
        pairs = run("d_pairs", both, update, NT)
        d_pairs = jnp.concatenate(
            [jnp.where(within, pairs[:CHUNK], 0.0), jnp.where(strict, pairs[CHUNK:], 0.0)], axis=0
        )
        d_up = run("d_up", d_pairs, kd[n], NN)
        if n > 0:
            d_up = d_up + run("d_up_state", both, state[n], NT)
        d_qu, d_ku = d_up[:CHUNK], d_up[CHUNK:]
        d_kd = run("d_kd", d_pairs, jnp.concatenate([qu[n], ku[n]], axis=0), TN)
        d_k = d_ku * up[n] + d_kd * down[n]
        d_sum = d_qu * qu[n] + d_ku * ku[n] - d_kd * kd[n]
        d_decay_end = jnp.zeros((1, DK), jnp.float32)
        if n < count - 1:
            d_kend = run("d_kend", update, adjoint[n + 1], NT)
            d_k = d_k + d_kend * (end[n] * down[n])
            ended = d_kend * kend[n]
            d_sum = d_sum - ended
            d_decay_end = jnp.sum(ended, axis=0, keepdims=True)
            if n > 0:
                kept = jnp.sum(jnp.transpose(adjoint[n + 1] * state[n]), axis=0, keepdims=True)
                d_decay_end = d_decay_end + end[n] * kept
        ddecay_ref[n] = (run("d_decay", running, d_sum, TN) + d_decay_end).astype(ddecay_ref.dtype)
        d_q = d_qu * up[n]
        d_q = rq[n] * (d_q - q[n] * jnp.sum(q[n] * d_q, axis=1, keepdims=True))
        d_k = rk[n] * (d_k - k[n] * jnp.sum(k[n] * d_k, axis=1, keepdims=True))
        grad_ref[here, 0:DK] = d_q.astype(grad_ref.dtype)
        grad_ref[here, DK : 2 * DK] = d_k.astype(grad_ref.dtype)
        grad_ref[here, 2 * DK : 3 * DK] = d_value.astype(grad_ref.dtype)
        aligned = jnp.sum(jnp.transpose(d_value * update), axis=0, keepdims=True)
        dlogit_ref[n : n + 1, :] = aligned * jnp.exp(-logit_ref[n : n + 1, :])


def split_two(x):
    high = narrow(x)
    return high, narrow(x - high.astype(jnp.float32))


def tail_rows(x):
    high, low = split_two(x)
    index = lax.broadcasted_iota(jnp.int32, (TAIL, x.shape[1]), 0)
    high = jnp.broadcast_to(high.astype(jnp.float32), index.shape)
    low = jnp.broadcast_to(low.astype(jnp.float32), index.shape)
    return narrow(jnp.where(index == 0, high, jnp.where(index == 1, low, 0.0)))


def lanes(start):
    return pl.ds(pl.multiple_of(start, DK), DK)


def tile_rows(start, size):
    return pl.ds(pl.multiple_of(start, 32), size)


def pack_tokens_kernel(where_ref, tokens_ref, tok_ref):
    share = tok_ref.shape[0]
    for j in range(tokens_ref.shape[1] // share):

        @pl.when(where_ref[2] == j)
        def _(j=j):
            block = tokens_ref[:, j * share : (j + 1) * share]
            full = share // DK
            for g in range(full):
                tok_ref[g * CHUNK : (g + 1) * CHUNK, :] = block[:, g * DK : (g + 1) * DK]
            rest = block[:, full * DK :]
            tok_ref[full * CHUNK :, :] = jnp.concatenate([rest[: CHUNK // 2], rest[CHUNK // 2 :]], axis=1)


def unpack_tokens_kernel(ctx, where_ref, *refs):
    tok_refs, all_ref, own_ref = refs[:4], refs[4], refs[5]
    place = where_ref[0]
    share = own_ref.shape[0]
    full = share // DK
    for j in range(4):
        block = where_ref[2 + j]
        for d in range(ctx):
            source = lax.rem(place + ctx - d, ctx)
            start = source * CHUNK
            base = d * share
            for g in range(full):
                piece = tok_refs[j][base + g * CHUNK : base + (g + 1) * CHUNK, :]
                all_ref[block, tile_rows(start, CHUNK), g * DK : (g + 1) * DK] = piece
            rest = tok_refs[j][base + full * CHUNK : base + share, :]
            all_ref[block, tile_rows(start, CHUNK // 2), full * DK :] = rest[:, : DK // 2]
            all_ref[block, tile_rows(start + CHUNK // 2, CHUNK // 2), full * DK :] = rest[:, DK // 2 :]
    for n in range(ctx):
        piece = all_ref[place, n * CHUNK : (n + 1) * CHUNK, :].astype(jnp.float32)
        own_ref[:, n * CHUNK : (n + 1) * CHUNK] = narrow(jnp.transpose(piece))


def pack_kernel(ctx, where_ref, wq_ref, wk_ref, wv_ref, decay_ref, cot_ref, logit_ref, *out_refs):
    place, group = where_ref[0], where_ref[1]
    half = wq_ref.shape[0] // 2
    for s in range(2):
        for d in range(ctx):
            head = 2 * lax.rem(place + d, ctx) + s
            column = lanes(head * DK)
            out = out_refs[s * ctx + d]
            size = out.shape[0] - EXTRA
            rows = slice(None) if d == 0 else tile_rows(group * half, half)
            for part, ref in enumerate((wq_ref, wk_ref, wv_ref)):
                out[0:size, part * DK : (part + 1) * DK] = ref[rows, column]
            decay = narrow(decay_ref[:, column])
            cot = cot_ref[:, column]
            out[size : size + 96, 0:DK] = decay[0:96]
            out[size : size + 32, DK : 2 * DK] = decay[96:128]
            out[size + 32 : size + 96, DK : 2 * DK] = cot[0:64]
            out[size : size + 64, 2 * DK : 3 * DK] = cot[64:128]
            out[size + 64 : size + 80, 2 * DK : 3 * DK] = tail_rows(logit_ref[pl.ds(head, 1), :])
            out[size + 80 : size + 96, 2 * DK : 3 * DK] = jnp.zeros((16, DK), out.dtype)


def head_kernel(ctx, slot, where_ref, *refs):
    all_ref, refs = refs[0], refs[1:]
    direct, refs = refs[:ctx], refs[ctx:]
    swapped, refs = refs[: ctx - 1], refs[ctx - 1 :]
    grad_ref, *back_refs = refs[:-8]
    w, raw, decay, cot, logit, out, dlogit, ddecay = refs[-8:]
    place, group = where_ref[0], where_ref[1]
    share = direct[0].shape[0] - EXTRA
    half = share // 2
    for d in range(ctx):
        source = lax.rem(place + ctx - d, ctx)
        ref = direct[d]
        if d == 0:
            w[tile_rows(source * share, share), :] = ref[0:share, :]
            size = share
        else:
            w[tile_rows(source * share + group * half, half), :] = ref[0:half, :]
            w[tile_rows(source * share + (1 - group) * half, half), :] = swapped[d - 1][0:half, :]
            size = half
        start = source * CHUNK
        decay[tile_rows(start, 96), :] = ref[size : size + 96, 0:DK].astype(jnp.float32)
        decay[tile_rows(start + 96, 32), :] = ref[size : size + 32, DK : 2 * DK].astype(jnp.float32)
        cot[tile_rows(start, 64), :] = ref[size + 32 : size + 96, DK : 2 * DK].astype(jnp.float32)
        cot[tile_rows(start + 64, 64), :] = ref[size : size + 64, 2 * DK : 3 * DK].astype(jnp.float32)
        tail = ref[size + 64 : size + 80, 2 * DK : 3 * DK].astype(jnp.float32)
        logit[pl.ds(source, 1), :] = tail[0:1] + tail[1:2]
    projected = 0.0
    for j in range(ctx):
        projected = projected + lax.dot_general(
            all_ref[j], w[j * share : (j + 1) * share, :], NN, preferred_element_type=jnp.float32
        )
    raw[...] = projected
    recurrence(raw, decay, logit, cot, out, grad_ref, dlogit, ddecay)
    for d in range(ctx):
        target = d if slot else lax.rem(place + d, ctx)
        back = back_refs[0].at[d] if slot else back_refs[d]
        back[0:CHUNK, :] = out[target]
        back[CHUNK : 2 * CHUNK, :] = ddecay[target]
        back[2 * CHUNK :, :] = tail_rows(dlogit[pl.ds(target, 1), :])


def weight_gradient_kernel(steps, where_ref, own_ref, *refs):
    out_refs = refs[-3:]

    def block(gradient):
        product = lax.dot_general(own_ref[...], gradient, NN, preferred_element_type=jnp.float32)
        for part in range(3):
            out_refs[part][...] = product[:, part * DK : (part + 1) * DK]

    for at, step in enumerate(steps):

        @pl.when(pl.program_id(0) == at)
        def _(at=at, step=step):
            if step < 3:
                block(refs[at][...])
            else:
                block(jnp.where(where_ref[10] == 1, refs[at + 1][...], refs[at][...]))


def unpack_kernel(ctx, where_ref, *refs):
    first_refs, second_ref, (out_ref, dlogit_ref, ddecay_ref) = refs[:ctx], refs[ctx], refs[ctx + 1 :]
    for d in range(ctx):
        source = lax.rem(where_ref[0] + ctx - d, ctx)
        for head, ref in ((2 * source, first_refs[d]), (2 * d + 1, second_ref.at[d])):
            column = lanes(head * DK)
            out_ref[:, column] = ref[0:CHUNK, :]
            ddecay_ref[:, column] = ref[CHUNK : 2 * CHUNK, :].astype(jnp.float32)
            tail = ref[2 * CHUNK :, :].astype(jnp.float32)
            dlogit_ref[pl.ds(head, 1), :] = tail[0:1] + tail[1:2]


def head_split(tokens, w_query, w_key, w_value, beta_logit, log_decay, grad_out):
    ctx = lax.axis_size("ctx")
    place = lax.axis_index("ctx")
    group = lax.axis_index("groups")
    across, core = lax.axis_index("fsdp"), lax.axis_index("head")
    length, depth = tokens.shape
    share, columns = w_query.shape
    total = ctx * length
    bf16, f32 = jnp.bfloat16, jnp.float32
    whole = pl.BlockSpec(memory_space=pltpu.VMEM)
    scalars = pl.BlockSpec(memory_space=pltpu.SMEM)
    sources = [place, place + 1 - 2 * (place % 2), (place + 2) % ctx, ctx - 1 - place]
    where = jnp.stack(
        [place, group]
        + [2 * a + c for c in (core, 1 - core) for a in (across, 1 - across)]
        + sources
        + [((place == 0) | (place == ctx - 1)).astype(jnp.int32)]
    ).astype(jnp.int32)

    def shape(dims, kind):
        return jax.ShapeDtypeStruct(dims, kind)

    def after(x, earlier):
        return lax.optimization_barrier((x, earlier))

    def along(x, axis, hop):
        count = lax.axis_size(axis)
        return lax.ppermute(x, axis, [(i, (i + hop) % count) for i in range(count)])

    tok = pl.pallas_call(
        pack_tokens_kernel,
        out_shape=shape((share, length), bf16),
        in_specs=[scalars, whole],
        out_specs=whole,
        compiler_params=pltpu.CompilerParams(vmem_limit_bytes=VMEM_LIMIT),
        name="pack_tokens",
    )(where, tokens)
    sizes = [share + EXTRA] + [share // 2 + EXTRA] * (ctx - 1)
    packed = pl.pallas_call(
        functools.partial(pack_kernel, ctx),
        out_shape=[shape((size, HEAD_COLUMNS), bf16) for size in sizes * 2],
        in_specs=[scalars] + [whole] * 6,
        out_specs=[whole] * (2 * ctx),
        compiler_params=pltpu.CompilerParams(vmem_limit_bytes=VMEM_LIMIT),
        name="pack",
    )(where, w_query, w_key, w_value, log_decay, grad_out, beta_logit)

    near = [along(tok, "ctx", d) for d in range(1, ctx)]
    first, near[0] = after(packed[1:ctx], near[0])
    first = [along(x, "ctx", d + 1) for d, x in enumerate(first)]
    tok = jnp.concatenate([tok] + near, axis=0)
    tok_x = along(tok, "fsdp", 1)
    half = share // 2
    swapped = [along(first[0][:half], "groups", 1)]
    (tok_c, tok_xc, first[1], first[2]), swapped[0] = after((tok, tok_x, first[1], first[2]), swapped[0])
    toks = (tok, tok_x, along(tok_c, "head", 1), along(tok_xc, "head", 1))
    all_tokens, own = pl.pallas_call(
        functools.partial(unpack_tokens_kernel, ctx),
        out_shape=[shape((ctx, total, share), bf16), shape((share, total), bf16)],
        in_specs=[scalars] + [whole] * 4,
        out_specs=[whole] * 2,
        compiler_params=pltpu.CompilerParams(vmem_limit_bytes=VMEM_LIMIT),
        name="unpack_tokens",
    )(where, *toks)
    swapped += [along(x[:half], "groups", 1) for x in first[1:]]
    second, first[1:] = after(packed[ctx + 1 :], first[1:])
    second = [along(x, "ctx", d + 1) for d, x in enumerate(second)]

    def products(slot, steps, parts, results):
        column = pl.BlockSpec((share, DK), lambda i, ref: (0, 2 * ref[6 + steps[0] + i] + slot))
        return pl.pallas_call(
            functools.partial(weight_gradient_kernel, steps),
            grid_spec=pltpu.PrefetchScalarGridSpec(
                num_scalar_prefetch=1,
                grid=(len(steps),),
                in_specs=[whole] * (1 + len(parts)) + [pl.BlockSpec(memory_space=pl.ANY)] * len(results),
                out_specs=[column] * 3,
            ),
            out_shape=[shape((share, columns), f32)] * 3,
            input_output_aliases={2 + len(parts) + i: i for i in range(len(results))},
            compiler_params=pltpu.CompilerParams(vmem_limit_bytes=VMEM_LIMIT),
            name=f"weight_gradient_{slot}_{steps[0]}",
        )(where, own, *parts, *results)

    grads, backs = [], []
    for slot, direct in enumerate((first, second)):
        if slot:
            swapped = [along(x[:half], "groups", 1) for x in direct]
        side = (2 * CHUNK + TAIL, DK)
        grad, *back = pl.pallas_call(
            functools.partial(head_kernel, ctx, slot),
            out_shape=[shape((total, HEAD_COLUMNS), bf16)]
            + ([shape((ctx,) + side, bf16)] if slot else [shape(side, bf16)] * ctx),
            in_specs=[scalars] + [whole] * (1 + ctx + ctx - 1),
            out_specs=[whole] * (2 if slot else 1 + ctx),
            scratch_shapes=[
                pltpu.VMEM((depth, HEAD_COLUMNS), bf16),
                pltpu.VMEM((total, HEAD_COLUMNS), f32),
                pltpu.VMEM((total, DK), f32),
                pltpu.VMEM((total, DV), f32),
                pltpu.VMEM((ctx, CHUNK), f32),
                pltpu.VMEM((ctx, CHUNK, DV), bf16),
                pltpu.VMEM((ctx, CHUNK), f32),
                pltpu.VMEM((ctx, CHUNK, DK), bf16),
            ],
            cost_estimate=pl.CostEstimate(flops=FLOPS[slot], transcendentals=0, bytes_accessed=FLOPS[slot] // 1000),
            compiler_params=pltpu.CompilerParams(vmem_limit_bytes=VMEM_LIMIT),
            name=f"head_{slot}",
        )(where, all_tokens, packed[slot * ctx], *direct, *swapped)
        if not slot:
            second[:], (grad, back) = after(second, (grad, back))
        if slot:
            backs.append(lax.all_to_all(back[0], "ctx", 0, 0))
        else:
            backs += [back[0]] + [along(back[d], "ctx", d) for d in range(1, ctx)]
        if slot:
            grad, (grads[0][1:3], backs[:ctx]) = after(grad, (grads[0][1:3], backs[:ctx]))
        two = lax.ppermute(grad, "ctx", [(0, 2), (1, 3), (2, 0), (3, 1)])
        pair = lax.ppermute(grad, "ctx", [(0, 1), (1, 0), (2, 3), (3, 2)])
        results = ()
        if slot:
            results = products(0, (0, 1, 2, 3), grads[0], ())
        (grad, two), (pair, results) = after((grad, two), (pair, results))
        middle = lax.ppermute(grad, "ctx", [(1, 2), (2, 1)])
        far = lax.ppermute(two, "ctx", [(2, 3), (1, 0)])
        grads.append([grad, pair, two, middle, far])
    results = products(1, (0, 1, 2), grads[1][:3], results)
    results = products(1, (3,), grads[1][3:], results)

    attn_out, grad_beta, grad_decay = pl.pallas_call(
        functools.partial(unpack_kernel, ctx),
        out_shape=[shape((length, columns), bf16), shape((columns // DK, length), f32), shape((length, columns), f32)],
        in_specs=[scalars] + [whole] * (ctx + 1),
        out_specs=[whole] * 3,
        compiler_params=pltpu.CompilerParams(vmem_limit_bytes=VMEM_LIMIT),
        name="unpack",
    )(where, *backs)
    return (attn_out, *results, grad_beta, grad_decay)


def prefix_2(x, axis, join, neutral, backward):
    count = lax.axis_size(axis)
    place = lax.axis_index(axis)
    ahead = count - 1 - place if backward else place
    gathered = jax.tree.map(
        lambda a, kind: lax.all_gather(a.astype(kind), axis), x, (jnp.bfloat16, jnp.bfloat16)
    )
    state = jax.tree.map(lambda a, e: jnp.zeros_like(a) + jnp.asarray(e, a.dtype), x, neutral)

    def one(hop, state):
        source = count - 1 - hop if backward else hop
        return join(
            state,
            jax.tree.map(
                lambda a, own: lax.dynamic_index_in_dim(a, source, 0, False).astype(own.dtype),
                gathered,
                x,
            ),
        )

    return lax.fori_loop(0, ahead, one, state)


def normalize(vectors):
    return vectors * lax.rsqrt(jnp.sum(vectors * vectors, axis=-1, keepdims=True) + epsilon)


def heads_first(matrix, heads):
    return matrix.reshape(matrix.shape[0], heads, -1).transpose(1, 0, 2)


def span_step(memory, queries, key_vecs, val_vecs, strength, forgetting_exponent):
    largest_value = lax.Precision.HIGHEST
    length = queries.shape[1]
    cumulate = jnp.cumsum(forgetting_exponent, axis=1)
    growth = jnp.exp(cumulate)
    shrink = jnp.exp(-cumulate)
    key_up = key_vecs * growth
    key_down = key_vecs * shrink
    query_up = queries * growth
    row_ids = lax.broadcasted_iota(jnp.int32, (length, length), 0)
    col_ids = lax.broadcasted_iota(jnp.int32, (length, length), 1)
    strict = (row_ids > col_ids).astype(jnp.float32)
    within = (row_ids >= col_ids).astype(jnp.float32)
    affinity = jnp.einsum("bcd,bsd->bcs", key_up, key_down, precision=largest_value) * strict
    system = jnp.eye(length, dtype=jnp.float32) + strength[:, :, None] * affinity
    target = strength[:, :, None] * (
        val_vecs - jnp.einsum("bcd,bdw->bcw", key_up, memory, precision=largest_value)
    )
    update = lax.linalg.triangular_solve(system, target, left_side=True, lower=True)
    scores = jnp.einsum("bcd,bsd->bcs", query_up, key_down, precision=largest_value) * within
    emitted = jnp.einsum("bcd,bdw->bcw", query_up, memory, precision=largest_value)
    emitted = emitted + jnp.einsum("bcs,bsw->bcw", scores, update, precision=largest_value)
    at_end = growth[:, -1, :]
    renewed = at_end[:, :, None] * memory + jnp.einsum(
        "bsd,bsw->bdw", key_down * at_end[:, None, :], update, precision=largest_value
    )
    return (emitted, renewed)


def scan_spans(memory, queries, key_vecs, val_vecs, strength, forgetting_exponent):
    count = queries.shape[1] // SPAN

    def to_blocks(array):
        shaped = array.reshape((array.shape[0], count, SPAN) + array.shape[2:])
        return jnp.swapaxes(shaped, 0, 1)

    def advance(carried, blocks):
        emitted, renewed = span_step(carried, *blocks)
        return (renewed, emitted)

    blocks = (
        to_blocks(queries),
        to_blocks(key_vecs),
        to_blocks(val_vecs),
        to_blocks(strength),
        to_blocks(forgetting_exponent),
    )
    final, emitted = lax.scan(advance, memory, blocks)
    emitted = jnp.swapaxes(emitted, 0, 1)
    return (emitted.reshape(emitted.shape[0], count * SPAN, emitted.shape[-1]), final)


def compose(earlier, later):
    largest_value = lax.Precision.HIGHEST
    joined = jnp.einsum("hij,hjk->hik", later[0], earlier[0], precision=largest_value)
    shifted = jnp.einsum("hij,hjv->hiv", later[0], earlier[1], precision=largest_value) + later[1]
    return (joined, shifted)


def per_device(tokens, w_query, w_key, w_value, beta_logit, log_decay, grad_out):
    largest_value = lax.Precision.HIGHEST
    length = tokens.shape[0]
    columns = w_query.shape[1]
    heads = columns // DK
    shard_rows = (
        lax.all_gather(w_query, "ctx", axis=0, tiled=True),
        lax.all_gather(w_key, "ctx", axis=0, tiled=True),
        lax.all_gather(w_value, "ctx", axis=0, tiled=True),
    )
    window = tokens
    query_raw, key_raw, value_raw = tuple(
        (jnp.dot(window, weights, preferred_element_type=jnp.float32) for weights in shard_rows)
    )

    def shard_pass(query_in, key_in, value_in, logits, log_gates):
        queries = normalize(heads_first(query_in, heads))
        key_vecs = normalize(heads_first(key_in, heads))
        val_vecs = heads_first(value_in, heads)
        widened = jnp.concatenate([jnp.zeros((heads, length, DK), jnp.float32), val_vecs], axis=2)
        initial = jnp.concatenate(
            [
                jnp.broadcast_to(jnp.eye(DK, dtype=jnp.float32), (heads, DK, DK)),
                jnp.zeros((heads, DK, DV), jnp.float32),
            ],
            axis=2,
        )
        return scan_spans(
            initial,
            queries,
            key_vecs,
            widened,
            jax.nn.sigmoid(logits),
            heads_first(log_gates, heads),
        )

    (mixed, final), pullback = jax.vjp(
        shard_pass, query_raw, key_raw, value_raw, beta_logit, log_decay
    )
    transit = final[:, :, :DK]
    offset = final[:, :, DK:]
    query_carried_over = mixed[:, :, :DK]
    local_output = mixed[:, :, DK:]
    output_cotangent = grad_out.reshape(length, heads, DV).transpose(1, 0, 2).astype(jnp.float32)
    contribution = jnp.einsum(
        "mij,mif->mjf", query_carried_over, output_cotangent, precision=largest_value
    )
    identity = (
        jnp.broadcast_to(jnp.eye(DK, dtype=jnp.float32), (heads, DK, DK)),
        jnp.zeros((heads, DK, DV), jnp.float32),
    )
    prefix = prefix_2((transit, offset), "ctx", compose, identity, False)
    incoming_state = prefix[1]
    suffix = prefix_2((jnp.swapaxes(transit, 1, 2), contribution), "ctx", compose, identity, True)
    adjoint_state = suffix[1]
    complete_output = local_output + jnp.einsum(
        "npg,ngj->npj", query_carried_over, incoming_state, precision=largest_value
    )
    attn_out = complete_output.transpose(1, 0, 2).reshape(length, heads * DV).astype(jnp.bfloat16)
    d_mixed = jnp.concatenate(
        [
            jnp.einsum("efu,egu->efg", output_cotangent, incoming_state, precision=largest_value),
            output_cotangent,
        ],
        axis=2,
    )
    d_final = jnp.concatenate(
        [
            jnp.einsum("pgx,pcx->pgc", adjoint_state, incoming_state, precision=largest_value),
            adjoint_state,
        ],
        axis=2,
    )
    d_query, d_key, d_value, grad_beta, grad_decay = pullback((d_mixed, d_final))
    grad_projected = jnp.concatenate([d_query, d_key, d_value], axis=1).astype(jnp.bfloat16)
    window = tokens
    summed = lax.psum_scatter(
        jnp.einsum("td,tc->dc", window, grad_projected, preferred_element_type=jnp.float32).astype(
            jnp.bfloat16
        ),
        "ctx",
        scatter_dimension=0,
        tiled=True,
    ).astype(jnp.float32)
    return (
        attn_out,
        summed[:, :columns],
        summed[:, columns : 2 * columns],
        summed[:, 2 * columns :],
        grad_beta,
        grad_decay,
    )


def device_program(tokens, w_query, *rest):
    ctx = lax.axis_size("ctx")
    heads = w_query.shape[1] // DK
    split = heads == 2 * ctx and ctx == 4 and tokens.shape[0] == CHUNK and w_query.shape[0] * ctx == tokens.shape[1]
    split = split and lax.axis_size("groups") == lax.axis_size("fsdp") == lax.axis_size("head") == 2
    split = split and w_query.shape[0] % 64 == 0
    return (head_split if split else per_device)(tokens, w_query, *rest)


def solution(mesh):
    return jax.shard_map(
        device_program,
        mesh=mesh,
        in_specs=(
            P(("groups", "ctx"), None),
            P("ctx", ("fsdp", "head")),
            P("ctx", ("fsdp", "head")),
            P("ctx", ("fsdp", "head")),
            P(("fsdp", "head"), ("groups", "ctx")),
            P(("groups", "ctx"), ("fsdp", "head")),
            P(("groups", "ctx"), ("fsdp", "head")),
        ),
        out_specs=(
            P(("groups", "ctx"), ("fsdp", "head")),
            P(("groups", "ctx"), ("fsdp", "head")),
            P(("groups", "ctx"), ("fsdp", "head")),
            P(("groups", "ctx"), ("fsdp", "head")),
            P(("fsdp", "head"), ("groups", "ctx")),
            P(("groups", "ctx"), ("fsdp", "head")),
        ),
        check_vma=False,
    )
```

```python
import functools

import jax
import jax.numpy as jnp
from jax import lax
from jax.experimental import pallas as pl
from jax.experimental.pallas import tpu as pltpu
from jax.sharding import PartitionSpec as P

DK = 128
DV = 128
SPAN = 64
CHUNK = 128
TAIL = 16
EXTRA = 96
VMEM_LIMIT = 20 * 2**20
FLOPS = (12_000_000_000, 12_000_000_000)
HEAD_COLUMNS = 2 * DK + DV

epsilon = 1e-06
HIGHEST = lax.Precision.HIGHEST
NN = (((1,), (0,)), ((), ()))
NT = (((1,), (1,)), ((), ()))
TN = (((0,), (0,)), ((), ()))


def narrow(x):
    return x.astype(jnp.bfloat16)


def dot(a, b, dims, passes):
    if passes == 6:
        return lax.dot_general(a, b, dims, precision=HIGHEST, preferred_element_type=jnp.float32)
    a_high, b_high = narrow(a), narrow(b)
    total = lax.dot_general(a_high, b_high, dims, preferred_element_type=jnp.float32)
    if passes >= 3:
        a_low = narrow(a - a_high.astype(jnp.float32))
        b_low = narrow(b - b_high.astype(jnp.float32))
        total = total + lax.dot_general(a_high, b_low, dims, preferred_element_type=jnp.float32)
        total = total + lax.dot_general(a_low, b_high, dims, preferred_element_type=jnp.float32)
    return total


PASSES = dict(
    decay=1, pairs=3, inverse=3, solve=3, read=1, carry=3, sent=1, scan=1, emit=1, update=1,
    d_update=3, d_value=3, d_pairs=1, d_up=1, d_up_state=1, d_kd=1, d_kend=1, d_decay=3,
)


def run(name, a, b, dims):
    return dot(a, b, dims, PASSES[name])


def recurrence(raw_ref, decay_ref, logit_ref, cot_ref, out_ref, grad_ref, dlogit_ref, ddecay_ref):
    count = raw_ref.shape[0] // CHUNK
    spans = range(count)
    rows = lax.broadcasted_iota(jnp.int32, (CHUNK, CHUNK), 0)
    cols = lax.broadcasted_iota(jnp.int32, (CHUNK, CHUNK), 1)
    within = rows >= cols
    strict = rows > cols
    diagonal = rows == cols
    running = within.astype(jnp.float32)

    q, k, v, rq, rk, up, down, end = [], [], [], [], [], [], [], []
    qu, ku, kd, kend, beta_row, cot = [], [], [], [], [], []
    for n in spans:
        here = slice(n * CHUNK, (n + 1) * CHUNK)
        q_raw = raw_ref[here, 0:DK]
        k_raw = raw_ref[here, DK : 2 * DK]
        v.append(raw_ref[here, 2 * DK : 3 * DK])
        rq.append(lax.rsqrt(jnp.sum(q_raw * q_raw, axis=1, keepdims=True) + epsilon))
        rk.append(lax.rsqrt(jnp.sum(k_raw * k_raw, axis=1, keepdims=True) + epsilon))
        q.append(q_raw * rq[n])
        k.append(k_raw * rk[n])
        summed = run("decay", running, decay_ref[here, :], NN)
        up.append(jnp.exp(summed))
        down.append(jnp.exp(-summed))
        end.append(up[n][CHUNK - 1 : CHUNK, :])
        qu.append(q[n] * up[n])
        ku.append(k[n] * up[n])
        kd.append(k[n] * down[n])
        kend.append(kd[n] * end[n])
        beta_row.append(jax.nn.sigmoid(logit_ref[n : n + 1, :]))
        cot.append(cot_ref[here, :])

    scores, system, inverse = [], [], []
    for n in spans:
        pairs = run("pairs", jnp.concatenate([qu[n], ku[n]], axis=0), kd[n], NT)
        scores.append(jnp.where(within, pairs[:CHUNK], 0.0))
        beta_col = jnp.transpose(jnp.broadcast_to(beta_row[n], (CHUNK, CHUNK)))
        system.append(jnp.where(strict, pairs[CHUNK:] * beta_col, 0.0))
        pair_block = (rows // 2) == (cols // 2)
        inverse.append(diagonal.astype(jnp.float32) - jnp.where(pair_block, system[n], 0.0))
    size = 2
    while size < CHUNK:
        joined = ((rows // (2 * size)) == (cols // (2 * size))) & ((rows // size) != (cols // size))
        halves = [run("inverse", jnp.where(joined, system[n], 0.0), inverse[n], NN) for n in spans]
        inverse = [inverse[n] - run("inverse", inverse[n], halves[n], NN) for n in spans]
        size *= 2

    solve = [inverse[n] * beta_row[n] for n in spans]
    wu = [run("solve", solve[n], jnp.concatenate([ku[n], v[n]], axis=1), NN) for n in spans]
    pwu = [run("read", scores[n], wu[n], NN) for n in spans]
    kwu = [run("carry", kend[n], wu[n], TN) for n in spans]
    query_through = [qu[n] - pwu[n][:, :DK] for n in spans]
    transit = [
        jnp.where(diagonal, jnp.broadcast_to(end[n], (DK, DK)), 0.0) - kwu[n][:, :DK] for n in spans
    ]
    sent = [run("sent", query_through[n], cot[n], TN) for n in spans]

    state = [None] * (count + 1)
    adjoint = [None] * (count + 1)
    for n in spans:
        m = count - 1 - n
        own = kwu[n][:, DK:]
        state[n + 1] = own if n == 0 else run("scan", transit[n], state[n], NN) + own
        adjoint[m] = sent[m] if n == 0 else run("scan", transit[m], adjoint[m + 1], TN) + sent[m]

    for n in spans:
        here = slice(n * CHUNK, (n + 1) * CHUNK)
        w = wu[n][:, :DK]
        update = wu[n][:, DK:]
        emitted = pwu[n][:, DK:]
        d_update = run("d_update", scores[n], cot[n], TN)
        if n > 0:
            emitted = emitted + run("emit", query_through[n], state[n], NN)
            update = update - run("update", w, state[n], NN)
        if n < count - 1:
            d_update = d_update + run("d_update", kend[n], adjoint[n + 1], NN)
        out_ref[n] = emitted.astype(out_ref.dtype)
        d_value = run("d_value", solve[n], d_update, TN)
        both = jnp.concatenate([cot[n], -d_value], axis=0)
        pairs = run("d_pairs", both, update, NT)
        d_pairs = jnp.concatenate(
            [jnp.where(within, pairs[:CHUNK], 0.0), jnp.where(strict, pairs[CHUNK:], 0.0)], axis=0
        )
        d_up = run("d_up", d_pairs, kd[n], NN)
        if n > 0:
            d_up = d_up + run("d_up_state", both, state[n], NT)
        d_qu, d_ku = d_up[:CHUNK], d_up[CHUNK:]
        d_kd = run("d_kd", d_pairs, jnp.concatenate([qu[n], ku[n]], axis=0), TN)
        d_k = d_ku * up[n] + d_kd * down[n]
        d_sum = d_qu * qu[n] + d_ku * ku[n] - d_kd * kd[n]
        d_decay_end = jnp.zeros((1, DK), jnp.float32)
        if n < count - 1:
            d_kend = run("d_kend", update, adjoint[n + 1], NT)
            d_k = d_k + d_kend * (end[n] * down[n])
            ended = d_kend * kend[n]
            d_sum = d_sum - ended
            d_decay_end = jnp.sum(ended, axis=0, keepdims=True)
            if n > 0:
                kept = jnp.sum(jnp.transpose(adjoint[n + 1] * state[n]), axis=0, keepdims=True)
                d_decay_end = d_decay_end + end[n] * kept
        ddecay_ref[n] = (run("d_decay", running, d_sum, TN) + d_decay_end).astype(ddecay_ref.dtype)
        d_q = d_qu * up[n]
        d_q = rq[n] * (d_q - q[n] * jnp.sum(q[n] * d_q, axis=1, keepdims=True))
        d_k = rk[n] * (d_k - k[n] * jnp.sum(k[n] * d_k, axis=1, keepdims=True))
        grad_ref[here, 0:DK] = d_q.astype(grad_ref.dtype)
        grad_ref[here, DK : 2 * DK] = d_k.astype(grad_ref.dtype)
        grad_ref[here, 2 * DK : 3 * DK] = d_value.astype(grad_ref.dtype)
        aligned = jnp.sum(jnp.transpose(d_value * update), axis=0, keepdims=True)
        dlogit_ref[n : n + 1, :] = aligned * jnp.exp(-logit_ref[n : n + 1, :])


def split_two(x):
    high = narrow(x)
    return high, narrow(x - high.astype(jnp.float32))


def tail_rows(x):
    high, low = split_two(x)
    index = lax.broadcasted_iota(jnp.int32, (TAIL, x.shape[1]), 0)
    high = jnp.broadcast_to(high.astype(jnp.float32), index.shape)
    low = jnp.broadcast_to(low.astype(jnp.float32), index.shape)
    return narrow(jnp.where(index == 0, high, jnp.where(index == 1, low, 0.0)))


def lanes(start):
    return pl.ds(pl.multiple_of(start, DK), DK)


def tile_rows(start, size):
    return pl.ds(pl.multiple_of(start, 32), size)


def pack_tokens_kernel(where_ref, tokens_ref, tok_ref):
    share = tok_ref.shape[0]
    for j in range(tokens_ref.shape[1] // share):

        @pl.when(where_ref[2] == j)
        def _(j=j):
            block = tokens_ref[:, j * share : (j + 1) * share]
            full = share // DK
            for g in range(full):
                tok_ref[g * CHUNK : (g + 1) * CHUNK, :] = block[:, g * DK : (g + 1) * DK]
            rest = block[:, full * DK :]
            tok_ref[full * CHUNK :, :] = jnp.concatenate([rest[: CHUNK // 2], rest[CHUNK // 2 :]], axis=1)


def unpack_tokens_kernel(ctx, where_ref, *refs):
    tok_refs, all_ref, own_ref = refs[:4], refs[4], refs[5]
    place = where_ref[0]
    share = own_ref.shape[0]
    full = share // DK
    for j in range(4):
        block = where_ref[2 + j]
        for d in range(ctx):
            source = lax.rem(place + ctx - d, ctx)
            start = source * CHUNK
            base = d * share
            for g in range(full):
                piece = tok_refs[j][base + g * CHUNK : base + (g + 1) * CHUNK, :]
                all_ref[block, tile_rows(start, CHUNK), g * DK : (g + 1) * DK] = piece
            rest = tok_refs[j][base + full * CHUNK : base + share, :]
            all_ref[block, tile_rows(start, CHUNK // 2), full * DK :] = rest[:, : DK // 2]
            all_ref[block, tile_rows(start + CHUNK // 2, CHUNK // 2), full * DK :] = rest[:, DK // 2 :]
    for n in range(ctx):
        piece = all_ref[place, n * CHUNK : (n + 1) * CHUNK, :].astype(jnp.float32)
        own_ref[:, n * CHUNK : (n + 1) * CHUNK] = narrow(jnp.transpose(piece))


def pack_kernel(ctx, where_ref, wq_ref, wk_ref, wv_ref, decay_ref, cot_ref, logit_ref, *out_refs):
    place, group = where_ref[0], where_ref[1]
    half = wq_ref.shape[0] // 2
    for s in range(2):
        for d in range(ctx):
            head = 2 * lax.rem(place + d, ctx) + s
            column = lanes(head * DK)
            out = out_refs[s * ctx + d]
            size = out.shape[0] - EXTRA
            rows = slice(None) if d == 0 else tile_rows(group * half, half)
            for part, ref in enumerate((wq_ref, wk_ref, wv_ref)):
                out[0:size, part * DK : (part + 1) * DK] = ref[rows, column]
            decay = narrow(decay_ref[:, column])
            cot = cot_ref[:, column]
            out[size : size + 96, 0:DK] = decay[0:96]
            out[size : size + 32, DK : 2 * DK] = decay[96:128]
            out[size + 32 : size + 96, DK : 2 * DK] = cot[0:64]
            out[size : size + 64, 2 * DK : 3 * DK] = cot[64:128]
            out[size + 64 : size + 80, 2 * DK : 3 * DK] = tail_rows(logit_ref[pl.ds(head, 1), :])
            out[size + 80 : size + 96, 2 * DK : 3 * DK] = jnp.zeros((16, DK), out.dtype)


def head_kernel(ctx, slot, where_ref, *refs):
    all_ref, refs = refs[0], refs[1:]
    direct, refs = refs[:ctx], refs[ctx:]
    swapped, refs = refs[: ctx - 1], refs[ctx - 1 :]
    grad_ref, *back_refs = refs[:-8]
    w, raw, decay, cot, logit, out, dlogit, ddecay = refs[-8:]
    place, group = where_ref[0], where_ref[1]
    share = direct[0].shape[0] - EXTRA
    half = share // 2
    for d in range(ctx):
        source = lax.rem(place + ctx - d, ctx)
        ref = direct[d]
        if d == 0:
            w[tile_rows(source * share, share), :] = ref[0:share, :]
            size = share
        else:
            w[tile_rows(source * share + group * half, half), :] = ref[0:half, :]
            w[tile_rows(source * share + (1 - group) * half, half), :] = swapped[d - 1][0:half, :]
            size = half
        start = source * CHUNK
        decay[tile_rows(start, 96), :] = ref[size : size + 96, 0:DK].astype(jnp.float32)
        decay[tile_rows(start + 96, 32), :] = ref[size : size + 32, DK : 2 * DK].astype(jnp.float32)
        cot[tile_rows(start, 64), :] = ref[size + 32 : size + 96, DK : 2 * DK].astype(jnp.float32)
        cot[tile_rows(start + 64, 64), :] = ref[size : size + 64, 2 * DK : 3 * DK].astype(jnp.float32)
        tail = ref[size + 64 : size + 80, 2 * DK : 3 * DK].astype(jnp.float32)
        logit[pl.ds(source, 1), :] = tail[0:1] + tail[1:2]
    projected = 0.0
    for j in range(ctx):
        projected = projected + lax.dot_general(
            all_ref[j], w[j * share : (j + 1) * share, :], NN, preferred_element_type=jnp.float32
        )
    raw[...] = projected
    recurrence(raw, decay, logit, cot, out, grad_ref, dlogit, ddecay)
    for d in range(ctx):
        target = d if slot else lax.rem(place + d, ctx)
        back = back_refs[0].at[d] if slot else back_refs[d]
        back[0:CHUNK, :] = out[target]
        back[CHUNK : 2 * CHUNK, :] = ddecay[target]
        back[2 * CHUNK :, :] = tail_rows(dlogit[pl.ds(target, 1), :])


def weight_gradient_kernel(steps, where_ref, own_ref, *refs):
    out_refs = refs[-3:]

    def block(gradient):
        product = lax.dot_general(own_ref[...], gradient, NN, preferred_element_type=jnp.float32)
        for part in range(3):
            out_refs[part][...] = product[:, part * DK : (part + 1) * DK]

    for at, step in enumerate(steps):

        @pl.when(pl.program_id(0) == at)
        def _(at=at, step=step):
            if step < 3:
                block(refs[at][...])
            else:
                block(jnp.where(where_ref[10] == 1, refs[at + 1][...], refs[at][...]))


def unpack_kernel(ctx, where_ref, *refs):
    first_refs, second_ref, (out_ref, dlogit_ref, ddecay_ref) = refs[:ctx], refs[ctx], refs[ctx + 1 :]
    for d in range(ctx):
        source = lax.rem(where_ref[0] + ctx - d, ctx)
        for head, ref in ((2 * source, first_refs[d]), (2 * d + 1, second_ref.at[d])):
            column = lanes(head * DK)
            out_ref[:, column] = ref[0:CHUNK, :]
            ddecay_ref[:, column] = ref[CHUNK : 2 * CHUNK, :].astype(jnp.float32)
            tail = ref[2 * CHUNK :, :].astype(jnp.float32)
            dlogit_ref[pl.ds(head, 1), :] = tail[0:1] + tail[1:2]


def head_split(tokens, w_query, w_key, w_value, beta_logit, log_decay, grad_out):
    ctx = lax.axis_size("ctx")
    place = lax.axis_index("ctx")
    group = lax.axis_index("groups")
    across, core = lax.axis_index("fsdp"), lax.axis_index("head")
    length, depth = tokens.shape
    share, columns = w_query.shape
    total = ctx * length
    bf16, f32 = jnp.bfloat16, jnp.float32
    whole = pl.BlockSpec(memory_space=pltpu.VMEM)
    scalars = pl.BlockSpec(memory_space=pltpu.SMEM)
    sources = [place, place + 1 - 2 * (place % 2), (place + 2) % ctx, ctx - 1 - place]
    where = jnp.stack(
        [place, group]
        + [2 * a + c for c in (core, 1 - core) for a in (across, 1 - across)]
        + sources
        + [((place == 0) | (place == ctx - 1)).astype(jnp.int32)]
    ).astype(jnp.int32)

    def shape(dims, kind):
        return jax.ShapeDtypeStruct(dims, kind)

    def after(x, earlier):
        return lax.optimization_barrier((x, earlier))

    def along(x, axis, hop):
        count = lax.axis_size(axis)
        return lax.ppermute(x, axis, [(i, (i + hop) % count) for i in range(count)])

    tok = pl.pallas_call(
        pack_tokens_kernel,
        out_shape=shape((share, length), bf16),
        in_specs=[scalars, whole],
        out_specs=whole,
        compiler_params=pltpu.CompilerParams(vmem_limit_bytes=VMEM_LIMIT),
        name="pack_tokens",
    )(where, tokens)
    sizes = [share + EXTRA] + [share // 2 + EXTRA] * (ctx - 1)
    packed = pl.pallas_call(
        functools.partial(pack_kernel, ctx),
        out_shape=[shape((size, HEAD_COLUMNS), bf16) for size in sizes * 2],
        in_specs=[scalars] + [whole] * 6,
        out_specs=[whole] * (2 * ctx),
        compiler_params=pltpu.CompilerParams(vmem_limit_bytes=VMEM_LIMIT),
        name="pack",
    )(where, w_query, w_key, w_value, log_decay, grad_out, beta_logit)

    near = [along(tok, "ctx", d) for d in range(1, ctx)]
    first, near[0] = after(packed[1:ctx], near[0])
    first = [along(x, "ctx", d + 1) for d, x in enumerate(first)]
    tok = jnp.concatenate([tok] + near, axis=0)
    tok_x = along(tok, "fsdp", 1)
    half = share // 2
    swapped = [along(first[0][:half], "groups", 1)]
    (tok_c, tok_xc, first[1], first[2]), swapped[0] = after((tok, tok_x, first[1], first[2]), swapped[0])
    toks = (tok, tok_x, along(tok_c, "head", 1), along(tok_xc, "head", 1))
    all_tokens, own = pl.pallas_call(
        functools.partial(unpack_tokens_kernel, ctx),
        out_shape=[shape((ctx, total, share), bf16), shape((share, total), bf16)],
        in_specs=[scalars] + [whole] * 4,
        out_specs=[whole] * 2,
        compiler_params=pltpu.CompilerParams(vmem_limit_bytes=VMEM_LIMIT),
        name="unpack_tokens",
    )(where, *toks)
    swapped += [along(x[:half], "groups", 1) for x in first[1:]]
    second, first[1:] = after(packed[ctx + 1 :], first[1:])
    second = [along(x, "ctx", d + 1) for d, x in enumerate(second)]

    def products(slot, steps, parts, results):
        column = pl.BlockSpec((share, DK), lambda i, ref: (0, 2 * ref[6 + steps[0] + i] + slot))
        return pl.pallas_call(
            functools.partial(weight_gradient_kernel, steps),
            grid_spec=pltpu.PrefetchScalarGridSpec(
                num_scalar_prefetch=1,
                grid=(len(steps),),
                in_specs=[whole] * (1 + len(parts)) + [pl.BlockSpec(memory_space=pl.ANY)] * len(results),
                out_specs=[column] * 3,
            ),
            out_shape=[shape((share, columns), f32)] * 3,
            input_output_aliases={2 + len(parts) + i: i for i in range(len(results))},
            compiler_params=pltpu.CompilerParams(vmem_limit_bytes=VMEM_LIMIT),
            name=f"weight_gradient_{slot}_{steps[0]}",
        )(where, own, *parts, *results)

    grads, backs = [], []
    for slot, direct in enumerate((first, second)):
        if slot:
            swapped = [early] + [along(x[:half], "groups", 1) for x in direct[1:]]
        side = (2 * CHUNK + TAIL, DK)
        grad, *back = pl.pallas_call(
            functools.partial(head_kernel, ctx, slot),
            out_shape=[shape((total, HEAD_COLUMNS), bf16)]
            + ([shape((ctx,) + side, bf16)] if slot else [shape(side, bf16)] * ctx),
            in_specs=[scalars] + [whole] * (1 + ctx + ctx - 1),
            out_specs=[whole] * (2 if slot else 1 + ctx),
            scratch_shapes=[
                pltpu.VMEM((depth, HEAD_COLUMNS), bf16),
                pltpu.VMEM((total, HEAD_COLUMNS), f32),
                pltpu.VMEM((total, DK), f32),
                pltpu.VMEM((total, DV), f32),
                pltpu.VMEM((ctx, CHUNK), f32),
                pltpu.VMEM((ctx, CHUNK, DV), bf16),
                pltpu.VMEM((ctx, CHUNK), f32),
                pltpu.VMEM((ctx, CHUNK, DK), bf16),
            ],
            cost_estimate=pl.CostEstimate(flops=FLOPS[slot], transcendentals=0, bytes_accessed=FLOPS[slot] // 1000),
            compiler_params=pltpu.CompilerParams(vmem_limit_bytes=VMEM_LIMIT),
            name=f"head_{slot}",
        )(where, all_tokens, packed[slot * ctx], *direct, *swapped)
        if not slot:
            second[0], grad = after(second[0], grad)
            early = along(second[0][:half], "groups", 1)
            (second[1:], grad, back), early = after((second[1:], grad, back), early)
        if slot:
            backs.append(lax.all_to_all(back[0], "ctx", 0, 0))
        else:
            backs += [back[0]] + [along(back[d], "ctx", d) for d in range(1, ctx)]
        if slot:
            grad, (grads[0][1:3], backs[:ctx]) = after(grad, (grads[0][1:3], backs[:ctx]))
        two = lax.ppermute(grad, "ctx", [(0, 2), (1, 3), (2, 0), (3, 1)])
        pair = lax.ppermute(grad, "ctx", [(0, 1), (1, 0), (2, 3), (3, 2)])
        results = ()
        if slot:
            results = products(0, (0, 1, 2, 3), grads[0], ())
        (grad, two), (pair, results) = after((grad, two), (pair, results))
        middle = lax.ppermute(grad, "ctx", [(1, 2), (2, 1)])
        far = lax.ppermute(two, "ctx", [(2, 3), (1, 0)])
        grads.append([grad, pair, two, middle, far])
    results = products(1, (0, 1, 2), grads[1][:3], results)
    results = products(1, (3,), grads[1][3:], results)

    attn_out, grad_beta, grad_decay = pl.pallas_call(
        functools.partial(unpack_kernel, ctx),
        out_shape=[shape((length, columns), bf16), shape((columns // DK, length), f32), shape((length, columns), f32)],
        in_specs=[scalars] + [whole] * (ctx + 1),
        out_specs=[whole] * 3,
        compiler_params=pltpu.CompilerParams(vmem_limit_bytes=VMEM_LIMIT),
        name="unpack",
    )(where, *backs)
    return (attn_out, *results, grad_beta, grad_decay)


def prefix_2(x, axis, join, neutral, backward):
    count = lax.axis_size(axis)
    place = lax.axis_index(axis)
    ahead = count - 1 - place if backward else place
    gathered = jax.tree.map(
        lambda a, kind: lax.all_gather(a.astype(kind), axis), x, (jnp.bfloat16, jnp.bfloat16)
    )
    state = jax.tree.map(lambda a, e: jnp.zeros_like(a) + jnp.asarray(e, a.dtype), x, neutral)

    def one(hop, state):
        source = count - 1 - hop if backward else hop
        return join(
            state,
            jax.tree.map(
                lambda a, own: lax.dynamic_index_in_dim(a, source, 0, False).astype(own.dtype),
                gathered,
                x,
            ),
        )

    return lax.fori_loop(0, ahead, one, state)


def normalize(vectors):
    return vectors * lax.rsqrt(jnp.sum(vectors * vectors, axis=-1, keepdims=True) + epsilon)


def heads_first(matrix, heads):
    return matrix.reshape(matrix.shape[0], heads, -1).transpose(1, 0, 2)


def span_step(memory, queries, key_vecs, val_vecs, strength, forgetting_exponent):
    largest_value = lax.Precision.HIGHEST
    length = queries.shape[1]
    cumulate = jnp.cumsum(forgetting_exponent, axis=1)
    growth = jnp.exp(cumulate)
    shrink = jnp.exp(-cumulate)
    key_up = key_vecs * growth
    key_down = key_vecs * shrink
    query_up = queries * growth
    row_ids = lax.broadcasted_iota(jnp.int32, (length, length), 0)
    col_ids = lax.broadcasted_iota(jnp.int32, (length, length), 1)
    strict = (row_ids > col_ids).astype(jnp.float32)
    within = (row_ids >= col_ids).astype(jnp.float32)
    affinity = jnp.einsum("bcd,bsd->bcs", key_up, key_down, precision=largest_value) * strict
    system = jnp.eye(length, dtype=jnp.float32) + strength[:, :, None] * affinity
    target = strength[:, :, None] * (
        val_vecs - jnp.einsum("bcd,bdw->bcw", key_up, memory, precision=largest_value)
    )
    update = lax.linalg.triangular_solve(system, target, left_side=True, lower=True)
    scores = jnp.einsum("bcd,bsd->bcs", query_up, key_down, precision=largest_value) * within
    emitted = jnp.einsum("bcd,bdw->bcw", query_up, memory, precision=largest_value)
    emitted = emitted + jnp.einsum("bcs,bsw->bcw", scores, update, precision=largest_value)
    at_end = growth[:, -1, :]
    renewed = at_end[:, :, None] * memory + jnp.einsum(
        "bsd,bsw->bdw", key_down * at_end[:, None, :], update, precision=largest_value
    )
    return (emitted, renewed)


def scan_spans(memory, queries, key_vecs, val_vecs, strength, forgetting_exponent):
    count = queries.shape[1] // SPAN

    def to_blocks(array):
        shaped = array.reshape((array.shape[0], count, SPAN) + array.shape[2:])
        return jnp.swapaxes(shaped, 0, 1)

    def advance(carried, blocks):
        emitted, renewed = span_step(carried, *blocks)
        return (renewed, emitted)

    blocks = (
        to_blocks(queries),
        to_blocks(key_vecs),
        to_blocks(val_vecs),
        to_blocks(strength),
        to_blocks(forgetting_exponent),
    )
    final, emitted = lax.scan(advance, memory, blocks)
    emitted = jnp.swapaxes(emitted, 0, 1)
    return (emitted.reshape(emitted.shape[0], count * SPAN, emitted.shape[-1]), final)


def compose(earlier, later):
    largest_value = lax.Precision.HIGHEST
    joined = jnp.einsum("hij,hjk->hik", later[0], earlier[0], precision=largest_value)
    shifted = jnp.einsum("hij,hjv->hiv", later[0], earlier[1], precision=largest_value) + later[1]
    return (joined, shifted)


def per_device(tokens, w_query, w_key, w_value, beta_logit, log_decay, grad_out):
    largest_value = lax.Precision.HIGHEST
    length = tokens.shape[0]
    columns = w_query.shape[1]
    heads = columns // DK
    shard_rows = (
        lax.all_gather(w_query, "ctx", axis=0, tiled=True),
        lax.all_gather(w_key, "ctx", axis=0, tiled=True),
        lax.all_gather(w_value, "ctx", axis=0, tiled=True),
    )
    window = tokens
    query_raw, key_raw, value_raw = tuple(
        (jnp.dot(window, weights, preferred_element_type=jnp.float32) for weights in shard_rows)
    )

    def shard_pass(query_in, key_in, value_in, logits, log_gates):
        queries = normalize(heads_first(query_in, heads))
        key_vecs = normalize(heads_first(key_in, heads))
        val_vecs = heads_first(value_in, heads)
        widened = jnp.concatenate([jnp.zeros((heads, length, DK), jnp.float32), val_vecs], axis=2)
        initial = jnp.concatenate(
            [
                jnp.broadcast_to(jnp.eye(DK, dtype=jnp.float32), (heads, DK, DK)),
                jnp.zeros((heads, DK, DV), jnp.float32),
            ],
            axis=2,
        )
        return scan_spans(
            initial,
            queries,
            key_vecs,
            widened,
            jax.nn.sigmoid(logits),
            heads_first(log_gates, heads),
        )

    (mixed, final), pullback = jax.vjp(
        shard_pass, query_raw, key_raw, value_raw, beta_logit, log_decay
    )
    transit = final[:, :, :DK]
    offset = final[:, :, DK:]
    query_carried_over = mixed[:, :, :DK]
    local_output = mixed[:, :, DK:]
    output_cotangent = grad_out.reshape(length, heads, DV).transpose(1, 0, 2).astype(jnp.float32)
    contribution = jnp.einsum(
        "mij,mif->mjf", query_carried_over, output_cotangent, precision=largest_value
    )
    identity = (
        jnp.broadcast_to(jnp.eye(DK, dtype=jnp.float32), (heads, DK, DK)),
        jnp.zeros((heads, DK, DV), jnp.float32),
    )
    prefix = prefix_2((transit, offset), "ctx", compose, identity, False)
    incoming_state = prefix[1]
    suffix = prefix_2((jnp.swapaxes(transit, 1, 2), contribution), "ctx", compose, identity, True)
    adjoint_state = suffix[1]
    complete_output = local_output + jnp.einsum(
        "npg,ngj->npj", query_carried_over, incoming_state, precision=largest_value
    )
    attn_out = complete_output.transpose(1, 0, 2).reshape(length, heads * DV).astype(jnp.bfloat16)
    d_mixed = jnp.concatenate(
        [
            jnp.einsum("efu,egu->efg", output_cotangent, incoming_state, precision=largest_value),
            output_cotangent,
        ],
        axis=2,
    )
    d_final = jnp.concatenate(
        [
            jnp.einsum("pgx,pcx->pgc", adjoint_state, incoming_state, precision=largest_value),
            adjoint_state,
        ],
        axis=2,
    )
    d_query, d_key, d_value, grad_beta, grad_decay = pullback((d_mixed, d_final))
    grad_projected = jnp.concatenate([d_query, d_key, d_value], axis=1).astype(jnp.bfloat16)
    window = tokens
    summed = lax.psum_scatter(
        jnp.einsum("td,tc->dc", window, grad_projected, preferred_element_type=jnp.float32).astype(
            jnp.bfloat16
        ),
        "ctx",
        scatter_dimension=0,
        tiled=True,
    ).astype(jnp.float32)
    return (
        attn_out,
        summed[:, :columns],
        summed[:, columns : 2 * columns],
        summed[:, 2 * columns :],
        grad_beta,
        grad_decay,
    )


def device_program(tokens, w_query, *rest):
    ctx = lax.axis_size("ctx")
    heads = w_query.shape[1] // DK
    split = heads == 2 * ctx and ctx == 4 and tokens.shape[0] == CHUNK and w_query.shape[0] * ctx == tokens.shape[1]
    split = split and lax.axis_size("groups") == lax.axis_size("fsdp") == lax.axis_size("head") == 2
    split = split and w_query.shape[0] % 64 == 0
    return (head_split if split else per_device)(tokens, w_query, *rest)


def solution(mesh):
    return jax.shard_map(
        device_program,
        mesh=mesh,
        in_specs=(
            P(("groups", "ctx"), None),
            P("ctx", ("fsdp", "head")),
            P("ctx", ("fsdp", "head")),
            P("ctx", ("fsdp", "head")),
            P(("fsdp", "head"), ("groups", "ctx")),
            P(("groups", "ctx"), ("fsdp", "head")),
            P(("groups", "ctx"), ("fsdp", "head")),
        ),
        out_specs=(
            P(("groups", "ctx"), ("fsdp", "head")),
            P(("groups", "ctx"), ("fsdp", "head")),
            P(("groups", "ctx"), ("fsdp", "head")),
            P(("groups", "ctx"), ("fsdp", "head")),
            P(("fsdp", "head"), ("groups", "ctx")),
            P(("groups", "ctx"), ("fsdp", "head")),
        ),
        check_vma=False,
    )
```
